32 devices in a mesh: dp: 16 (over z, y, x), shard: 2 (over core).
Axes of the slice: x: 2, y: 2, z: 4, core: 2. Of those that a mesh axis runs over, the one named last changes fastest.
Arguments:
- inputs: bfloat16 [32, 768, 576], P(None, ('dp', 'shard')), may hold values from -6 to 6
- cotangent: bfloat16 [32, 768, 576], P(None, ('dp', 'shard')), may hold values from -6 to 6
- lengths: int32 [32], replicated, may hold values from 1 to 768, 14745 in all
- assignment: int32 [32], replicated, may hold values from 0 to 31, each once
- return_order: int32 [32], replicated, may hold values from 0 to 31, each once
- master: float32 [3540096], P('shard'), as said below
- momentum: float32 [3540096], P('shard'), as said below
- average: float32 [3540096], P('shard'), as said below
Outputs:
- block_output: bfloat16 [32, 768, 576], P(None, ('dp', 'shard'))
- input_grad: bfloat16 [32, 768, 576], P(None, ('dp', 'shard'))
- weight_grad: float32 [3540096], P('shard')
- new_momentum: float32 [3540096], P('shard')
- new_master: float32 [3540096], P('shard')
- new_average: float32 [3540096], P('shard')
The draws below stay inside these ranges and needn't reach their ends.
Inputs may be any that keep to these rules, and one draw needn't show every extreme that they name: `lengths`: the longest live length is exactly 768. `assignment`: each slot gets a different sequence. `return_order`: each slot fills one output row. `master`: packed in the weights' order. `momentum`: packed in the weights' order. `average`: packed in the weights' order.
All inputs are finite; a program needn't handle non-finite values.
Results may differ from the reference program's by a relative error of at most 0.017.
The reference program's roundings to bfloat16 on the way count: a program that leaves them out, or rounds other values in their place, can miss the bound.
Values may be sent and summed in bfloat16 or wider, within the bound.
No kernel may reach another device: no remote copies, remote signals or barrier semaphores. Data moves between devices by JAX's collectives and lax.ppermute only.
A program may use at most 192 MiB of HBM per device.

```python
import math
import jax
import jax.numpy as jnp
import numpy as np
from jax import lax

D = 576
H = 9
KV = 3
HD = 64
FF = 1536
L = 768
NSEQ = 32


GRAD_FACTORS = [1.0, 1.0, 0.3, 0.3, 0.5, 0.3, 0.4, 0.4, 0.5]


def segment_list():
    return [(D, 0), (D, 1), (D * H * HD, 2), (D * KV * HD, 3), (D * KV * HD, 4), (H * HD * D, 5), (D * FF, 6), (D * FF, 7), (FF * D, 8)]


def spread_of(segment_kind):
    spreads = [0.0, 0.0, 1.5 * D ** (-0.5), D ** (-0.5), D ** (-0.5), 4.0 * (H * HD) ** (-0.5), D ** (-0.5), D ** (-0.5), 2.0 * FF ** (-0.5)]
    return spreads[segment_kind]


def weight_like(key, salt):
    pieces = []
    for seg_count, segment_kind in segment_list():
        sub_key = jax.random.fold_in(key, salt + segment_kind)
        if segment_kind < 2:
            pieces.append(1.0 + 0.3 * jax.random.uniform(sub_key, (seg_count,), jnp.float32, -1.0, 1.0))
        else:
            pieces.append(spread_of(segment_kind) * jax.random.truncated_normal(sub_key, -4.0, 4.0, (seg_count,), jnp.float32))
    return jnp.concatenate(pieces)


def draw_master(key, part):
    return weight_like(key, 100)


def draw_average(key, part):
    return weight_like(key, 200)


def draw_momentum(key, part):
    grad_unit = 0.8 * (0.6 * L / NSEQ) ** 0.5
    pieces = []
    for seg_count, segment_kind in segment_list():
        sub_key = jax.random.fold_in(key, 300 + segment_kind)
        pieces.append(grad_unit * GRAD_FACTORS[segment_kind] * jax.random.truncated_normal(sub_key, -4.0, 4.0, (seg_count,), jnp.float32))
    return jnp.concatenate(pieces)


def steps_of(rng, extent, cuts, smallest, high):
    gain, own = 1.0, jax.random.fold_in(rng, 6)
    for dim, parts in cuts:
        draws = jnp.exp(jax.random.uniform(jax.random.fold_in(own, dim), (parts,), jnp.float32, smallest / len(cuts), high / len(cuts)))
        gain = gain * jnp.repeat(draws, extent[dim] // parts).reshape([-1 if axis == dim else 1 for axis in range(len(extent))])
    return gain


def profile(number_of, total, most, lean):
    portions = [(1 << 20) // math.isqrt(rank ** lean) + 1 for rank in range(2, number_of + 1)]
    surplus, holding = total - most - (number_of - 1), [1] * (number_of - 1)
    while surplus > 0:
        candidates = [i for i in range(number_of - 1) if holding[i] < most]
        mass, remaining = sum([portions[i] for i in candidates]), surplus
        for i in candidates:
            more = min(most - holding[i], max(1, remaining * portions[i] // mass), surplus)
            holding[i] = holding[i] + more
            surplus = surplus - more
    return np.array([most] + holding)


def ragged_sizes(own_key, count, total, reach, lean):
    if count == 2:
        one = jax.random.randint(own_key, (), max(1, total - reach), min(reach, total - 1) + 1)
        return jnp.stack([one, total - one])
    sizes = jnp.asarray(profile(count, total, reach, lean), jnp.int32)
    couples = (count - 1) // 2
    giver, taker = sizes[1:1 + 2 * couples:2], sizes[2:2 + 2 * couples:2]
    margin = jnp.minimum(giver - 1, reach - taker)
    shifted = jax.random.randint(jax.random.fold_in(own_key, 1), (couples,), 0, 1 << 20) % (margin + 1)
    sizes = sizes.at[1:1 + 2 * couples:2].set(giver - shifted).at[2:2 + 2 * couples:2].set(taker + shifted)
    return sizes[jax.random.permutation(jax.random.fold_in(own_key, 2), count)]


def bell_draw(own_key, extent, spread, limit, split=(), kind=jnp.bfloat16):
    factor_of = steps_of(own_key, extent, split, -0.22, 0.18) if split else 1.0
    array = jax.random.normal(own_key, extent, jnp.float32) * spread * factor_of
    return jnp.minimum(jnp.maximum(array, -limit), limit).astype(kind)


def setup_inputs(seed: int = 0) -> dict:
    arg_keys = jax.random.split(jax.random.key(seed), 9)
    inputs = bell_draw(arg_keys[0], (NSEQ, L, D), 1.0, 6.0, ((1, 32),))
    cotangent = bell_draw(arg_keys[1], (NSEQ, L, D), 1.0, 6.0, ((1, 32),))
    lengths = ragged_sizes(arg_keys[2], NSEQ, NSEQ * L * 3 // 5, L, 2).astype(jnp.int32)
    assignment = jax.random.permutation(arg_keys[3], NSEQ).astype(jnp.int32)
    return_order = jax.random.permutation(arg_keys[4], NSEQ).astype(jnp.int32)
    master = draw_master(jax.random.fold_in(arg_keys[8], 71), 0)
    momentum = draw_momentum(jax.random.fold_in(arg_keys[8], 71), 0)
    average = draw_average(jax.random.fold_in(arg_keys[8], 71), 0)
    return {"inputs": inputs, "cotangent": cotangent, "lengths": lengths, "assignment": assignment, "return_order": return_order, "master": master, "momentum": momentum, "average": average}


EPSILON = 1e-05
MOMENTUM_DECAY = 0.55
AVERAGE_DECAY = 0.45
HIGHEST_PRECISION = lax.Precision.HIGHEST

@jax.custom_vjp
def low(v):
    return lax.optimization_barrier(v.astype(jnp.bfloat16)).astype(jnp.float32)

@jax.custom_vjp
def low_back(v):
    return v

def low_keep(v):
    return (low(v), None)

def low_pass(kept, grad):
    return (grad,)

def back_keep(v):
    return (v, None)

def back_low(kept, grad):
    return (low(grad),)
low.defvjp(low_keep, low_pass)
low_back.defvjp(back_keep, back_low)

def unpack(flat_params):
    shapes = [(D,), (D,), (D, H * HD), (D, KV * HD), (D, KV * HD), (H * HD, D), (D, FF), (D, FF), (FF, D)]
    pieces = []
    offset = 0
    for tensor_shape in shapes:
        length = math.prod(tensor_shape)
        pieces.append(flat_params[offset:offset + length].reshape(tensor_shape))
        offset += length
    return pieces

def rope_tables(seq_len, head_size):
    half_size = head_size // 2
    frequency = jnp.exp(jnp.arange(half_size, dtype=jnp.float32) * (-2.0 * math.log(10000.0) / head_size))
    angles = jnp.arange(seq_len, dtype=jnp.float32)[:, None] * frequency[None, :]
    return (jnp.cos(angles), jnp.sin(angles))

def rotate(tensor, cosine, sine_val):
    half_size = tensor.shape[-1] // 2
    first_half = tensor[..., :half_size]
    second_half = tensor[..., half_size:]
    cosine = cosine[:, None, :]
    sine_val = sine_val[:, None, :]
    return jnp.concatenate([first_half * cosine - second_half * sine_val, second_half * cosine + first_half * sine_val], axis=-1)

def product(left_op, right_op):
    return jnp.dot(left_op, right_op, precision=HIGHEST_PRECISION)

def layer_forward(params, stream, live_len):
    g_attn, g_mlp, w_query, w_key, w_value, w_out, w_gate, w_up, w_down = params
    group_size = H // KV
    cosine, sine_val = rope_tables(L, HD)
    position = jnp.arange(L, dtype=jnp.int32)
    live_rows = (position < live_len).astype(jnp.float32)[:, None]
    allowed = (position[None, :] <= position[:, None]) & (position[None, :] < live_len)
    norm_attn = lax.rsqrt(lax.optimization_barrier(jnp.mean(stream * stream, axis=-1, keepdims=True)) + EPSILON)
    normed = low(stream * norm_attn * g_attn)
    queries = low_back(product(normed, w_query))
    keys_lin = low_back(product(normed, w_key))
    values = low(low_back(product(normed, w_value))).reshape(L, KV, HD)
    queries_rot = low(rotate(queries.reshape(L, H, HD), cosine, sine_val)).reshape(L, KV, group_size, HD)
    keys_rot = low(rotate(keys_lin.reshape(L, KV, HD), cosine, sine_val))
    scores = jnp.einsum('ikgd,jkd->kgij', queries_rot, keys_rot, precision=HIGHEST_PRECISION) * HD ** (-0.5)
    scores = low_back(jnp.where(allowed[None, None], scores, -1000000000.0))
    row_max = lax.optimization_barrier(jnp.max(scores, axis=-1, keepdims=True))
    exponent = jnp.exp(scores - row_max)
    attn_prob = exponent / lax.optimization_barrier(jnp.sum(exponent, axis=-1, keepdims=True))
    attn_mixed = jnp.einsum('kgij,jkd->ikgd', low(attn_prob), values, precision=HIGHEST_PRECISION)
    attn_mixed = low(low_back(attn_mixed.reshape(L, H * HD)))
    hidden1 = stream + low_back(product(attn_mixed, w_out))
    norm_mlp = lax.rsqrt(lax.optimization_barrier(jnp.mean(hidden1 * hidden1, axis=-1, keepdims=True)) + EPSILON)
    normed2 = low(hidden1 * norm_mlp * g_mlp)
    gate_val = low_back(product(normed2, w_gate))
    up_val = low_back(product(normed2, w_up))
    inner_act = low(jax.nn.silu(gate_val) * up_val)
    return (hidden1 + low_back(product(inner_act, w_down))) * live_rows

def add_pair(summed, addend):
    return summed + addend

def reference(inputs, cotangent, lengths, assignment, return_order, master, momentum, average):
    params = unpack(low(master))
    forward = jax.checkpoint(layer_forward)

    def one_sequence(running, row_id):
        my_slot = return_order[row_id]
        sequence = assignment[my_slot]
        live_len = lengths[sequence]
        seq_in = inputs[sequence].astype(jnp.float32)

        def apply_layer(weights, stream):
            return forward(weights, stream, live_len)
        result, pullback = jax.vjp(apply_layer, params, seq_in)
        grads, d_stream = pullback(cotangent[row_id].astype(jnp.float32))
        running = jax.tree.map(add_pair, running, grads)
        return (running, (result.astype(jnp.bfloat16), d_stream.astype(jnp.bfloat16)))
    initial = [jnp.zeros_like(tensor) for tensor in params]
    totals, (block_output, input_grad) = lax.scan(one_sequence, initial, jnp.arange(NSEQ, dtype=jnp.int32))
    weight_grad = jnp.concatenate([tensor.reshape(-1) for tensor in totals]) / NSEQ
    learning = (NSEQ / (0.6 * L)) ** 0.5 / D ** 0.5
    new_momentum = MOMENTUM_DECAY * momentum + weight_grad
    new_master = master - learning * (weight_grad + MOMENTUM_DECAY * new_momentum)
    new_average = AVERAGE_DECAY * average + (1.0 - AVERAGE_DECAY) * new_master
    return (block_output, input_grad, weight_grad, new_momentum, new_master, new_average)
```

```python
import functools
import math

import jax
import jax.numpy as jnp
from jax import lax
from jax.experimental import pallas as pl
from jax.experimental.pallas import tpu as pltpu
from jax.sharding import PartitionSpec as P

D = 576
H = 9
KV = 3
HD = 64
FF = 1536
LANES = 128
BLOCK = 256
Q_TILES = 5
PAD_D = Q_TILES * LANES
KV_COLS = 2 * KV * HD
FF_TILES = FF // LANES
ATT_TILES = 12
ATT_ROWS = 6 * D + LANES
MLP_ROWS = 18 * D
FLAT_ROWS = 27657
HALF = FLAT_ROWS * LANES // 2
OUT_ROWS = 13832

EPSILON = 1e-05
MOMENTUM_DECAY = 0.55
AVERAGE_DECAY = 0.45
MASKED = -1000000000.0

BF = jnp.bfloat16
F32 = jnp.float32
VMEM_LIMIT = 60 * 1024 * 1024


def nn(a, b):
    return jnp.dot(a, b, preferred_element_type=F32)


def nt(a, b):
    return lax.dot_general(a, b, (((1,), (1,)), ((), ())), preferred_element_type=F32)


def tn(a, b):
    return lax.dot_general(a, b, (((0,), (0,)), ((), ())), preferred_element_type=F32)


def tile(value, index):
    return value[:, index * LANES : (index + 1) * LANES]


def low_half(rows):
    return lax.broadcasted_iota(jnp.int32, (rows, LANES), 1) < HD


def swap_halves(value):
    lane = lax.broadcasted_iota(jnp.int32, value.shape, 1)
    return jnp.where(lane % HD < HD // 2, pltpu.roll(value, 96, 1), pltpu.roll(value, 32, 1))


def flip(value):
    return pltpu.roll(value, HD, 1)


def rms(value):
    return lax.rsqrt(jnp.mean(value * value, axis=-1, keepdims=True) + EPSILON)


def attention_forward(
    x_ref, ga_ref, wq_ref, wkv_ref, wo_ref, cos_ref, sin_ref,
    h1_ref, mixed_ref, q_ref, k_ref, v_ref, lse_ref, o_acc,
):
    seq_len = x_ref.shape[0]
    low = low_half(BLOCK)

    def project(b, carry):
        rows = pl.ds(pl.multiple_of(b * BLOCK, BLOCK), BLOCK)
        stream = x_ref[rows, :].astype(F32)
        normed = (stream * rms(stream) * ga_ref[...]).astype(BF)
        cosine = cos_ref[rows, :]
        sine = sin_ref[rows, :]

        def rope(value):
            return value * cosine + swap_halves(value) * sine

        queries = nn(normed, wq_ref[...])
        for j in range(Q_TILES):
            q_ref[j, rows, :] = (rope(tile(queries, j)) * HD ** (-0.5)).astype(BF)
        keys_values = nn(normed, wkv_ref[...])
        first = rope(tile(keys_values, 0))
        second = tile(keys_values, 1)
        third = tile(keys_values, 2)
        mid = rope(second)

        def put(ref, index, value):
            ref[index, rows, :] = value.astype(BF)

        put(k_ref, 0, jnp.where(low, first, 0.0))
        put(k_ref, 1, jnp.where(low, 0.0, flip(first)))
        put(k_ref, 2, jnp.where(low, flip(first), 0.0))
        put(k_ref, 3, jnp.where(low, 0.0, first))
        put(k_ref, 4, jnp.where(low, mid, 0.0))
        put(k_ref, 5, jnp.where(low, 0.0, flip(mid)))
        put(v_ref, 0, jnp.where(low, flip(second), 0.0))
        put(v_ref, 1, jnp.where(low, 0.0, second))
        put(v_ref, 2, jnp.where(low, third, 0.0))
        put(v_ref, 3, jnp.where(low, 0.0, flip(third)))
        put(v_ref, 4, jnp.where(low, flip(third), 0.0))
        put(v_ref, 5, jnp.where(low, 0.0, third))
        return carry

    lax.fori_loop(0, seq_len // BLOCK, project, 0)
    lane = lax.broadcasted_iota(jnp.int32, (BLOCK, LANES), 1)
    keep = lax.broadcasted_iota(jnp.int32, (BLOCK, BLOCK), 1) <= lax.broadcasted_iota(
        jnp.int32, (BLOCK, BLOCK), 0
    )
    for b in range(seq_len // BLOCK):
        rows = slice(b * BLOCK, (b + 1) * BLOCK)
        n_keys = (b + 1) * BLOCK
        o_acc[...] = jnp.zeros_like(o_acc)

        def group(g, lse, rows=rows, n_keys=n_keys):
            for u in range(3):
                head = 3 * g + u
                j = head // 2
                side = 2 * g + head % 2
                scores = nt(q_ref[j, rows, :], k_ref[side, 0:n_keys, :])
                diag = jnp.where(keep, scores[:, n_keys - BLOCK :], MASKED)
                if n_keys > BLOCK:
                    scores = jnp.concatenate([scores[:, : n_keys - BLOCK], diag], axis=1)
                else:
                    scores = diag
                row_max = jnp.max(scores, axis=-1, keepdims=True)
                exponent = jnp.exp(scores - row_max)
                total = jnp.sum(exponent, axis=-1, keepdims=True)
                prob = (exponent * (1.0 / total)).astype(BF)
                o_acc[j] += nn(prob, v_ref[side, 0:n_keys, :])
                lse = jnp.where(lane == head, row_max + jnp.log(total), lse)
            return lse

        lse = lax.fori_loop(0, KV, group, jnp.zeros((BLOCK, LANES), F32))
        lse_ref[:, rows] = lse.T[:16]
        mixed = jnp.concatenate([o_acc[j].astype(BF) for j in range(Q_TILES)], axis=1)
        mixed_ref[rows, :] = mixed
        h1_ref[rows, :] = x_ref[rows, :].astype(F32) + nn(mixed, wo_ref[...])


def mlp_pass(
    core_ref, n_ref, h1_ref, cot_ref, gm_ref, wg_ref, wu_ref, wd_ref,
    out_ref, dh1_ref, ggm_ref, keep_ref, send_ref,
    nm_s, inner_s, back_s, dg_s, du_s, grads, sem,
):
    seq_len = h1_ref.shape[0]
    core = core_ref[0]
    live_len = n_ref[0]

    def block(b, ggm):
        start = pl.multiple_of(b * BLOCK, BLOCK)
        rows = pl.ds(start, BLOCK)
        hidden1 = h1_ref[rows, :]
        r2 = rms(hidden1)
        gain = gm_ref[...]
        normed2 = (hidden1 * r2 * gain).astype(BF)
        nm_s[rows, :] = normed2
        live = (
            start + lax.broadcasted_iota(jnp.int32, (BLOCK, 1), 0) < live_len
        ).astype(F32)
        gate = nn(normed2, wg_ref[...])
        up = nn(normed2, wu_ref[...])
        sig = jax.nn.sigmoid(gate)
        silu = gate * sig
        inner = (silu * up).astype(BF)
        inner_s[rows, :] = inner
        out_ref[rows, :] = ((hidden1 + nn(inner, wd_ref[...])) * live).astype(BF)
        back = cot_ref[rows, :].astype(F32) * live
        back_low = back.astype(BF)
        back_s[rows, :] = back_low
        d_inner = nt(back_low, wd_ref[...])
        d_gate = (d_inner * up * sig * (1.0 + gate * (1.0 - sig))).astype(BF)
        d_up = (d_inner * silu).astype(BF)
        dg_s[rows, :] = d_gate
        du_s[rows, :] = d_up
        d_normed2 = nt(d_gate, wg_ref[...]) + nt(d_up, wu_ref[...])
        scaled = d_normed2 * gain
        dh1_ref[rows, :] = (
            back
            + r2 * scaled
            - hidden1 * (r2 * r2 * r2) * jnp.mean(scaled * hidden1, axis=-1, keepdims=True)
        )
        return ggm + jnp.sum(d_normed2 * hidden1 * r2, axis=0, keepdims=True)

    ggm_ref[...] = lax.fori_loop(0, seq_len // BLOCK, block, jnp.zeros((1, D), F32))

    def weights(c, carry):
        cols = pl.ds(pl.multiple_of(c * 2 * LANES, 2 * LANES), 2 * LANES)
        normed2 = nm_s[...]
        grad_gate = tn(normed2, dg_s[:, cols]).astype(BF)
        grad_up = tn(normed2, du_s[:, cols]).astype(BF)
        grad_down = tn(back_s[...], inner_s[:, cols]).astype(BF)
        part = c // 3
        for t in range(2):
            grads[0, 2 * c + t] = tile(grad_gate, t)
            grads[1, 2 * c + t] = tile(grad_up, t)
            grads[part, FF_TILES + 2 * (c - 3 * part) + t] = tile(grad_down, t)
        return carry

    lax.fori_loop(0, FF_TILES // 2, weights, 0)
    first = pltpu.make_async_copy(grads.at[1 - core], send_ref, sem.at[0])
    second = pltpu.make_async_copy(grads.at[core], keep_ref, sem.at[1])
    first.start()
    second.start()
    first.wait()
    second.wait()


def attention_backward(
    core_ref, x_ref, ga_ref, dh1_ref, mixed_ref, q_ref, k_ref, v_ref, lse_ref,
    wq_ref, wkv_ref, wo_ref, cos_ref, sin_ref, ggm_ref,
    dx_ref, keep_ref, send_ref,
    dm_s, dq_acc, dk_acc, dv_acc, dq_s, dkv_s, nm_s, da_s, grads, sem,
):
    seq_len = x_ref.shape[0]
    n_blocks = seq_len // BLOCK
    core = core_ref[0]
    low = low_half(BLOCK)

    def prepare(b, carry):
        rows = pl.ds(pl.multiple_of(b * BLOCK, BLOCK), BLOCK)
        d_attn = dh1_ref[rows, :].astype(BF)
        da_s[rows, :] = d_attn
        d_mixed = nt(d_attn, wo_ref[...]).astype(BF)
        for j in range(Q_TILES):
            dm_s[j, rows, :] = tile(d_mixed, j)
        stream = x_ref[rows, :].astype(F32)
        nm_s[rows, :] = (stream * rms(stream) * ga_ref[...]).astype(BF)
        return carry

    lax.fori_loop(0, n_blocks, prepare, 0)
    dq_acc[...] = jnp.zeros_like(dq_acc)
    dk_acc[...] = jnp.zeros_like(dk_acc)
    dv_acc[...] = jnp.zeros_like(dv_acc)
    keep = lax.broadcasted_iota(jnp.int32, (BLOCK, BLOCK), 0) <= lax.broadcasted_iota(
        jnp.int32, (BLOCK, BLOCK), 1
    )
    for b in range(n_blocks):
        rows = slice(b * BLOCK, (b + 1) * BLOCK)
        n_keys = (b + 1) * BLOCK

        def group(g, carry, rows=rows, n_keys=n_keys):
            for u in range(3):
                head = 3 * g + u
                j = head // 2
                side = 2 * g + head % 2
                queries = q_ref[j, rows, :]
                d_mixed = dm_s[j, rows, :]
                keys = k_ref[side, 0:n_keys, :]
                values = v_ref[side, 0:n_keys, :]
                prob = jnp.exp(nt(keys, queries) - lse_ref[pl.ds(head, 1), rows])
                diag = jnp.where(keep, prob[n_keys - BLOCK :, :], 0.0)
                if n_keys > BLOCK:
                    prob = jnp.concatenate([prob[: n_keys - BLOCK, :], diag], axis=0)
                else:
                    prob = diag
                d_prob = nt(values, d_mixed)
                delta = jnp.sum(d_prob * prob, axis=0, keepdims=True)
                d_score = (prob * (d_prob - delta)).astype(BF)
                dv_acc[side, 0:n_keys, :] += nn(prob.astype(BF), d_mixed)
                dk_acc[side, 0:n_keys, :] += nn(d_score, queries)
                dq_acc[j, rows, :] += tn(d_score, keys)
            return carry

        lax.fori_loop(0, KV, group, 0)

    def finish(b, gga):
        rows = pl.ds(pl.multiple_of(b * BLOCK, BLOCK), BLOCK)
        cosine = cos_ref[rows, :]
        sine = sin_ref[rows, :]

        def unrope(value):
            return value * cosine - swap_halves(value) * sine

        for j in range(Q_TILES):
            d_query = unrope(dq_acc[j, rows, :]) * HD ** (-0.5)
            dq_s[rows, j * LANES : (j + 1) * LANES] = d_query.astype(BF)
        dk = [dk_acc[i, rows, :] for i in range(6)]
        dv = [dv_acc[i, rows, :] for i in range(6)]
        first = jnp.where(low, dk[0] + flip(dk[1]), flip(dk[2]) + dk[3])
        mid = unrope(dk[4] + flip(dk[5]))
        second = jnp.where(low, mid, flip(dv[0]) + dv[1])
        third = jnp.where(low, dv[2] + flip(dv[3]), flip(dv[4]) + dv[5])
        dkv_s[rows, 0:LANES] = unrope(first).astype(BF)
        dkv_s[rows, LANES : 2 * LANES] = second.astype(BF)
        dkv_s[rows, 2 * LANES :] = third.astype(BF)
        d_normed = nt(dq_s[rows, :], wq_ref[...]) + nt(dkv_s[rows, :], wkv_ref[...])
        stream = x_ref[rows, :].astype(F32)
        r1 = rms(stream)
        scaled = d_normed * ga_ref[...]
        dx_ref[rows, :] = (
            dh1_ref[rows, :]
            + r1 * scaled
            - stream * (r1 * r1 * r1) * jnp.mean(scaled * stream, axis=-1, keepdims=True)
        ).astype(BF)
        return gga + jnp.sum(d_normed * stream * r1, axis=0, keepdims=True)

    gga = lax.fori_loop(0, n_blocks, finish, jnp.zeros((1, D), F32))
    grads[...] = jnp.zeros_like(grads)

    def slot(index):
        return index // 6, pl.ds((index % 6) * D, D)

    def put(index, value):
        half, rows = slot(index)
        grads[half, rows, :] = value.astype(BF)

    grad_q = tn(nm_s[...], dq_s[...])
    grad_o = tn(mixed_ref[...], da_s[...])[:D]
    for t in range(4):
        put(t, tile(grad_q, t))
        put(5 + t, tile(grad_o, t))
    put(4, jnp.concatenate([grad_q[:, 4 * LANES : D], grad_o[:, 4 * LANES : D]], axis=1))
    grad_kv = tn(nm_s[...], dkv_s[...])
    for t in range(3):
        put(9 + t, tile(grad_kv, t))
    base = 6 * D
    for row, value in ((0, gga), (16, ggm_ref[...])):
        for t in range(Q_TILES):
            width = min(LANES, D - t * LANES)
            piece = value[:, t * LANES : t * LANES + width]
            if width < LANES:
                piece = jnp.concatenate([piece, jnp.zeros((1, LANES - width), F32)], axis=1)
            whole = jnp.where(
                lax.broadcasted_iota(jnp.int32, (16, LANES), 0) == t,
                jnp.broadcast_to(piece, (16, LANES)),
                0.0 if t == 0 else whole,
            )
        grads[0, base + row : base + row + 16, :] = whole.astype(BF)
    first = pltpu.make_async_copy(grads.at[1 - core], send_ref, sem.at[0])
    second = pltpu.make_async_copy(grads.at[core], keep_ref, sem.at[1])
    first.start()
    second.start()
    first.wait()
    second.wait()


def flatten_gradient(core_ref, mlp_ref, att_ref, swap_ref, out_ref, flat, tmp):
    core = core_ref[0]

    def store(row, count, stride, value):
        flat[pl.ds(row, count, stride=stride), :] = value

    def split_rows(values, rows):
        for index, value in enumerate(values):
            tmp[pl.ds(index * D, rows), :] = value
        even = [tmp[pl.ds(i * D, rows // 2, stride=2), :] for i in range(len(values))]
        odd = [tmp[pl.ds(i * D + 1, rows // 2, stride=2), :] for i in range(len(values))]
        return even, odd

    def put_wide(values, rows, row):
        even, odd = split_rows(values, rows)
        low = low_half(rows // 2)
        turned = [flip(value) for value in odd]
        for c in range(4):
            store(row + c, rows // 2, 9, even[c])
        store(row + 4, rows // 2, 9, jnp.where(low, even[4], turned[0]))
        for c in range(4):
            store(row + 5 + c, rows // 2, 9, jnp.where(low, turned[c], turned[c + 1]))

    @pl.when(core == 0)
    def _():
        def attention(index):
            ref = att_ref if index < 6 else swap_ref
            return ref[pl.ds((index % 6) * D, D), :].astype(F32)

        base = 6 * D
        gain_a = att_ref[base : base + 16, :].astype(F32)
        gain_m = flip(att_ref[base + 16 : base + 32, :].astype(F32))
        low16 = low_half(1)
        for r in range(4):
            flat[r : r + 1, :] = gain_a[r : r + 1]
        flat[4:5, :] = jnp.where(low16, gain_a[4:5], gain_m[0:1])
        for r in range(4):
            flat[5 + r : 6 + r, :] = jnp.where(low16, gain_m[r : r + 1], gain_m[r + 1 : r + 2])
        shared = attention(4)
        put_wide([attention(t) for t in range(4)] + [shared], D, 9)
        put_wide([attention(5 + t) for t in range(4)] + [flip(shared)], D, 4329)
        even, odd = split_rows([attention(9 + t) for t in range(3)], D)
        low = low_half(D // 2)
        a, b, c = even
        store(2601, D // 2, 3, a)
        store(2602, D // 2, 3, jnp.where(low, b, flip(odd[0])))
        store(2603, D // 2, 3, jnp.where(low, flip(odd[0]), flip(odd[1])))
        store(3465, D // 2, 3, jnp.where(low, flip(b), flip(c)))
        store(3466, D // 2, 3, jnp.where(low, flip(c), odd[1]))
        store(3467, D // 2, 3, odd[2])
        for t in range(FF_TILES):
            store(6921 + t, D, FF_TILES, mlp_ref[t * D : (t + 1) * D, :].astype(F32))
        out_ref[...] = flat[0:OUT_ROWS, :].astype(BF)

    @pl.when(core == 1)
    def _():
        base = 6 * D
        flat[0:8, :] = swap_ref[base : base + 16, :].astype(F32)[0:8]
        for t in range(FF_TILES):
            store(5 + t, D, FF_TILES, mlp_ref[t * D : (t + 1) * D, :].astype(F32))
        for t in range(FF_TILES):
            ref, start = (swap_ref, t * D) if t < 6 else (mlp_ref, (FF_TILES + t - 6) * D)
            whole = ref[start : start + D, :].astype(F32)
            pieces = [whole[c * LANES : (c + 1) * LANES].T for c in range(4)]
            last = jnp.concatenate([whole[4 * LANES :], jnp.zeros((LANES - HD, LANES), F32)], axis=0)
            put_wide(pieces + [last.T], LANES, 6917 + 9 * HD * t)

        def shift(i, carry):
            rows = 8 * 133
            start = pl.multiple_of(i * rows, rows)
            low = low_half(rows)
            here = flip(flat[pl.ds(start, rows), :])
            after = flip(flat[pl.ds(start + 1, rows), :])
            out_ref[pl.ds(start, rows), :] = jnp.where(low, here, after).astype(BF)
            return carry

        lax.fori_loop(0, OUT_ROWS // (8 * 133), shift, 0)


def vmem():
    return pl.BlockSpec(memory_space=pltpu.VMEM)


def smem():
    return pl.BlockSpec(memory_space=pltpu.SMEM)


def hbm():
    return pl.BlockSpec(memory_space=pl.ANY)


def call(kernel, outs, in_specs, out_specs, scratch, flops, name):
    n_bytes = sum(math.prod(shape) * jnp.dtype(kind).itemsize for shape, kind in outs)
    return pl.pallas_call(
        kernel,
        out_shape=[jax.ShapeDtypeStruct(shape, kind) for shape, kind in outs],
        in_specs=in_specs,
        out_specs=out_specs,
        scratch_shapes=scratch,
        compiler_params=pltpu.CompilerParams(vmem_limit_bytes=VMEM_LIMIT),
        cost_estimate=pl.CostEstimate(
            flops=int(flops), bytes_accessed=int(2 * n_bytes), transcendentals=0
        ),
        name=name,
    )


def rope_tables(seq_len):
    lane = jnp.arange(LANES, dtype=jnp.int32)
    which = (lane % (HD // 2)).astype(F32)
    frequency = jnp.exp(which * (-2.0 * math.log(10000.0) / HD))
    angles = jnp.arange(seq_len, dtype=F32)[:, None] * frequency[None, :]
    sign = jnp.where(lane % HD < HD // 2, -1.0, 1.0)
    return jnp.cos(angles), jnp.sin(angles) * sign[None, :]


def run_attention_forward(x, gain, wq, wkv, wo, cosine, sine):
    seq_len = x.shape[0]
    outs = [
        ((seq_len, D), F32),
        ((seq_len, PAD_D), BF),
        ((Q_TILES, seq_len, LANES), BF),
        ((6, seq_len, LANES), BF),
        ((6, seq_len, LANES), BF),
        ((16, seq_len), F32),
    ]
    return call(
        attention_forward,
        outs,
        [vmem()] * 7,
        [vmem()] * 6,
        [pltpu.VMEM((Q_TILES, BLOCK, LANES), F32)],
        1.2e10,
        "attention_forward",
    )(x, gain, wq, wkv, wo, cosine, sine)


def run_mlp(core, live_len, hidden1, cot, gain, wg, wu, wd):
    seq_len = hidden1.shape[0]
    outs = [
        ((seq_len, D), BF),
        ((seq_len, D), F32),
        ((1, D), F32),
        ((18, D, LANES), BF),
        ((18, D, LANES), BF),
    ]
    return call(
        mlp_pass,
        outs,
        [smem()] * 2 + [vmem()] * 6,
        [vmem()] * 3 + [hbm()] * 2,
        [
            pltpu.VMEM((seq_len, D), BF),
            pltpu.VMEM((seq_len, FF), BF),
            pltpu.VMEM((seq_len, D), BF),
            pltpu.VMEM((seq_len, FF), BF),
            pltpu.VMEM((seq_len, FF), BF),
            pltpu.VMEM((2, 18, D, LANES), BF),
            pltpu.SemaphoreType.DMA((2,)),
        ],
        2.0e10,
        "mlp_pass",
    )(core, live_len, hidden1, cot, gain, wg, wu, wd)


def run_attention_backward(core, x, gain, dh1, mixed, q, k, v, lse, wq, wkv, wo, cosine, sine, ggm):
    seq_len = x.shape[0]
    outs = [((seq_len, D), BF), ((ATT_ROWS, LANES), BF), ((ATT_ROWS, LANES), BF)]
    return call(
        attention_backward,
        outs,
        [smem()] + [vmem()] * 14,
        [vmem()] + [hbm()] * 2,
        [
            pltpu.VMEM((Q_TILES, seq_len, LANES), BF),
            pltpu.VMEM((Q_TILES, seq_len, LANES), F32),
            pltpu.VMEM((6, seq_len, LANES), F32),
            pltpu.VMEM((6, seq_len, LANES), F32),
            pltpu.VMEM((seq_len, PAD_D), BF),
            pltpu.VMEM((seq_len, KV_COLS), BF),
            pltpu.VMEM((seq_len, D), BF),
            pltpu.VMEM((seq_len, D), BF),
            pltpu.VMEM((2, ATT_ROWS, LANES), BF),
            pltpu.SemaphoreType.DMA((2,)),
        ],
        3.0e10,
        "attention_backward",
    )(core, x, gain, dh1, mixed, q, k, v, lse, wq, wkv, wo, cosine, sine, ggm)


def run_flatten(core, mlp, att, swap):
    return call(
        flatten_gradient,
        [((OUT_ROWS, LANES), BF)],
        [smem()] + [vmem()] * 3,
        [vmem()],
        [pltpu.VMEM((13848, LANES), F32), pltpu.VMEM((Q_TILES * D, LANES), F32)],
        1e9,
        "flatten_gradient",
    )(core, mlp, att, swap)[0]


def add_low(a, b):
    return (a.astype(F32) + b.astype(F32)).astype(BF)


def sum_over_dp(parts):
    size = lax.axis_size("dp")
    index = lax.axis_index("dp")
    n_bits = size.bit_length() - 1

    def swap(value, bit):
        return lax.ppermute(value, "dp", [(i, i ^ (1 << bit)) for i in range(size)])

    values = [value for value, _ in parts]
    for step in range(n_bits):
        for p, (_, order) in enumerate(parts):
            bit = order[step]
            mine = (index >> bit) & 1
            halves = values[p].reshape(2, values[p].shape[0] // 2, LANES)
            sent = lax.dynamic_index_in_dim(halves, 1 - mine, 0, keepdims=False)
            kept = lax.dynamic_index_in_dim(halves, mine, 0, keepdims=False)
            values[p] = add_low(kept, swap(sent, bit))
    for step in reversed(range(n_bits)):
        for p, (_, order) in enumerate(parts):
            bit = order[step]
            mine = (index >> bit) & 1
            got = swap(values[p], bit)
            values[p] = jnp.where(
                mine == 0,
                jnp.concatenate([values[p], got], axis=0),
                jnp.concatenate([got, values[p]], axis=0),
            )
    return values


def bit_orders():
    n_bits = lax.axis_size("dp").bit_length() - 1
    base = list(range(n_bits))
    head = base[:3] if n_bits >= 3 else base
    return [head[r:] + head[:r] + base[len(head) :] for r in range(3)]


def swap_cores(value):
    return lax.ppermute(value, "shard", [(0, 1), (1, 0)])


def on_device(inputs, cotangent, lengths, assignment, return_order, master, momentum, average):
    nseq_all, block_rows, _ = inputs.shape
    axes = ("dp", "shard")
    seq_len = block_rows * lax.axis_size("dp") * lax.axis_size("shard")
    my_slot = lax.axis_index(axes)
    core = lax.axis_index("shard")
    core_arr = core.astype(jnp.int32).reshape(1)

    seq_ids = jnp.arange(nseq_all, dtype=jnp.int32)
    inverse = jnp.sum(
        jnp.where(return_order[None, :] == seq_ids[:, None], seq_ids[None, :], 0), axis=1
    )

    def exchange(value):
        return lax.all_to_all(value, axes, split_axis=0, concat_axis=0, tiled=True)

    x = exchange(jnp.take(inputs, assignment, axis=0)).reshape(seq_len, D)
    cot = exchange(jnp.take(cotangent, inverse, axis=0)).reshape(seq_len, D)
    my_sequence = jnp.sum(jnp.where(seq_ids == my_slot, assignment, 0))
    live_len = jnp.sum(jnp.where(seq_ids == my_sequence, lengths, 0)).reshape(1)

    own = master.astype(BF)
    other = swap_cores(own)
    first = jnp.where(core == 0, own, other)
    second = jnp.where(core == 0, other, own)
    gain_attn = first[:D].astype(F32).reshape(1, D)
    gain_mlp = first[D : 2 * D].astype(F32).reshape(1, D)
    offset = 2 * D
    pieces = []
    for rows, cols in ((D, D), (D, KV * HD), (D, KV * HD), (D, D)):
        pieces.append(first[offset : offset + rows * cols].reshape(rows, cols))
        offset += rows * cols
    wq = jnp.pad(pieces[0], ((0, 0), (0, PAD_D - D)))
    wkv = jnp.concatenate([pieces[1], pieces[2]], axis=1)
    wo = jnp.pad(pieces[3], ((0, PAD_D - D), (0, 0)))
    tail = D
    wg = jnp.concatenate([first[offset:], second[:tail]]).reshape(D, FF)
    wu = second[tail : tail + D * FF].reshape(D, FF)
    wd = second[tail + D * FF :].reshape(FF, D)

    cosine, sine = rope_tables(seq_len)
    hidden1, mixed, q, k, v, lse = run_attention_forward(x, gain_attn, wq, wkv, wo, cosine, sine)
    result, dh1, ggm, mlp_keep, mlp_send = run_mlp(
        core_arr, live_len, hidden1, cot, gain_mlp, wg, wu, wd
    )
    back_out = exchange(result.reshape(nseq_all, block_rows, D))
    mlp = add_low(mlp_keep, swap_cores(mlp_send)).reshape(3, MLP_ROWS // 3, LANES)
    orders = bit_orders()
    mlp = jnp.concatenate(sum_over_dp([(mlp[p], orders[p]) for p in range(3)]), axis=0)

    d_stream, att_keep, att_send = run_attention_backward(
        core_arr, x, gain_attn, dh1, mixed, q, k, v, lse, wq, wkv, wo, cosine, sine, ggm
    )
    back_grad = exchange(d_stream.reshape(nseq_all, block_rows, D))
    att = add_low(att_keep, swap_cores(att_send))
    att = sum_over_dp([(att, orders[0])])[0]

    gate_tail = mlp.reshape(18, D, LANES)[7:12, D - 1, :]
    from_zero = jnp.concatenate(
        [mlp[FF_TILES * D :], jnp.pad(gate_tail, ((0, LANES - 5), (0, 0)))], axis=0
    )
    swapped = swap_cores(jnp.where(core == 0, from_zero, att))
    flat = run_flatten(core_arr, mlp, att, swapped).reshape(-1)[: master.shape[0]]

    weight_grad = flat.astype(F32) / nseq_all
    learning = (nseq_all / (0.6 * seq_len)) ** 0.5 / D**0.5
    new_momentum = MOMENTUM_DECAY * momentum + weight_grad
    new_master = master - learning * (weight_grad + MOMENTUM_DECAY * new_momentum)
    new_average = AVERAGE_DECAY * average + (1.0 - AVERAGE_DECAY) * new_master
    block_output = jnp.take(back_out, return_order, axis=0)
    input_grad = jnp.take(back_grad, return_order, axis=0)
    return (block_output, input_grad, weight_grad, new_momentum, new_master, new_average)


def solution(mesh):
    rows = P(None, ("dp", "shard"), None)
    flat = P("shard")
    return jax.shard_map(
        on_device,
        mesh=mesh,
        in_specs=(rows, rows, P(), P(), P(), flat, flat, flat),
        out_specs=(rows, rows, flat, flat, flat, flat),
        check_vma=False,
    )
```

```python
import functools
import math

import jax
import jax.numpy as jnp
from jax import lax
from jax.experimental import pallas as pl
from jax.experimental.pallas import tpu as pltpu
from jax.sharding import PartitionSpec as P

D = 576
H = 9
KV = 3
HD = 64
FF = 1536
LANES = 128
BLOCK = 256
Q_TILES = 5
PAD_D = Q_TILES * LANES
KV_COLS = 2 * KV * HD
FF_TILES = FF // LANES
DOWN_FIRST = 4
EARLY_TILES = 21
EARLY_ROWS = 12288
EXTRA = EARLY_TILES * D
HALF = 27657 * LANES // 2
PART_ROWS = EARLY_ROWS // 3
SWAP_START = EXTRA - DOWN_FIRST * D - 2 * PART_ROWS
SWAP_TAIL = EXTRA + 16 - 2 * PART_ROWS
REST_FIRST = 2 * PART_ROWS - FF_TILES * D
REST_SLOT = REST_FIRST + 16
REST = REST_SLOT + 16
LATE_HALF = 2432
HALF_ROWS = 13832
FLAT_SCRATCH = 13848
O_ROW = 4329
GATE_ROW = 6921
MLP_COLS = 256
MLP_BLOCK = 256
CHUNK = 576
STEP = 288
LATE_CHUNKS = 7

EPSILON = 1e-05
MOMENTUM_DECAY = 0.55
AVERAGE_DECAY = 0.45
MASKED = -1000000000.0

BF = jnp.bfloat16
F32 = jnp.float32
MIB = 1024 * 1024


def nn(a, b):
    return jnp.dot(a, b, preferred_element_type=F32)


def nt(a, b):
    return lax.dot_general(a, b, (((1,), (1,)), ((), ())), preferred_element_type=F32)


def tn(a, b):
    return lax.dot_general(a, b, (((0,), (0,)), ((), ())), preferred_element_type=F32)


def tile(value, index):
    return value[:, index * LANES : (index + 1) * LANES]


def low_half(rows):
    return lax.broadcasted_iota(jnp.int32, (rows, LANES), 1) < HD


def swap_halves(value):
    lane = lax.broadcasted_iota(jnp.int32, value.shape, 1)
    return jnp.where(lane % HD < HD // 2, pltpu.roll(value, 96, 1), pltpu.roll(value, 32, 1))


def flip(value):
    return pltpu.roll(value, HD, 1)


def rms(value):
    return lax.rsqrt(jnp.mean(value * value, axis=-1, keepdims=True) + EPSILON)


def attention_forward(
    x_ref, ga_ref, wq_ref, wkv_ref, wo_ref, cos_ref, sin_ref,
    h1_ref, mixed_ref, q_ref, k_ref, v_ref, lse_ref, o_acc,
):
    seq_len = x_ref.shape[0]
    low = low_half(BLOCK)

    def project(b, carry):
        rows = pl.ds(pl.multiple_of(b * BLOCK, BLOCK), BLOCK)
        stream = x_ref[rows, :].astype(F32)
        normed = (stream * rms(stream) * ga_ref[...]).astype(BF)
        cosine = cos_ref[rows, :]
        sine = sin_ref[rows, :]

        def rope(value):
            return value * cosine + swap_halves(value) * sine

        queries = nn(normed, wq_ref[...])
        for j in range(Q_TILES):
            q_ref[j, rows, :] = (rope(tile(queries, j)) * HD ** (-0.5)).astype(BF)
        keys_values = nn(normed, wkv_ref[...])
        first = rope(tile(keys_values, 0))
        second = tile(keys_values, 1)
        third = tile(keys_values, 2)
        mid = rope(second)

        def put(ref, index, value):
            ref[index, rows, :] = value.astype(BF)

        put(k_ref, 0, jnp.where(low, first, 0.0))
        put(k_ref, 1, jnp.where(low, 0.0, flip(first)))
        put(k_ref, 2, jnp.where(low, flip(first), 0.0))
        put(k_ref, 3, jnp.where(low, 0.0, first))
        put(k_ref, 4, jnp.where(low, mid, 0.0))
        put(k_ref, 5, jnp.where(low, 0.0, flip(mid)))
        put(v_ref, 0, jnp.where(low, flip(second), 0.0))
        put(v_ref, 1, jnp.where(low, 0.0, second))
        put(v_ref, 2, jnp.where(low, third, 0.0))
        put(v_ref, 3, jnp.where(low, 0.0, flip(third)))
        put(v_ref, 4, jnp.where(low, flip(third), 0.0))
        put(v_ref, 5, jnp.where(low, 0.0, third))
        return carry

    lax.fori_loop(0, seq_len // BLOCK, project, 0)
    lane = lax.broadcasted_iota(jnp.int32, (BLOCK, LANES), 1)
    keep = lax.broadcasted_iota(jnp.int32, (BLOCK, BLOCK), 1) <= lax.broadcasted_iota(
        jnp.int32, (BLOCK, BLOCK), 0
    )
    for b in range(seq_len // BLOCK):
        rows = slice(b * BLOCK, (b + 1) * BLOCK)
        n_keys = (b + 1) * BLOCK
        o_acc[...] = jnp.zeros_like(o_acc)

        def group(g, lse, rows=rows, n_keys=n_keys):
            for u in range(3):
                head = 3 * g + u
                j = head // 2
                side = 2 * g + head % 2
                scores = nt(q_ref[j, rows, :], k_ref[side, 0:n_keys, :])
                diag = jnp.where(keep, scores[:, n_keys - BLOCK :], MASKED)
                if n_keys > BLOCK:
                    scores = jnp.concatenate([scores[:, : n_keys - BLOCK], diag], axis=1)
                else:
                    scores = diag
                row_max = jnp.max(scores, axis=-1, keepdims=True)
                exponent = jnp.exp(scores - row_max)
                total = jnp.sum(exponent, axis=-1, keepdims=True)
                prob = (exponent * (1.0 / total)).astype(BF)
                o_acc[j] += nn(prob, v_ref[side, 0:n_keys, :])
                lse = jnp.where(lane == head, row_max + jnp.log(total), lse)
            return lse

        lse = lax.fori_loop(0, KV, group, jnp.zeros((BLOCK, LANES), F32))
        lse_ref[:, rows] = lse.T[:16]
        mixed = jnp.concatenate([o_acc[j].astype(BF) for j in range(Q_TILES)], axis=1)
        mixed_ref[rows, :] = mixed
        h1_ref[rows, :] = x_ref[rows, :].astype(F32) + nn(mixed, wo_ref[...])


def prepare_weights(
    core_ref, own_ref, other_ref,
    ga_ref, gm_ref, wq_ref, wkv_ref, wo_ref, wg_ref, wu_ref, wd_ref,
    both, flat, tmp, sem,
):
    core = core_ref[0]
    copies = [
        pltpu.make_async_copy(own_ref, both.at[core], sem.at[0]),
        pltpu.make_async_copy(other_ref, both.at[1 - core], sem.at[1]),
    ]
    for copy in copies:
        copy.start()
    for copy in copies:
        copy.wait()
    step = HALF_ROWS // 13

    def widen(which):
        def body(i, carry):
            rows = pl.ds(pl.multiple_of(i * step, 8), step)
            flat[rows, :] = both[which, rows, :].astype(F32)
            return carry

        lax.fori_loop(0, 13, body, 0)

    def interleave(even, odd, pairs, out_ref, first_row, pad):
        low = low_half(2 * pairs)
        for t in range(Q_TILES):
            tmp[pl.ds(t * D, pairs, stride=2), :] = even[t]
            tmp[pl.ds(t * D + 1, pairs, stride=2), :] = odd[t]
        rows = pl.ds(first_row, 2 * pairs)
        for t in range(Q_TILES):
            value = tmp[t * D : t * D + 2 * pairs, :]
            if t < 4:
                out_ref[rows, t * LANES : (t + 1) * LANES] = value.astype(BF)
            elif pad:
                out_ref[rows, t * LANES :] = jnp.where(low, value, 0.0).astype(BF)
            else:
                out_ref[rows, t * LANES :] = value[:, :HD].astype(BF)

    def wide(row, out_ref, pad):
        pairs = D // 2
        low = low_half(pairs)
        cols = [flat[pl.ds(row + c, pairs, stride=9), :] for c in range(9)]
        turned = [flip(cols[c]) for c in range(4, 9)]
        odd = [jnp.where(low, turned[t], turned[t + 1]) for t in range(4)] + [turned[4]]
        interleave(cols[:5], odd, pairs, out_ref, 0, pad)

    widen(0)
    low1 = low_half(1)
    turned = [flip(flat[4 + r : 5 + r, :]) for r in range(5)]
    for r in range(4):
        ga_ref[:, r * LANES : (r + 1) * LANES] = flat[r : r + 1, :]
        gm_ref[:, r * LANES : (r + 1) * LANES] = jnp.where(low1, turned[r], turned[r + 1])
    ga_ref[:, 4 * LANES :] = flat[4:5, :HD]
    gm_ref[:, 4 * LANES :] = turned[4][:, :HD]
    wide(9, wq_ref, True)
    wide(O_ROW, wo_ref, False)
    wo_ref[D:, :] = jnp.zeros((PAD_D - D, D), BF)
    pairs = D // 2
    low = low_half(pairs)
    narrow = []
    for row in (2601, 3465):
        cols = [flat[pl.ds(row + c, pairs, stride=3), :] for c in range(3)]
        turned = [flip(cols[1]), flip(cols[2])]
        even = cols[:2]
        odd = [jnp.where(low, turned[0], turned[1]), turned[1]]
        for t in range(2):
            tmp[pl.ds(t * D, pairs, stride=2), :] = even[t]
            tmp[pl.ds(t * D + 1, pairs, stride=2), :] = odd[t]
        narrow.append((tmp[0:D, :], tmp[D : 2 * D, :]))
    (k0, k1), (v0, v1) = narrow
    low = low_half(D)
    v0 = flip(v0)
    v1 = flip(v1)
    wkv_ref[:, 0:LANES] = k0.astype(BF)
    wkv_ref[:, LANES : 2 * LANES] = jnp.where(low, k1, v0).astype(BF)
    wkv_ref[:, 2 * LANES :] = jnp.where(low, v0, v1).astype(BF)
    head = both[1, 0:16, :].astype(F32)
    turned = flip(head)
    for r in range(5):
        row = GATE_ROW + FF_TILES * (D - 1) + 7 + r
        before = flat[row : row + 1, :] if r == 0 else turned[r - 1 : r]
        flat[row : row + 1, :] = jnp.where(low1, before, turned[r : r + 1])
    for t in range(FF_TILES):
        wg_ref[:, t * LANES : (t + 1) * LANES] = flat[
            pl.ds(GATE_ROW + t, D, stride=FF_TILES), :
        ].astype(BF)
    widen(1)
    here = flip(flat[pl.ds(4, D, stride=FF_TILES), :])
    for t in range(FF_TILES):
        after = flip(flat[pl.ds(5 + t, D, stride=FF_TILES), :])
        wu_ref[:, t * LANES : (t + 1) * LANES] = jnp.where(low, here, after).astype(BF)
        here = after

    def down(i, carry):
        n_pairs = 96
        low = low_half(n_pairs)
        start = 6916 + 9 * n_pairs * i
        cols = [flat[pl.ds(start + c, n_pairs, stride=9), :] for c in range(10)]
        turned = [flip(cols[c]) for c in range(6)]
        even = [jnp.where(low, turned[c], turned[c + 1]) for c in range(5)]
        interleave(even, cols[5:], n_pairs, wd_ref, pl.multiple_of(2 * n_pairs * i, 16), False)
        return carry

    lax.fori_loop(0, FF // 192, down, 0)


def transposed(value):
    rows = value.shape[0]
    pieces = [tile(value, t) for t in range(4)]
    pieces.append(
        jnp.concatenate([value[:, 4 * LANES :], jnp.zeros((rows, LANES - HD), F32)], axis=1)
    )
    return jnp.concatenate([piece.T for piece in pieces], axis=0)


def mlp_pass(
    core_ref, slot_ref, lengths_ref, assignment_ref,
    h1_hbm, cot_hbm, mixed_hbm, gm_ref, wo_hbm, wg_hbm, wu_hbm, wd_hbm,
    out_hbm, dh1_hbm, dm_hbm, ggm_ref, keep_ref, send_ref,
    h1_ref, cot_ref, mixed_ref, wo_ref, wg_ref, wu_ref, wd_ref, out_ref, dh1_ref, dm_ref,
    nmt_s, backt_s, inner_s, dg_s, du_s, da_s, grads, in_sem, out_sem, sem,
):
    seq_len = h1_ref.shape[0]
    core = core_ref[0]
    live_len = lengths_ref[assignment_ref[slot_ref[0]]]
    n_cols = FF // MLP_COLS
    loads = [
        pltpu.make_async_copy(source, target, in_sem.at[i])
        for i, (source, target) in enumerate(
            (
                (h1_hbm, h1_ref),
                (cot_hbm, cot_ref),
                (wg_hbm, wg_ref),
                (wu_hbm, wu_ref),
                (wd_hbm, wd_ref),
                (wo_hbm, wo_ref),
                (mixed_hbm, mixed_ref),
            )
        )
    ]
    for copy in loads:
        copy.start()
    for copy in loads[:6]:
        copy.wait()

    def results(b):
        rows = pl.ds(pl.multiple_of(b * MLP_BLOCK, MLP_BLOCK), MLP_BLOCK)
        pairs = [(out_ref.at[rows], out_hbm.at[rows]), (dh1_ref.at[rows], dh1_hbm.at[rows])]
        pairs.append((dm_ref.at[:, rows], dm_hbm.at[:, rows]))
        return [
            pltpu.make_async_copy(source, target, out_sem.at[b, i])
            for i, (source, target) in enumerate(pairs)
        ]

    def block(b, ggm):
        start = pl.multiple_of(b * MLP_BLOCK, MLP_BLOCK)
        rows = pl.ds(start, MLP_BLOCK)
        hidden1 = h1_ref[rows, :]
        r2 = rms(hidden1)
        gain = gm_ref[...]
        normed2_wide = hidden1 * r2 * gain
        normed2 = normed2_wide.astype(BF)
        nmt_s[:, rows] = transposed(normed2_wide).astype(BF)
        live = (
            start + lax.broadcasted_iota(jnp.int32, (MLP_BLOCK, 1), 0) < live_len
        ).astype(F32)

        back = cot_ref[rows, :].astype(F32) * live
        back_low = back.astype(BF)
        backt_s[:, rows] = transposed(back).astype(BF)
        for c in range(n_cols):
            cols = slice(c * MLP_COLS, (c + 1) * MLP_COLS)
            gate = nn(normed2, wg_ref[:, cols])
            up = nn(normed2, wu_ref[:, cols])
            d_inner = nt(back_low, wd_ref[cols, :])
            sig = jax.nn.sigmoid(gate)
            silu = gate * sig
            inner_s[rows, cols] = (silu * up).astype(BF)
            dg_s[rows, cols] = (d_inner * up * sig * (1.0 + gate * (1.0 - sig))).astype(BF)
            du_s[rows, cols] = (d_inner * silu).astype(BF)
        out_ref[rows, :] = ((hidden1 + nn(inner_s[rows, :], wd_ref[...])) * live).astype(BF)
        d_normed2 = nt(dg_s[rows, :], wg_ref[...]) + nt(du_s[rows, :], wu_ref[...])
        scaled = d_normed2 * gain
        d_hidden1 = (
            back
            + r2 * scaled
            - hidden1 * (r2 * r2 * r2) * jnp.mean(scaled * hidden1, axis=-1, keepdims=True)
        )
        dh1_ref[rows, :] = d_hidden1
        d_attn = d_hidden1.astype(BF)
        da_s[rows, :] = d_attn

        d_mixed = nt(d_attn, wo_ref[...]).astype(BF)
        for j in range(Q_TILES):
            dm_ref[j, rows, :] = tile(d_mixed, j)
        for copy in results(b):
            copy.start()
        return ggm + jnp.sum(d_normed2 * hidden1 * r2, axis=0, keepdims=True)

    ggm_ref[...] = lax.fori_loop(0, seq_len // MLP_BLOCK, block, jnp.zeros((1, D), F32))

    def put(half, index, value):
        grads[half, pl.ds(pl.multiple_of(index * D, D), D), :] = value

    def leave(c):
        rows = pl.ds(pl.multiple_of(2 * c * D, D), 2 * D)
        return [
            pltpu.make_async_copy(grads.at[1 - core, rows], send_ref.at[rows], sem.at[c, 0]),
            pltpu.make_async_copy(grads.at[core, rows], keep_ref.at[rows], sem.at[c, 1]),
        ]

    def weights(c, carry):
        cols = pl.ds(pl.multiple_of(c * 2 * LANES, 2 * LANES), 2 * LANES)
        grad_gate = nn(nmt_s[:D, :], dg_s[:, cols]).astype(BF)
        grad_up = nn(nmt_s[:D, :], du_s[:, cols]).astype(BF)
        for t in range(2):
            put(0, 2 * c + t, tile(grad_gate, t))
            put(1, 2 * c + t, tile(grad_up, t))
        for copy in leave(c):
            copy.start()
        grad_down = nn(backt_s[:D, :], inner_s[:, cols]).astype(BF)
        part = jnp.where(c < DOWN_FIRST // 2, 0, 1)
        base = jnp.where(c < DOWN_FIRST // 2, FF_TILES + Q_TILES, FF_TILES - DOWN_FIRST)
        for t in range(2):
            put(part, base + 2 * c + t, tile(grad_down, t))
        return carry

    lax.fori_loop(0, n_cols, weights, 0)
    loads[6].wait()
    grad_o = tn(mixed_ref[...], da_s[...])[:D]
    for t in range(4):
        put(0, FF_TILES + t, tile(grad_o, t).astype(BF))
    put(0, FF_TILES + 4, half_tile(grad_o).astype(BF))
    grads[0, EXTRA:, :] = jnp.zeros((EARLY_ROWS - EXTRA, LANES), BF)
    grads[1, EXTRA - D :, :] = jnp.zeros((EARLY_ROWS - EXTRA + D, LANES), BF)
    row = lax.broadcasted_iota(jnp.int32, (16, LANES), 0)
    rest = jnp.zeros((16, LANES), F32)
    for r in range(5):
        start = (8 + r) * D - 16
        last = grads[0, start : start + 16, :].astype(F32)[15:16]
        rest = jnp.where(row == r, jnp.broadcast_to(last, (16, LANES)), rest)
    grads[0, EXTRA + 16 : EXTRA + 32, :] = rest.astype(BF)
    rows = pl.ds(FF_TILES * D, EARLY_ROWS - FF_TILES * D)
    final = [
        pltpu.make_async_copy(grads.at[1 - core, rows], send_ref.at[rows], sem.at[n_cols, 0]),
        pltpu.make_async_copy(grads.at[core, rows], keep_ref.at[rows], sem.at[n_cols, 1]),
    ]
    for copy in final:
        copy.start()

    def drain(c, carry):
        for copy in leave(c):
            copy.wait()
        return carry

    def drain_results(b, carry):
        for copy in results(b):
            copy.wait()
        return carry

    lax.fori_loop(0, n_cols, drain, 0)
    lax.fori_loop(0, seq_len // MLP_BLOCK, drain_results, 0)
    for copy in final:
        copy.wait()


def half_tile(value):
    rows = value.shape[0]
    return jnp.concatenate([value[:, 4 * LANES : D], jnp.zeros((rows, HD), value.dtype)], axis=1)


def gain_rows(value):
    row = lax.broadcasted_iota(jnp.int32, (16, LANES), 0)
    whole = jnp.zeros((16, LANES), F32)
    for t in range(Q_TILES):
        piece = tile(value, t) if t < 4 else half_tile(value)
        whole = jnp.where(row == t, jnp.broadcast_to(piece, (16, LANES)), whole)
    return whole


def backward_group(
    g, q0_ref, q1_ref, dm0_ref, dm1_ref, k_ref, v_ref, lse_ref,
    dq_ref, dk_ref, dv_ref, dk_acc, dv_acc,
):
    seq_len = dk_ref.shape[0]
    low = low_half(seq_len)
    dq_ref[...] = jnp.zeros_like(dq_ref)
    dk_acc[...] = jnp.zeros_like(dk_acc)
    dv_acc[...] = jnp.zeros_like(dv_acc)
    keep = lax.broadcasted_iota(jnp.int32, (BLOCK, BLOCK), 0) <= lax.broadcasted_iota(
        jnp.int32, (BLOCK, BLOCK), 1
    )
    for b in range(seq_len // BLOCK):
        rows = slice(b * BLOCK, (b + 1) * BLOCK)
        n_keys = (b + 1) * BLOCK
        for u in range(3):
            head = 3 * g + u
            j = head // 2 - (3 * g) // 2
            side = head % 2
            queries = (q0_ref, q1_ref)[j][0, rows, :]
            d_mixed = (dm0_ref, dm1_ref)[j][0, rows, :]
            keys = k_ref[side, 0:n_keys, :]
            values = v_ref[side, 0:n_keys, :]
            prob = jnp.exp(nt(keys, queries) - lse_ref[head : head + 1, rows])
            diag = jnp.where(keep, prob[n_keys - BLOCK :, :], 0.0)
            if n_keys > BLOCK:
                prob = jnp.concatenate([prob[: n_keys - BLOCK, :], diag], axis=0)
            else:
                prob = diag
            d_prob = nt(values, d_mixed)
            delta = jnp.sum(d_prob * prob, axis=0, keepdims=True)
            d_score = (prob * (d_prob - delta)).astype(BF)
            dv_acc[side, 0:n_keys, :] += nn(prob.astype(BF), d_mixed)
            dk_acc[side, 0:n_keys, :] += nn(d_score, queries)
            dq_ref[j, rows, :] += tn(d_score, keys)
    dk_ref[...] = dk_acc[0] + flip(dk_acc[1])
    dv_ref[...] = dv_acc[0] + flip(dv_acc[1])


def backward_finish(
    x_ref, ga_ref, dh1_ref, dqa_ref, dqb_ref, dqc_ref, dka_ref, dkb_ref, dkc_ref,
    dva_ref, dvb_ref, dvc_ref, wq_ref, wkv_ref, cos_ref, sin_ref,
    dx_ref, dq_s, dkv_s, nm_s, gga_ref,
):
    seq_len = x_ref.shape[0]
    low = low_half(BLOCK)

    def block(b, gga):
        rows = pl.ds(pl.multiple_of(b * BLOCK, BLOCK), BLOCK)
        cosine = cos_ref[rows, :]
        sine = sin_ref[rows, :]

        def unrope(value):
            return value * cosine - swap_halves(value) * sine

        d_rot = [
            dqa_ref[0, rows, :],
            dqa_ref[1, rows, :] + dqb_ref[0, rows, :],
            dqb_ref[1, rows, :],
            dqc_ref[0, rows, :],
            dqc_ref[1, rows, :],
        ]
        for j in range(Q_TILES):
            d_query = unrope(d_rot[j]) * HD ** (-0.5)
            dq_s[rows, j * LANES : (j + 1) * LANES] = d_query.astype(BF)
        dk = [ref[rows, :] for ref in (dka_ref, dkb_ref, dkc_ref)]
        dv = [ref[rows, :] for ref in (dva_ref, dvb_ref, dvc_ref)]
        first = unrope(jnp.where(low, dk[0], flip(dk[1])))
        second = jnp.where(low, unrope(dk[2]), flip(dv[0]))
        third = jnp.where(low, dv[1], flip(dv[2]))
        dkv_s[rows, 0:LANES] = first.astype(BF)
        dkv_s[rows, LANES : 2 * LANES] = second.astype(BF)
        dkv_s[rows, 2 * LANES :] = third.astype(BF)
        d_normed = nt(dq_s[rows, :], wq_ref[...]) + nt(dkv_s[rows, :], wkv_ref[...])
        stream = x_ref[rows, :].astype(F32)
        r1 = rms(stream)
        gain = ga_ref[...]
        nm_s[rows, :] = (stream * r1 * gain).astype(BF)
        scaled = d_normed * gain
        dx_ref[rows, :] = (
            dh1_ref[rows, :]
            + r1 * scaled
            - stream * (r1 * r1 * r1) * jnp.mean(scaled * stream, axis=-1, keepdims=True)
        ).astype(BF)
        return gga + jnp.sum(d_normed * stream * r1, axis=0, keepdims=True)

    gga_ref[...] = lax.fori_loop(0, seq_len // BLOCK, block, jnp.zeros((1, D), F32))


def late_weights(
    core_ref, nm_s, dq_s, dkv_s, gga_ref, ggm_ref, keep_ref, send_ref, late, sem
):
    grad_q = tn(nm_s[...], dq_s[...]).astype(BF)
    grad_kv = tn(nm_s[...], dkv_s[...]).astype(BF)
    for t in range(Q_TILES):
        late[t * D : (t + 1) * D, :] = tile(grad_q, t)
    for t in range(3):
        late[(Q_TILES + t) * D : (Q_TILES + t + 1) * D, :] = tile(grad_kv, t)
    late[8 * D :, :] = jnp.zeros((2 * LATE_HALF - 8 * D, LANES), BF)
    late[8 * D : 8 * D + 16, :] = gain_rows(gga_ref[...]).astype(BF)
    late[8 * D + 16 : 8 * D + 32, :] = gain_rows(ggm_ref[...]).astype(BF)
    copies = []
    for i, (which, ref) in enumerate(((1 - core_ref[0], send_ref), (core_ref[0], keep_ref))):
        rows = pl.ds(pl.multiple_of(which * LATE_HALF, 8), LATE_HALF)
        copies.append(pltpu.make_async_copy(late.at[rows], ref, sem.at[i]))
    for copy in copies:
        copy.start()
    for copy in copies:
        copy.wait()


def gather_sum(bits_ref, *refs, n_parts, rows, split, merge, joined):
    n_in = 1 if joined else n_parts
    kept, got = refs[:n_in], refs[n_in : 2 * n_in]
    kinds = 2 if split else 1
    n_out = kinds * (1 if merge else n_parts)
    outs = refs[2 * n_in : 2 * n_in + n_out]
    scratch, sem = refs[2 * n_in + n_out :]
    size = rows // kinds
    copies = []
    for p in range(n_parts):
        if joined:
            part = slice(p * rows, (p + 1) * rows)
            total = kept[0][part, :].astype(F32) + got[0][part, :].astype(F32)
        else:
            total = kept[p][...].astype(F32) + got[p][...].astype(F32)
        scratch[p] = total.astype(BF)
        for i in range(kinds):
            if merge:
                target = outs[i].at[pl.ds(p * size, size)]
            else:
                target = outs[p + i * n_parts]
            start = (bits_ref[p] if i else 1 - bits_ref[p]) * size if split else 0
            source = scratch.at[p, pl.ds(pl.multiple_of(start, 8), size)]
            copies.append(pltpu.make_async_copy(source, target, sem.at[2 * p + i]))
            copies[-1].start()
    for copy in copies:
        copy.wait()


def join_halves(bits_ref, *refs, n_parts, rows, merged):
    n_in = 1 if merged else n_parts
    own, got, outs = refs[:n_in], refs[n_in : 2 * n_in], refs[2 * n_in : 2 * n_in + n_parts]
    sem = refs[2 * n_in + n_parts]
    copies = []
    for p in range(n_parts):
        for i, (group, which) in enumerate(((own, bits_ref[p]), (got, 1 - bits_ref[p]))):
            source = group[0].at[pl.ds(p * rows, rows)] if merged else group[p]
            span = pl.ds(pl.multiple_of(which * rows, 8), rows)
            copies.append(pltpu.make_async_copy(source, outs[p].at[span], sem.at[2 * p + i]))
            copies[-1].start()
    for copy in copies:
        copy.wait()


def put_wide(flat, tmp, values, rows, row):
    pairs = rows // 2
    for index, value in enumerate(values):
        tmp[pl.ds(index * D, rows), :] = value
    even = [tmp[pl.ds(i * D, pairs, stride=2), :] for i in range(Q_TILES)]
    odd = [flip(tmp[pl.ds(i * D + 1, pairs, stride=2), :]) for i in range(Q_TILES)]
    low = low_half(pairs)
    for c in range(4):
        flat[pl.ds(row + c, pairs, stride=9), :] = even[c]
    flat[pl.ds(row + 4, pairs, stride=9), :] = jnp.where(low, even[4], odd[0])
    for c in range(4):
        flat[pl.ds(row + 5 + c, pairs, stride=9), :] = jnp.where(low, odd[c], odd[c + 1])


def update_rule(scale, rate, grad, master, momentum, average):
    weight_grad = grad * scale
    new_momentum = MOMENTUM_DECAY * momentum + weight_grad
    new_master = master - rate * (weight_grad + MOMENTUM_DECAY * new_momentum)
    new_average = AVERAGE_DECAY * average + (1.0 - AVERAGE_DECAY) * new_master
    return weight_grad, new_momentum, new_master, new_average


class Chunks:
    def __init__(self, rows, base, count, rule, refs):
        self.rows, self.base, self.count, self.rule = rows, base, count, rule
        self.ins, self.outs, self.in_buf, self.out_buf, self.in_sem, self.out_sem = refs
        self.size = rows * LANES

    def span(self, c):
        return pl.ds(pl.multiple_of((self.base + c * self.rows) * LANES, LANES), self.size)

    def place(self, index, start=0, length=None):
        start = pl.multiple_of(index * self.size + start, 8 * LANES)
        return pl.ds(start, self.size if length is None else length)

    def fetch(self, c):
        return [
            pltpu.make_async_copy(
                self.ins[i].at[self.span(c)],
                self.in_buf.at[self.place(c * 3 + i)],
                self.in_sem.at[c, i],
            )
            for i in range(3)
        ]

    def flush(self, c):
        return [
            pltpu.make_async_copy(
                self.out_buf.at[self.place(c * 4 + i)],
                self.outs[i].at[self.span(c)],
                self.out_sem.at[c, i],
            )
            for i in range(4)
        ]

    def start(self):
        def body(c, carry):
            for copy in self.fetch(c):
                copy.start()
            return carry

        lax.fori_loop(0, self.count, body, 0)

    def run(self, stage, gradient):
        sub = STEP * LANES

        def body(c, carry):
            stage(c)
            for copy in self.fetch(c):
                copy.wait()

            def step(s, inner):
                grad = gradient(c, s * STEP, STEP).reshape(sub)
                values = self.rule(
                    grad, *[self.in_buf[self.place(c * 3 + i, s * sub, sub)] for i in range(3)]
                )
                for i in range(4):
                    self.out_buf[self.place(c * 4 + i, s * sub, sub)] = values[i]
                return inner

            lax.fori_loop(0, self.rows // STEP, step, 0)
            for copy in self.flush(c):
                copy.start()
            return carry

        def drain(c, carry):
            for copy in self.flush(c):
                copy.wait()
            return carry

        lax.fori_loop(0, self.count, body, 0)
        return lambda: lax.fori_loop(0, self.count, drain, 0)


class Extra:
    def __init__(self, start, ins, outs, rest):
        self.bufs, self.sem = rest[:8], rest[8]
        count = self.bufs[0].shape[0]
        span = pl.ds(start, count)
        self.count = count
        self.loads = [
            pltpu.make_async_copy(ins[i].at[span], self.bufs[i], self.sem.at[i]) for i in range(3)
        ]
        self.stores = [
            pltpu.make_async_copy(self.bufs[3 + i], outs[i].at[span], self.sem.at[3 + i])
            for i in range(4)
        ]

    def start(self):
        for copy in self.loads:
            copy.start()

    def finish(self, grad, rule):
        for copy in self.loads:
            copy.wait()
        self.bufs[7][...] = grad.reshape(grad.shape[0] * LANES)
        values = rule(self.bufs[7][pl.ds(0, self.count)], *[self.bufs[i][...] for i in range(3)])
        for i in range(4):
            self.bufs[3 + i][...] = values[i]
            self.stores[i].start()

    def drain(self):
        for copy in self.stores:
            copy.wait()


def shifted(flat, row, count):
    here = flip(flat[pl.ds(row - 1, count), :])
    after = flip(flat[pl.ds(row, count), :])
    return jnp.where(low_half(count), here, after)


def load_parts(pieces, sem):
    copies = [
        pltpu.make_async_copy(source, target, sem.at[i]) for i, (source, target) in enumerate(pieces)
    ]
    for copy in copies:
        copy.start()
    return copies


FLAT_BASE = 8
TAIL_ZERO = HALF - (GATE_ROW + 11 * CHUNK) * LANES
TAIL_ONE = HALF - (6916 + 11 * CHUNK) * LANES


def update_first(scale, rate, core_ref, bits_ref, *rest):
    halves, ins, outs = rest[:4], rest[4:7], rest[7:11]
    early_ref, flat, in_buf, out_buf, in_sem, out_sem, part_sem = rest[11:18]
    refs = (ins, outs, in_buf, out_buf, in_sem, out_sem)
    core = core_ref[0]
    rule = functools.partial(update_rule, scale, rate)
    half = PART_ROWS // 2
    pieces = []
    for p in range(2):
        for i, which in enumerate((bits_ref[p], 1 - bits_ref[p])):
            span = pl.ds(pl.multiple_of(p * PART_ROWS + which * half, 8), half)
            pieces.append((halves[2 * p + i], early_ref.at[span]))
    copies = load_parts(pieces, part_sem)
    extra = Extra((GATE_ROW + 11 * CHUNK) * LANES, ins, outs, rest[18:])
    base = jnp.where(core == 0, GATE_ROW, 4)
    chunks = Chunks(CHUNK, base, 11 + core, rule, refs)
    chunks.start()

    @pl.when(core == 0)
    def _():
        extra.start()

    for copy in copies:
        copy.wait()
    flat[0:FLAT_BASE, :] = jnp.zeros((FLAT_BASE, LANES), F32)

    def stage(c):
        for t in range(FF_TILES):
            rows = pl.ds(pl.multiple_of(t * D + c * 48, 16), 48)
            flat[pl.ds(FLAT_BASE + t, 48, stride=FF_TILES), :] = early_ref[rows, :].astype(F32)

    def gradient(c, start, count):
        row = pl.multiple_of(FLAT_BASE + start, 8)
        return jnp.where(core == 0, flat[pl.ds(row, count), :], shifted(flat, row, count))

    def stage_next(c):
        flat[FLAT_BASE - 1 : FLAT_BASE, :] = flat[FLAT_BASE + CHUNK - 1 : FLAT_BASE + CHUNK, :]
        stage(c)

    drain = chunks.run(stage_next, gradient)

    @pl.when(core == 0)
    def _():
        stage(11)
        extra.finish(flat[FLAT_BASE : FLAT_BASE + CHUNK, :], rule)

    drain()

    @pl.when(core == 0)
    def _():
        extra.drain()


def update_second(scale, rate, core_ref, bits_ref, *rest):
    halves, ins, outs = rest[:8], rest[8:11], rest[15:19]
    flat, tmp, part_ref, swap_ref, first_ref, in_buf, out_buf, in_sem, out_sem, part_sem = rest[19:29]
    refs = (ins, outs, in_buf, out_buf, in_sem, out_sem)
    tail = Extra((6916 + 11 * CHUNK) * LANES, ins, outs, rest[29:38])
    head = Extra(0, ins, outs, rest[38:])
    rule = functools.partial(update_rule, scale, rate)
    half = PART_ROWS // 2
    pieces = []
    for i in range(2):
        which = [1 - bits_ref[p] if i else bits_ref[p] for p in range(3)]

        def rows(start, p, size, which=which):
            return pl.ds(pl.multiple_of(start + which[p] * size, 16), size)

        source = halves[2 + i].at[pl.ds(half - REST_SLOT, REST_SLOT)]
        pieces.append((source, part_ref.at[rows(0, 1, REST_SLOT)]))
        pieces.append((halves[4 + i], part_ref.at[rows(2 * REST_SLOT, 2, half)]))
        pieces.append((halves[6 + i], swap_ref.at[rows(0, 2, half)]))
        pieces.append((halves[i].at[pl.ds(0, 16)], first_ref.at[rows(0, 0, 16)]))
    parts = load_parts(pieces, part_sem)

    @pl.when(core_ref[0] == 0)
    def _():
        def stage(c):
            values = []
            for t in range(Q_TILES):
                rows = pl.ds(pl.multiple_of(REST + t * D + c * 64, 16), 64)
                values.append(part_ref[rows, :].astype(F32))
            put_wide(flat, tmp, values, 64, FLAT_BASE)

        def gradient(c, start, count):
            return flat[pl.ds(pl.multiple_of(FLAT_BASE + start, 8), count), :]

        chunks = Chunks(CHUNK // 2, O_ROW, 9, rule, refs)
        chunks.start()
        for copy in parts:
            copy.wait()
        chunks.run(stage, gradient)()

    @pl.when(core_ref[0] == 1)
    def _():
        head.start()
        chunks = Chunks(CHUNK, 6916, 11, rule, refs)
        chunks.start()
        tail.start()
        for copy in parts:
            copy.wait()
        flat[0:FLAT_BASE, :] = jnp.zeros((FLAT_BASE, LANES), F32)
        flat[FLAT_BASE : FLAT_BASE + 8, :] = swap_ref[SWAP_TAIL : SWAP_TAIL + 16, :].astype(F32)[0:8]
        flat[FLAT_BASE + 5 : FLAT_BASE + 6, :] = first_ref[0:16, :].astype(F32)[0:1]
        head.finish(shifted(flat, FLAT_BASE + 1, 8), rule)
        row = FLAT_BASE + CHUNK - 1
        flat[row : row + 1, :] = part_ref[REST - 16 : REST, :].astype(F32)[15:16]

        def stage(c):
            flat[FLAT_BASE - 1 : FLAT_BASE, :] = flat[FLAT_BASE + CHUNK - 1 : FLAT_BASE + CHUNK, :]
            inside = c < DOWN_FIRST
            here = pl.ds(pl.multiple_of(SWAP_START + jnp.where(inside, c, 0) * D, 16), D)
            there = pl.ds(pl.multiple_of(REST + jnp.where(inside, 0, c - DOWN_FIRST) * D, 16), D)
            whole = jnp.where(inside, swap_ref[here, :].astype(F32), part_ref[there, :].astype(F32))
            pieces = [whole[i * LANES : (i + 1) * LANES].T for i in range(4)]
            half = jnp.concatenate([whole[4 * LANES :], jnp.zeros((LANES - HD, LANES), F32)], axis=0)
            put_wide(flat, tmp, pieces + [half.T], LANES, FLAT_BASE)

        def gradient(c, start, count):
            return shifted(flat, FLAT_BASE + start, count)

        drain = chunks.run(stage, gradient)
        stage(11)
        flat[FLAT_BASE + CHUNK :, :] = jnp.zeros((8, LANES), F32)
        tail.finish(shifted(flat, FLAT_BASE, CHUNK + 8), rule)
        head.drain()
        drain()
        tail.drain()


def update_late(scale, rate, core_ref, own_ref, other_ref, *rest):
    ins, outs = rest[:3], rest[7:11]
    flat, tmp, late_ref, in_buf, out_buf, in_sem, out_sem = rest[11:18]
    refs = (ins, outs, in_buf, out_buf, in_sem, out_sem)
    extra = Extra(LATE_CHUNKS * CHUNK * LANES, ins, outs, rest[18:])
    rule = functools.partial(update_rule, scale, rate)

    @pl.when(core_ref[0] == 0)
    def _():
        chunks = Chunks(CHUNK, 0, LATE_CHUNKS, rule, refs)
        chunks.start()
        extra.start()
        late_ref[:LATE_HALF, :] = own_ref[...]
        late_ref[LATE_HALF:, :] = other_ref[...]

        def late(index):
            return late_ref[index * D : (index + 1) * D, :].astype(F32)

        low1 = low_half(1)
        gain_a = late_ref[8 * D : 8 * D + 16, :].astype(F32)
        gain_m = flip(late_ref[8 * D + 16 : 8 * D + 32, :].astype(F32))
        for r in range(4):
            flat[r : r + 1, :] = gain_a[r : r + 1]
        flat[4:5, :] = jnp.where(low1, gain_a[4:5], gain_m[0:1])
        for r in range(4):
            flat[5 + r : 6 + r, :] = jnp.where(low1, gain_m[r : r + 1], gain_m[r + 1 : r + 2])
        put_wide(flat, tmp, [late(t) for t in range(Q_TILES)], D, 9)
        pairs = D // 2
        for t in range(3):
            tmp[pl.ds(t * D, D), :] = late(Q_TILES + t)
        even = [tmp[pl.ds(i * D, pairs, stride=2), :] for i in range(3)]
        odd = [tmp[pl.ds(i * D + 1, pairs, stride=2), :] for i in range(3)]
        low = low_half(pairs)
        turned = [flip(odd[0]), flip(odd[1]), flip(even[1]), flip(even[2])]
        rows = (
            (2601, even[0]),
            (2602, jnp.where(low, even[1], turned[0])),
            (2603, jnp.where(low, turned[0], turned[1])),
            (3465, jnp.where(low, turned[2], turned[3])),
            (3466, jnp.where(low, turned[3], odd[1])),
            (3467, odd[2]),
        )
        for row, value in rows:
            flat[pl.ds(row, pairs, stride=3), :] = value

        def gradient(c, start, count):
            return flat[pl.ds(pl.multiple_of(c * CHUNK + start, 8), count), :]

        drain = chunks.run(lambda c: None, gradient)
        start = LATE_CHUNKS * CHUNK
        extra.finish(flat[start : start + 304, :], rule)
        drain()
        extra.drain()


def vmem():
    return pl.BlockSpec(memory_space=pltpu.VMEM)


def smem():
    return pl.BlockSpec(memory_space=pltpu.SMEM)


def hbm():
    return pl.BlockSpec(memory_space=pl.ANY)


def call(kernel, outs, in_specs, out_specs, scratch, flops, name, limit, aliases=None):
    n_bytes = sum(math.prod(shape) * jnp.dtype(kind).itemsize for shape, kind in outs)
    return pl.pallas_call(
        kernel,
        out_shape=[jax.ShapeDtypeStruct(shape, kind) for shape, kind in outs],
        in_specs=in_specs,
        out_specs=out_specs,
        scratch_shapes=scratch,
        input_output_aliases=aliases or {},
        compiler_params=pltpu.CompilerParams(vmem_limit_bytes=limit * MIB),
        cost_estimate=pl.CostEstimate(
            flops=int(flops), bytes_accessed=int(2 * n_bytes), transcendentals=0
        ),
        name=name,
    )


def rope_tables(seq_len):
    lane = jnp.arange(LANES, dtype=jnp.int32)
    which = (lane % (HD // 2)).astype(F32)
    frequency = jnp.exp(which * (-2.0 * math.log(10000.0) / HD))
    angles = jnp.arange(seq_len, dtype=F32)[:, None] * frequency[None, :]
    sign = jnp.where(lane % HD < HD // 2, -1.0, 1.0)
    return jnp.cos(angles), jnp.sin(angles) * sign[None, :]


def run_prepare(core, own, other):
    outs = [
        ((1, D), F32),
        ((1, D), F32),
        ((D, PAD_D), BF),
        ((D, KV_COLS), BF),
        ((PAD_D, D), BF),
        ((D, FF), BF),
        ((D, FF), BF),
        ((FF, D), BF),
    ]
    scratch = [
        pltpu.VMEM((2, HALF_ROWS, LANES), BF),
        pltpu.VMEM((FLAT_SCRATCH, LANES), F32),
        pltpu.VMEM((Q_TILES * D, LANES), F32),
        pltpu.SemaphoreType.DMA((2,)),
    ]
    return call(
        prepare_weights,
        outs,
        [smem()] + [hbm()] * 2,
        [vmem()] * 8,
        scratch,
        1e10,
        "prepare_weights",
        60,
    )(core, own, other)


def run_attention_forward(x, gain, wq, wkv, wo, cosine, sine):
    seq_len = x.shape[0]
    outs = [
        ((seq_len, D), F32),
        ((seq_len, PAD_D), BF),
        ((Q_TILES, seq_len, LANES), BF),
        ((6, seq_len, LANES), BF),
        ((6, seq_len, LANES), BF),
        ((16, seq_len), F32),
    ]
    return call(
        attention_forward,
        outs,
        [vmem()] * 7,
        [vmem()] * 6,
        [pltpu.VMEM((Q_TILES, BLOCK, LANES), F32)],
        1.5e10,
        "attention_forward",
        60,
    )(x, gain, wq, wkv, wo, cosine, sine)


def run_mlp(core, slot, lengths, assignment, hidden1, cot, mixed, gain, wo, wg, wu, wd):
    seq_len = hidden1.shape[0]
    outs = [
        ((seq_len, D), BF),
        ((seq_len, D), F32),
        ((Q_TILES, seq_len, LANES), BF),
        ((1, D), F32),
        ((EARLY_ROWS, LANES), BF),
        ((EARLY_ROWS, LANES), BF),
    ]
    return call(
        mlp_pass,
        outs,
        [smem()] * 4 + [hbm()] * 3 + [vmem()] + [hbm()] * 4,
        [hbm()] * 3 + [vmem()] + [hbm()] * 2,
        [
            pltpu.VMEM((seq_len, D), F32),
            pltpu.VMEM((seq_len, D), BF),
            pltpu.VMEM((seq_len, PAD_D), BF),
            pltpu.VMEM((PAD_D, D), BF),
            pltpu.VMEM((D, FF), BF),
            pltpu.VMEM((D, FF), BF),
            pltpu.VMEM((FF, D), BF),
            pltpu.VMEM((seq_len, D), BF),
            pltpu.VMEM((seq_len, D), F32),
            pltpu.VMEM((Q_TILES, seq_len, LANES), BF),
            pltpu.VMEM((PAD_D, seq_len), BF),
            pltpu.VMEM((PAD_D, seq_len), BF),
            pltpu.VMEM((seq_len, FF), BF),
            pltpu.VMEM((seq_len, FF), BF),
            pltpu.VMEM((seq_len, FF), BF),
            pltpu.VMEM((seq_len, D), BF),
            pltpu.VMEM((2, EARLY_ROWS, LANES), BF),
            pltpu.SemaphoreType.DMA((7,)),
            pltpu.SemaphoreType.DMA((seq_len // MLP_BLOCK, 3)),
            pltpu.SemaphoreType.DMA((FF_TILES // 2 + 1, 2)),
        ],
        2.5e10,
        "mlp_pass",
        60,
    )(core, slot, lengths, assignment, hidden1, cot, mixed, gain, wo, wg, wu, wd)


def run_backward_group(g, q, dm, k, v, lse):
    seq_len = q.shape[1]
    j0 = 3 * g // 2

    def part(count, index):
        return pl.BlockSpec((count, seq_len, LANES), lambda i: (index, 0, 0))

    outs = [((2, seq_len, LANES), F32), ((seq_len, LANES), F32), ((seq_len, LANES), F32)]
    whole = pl.BlockSpec((seq_len, LANES), lambda i: (0, 0))
    return pl.pallas_call(
        functools.partial(backward_group, g),
        grid=(1,),
        out_shape=[jax.ShapeDtypeStruct(shape, kind) for shape, kind in outs],
        in_specs=[
            part(1, j0),
            part(1, j0 + 1),
            part(1, j0),
            part(1, j0 + 1),
            part(2, g),
            part(2, g),
            pl.BlockSpec((16, seq_len), lambda i: (0, 0)),
        ],
        out_specs=[part(2, 0), whole, whole],
        scratch_shapes=[pltpu.VMEM((2, seq_len, LANES), F32)] * 2,
        compiler_params=pltpu.CompilerParams(vmem_limit_bytes=60 * MIB),
        cost_estimate=pl.CostEstimate(
            flops=int(8e9), bytes_accessed=int(3e6), transcendentals=0
        ),
        name="backward_group",
    )(q, q, dm, dm, k, v, lse)


def run_backward_finish(x, gain, dh1, groups, wq, wkv, cosine, sine):
    seq_len = x.shape[0]
    outs = [
        ((seq_len, D), BF),
        ((seq_len, PAD_D), BF),
        ((seq_len, KV_COLS), BF),
        ((seq_len, D), BF),
        ((1, D), F32),
    ]
    dq, dk, dv = zip(*groups)
    return call(
        backward_finish,
        outs,
        [vmem()] * 16,
        [vmem()] * 5,
        [],
        4e9,
        "backward_finish",
        60,
    )(x, gain, dh1, *dq, *dk, *dv, wq, wkv, cosine, sine)


def run_late_weights(core, normed, d_query, d_kv, gga, ggm):
    outs = [((LATE_HALF, LANES), BF), ((LATE_HALF, LANES), BF)]
    return call(
        late_weights,
        outs,
        [smem()] + [vmem()] * 5,
        [hbm()] * 2,
        [pltpu.VMEM((2 * LATE_HALF, LANES), BF), pltpu.SemaphoreType.DMA((2,))],
        4e9,
        "late_weights",
        60,
    )(core, normed, d_query, d_kv, gga, ggm)


def run_sum(bits, kept, got, split, merge=False, n_parts=None):
    joined = n_parts is not None
    n_parts = n_parts or len(kept)
    rows = kept[0].shape[0] // (n_parts if joined else 1)
    kinds = 2 if split else 1
    n_out = 1 if merge else n_parts
    out_rows = rows // kinds * (n_parts if merge else 1)
    results = call(
        functools.partial(
            gather_sum, n_parts=n_parts, rows=rows, split=split, merge=merge, joined=joined
        ),
        [((out_rows, LANES), BF)] * (kinds * n_out),
        [smem()] + [vmem()] * (2 * len(kept)),
        [hbm()] * (kinds * n_out),
        [pltpu.VMEM((n_parts, rows, LANES), BF), pltpu.SemaphoreType.DMA((2 * n_parts,))],
        1e6,
        "gather_sum",
        12,
    )(bits, *kept, *got)
    return list(results[:n_out]), list(results[n_out:])


def run_join(bits, own, got, n_parts):
    merged = len(own) < n_parts
    rows = own[0].shape[0] // (n_parts if merged else 1)
    return call(
        functools.partial(join_halves, n_parts=n_parts, rows=rows, merged=merged),
        [((2 * rows, LANES), BF)] * n_parts,
        [smem()] + [hbm()] * (2 * len(own)),
        [hbm()] * n_parts,
        [pltpu.SemaphoreType.DMA((2 * n_parts,))],
        1e6,
        "join_halves",
        4,
    )(bits, *own, *got)


def chunk_scratch(count):
    return [
        pltpu.VMEM((3 * count * CHUNK * LANES,), F32),
        pltpu.VMEM((4 * count * CHUNK * LANES,), F32),
        pltpu.SemaphoreType.DMA((12, 3)),
        pltpu.SemaphoreType.DMA((12, 4)),
    ]


def extra_scratch(count, n_rows):
    bufs = [pltpu.VMEM((count,), F32)] * 7 + [pltpu.VMEM((n_rows * LANES,), F32)]
    return bufs + [pltpu.SemaphoreType.DMA((7,))]


def run_update_first(scale, rate, core, bits, halves, state):
    scratch = [
        pltpu.VMEM((2 * PART_ROWS, LANES), BF),
        pltpu.VMEM((FLAT_BASE + CHUNK, LANES), F32),
        *chunk_scratch(12),
        pltpu.SemaphoreType.DMA((4,)),
        *extra_scratch(TAIL_ZERO, CHUNK),
    ]
    return call(
        functools.partial(update_first, scale, rate),
        [(state[0].shape, F32)] * 4,
        [smem()] * 2 + [hbm()] * 7,
        [hbm()] * 4,
        scratch,
        1e9,
        "update_first",
        60,
    )(core, bits, *halves, *state)


def run_update_second(scale, rate, core, bits, halves, state, done):
    scratch = [
        pltpu.VMEM((FLAT_BASE + CHUNK + 8, LANES), F32),
        pltpu.VMEM((Q_TILES * D, LANES), F32),
        pltpu.VMEM((2 * REST_SLOT + PART_ROWS, LANES), BF),
        pltpu.VMEM((PART_ROWS, LANES), BF),
        pltpu.VMEM((32, LANES), BF),
        *chunk_scratch(11),
        pltpu.SemaphoreType.DMA((8,)),
        *extra_scratch(TAIL_ONE, CHUNK + 8),
        *extra_scratch(5 * LANES, 8),
    ]
    return call(
        functools.partial(update_second, scale, rate),
        [(state[0].shape, F32)] * 4,
        [smem()] * 2 + [hbm()] * 15,
        [hbm()] * 4,
        scratch,
        1e9,
        "update_second",
        60,
        {13 + i: i for i in range(4)},
    )(core, bits, *halves, *state, *done)


def run_update_late(scale, rate, core, own, other, state, done):
    last_rows = O_ROW - LATE_CHUNKS * CHUNK
    scratch = [
        pltpu.VMEM((4336, LANES), F32),
        pltpu.VMEM((Q_TILES * D, LANES), F32),
        pltpu.VMEM((2 * LATE_HALF, LANES), BF),
        *chunk_scratch(LATE_CHUNKS),
        *extra_scratch(last_rows * LANES, 304),
    ]
    return call(
        functools.partial(update_late, scale, rate),
        [(state[0].shape, F32)] * 4,
        [smem()] + [vmem()] * 2 + [hbm()] * 7,
        [hbm()] * 4,
        scratch,
        1e9,
        "update_late",
        60,
        {6 + i: i for i in range(4)},
    )(core, own, other, *state, *done)


def add_low(a, b):
    return (a.astype(F32) + b.astype(F32)).astype(BF)


def xor_swap(value, bit):
    size = lax.axis_size("dp")
    return lax.ppermute(value, "dp", [(i, i ^ (1 << bit)) for i in range(size)])


def tie(value, *others):
    return lax.optimization_barrier((value, *others))


def my_bits(orders, step):
    index = lax.axis_index("dp")
    return jnp.stack([(index >> order[step]) & 1 for order in orders]).astype(jnp.int32)


def spread(blocks, far):
    size = lax.axis_size("dp")
    near = min(size, 4)
    if far:
        groups = [[g * near + i for g in range(size // near)] for i in range(near)]
    else:
        groups = [[g * near + i for i in range(near)] for g in range(size // near)]
    return lax.all_to_all(
        blocks, "dp", split_axis=0, concat_axis=0, tiled=True, axis_index_groups=groups
    )


def group_size(far):
    size = lax.axis_size("dp")
    return size // min(size, 4) if far else min(size, 4)


def scatter_sum(value):
    count = group_size(False)
    blocks = spread(value.reshape(count, value.shape[0] // count, LANES), False)
    return jnp.sum(blocks.astype(F32), axis=0).astype(BF)


def copies(value, far):
    return spread(jnp.broadcast_to(value[None], (group_size(far), *value.shape)), far)


def bit_orders():
    n_bits = lax.axis_size("dp").bit_length() - 1
    base = list(range(n_bits))
    head = base[:3] if n_bits >= 3 else base
    return [head[r:] + head[:r] + base[len(head) :] for r in range(3)]


def on_device(inputs, cotangent, lengths, assignment, return_order, master, momentum, average):
    nseq_all, block_rows, _ = inputs.shape
    axes = ("dp", "shard")
    seq_len = block_rows * lax.axis_size("dp") * lax.axis_size("shard")
    my_slot = lax.axis_index(axes)
    core = lax.axis_index("shard")
    core_arr = core.astype(jnp.int32).reshape(1)

    seq_ids = jnp.arange(nseq_all, dtype=jnp.int32)
    inverse = jnp.sum(
        jnp.where(return_order[None, :] == seq_ids[:, None], seq_ids[None, :], 0), axis=1
    )

    def pick(array, index):
        return array.at[index].get(mode="promise_in_bounds")

    def exchange(value):
        return lax.all_to_all(value, axes, split_axis=0, concat_axis=0, tiled=True)

    sent_in, master_in = tie(pick(inputs, assignment), master)
    x = exchange(sent_in).reshape(seq_len, D)
    slot_arr = my_slot.astype(jnp.int32).reshape(1)

    own = jnp.pad(master_in.astype(BF), (0, HALF_ROWS * LANES - master.shape[0]))
    own = own.reshape(HALF_ROWS, LANES)
    other = lax.ppermute(own, "shard", [(0, 1), (1, 0)])
    gain_attn, gain_mlp, wq, wkv, wo, wg, wu, wd = run_prepare(core_arr, own, other)

    cosine, sine = rope_tables(seq_len)
    sent_cot, gain_attn, cosine = tie(pick(cotangent, inverse), gain_attn, cosine)
    cot = exchange(sent_cot).reshape(seq_len, D)
    hidden1, mixed, q, k, v, lse = run_attention_forward(x, gain_attn, wq, wkv, wo, cosine, sine)
    result, dh1, dm, ggm, early_keep, early_send = run_mlp(
        core_arr, slot_arr, lengths, assignment, hidden1, cot, mixed, gain_mlp, wo, wg, wu, wd
    )
    back_out = exchange(result.reshape(nseq_all, block_rows, D))

    orders = bit_orders()
    n_bits = len(orders[0])

    def swap_parts(parts, step):
        return [xor_swap(part, order[step]) for part, order in zip(parts, orders)]

    got = lax.ppermute(early_send, "shard", [(0, 1), (1, 0)])
    groups = [run_backward_group(0, q, dm, k, v, lse)]
    lse, got = tie(lse, got)
    sent, kept = run_sum(my_bits(orders, 0), [early_keep], [got], True, n_parts=3)
    lse, *kept = tie(lse, *kept)
    got = swap_parts(sent, 0)
    groups.append(run_backward_group(1, q, dm, k, v, lse))
    groups.append(run_backward_group(2, q, dm, k, v, lse))
    sent, kept = run_sum(my_bits(orders, 1), kept, got, True)
    dh1, back_out, *kept = tie(dh1, back_out, *kept)
    got = swap_parts(sent, 1)
    d_stream, d_query, d_kv, normed, gga = run_backward_finish(
        x, gain_attn, dh1, groups, wq, wkv, cosine, sine
    )
    last_bit = n_bits - 1
    for step in range(2, n_bits):
        if step > 2:
            got = swap_parts(sent, step - 1)
        sent, kept = run_sum(my_bits(orders, step), kept, got, True, merge=step == last_bit)
        if step == 2:
            gga, *kept = tie(gga, *kept)
            late_keep, late_send = run_late_weights(core_arr, normed, d_query, d_kv, gga, ggm)
            late_send, *kept = tie(late_send, *kept)
        if step == last_bit:
            late_send, sent[0] = tie(late_send, sent[0])
    got = [xor_swap(sent[0], last_bit)]
    late_got = lax.ppermute(late_send, "shard", [(0, 1), (1, 0)])
    early, _ = run_sum(my_bits(orders, last_bit)[:1], kept, got, False)
    late, _ = run_sum(my_bits(orders, 0)[:1], [late_keep], [late_got], False)
    late, block_output, early[0] = tie(late[0], pick(back_out, return_order), early[0])
    late = scatter_sum(late)
    early = run_join(my_bits(orders, last_bit), early, [xor_swap(early[0], last_bit)], 3)
    late, *early = tie(late, *early)
    late = jnp.sum(copies(late, True).astype(F32), axis=0).astype(BF)
    for step in reversed(range(1, last_bit)):
        early = run_join(my_bits(orders, step), early, swap_parts(early, step), 3)
        if step == last_bit - 1:
            late, *early = tie(late, *early)
            late = copies(late, False).reshape(-1, LANES)
    got = swap_parts(early, 0)
    swap_own = lax.ppermute(early[2], "shard", [(0, 1)])
    bits = my_bits(orders, 0)
    scale = 1.0 / nseq_all
    rate = (nseq_all / (0.6 * seq_len)) ** 0.5 / D**0.5
    state = (master, momentum, average)
    d_stream, late, swap_own, *got = tie(d_stream, late, swap_own, *got)
    back_grad = exchange(d_stream.reshape(nseq_all, block_rows, D))
    late_other = lax.ppermute(late, "shard", [(1, 0)])
    swap_got = lax.ppermute(got[2], "shard", [(0, 1)])
    halves = [early[0], got[0], early[1], got[1], early[2], got[2], swap_own, swap_got]
    done = run_update_first(scale, rate, core_arr, bits, halves[:4], state)
    done = run_update_second(scale, rate, core_arr, bits, halves, state, done)
    weight_grad, new_momentum, new_master, new_average = run_update_late(
        scale, rate, core_arr, late, late_other, state, done
    )
    input_grad = pick(back_grad, return_order)
    return (block_output, input_grad, weight_grad, new_momentum, new_master, new_average)


def solution(mesh):
    rows = P(None, ("dp", "shard"), None)
    flat = P("shard")
    return jax.shard_map(
        on_device,
        mesh=mesh,
        in_specs=(rows, rows, P(), P(), P(), flat, flat, flat),
        out_specs=(rows, rows, flat, flat, flat, flat),
        check_vma=False,
    )
```

```python
import functools
import math

import jax
import jax.numpy as jnp
from jax import lax
from jax.experimental import pallas as pl
from jax.experimental.pallas import tpu as pltpu
from jax.sharding import PartitionSpec as P

D = 576
H = 9
KV = 3
HD = 64
FF = 1536
LANES = 128
BLOCK = 256
Q_TILES = 5
PAD_D = Q_TILES * LANES
KV_COLS = 2 * KV * HD
FF_TILES = FF // LANES
DOWN_FIRST = 4
EARLY_TILES = 21
EARLY_ROWS = 12288
EXTRA = EARLY_TILES * D
HALF = 27657 * LANES // 2
PART_ROWS = EARLY_ROWS // 3
SWAP_START = EXTRA - DOWN_FIRST * D - 2 * PART_ROWS
SWAP_TAIL = EXTRA + 16 - 2 * PART_ROWS
REST_FIRST = 2 * PART_ROWS - FF_TILES * D
REST_SLOT = REST_FIRST + 16
REST = REST_SLOT + 16
LATE_HALF = 2432
HALF_ROWS = 13832
FLAT_SCRATCH = 13848
O_ROW = 4329
GATE_ROW = 6921
MLP_COLS = 256
MLP_UNROLL = 6
MLP_BLOCK = 256
CHUNK = 576
STEP = 288
LATE_CHUNKS = 7

EPSILON = 1e-05
MOMENTUM_DECAY = 0.55
AVERAGE_DECAY = 0.45
MASKED = -1000000000.0

BF = jnp.bfloat16
F32 = jnp.float32
MIB = 1024 * 1024


def nn(a, b):
    return jnp.dot(a, b, preferred_element_type=F32)


def nt(a, b):
    return lax.dot_general(a, b, (((1,), (1,)), ((), ())), preferred_element_type=F32)


def tn(a, b):
    return lax.dot_general(a, b, (((0,), (0,)), ((), ())), preferred_element_type=F32)


def tile(value, index):
    return value[:, index * LANES : (index + 1) * LANES]


def low_half(rows):
    return lax.broadcasted_iota(jnp.int32, (rows, LANES), 1) < HD


def swap_halves(value):
    lane = lax.broadcasted_iota(jnp.int32, value.shape, 1)
    return jnp.where(lane % HD < HD // 2, pltpu.roll(value, 96, 1), pltpu.roll(value, 32, 1))


def flip(value):
    return pltpu.roll(value, HD, 1)


def rms(value):
    return lax.rsqrt(jnp.mean(value * value, axis=-1, keepdims=True) + EPSILON)


def attention_forward(
    x_ref, ga_ref, wq_ref, wkv_ref, wo_ref, cos_ref, sin_ref,
    h1_ref, mixed_ref, q_ref, k_ref, v_ref, lse_ref, o_acc,
):
    seq_len = x_ref.shape[0]
    low = low_half(BLOCK)

    def project(b, carry):
        rows = pl.ds(pl.multiple_of(b * BLOCK, BLOCK), BLOCK)
        stream = x_ref[rows, :].astype(F32)
        normed = (stream * rms(stream) * ga_ref[...]).astype(BF)
        cosine = cos_ref[rows, :]
        sine = sin_ref[rows, :]

        def rope(value):
            return value * cosine + swap_halves(value) * sine

        queries = nn(normed, wq_ref[...])
        for j in range(Q_TILES):
            q_ref[j, rows, :] = (rope(tile(queries, j)) * HD ** (-0.5)).astype(BF)
        keys_values = nn(normed, wkv_ref[...])
        first = rope(tile(keys_values, 0))
        second = tile(keys_values, 1)
        third = tile(keys_values, 2)
        mid = rope(second)

        def put(ref, index, value):
            ref[index, rows, :] = value.astype(BF)

        put(k_ref, 0, jnp.where(low, first, 0.0))
        put(k_ref, 1, jnp.where(low, 0.0, flip(first)))
        put(k_ref, 2, jnp.where(low, flip(first), 0.0))
        put(k_ref, 3, jnp.where(low, 0.0, first))
        put(k_ref, 4, jnp.where(low, mid, 0.0))
        put(k_ref, 5, jnp.where(low, 0.0, flip(mid)))
        put(v_ref, 0, jnp.where(low, flip(second), 0.0))
        put(v_ref, 1, jnp.where(low, 0.0, second))
        put(v_ref, 2, jnp.where(low, third, 0.0))
        put(v_ref, 3, jnp.where(low, 0.0, flip(third)))
        put(v_ref, 4, jnp.where(low, flip(third), 0.0))
        put(v_ref, 5, jnp.where(low, 0.0, third))
        return carry

    lax.fori_loop(0, seq_len // BLOCK, project, 0)
    lane = lax.broadcasted_iota(jnp.int32, (BLOCK, LANES), 1)
    keep = lax.broadcasted_iota(jnp.int32, (BLOCK, BLOCK), 1) <= lax.broadcasted_iota(
        jnp.int32, (BLOCK, BLOCK), 0
    )
    for b in range(seq_len // BLOCK):
        rows = slice(b * BLOCK, (b + 1) * BLOCK)
        n_keys = (b + 1) * BLOCK
        o_acc[...] = jnp.zeros_like(o_acc)

        def group(g, lse, rows=rows, n_keys=n_keys):
            for u in range(3):
                head = 3 * g + u
                j = head // 2
                side = 2 * g + head % 2
                scores = nt(q_ref[j, rows, :], k_ref[side, 0:n_keys, :])
                diag = jnp.where(keep, scores[:, n_keys - BLOCK :], MASKED)
                if n_keys > BLOCK:
                    scores = jnp.concatenate([scores[:, : n_keys - BLOCK], diag], axis=1)
                else:
                    scores = diag
                row_max = jnp.max(scores, axis=-1, keepdims=True)
                exponent = jnp.exp(scores - row_max)
                total = jnp.sum(exponent, axis=-1, keepdims=True)
                prob = (exponent * (1.0 / total)).astype(BF)
                o_acc[j] += nn(prob, v_ref[side, 0:n_keys, :])
                lse = jnp.where(lane == head, row_max + jnp.log(total), lse)
            return lse

        lse = lax.fori_loop(0, KV, group, jnp.zeros((BLOCK, LANES), F32))
        lse_ref[:, rows] = lse.T[:16]
        mixed = jnp.concatenate([o_acc[j].astype(BF) for j in range(Q_TILES)], axis=1)
        mixed_ref[rows, :] = mixed
        h1_ref[rows, :] = x_ref[rows, :].astype(F32) + nn(mixed, wo_ref[...])


def prepare_weights(
    core_ref, own_ref, other_ref,
    ga_ref, gm_ref, wq_ref, wkv_ref, wo_ref, wg_ref, wu_ref, wd_ref,
    both, flat, tmp, sem,
):
    core = core_ref[0]
    copies = [
        pltpu.make_async_copy(own_ref, both.at[core], sem.at[0]),
        pltpu.make_async_copy(other_ref, both.at[1 - core], sem.at[1]),
    ]
    for copy in copies:
        copy.start()
    for copy in copies:
        copy.wait()
    step = HALF_ROWS // 13

    def widen(which):
        def body(i, carry):
            rows = pl.ds(pl.multiple_of(i * step, 8), step)
            flat[rows, :] = both[which, rows, :].astype(F32)
            return carry

        lax.fori_loop(0, 13, body, 0)

    def interleave(even, odd, pairs, out_ref, first_row, pad):
        low = low_half(2 * pairs)
        for t in range(Q_TILES):
            tmp[pl.ds(t * D, pairs, stride=2), :] = even[t]
            tmp[pl.ds(t * D + 1, pairs, stride=2), :] = odd[t]
        rows = pl.ds(first_row, 2 * pairs)
        for t in range(Q_TILES):
            value = tmp[t * D : t * D + 2 * pairs, :]
            if t < 4:
                out_ref[rows, t * LANES : (t + 1) * LANES] = value.astype(BF)
            elif pad:
                out_ref[rows, t * LANES :] = jnp.where(low, value, 0.0).astype(BF)
            else:
                out_ref[rows, t * LANES :] = value[:, :HD].astype(BF)

    def wide(row, out_ref, pad):
        pairs = D // 2
        low = low_half(pairs)
        cols = [flat[pl.ds(row + c, pairs, stride=9), :] for c in range(9)]
        turned = [flip(cols[c]) for c in range(4, 9)]
        odd = [jnp.where(low, turned[t], turned[t + 1]) for t in range(4)] + [turned[4]]
        interleave(cols[:5], odd, pairs, out_ref, 0, pad)

    widen(0)
    low1 = low_half(1)
    turned = [flip(flat[4 + r : 5 + r, :]) for r in range(5)]
    for r in range(4):
        ga_ref[:, r * LANES : (r + 1) * LANES] = flat[r : r + 1, :]
        gm_ref[:, r * LANES : (r + 1) * LANES] = jnp.where(low1, turned[r], turned[r + 1])
    ga_ref[:, 4 * LANES :] = flat[4:5, :HD]
    gm_ref[:, 4 * LANES :] = turned[4][:, :HD]
    wide(9, wq_ref, True)
    wide(O_ROW, wo_ref, False)
    wo_ref[D:, :] = jnp.zeros((PAD_D - D, D), BF)
    pairs = D // 2
    low = low_half(pairs)
    narrow = []
    for row in (2601, 3465):
        cols = [flat[pl.ds(row + c, pairs, stride=3), :] for c in range(3)]
        turned = [flip(cols[1]), flip(cols[2])]
        even = cols[:2]
        odd = [jnp.where(low, turned[0], turned[1]), turned[1]]
        for t in range(2):
            tmp[pl.ds(t * D, pairs, stride=2), :] = even[t]
            tmp[pl.ds(t * D + 1, pairs, stride=2), :] = odd[t]
        narrow.append((tmp[0:D, :], tmp[D : 2 * D, :]))
    (k0, k1), (v0, v1) = narrow
    low = low_half(D)
    v0 = flip(v0)
    v1 = flip(v1)
    wkv_ref[:, 0:LANES] = k0.astype(BF)
    wkv_ref[:, LANES : 2 * LANES] = jnp.where(low, k1, v0).astype(BF)
    wkv_ref[:, 2 * LANES :] = jnp.where(low, v0, v1).astype(BF)
    head = both[1, 0:16, :].astype(F32)
    turned = flip(head)
    for r in range(5):
        row = GATE_ROW + FF_TILES * (D - 1) + 7 + r
        before = flat[row : row + 1, :] if r == 0 else turned[r - 1 : r]
        flat[row : row + 1, :] = jnp.where(low1, before, turned[r : r + 1])
    for t in range(FF_TILES):
        wg_ref[:, t * LANES : (t + 1) * LANES] = flat[
            pl.ds(GATE_ROW + t, D, stride=FF_TILES), :
        ].astype(BF)
    widen(1)
    here = flip(flat[pl.ds(4, D, stride=FF_TILES), :])
    for t in range(FF_TILES):
        after = flip(flat[pl.ds(5 + t, D, stride=FF_TILES), :])
        wu_ref[:, t * LANES : (t + 1) * LANES] = jnp.where(low, here, after).astype(BF)
        here = after

    def down(i, carry):
        n_pairs = 96
        low = low_half(n_pairs)
        start = 6916 + 9 * n_pairs * i
        cols = [flat[pl.ds(start + c, n_pairs, stride=9), :] for c in range(10)]
        turned = [flip(cols[c]) for c in range(6)]
        even = [jnp.where(low, turned[c], turned[c + 1]) for c in range(5)]
        interleave(even, cols[5:], n_pairs, wd_ref, pl.multiple_of(2 * n_pairs * i, 16), False)
        return carry

    lax.fori_loop(0, FF // 192, down, 0)


def transposed(value):
    rows = value.shape[0]
    pieces = [tile(value, t) for t in range(4)]
    pieces.append(
        jnp.concatenate([value[:, 4 * LANES :], jnp.zeros((rows, LANES - HD), F32)], axis=1)
    )
    return jnp.concatenate([piece.T for piece in pieces], axis=0)


def mlp_pass(
    core_ref, slot_ref, lengths_ref, assignment_ref,
    h1_hbm, cot_hbm, mixed_hbm, gm_ref, wo_hbm, wg_hbm, wu_hbm, wd_hbm,
    out_hbm, dh1_hbm, dm_hbm, ggm_ref, keep_ref, send_ref,
    h1_ref, cot_ref, mixed_ref, wo_ref, wg_ref, wu_ref, wd_ref, out_ref, dh1_ref, dm_ref,
    nmt_s, backt_s, inner_s, dg_s, du_s, da_s, grads, in_sem, out_sem, sem,
):
    seq_len = h1_ref.shape[0]
    core = core_ref[0]
    live_len = lengths_ref[assignment_ref[slot_ref[0]]]
    n_cols = FF // MLP_COLS
    loads = [
        pltpu.make_async_copy(source, target, in_sem.at[i])
        for i, (source, target) in enumerate(
            (
                (h1_hbm, h1_ref),
                (cot_hbm, cot_ref),
                (wg_hbm, wg_ref),
                (wu_hbm, wu_ref),
                (wd_hbm, wd_ref),
                (wo_hbm, wo_ref),
                (mixed_hbm, mixed_ref),
            )
        )
    ]
    for copy in loads:
        copy.start()
    for copy in loads[:6]:
        copy.wait()

    def results(b):
        rows = pl.ds(pl.multiple_of(b * MLP_BLOCK, MLP_BLOCK), MLP_BLOCK)
        pairs = [(out_ref.at[rows], out_hbm.at[rows]), (dh1_ref.at[rows], dh1_hbm.at[rows])]
        pairs.append((dm_ref.at[:, rows], dm_hbm.at[:, rows]))
        return [
            pltpu.make_async_copy(source, target, out_sem.at[b, i])
            for i, (source, target) in enumerate(pairs)
        ]

    def block(b, ggm):
        start = pl.multiple_of(b * MLP_BLOCK, MLP_BLOCK)
        rows = pl.ds(start, MLP_BLOCK)
        hidden1 = h1_ref[rows, :]
        r2 = rms(hidden1)
        gain = gm_ref[...]
        normed2_wide = hidden1 * r2 * gain
        normed2 = normed2_wide.astype(BF)
        nmt_s[:, rows] = transposed(normed2_wide).astype(BF)
        live = (
            start + lax.broadcasted_iota(jnp.int32, (MLP_BLOCK, 1), 0) < live_len
        ).astype(F32)

        back = cot_ref[rows, :].astype(F32) * live
        back_low = back.astype(BF)
        backt_s[:, rows] = transposed(back).astype(BF)
        def columns(c):
            cols = pl.ds(pl.multiple_of(c * MLP_COLS, MLP_COLS), MLP_COLS)
            gate = nn(normed2, wg_ref[:, cols])
            up = nn(normed2, wu_ref[:, cols])
            d_inner = nt(back_low, wd_ref[cols, :])
            sig = jax.nn.sigmoid(gate)
            silu = gate * sig
            inner_s[rows, cols] = (silu * up).astype(BF)
            dg_s[rows, cols] = (d_inner * up * sig * (1.0 + gate * (1.0 - sig))).astype(BF)
            du_s[rows, cols] = (d_inner * silu).astype(BF)

        def some_columns(i, carry):
            for c in range(MLP_UNROLL):
                columns(MLP_UNROLL * i + c)
            return carry

        lax.fori_loop(0, n_cols // MLP_UNROLL, some_columns, 0)
        out_ref[rows, :] = ((hidden1 + nn(inner_s[rows, :], wd_ref[...])) * live).astype(BF)
        d_normed2 = nt(dg_s[rows, :], wg_ref[...]) + nt(du_s[rows, :], wu_ref[...])
        scaled = d_normed2 * gain
        d_hidden1 = (
            back
            + r2 * scaled
            - hidden1 * (r2 * r2 * r2) * jnp.mean(scaled * hidden1, axis=-1, keepdims=True)
        )
        dh1_ref[rows, :] = d_hidden1
        d_attn = d_hidden1.astype(BF)
        da_s[rows, :] = d_attn

        d_mixed = nt(d_attn, wo_ref[...]).astype(BF)
        for j in range(Q_TILES):
            dm_ref[j, rows, :] = tile(d_mixed, j)
        for copy in results(b):
            copy.start()
        return ggm + jnp.sum(d_normed2 * hidden1 * r2, axis=0, keepdims=True)

    ggm_ref[...] = lax.fori_loop(0, seq_len // MLP_BLOCK, block, jnp.zeros((1, D), F32))

    def put(half, index, value):
        grads[half, pl.ds(pl.multiple_of(index * D, D), D), :] = value

    def leave(c):
        rows = pl.ds(pl.multiple_of(2 * c * D, D), 2 * D)
        return [
            pltpu.make_async_copy(grads.at[1 - core, rows], send_ref.at[rows], sem.at[c, 0]),
            pltpu.make_async_copy(grads.at[core, rows], keep_ref.at[rows], sem.at[c, 1]),
        ]

    def weights(c, carry):
        cols = pl.ds(pl.multiple_of(c * 2 * LANES, 2 * LANES), 2 * LANES)
        grad_gate = nn(nmt_s[:D, :], dg_s[:, cols]).astype(BF)
        grad_up = nn(nmt_s[:D, :], du_s[:, cols]).astype(BF)
        for t in range(2):
            put(0, 2 * c + t, tile(grad_gate, t))
            put(1, 2 * c + t, tile(grad_up, t))
        for copy in leave(c):
            copy.start()
        grad_down = nn(backt_s[:D, :], inner_s[:, cols]).astype(BF)
        part = jnp.where(c < DOWN_FIRST // 2, 0, 1)
        base = jnp.where(c < DOWN_FIRST // 2, FF_TILES + Q_TILES, FF_TILES - DOWN_FIRST)
        for t in range(2):
            put(part, base + 2 * c + t, tile(grad_down, t))
        return carry

    lax.fori_loop(0, n_cols, weights, 0)
    loads[6].wait()
    grad_o = tn(mixed_ref[...], da_s[...])[:D]
    for t in range(4):
        put(0, FF_TILES + t, tile(grad_o, t).astype(BF))
    put(0, FF_TILES + 4, half_tile(grad_o).astype(BF))
    grads[0, EXTRA:, :] = jnp.zeros((EARLY_ROWS - EXTRA, LANES), BF)
    grads[1, EXTRA - D :, :] = jnp.zeros((EARLY_ROWS - EXTRA + D, LANES), BF)
    row = lax.broadcasted_iota(jnp.int32, (16, LANES), 0)
    rest = jnp.zeros((16, LANES), F32)
    for r in range(5):
        start = (8 + r) * D - 16
        last = grads[0, start : start + 16, :].astype(F32)[15:16]
        rest = jnp.where(row == r, jnp.broadcast_to(last, (16, LANES)), rest)
    grads[0, EXTRA + 16 : EXTRA + 32, :] = rest.astype(BF)
    rows = pl.ds(FF_TILES * D, EARLY_ROWS - FF_TILES * D)
    final = [
        pltpu.make_async_copy(grads.at[1 - core, rows], send_ref.at[rows], sem.at[n_cols, 0]),
        pltpu.make_async_copy(grads.at[core, rows], keep_ref.at[rows], sem.at[n_cols, 1]),
    ]
    for copy in final:
        copy.start()

    def drain(c, carry):
        for copy in leave(c):
            copy.wait()
        return carry

    def drain_results(b, carry):
        for copy in results(b):
            copy.wait()
        return carry

    lax.fori_loop(0, n_cols, drain, 0)
    lax.fori_loop(0, seq_len // MLP_BLOCK, drain_results, 0)
    for copy in final:
        copy.wait()


def half_tile(value):
    rows = value.shape[0]
    return jnp.concatenate([value[:, 4 * LANES : D], jnp.zeros((rows, HD), value.dtype)], axis=1)


def gain_rows(value):
    row = lax.broadcasted_iota(jnp.int32, (16, LANES), 0)
    whole = jnp.zeros((16, LANES), F32)
    for t in range(Q_TILES):
        piece = tile(value, t) if t < 4 else half_tile(value)
        whole = jnp.where(row == t, jnp.broadcast_to(piece, (16, LANES)), whole)
    return whole


def backward_groups(
    first, q_ref, dm_ref, k_ref, v_ref, lse_ref, dq_ref, dk_ref, dv_ref, dk_acc, dv_acc
):
    seq_len = q_ref.shape[1]
    group = first + pl.program_id(0)
    dq_ref[...] = jnp.zeros_like(dq_ref)
    dk_acc[...] = jnp.zeros_like(dk_acc)
    dv_acc[...] = jnp.zeros_like(dv_acc)
    keep = lax.broadcasted_iota(jnp.int32, (BLOCK, BLOCK), 0) <= lax.broadcasted_iota(
        jnp.int32, (BLOCK, BLOCK), 1
    )
    for b in range(seq_len // BLOCK):
        rows = slice(b * BLOCK, (b + 1) * BLOCK)
        n_keys = (b + 1) * BLOCK
        for u in range(3):
            head = 3 * group + u
            j = lax.shift_right_logical(head, 1)
            own = j - lax.shift_right_logical(3 * group, 1)
            side = head - 2 * j
            queries = q_ref[j, rows, :]
            d_mixed = dm_ref[j, rows, :]
            keys = k_ref[side, 0:n_keys, :]
            values = v_ref[side, 0:n_keys, :]
            prob = jnp.exp(nt(keys, queries) - lse_ref[pl.ds(head, 1), rows])
            diag = jnp.where(keep, prob[n_keys - BLOCK :, :], 0.0)
            if n_keys > BLOCK:
                prob = jnp.concatenate([prob[: n_keys - BLOCK, :], diag], axis=0)
            else:
                prob = diag
            d_prob = nt(values, d_mixed)
            delta = jnp.sum(d_prob * prob, axis=0, keepdims=True)
            d_score = (prob * (d_prob - delta)).astype(BF)
            dv_acc[side, 0:n_keys, :] += nn(prob.astype(BF), d_mixed)
            dk_acc[side, 0:n_keys, :] += nn(d_score, queries)
            dq_ref[0, own, rows, :] += tn(d_score, keys)
    dk_ref[0] = dk_acc[0] + flip(dk_acc[1])
    dv_ref[0] = dv_acc[0] + flip(dv_acc[1])


def backward_finish(
    x_ref, ga_ref, dh1_ref, dqa_ref, dka_ref, dva_ref, dqb_ref, dkb_ref, dvb_ref,
    wq_ref, wkv_ref, cos_ref, sin_ref,
    dx_ref, dq_s, dkv_s, nm_s, gga_ref,
):
    seq_len = x_ref.shape[0]
    low = low_half(BLOCK)

    def block(b, gga):
        rows = pl.ds(pl.multiple_of(b * BLOCK, BLOCK), BLOCK)
        cosine = cos_ref[rows, :]
        sine = sin_ref[rows, :]

        def unrope(value):
            return value * cosine - swap_halves(value) * sine

        d_rot = [
            dqa_ref[0, 0, rows, :],
            dqa_ref[0, 1, rows, :] + dqb_ref[0, 0, rows, :],
            dqb_ref[0, 1, rows, :],
            dqb_ref[1, 0, rows, :],
            dqb_ref[1, 1, rows, :],
        ]
        for j in range(Q_TILES):
            d_query = unrope(d_rot[j]) * HD ** (-0.5)
            dq_s[rows, j * LANES : (j + 1) * LANES] = d_query.astype(BF)
        dk = [dka_ref[0, rows, :], dkb_ref[0, rows, :], dkb_ref[1, rows, :]]
        dv = [dva_ref[0, rows, :], dvb_ref[0, rows, :], dvb_ref[1, rows, :]]
        first = unrope(jnp.where(low, dk[0], flip(dk[1])))
        second = jnp.where(low, unrope(dk[2]), flip(dv[0]))
        third = jnp.where(low, dv[1], flip(dv[2]))
        dkv_s[rows, 0:LANES] = first.astype(BF)
        dkv_s[rows, LANES : 2 * LANES] = second.astype(BF)
        dkv_s[rows, 2 * LANES :] = third.astype(BF)
        d_normed = nt(dq_s[rows, :], wq_ref[...]) + nt(dkv_s[rows, :], wkv_ref[...])
        stream = x_ref[rows, :].astype(F32)
        r1 = rms(stream)
        gain = ga_ref[...]
        nm_s[rows, :] = (stream * r1 * gain).astype(BF)
        scaled = d_normed * gain
        dx_ref[rows, :] = (
            dh1_ref[rows, :]
            + r1 * scaled
            - stream * (r1 * r1 * r1) * jnp.mean(scaled * stream, axis=-1, keepdims=True)
        ).astype(BF)
        return gga + jnp.sum(d_normed * stream * r1, axis=0, keepdims=True)

    gga_ref[...] = lax.fori_loop(0, seq_len // BLOCK, block, jnp.zeros((1, D), F32))


def late_weights(
    core_ref, nm_s, dq_s, dkv_s, gga_ref, ggm_ref, keep_ref, send_ref, late, sem
):
    grad_q = tn(nm_s[...], dq_s[...]).astype(BF)
    grad_kv = tn(nm_s[...], dkv_s[...]).astype(BF)
    for t in range(Q_TILES):
        late[t * D : (t + 1) * D, :] = tile(grad_q, t)
    for t in range(3):
        late[(Q_TILES + t) * D : (Q_TILES + t + 1) * D, :] = tile(grad_kv, t)
    late[8 * D :, :] = jnp.zeros((2 * LATE_HALF - 8 * D, LANES), BF)
    late[8 * D : 8 * D + 16, :] = gain_rows(gga_ref[...]).astype(BF)
    late[8 * D + 16 : 8 * D + 32, :] = gain_rows(ggm_ref[...]).astype(BF)
    copies = []
    for i, (which, ref) in enumerate(((1 - core_ref[0], send_ref), (core_ref[0], keep_ref))):
        rows = pl.ds(pl.multiple_of(which * LATE_HALF, 8), LATE_HALF)
        copies.append(pltpu.make_async_copy(late.at[rows], ref, sem.at[i]))
    for copy in copies:
        copy.start()
    for copy in copies:
        copy.wait()


def gather_sum(bits_ref, *refs, n_parts, rows, split, merge, joined):
    n_in = 1 if joined else n_parts
    kept, got = refs[:n_in], refs[n_in : 2 * n_in]
    kinds = 2 if split else 1
    n_out = kinds * (1 if merge else n_parts)
    outs = refs[2 * n_in : 2 * n_in + n_out]
    scratch, sem = refs[2 * n_in + n_out :]
    size = rows // kinds
    copies = []
    for p in range(n_parts):
        if joined:
            part = slice(p * rows, (p + 1) * rows)
            total = kept[0][part, :].astype(F32) + got[0][part, :].astype(F32)
        else:
            total = kept[p][...].astype(F32) + got[p][...].astype(F32)
        scratch[p] = total.astype(BF)
        for i in range(kinds):
            if merge:
                target = outs[i].at[pl.ds(p * size, size)]
            else:
                target = outs[p + i * n_parts]
            start = (bits_ref[p] if i else 1 - bits_ref[p]) * size if split else 0
            source = scratch.at[p, pl.ds(pl.multiple_of(start, 8), size)]
            copies.append(pltpu.make_async_copy(source, target, sem.at[2 * p + i]))
            copies[-1].start()
    for copy in copies:
        copy.wait()


def join_halves(bits_ref, *refs, n_parts, rows, merged):
    n_in = 1 if merged else n_parts
    own, got, outs = refs[:n_in], refs[n_in : 2 * n_in], refs[2 * n_in : 2 * n_in + n_parts]
    sem = refs[2 * n_in + n_parts]
    copies = []
    for p in range(n_parts):
        for i, (group, which) in enumerate(((own, bits_ref[p]), (got, 1 - bits_ref[p]))):
            source = group[0].at[pl.ds(p * rows, rows)] if merged else group[p]
            span = pl.ds(pl.multiple_of(which * rows, 8), rows)
            copies.append(pltpu.make_async_copy(source, outs[p].at[span], sem.at[2 * p + i]))
            copies[-1].start()
    for copy in copies:
        copy.wait()


def put_wide(flat, tmp, values, rows, row):
    pairs = rows // 2
    for index, value in enumerate(values):
        tmp[pl.ds(index * D, rows), :] = value
    even = [tmp[pl.ds(i * D, pairs, stride=2), :] for i in range(Q_TILES)]
    odd = [flip(tmp[pl.ds(i * D + 1, pairs, stride=2), :]) for i in range(Q_TILES)]
    low = low_half(pairs)
    for c in range(4):
        flat[pl.ds(row + c, pairs, stride=9), :] = even[c]
    flat[pl.ds(row + 4, pairs, stride=9), :] = jnp.where(low, even[4], odd[0])
    for c in range(4):
        flat[pl.ds(row + 5 + c, pairs, stride=9), :] = jnp.where(low, odd[c], odd[c + 1])


def update_rule(scale, rate, grad, master, momentum, average):
    weight_grad = grad * scale
    new_momentum = MOMENTUM_DECAY * momentum + weight_grad
    new_master = master - rate * (weight_grad + MOMENTUM_DECAY * new_momentum)
    new_average = AVERAGE_DECAY * average + (1.0 - AVERAGE_DECAY) * new_master
    return weight_grad, new_momentum, new_master, new_average


class Chunks:
    def __init__(self, rows, base, count, rule, refs):
        self.rows, self.base, self.count, self.rule = rows, base, count, rule
        self.ins, self.outs, self.in_buf, self.out_buf, self.in_sem, self.out_sem = refs
        self.size = rows * LANES

    def span(self, c):
        return pl.ds(pl.multiple_of((self.base + c * self.rows) * LANES, LANES), self.size)

    def place(self, index, start=0, length=None):
        start = pl.multiple_of(index * self.size + start, 8 * LANES)
        return pl.ds(start, self.size if length is None else length)

    def fetch(self, c):
        return [
            pltpu.make_async_copy(
                self.ins[i].at[self.span(c)],
                self.in_buf.at[self.place(c * 3 + i)],
                self.in_sem.at[c, i],
            )
            for i in range(3)
        ]

    def flush(self, c):
        return [
            pltpu.make_async_copy(
                self.out_buf.at[self.place(c * 4 + i)],
                self.outs[i].at[self.span(c)],
                self.out_sem.at[c, i],
            )
            for i in range(4)
        ]

    def start(self):
        def body(c, carry):
            for copy in self.fetch(c):
                copy.start()
            return carry

        lax.fori_loop(0, self.count, body, 0)

    def run(self, stage, gradient):
        sub = STEP * LANES

        def body(c, carry):
            stage(c)
            for copy in self.fetch(c):
                copy.wait()

            def step(s, inner):
                grad = gradient(c, s * STEP, STEP).reshape(sub)
                values = self.rule(
                    grad, *[self.in_buf[self.place(c * 3 + i, s * sub, sub)] for i in range(3)]
                )
                for i in range(4):
                    self.out_buf[self.place(c * 4 + i, s * sub, sub)] = values[i]
                return inner

            lax.fori_loop(0, self.rows // STEP, step, 0)
            for copy in self.flush(c):
                copy.start()
            return carry

        def drain(c, carry):
            for copy in self.flush(c):
                copy.wait()
            return carry

        lax.fori_loop(0, self.count, body, 0)
        return lambda: lax.fori_loop(0, self.count, drain, 0)


class Extra:
    def __init__(self, start, ins, outs, rest):
        self.bufs, self.sem = rest[:8], rest[8]
        count = self.bufs[0].shape[0]
        span = pl.ds(start, count)
        self.count = count
        self.loads = [
            pltpu.make_async_copy(ins[i].at[span], self.bufs[i], self.sem.at[i]) for i in range(3)
        ]
        self.stores = [
            pltpu.make_async_copy(self.bufs[3 + i], outs[i].at[span], self.sem.at[3 + i])
            for i in range(4)
        ]

    def start(self):
        for copy in self.loads:
            copy.start()

    def finish(self, grad, rule):
        for copy in self.loads:
            copy.wait()
        self.bufs[7][...] = grad.reshape(grad.shape[0] * LANES)
        values = rule(self.bufs[7][pl.ds(0, self.count)], *[self.bufs[i][...] for i in range(3)])
        for i in range(4):
            self.bufs[3 + i][...] = values[i]
            self.stores[i].start()

    def drain(self):
        for copy in self.stores:
            copy.wait()


def shifted(flat, row, count):
    here = flip(flat[pl.ds(row - 1, count), :])
    after = flip(flat[pl.ds(row, count), :])
    return jnp.where(low_half(count), here, after)


def load_parts(pieces, sem):
    copies = [
        pltpu.make_async_copy(source, target, sem.at[i]) for i, (source, target) in enumerate(pieces)
    ]
    for copy in copies:
        copy.start()
    return copies


FLAT_BASE = 8
TAIL_ZERO = HALF - (GATE_ROW + 11 * CHUNK) * LANES
TAIL_ONE = HALF - (6916 + 11 * CHUNK) * LANES


def update_first(scale, rate, core_ref, bits_ref, *rest):
    halves, ins, outs = rest[:4], rest[4:7], rest[7:11]
    early_ref, flat, in_buf, out_buf, in_sem, out_sem, part_sem = rest[11:18]
    refs = (ins, outs, in_buf, out_buf, in_sem, out_sem)
    core = core_ref[0]
    rule = functools.partial(update_rule, scale, rate)
    half = PART_ROWS // 2
    pieces = []
    for p in range(2):
        for i, which in enumerate((bits_ref[p], 1 - bits_ref[p])):
            span = pl.ds(pl.multiple_of(p * PART_ROWS + which * half, 8), half)
            pieces.append((halves[2 * p + i], early_ref.at[span]))
    copies = load_parts(pieces, part_sem)
    extra = Extra((GATE_ROW + 11 * CHUNK) * LANES, ins, outs, rest[18:])
    base = jnp.where(core == 0, GATE_ROW, 4)
    chunks = Chunks(CHUNK, base, 11 + core, rule, refs)
    chunks.start()

    @pl.when(core == 0)
    def _():
        extra.start()

    for copy in copies:
        copy.wait()
    flat[0:FLAT_BASE, :] = jnp.zeros((FLAT_BASE, LANES), F32)

    def stage(c):
        for t in range(FF_TILES):
            rows = pl.ds(pl.multiple_of(t * D + c * 48, 16), 48)
            flat[pl.ds(FLAT_BASE + t, 48, stride=FF_TILES), :] = early_ref[rows, :].astype(F32)

    def gradient(c, start, count):
        row = pl.multiple_of(FLAT_BASE + start, 8)
        return jnp.where(core == 0, flat[pl.ds(row, count), :], shifted(flat, row, count))

    def stage_next(c):
        flat[FLAT_BASE - 1 : FLAT_BASE, :] = flat[FLAT_BASE + CHUNK - 1 : FLAT_BASE + CHUNK, :]
        stage(c)

    drain = chunks.run(stage_next, gradient)

    @pl.when(core == 0)
    def _():
        stage(11)
        extra.finish(flat[FLAT_BASE : FLAT_BASE + CHUNK, :], rule)

    drain()

    @pl.when(core == 0)
    def _():
        extra.drain()


def update_second(scale, rate, core_ref, bits_ref, *rest):
    halves, ins, outs = rest[:8], rest[8:11], rest[15:19]
    flat, tmp, part_ref, swap_ref, first_ref, in_buf, out_buf, in_sem, out_sem, part_sem = rest[19:29]
    refs = (ins, outs, in_buf, out_buf, in_sem, out_sem)
    tail = Extra((6916 + 11 * CHUNK) * LANES, ins, outs, rest[29:38])
    head = Extra(0, ins, outs, rest[38:])
    rule = functools.partial(update_rule, scale, rate)
    half = PART_ROWS // 2
    pieces = []
    for i in range(2):
        which = [1 - bits_ref[p] if i else bits_ref[p] for p in range(3)]

        def rows(start, p, size, which=which):
            return pl.ds(pl.multiple_of(start + which[p] * size, 16), size)

        source = halves[2 + i].at[pl.ds(half - REST_SLOT, REST_SLOT)]
        pieces.append((source, part_ref.at[rows(0, 1, REST_SLOT)]))
        pieces.append((halves[4 + i], part_ref.at[rows(2 * REST_SLOT, 2, half)]))
        pieces.append((halves[6 + i], swap_ref.at[rows(0, 2, half)]))
        pieces.append((halves[i].at[pl.ds(0, 16)], first_ref.at[rows(0, 0, 16)]))
    parts = load_parts(pieces, part_sem)

    @pl.when(core_ref[0] == 0)
    def _():
        def stage(c):
            values = []
            for t in range(Q_TILES):
                rows = pl.ds(pl.multiple_of(REST + t * D + c * 64, 16), 64)
                values.append(part_ref[rows, :].astype(F32))
            put_wide(flat, tmp, values, 64, FLAT_BASE)

        def gradient(c, start, count):
            return flat[pl.ds(pl.multiple_of(FLAT_BASE + start, 8), count), :]

        chunks = Chunks(CHUNK // 2, O_ROW, 9, rule, refs)
        chunks.start()
        for copy in parts:
            copy.wait()
        chunks.run(stage, gradient)()

    @pl.when(core_ref[0] == 1)
    def _():
        head.start()
        chunks = Chunks(CHUNK, 6916, 11, rule, refs)
        chunks.start()
        tail.start()
        for copy in parts:
            copy.wait()
        flat[0:FLAT_BASE, :] = jnp.zeros((FLAT_BASE, LANES), F32)
        flat[FLAT_BASE : FLAT_BASE + 8, :] = swap_ref[SWAP_TAIL : SWAP_TAIL + 16, :].astype(F32)[0:8]
        flat[FLAT_BASE + 5 : FLAT_BASE + 6, :] = first_ref[0:16, :].astype(F32)[0:1]
        head.finish(shifted(flat, FLAT_BASE + 1, 8), rule)
        row = FLAT_BASE + CHUNK - 1
        flat[row : row + 1, :] = part_ref[REST - 16 : REST, :].astype(F32)[15:16]

        def stage(c):
            flat[FLAT_BASE - 1 : FLAT_BASE, :] = flat[FLAT_BASE + CHUNK - 1 : FLAT_BASE + CHUNK, :]
            inside = c < DOWN_FIRST
            here = pl.ds(pl.multiple_of(SWAP_START + jnp.where(inside, c, 0) * D, 16), D)
            there = pl.ds(pl.multiple_of(REST + jnp.where(inside, 0, c - DOWN_FIRST) * D, 16), D)
            whole = jnp.where(inside, swap_ref[here, :].astype(F32), part_ref[there, :].astype(F32))
            pieces = [whole[i * LANES : (i + 1) * LANES].T for i in range(4)]
            half = jnp.concatenate([whole[4 * LANES :], jnp.zeros((LANES - HD, LANES), F32)], axis=0)
            put_wide(flat, tmp, pieces + [half.T], LANES, FLAT_BASE)

        def gradient(c, start, count):
            return shifted(flat, FLAT_BASE + start, count)

        drain = chunks.run(stage, gradient)
        stage(11)
        flat[FLAT_BASE + CHUNK :, :] = jnp.zeros((8, LANES), F32)
        tail.finish(shifted(flat, FLAT_BASE, CHUNK + 8), rule)
        head.drain()
        drain()
        tail.drain()


def update_late(scale, rate, core_ref, own_ref, other_ref, *rest):
    ins, outs = rest[:3], rest[7:11]
    flat, tmp, late_ref, in_buf, out_buf, in_sem, out_sem = rest[11:18]
    refs = (ins, outs, in_buf, out_buf, in_sem, out_sem)
    extra = Extra(LATE_CHUNKS * CHUNK * LANES, ins, outs, rest[18:])
    rule = functools.partial(update_rule, scale, rate)

    @pl.when(core_ref[0] == 0)
    def _():
        chunks = Chunks(CHUNK, 0, LATE_CHUNKS, rule, refs)
        chunks.start()
        extra.start()
        late_ref[:LATE_HALF, :] = own_ref[...]
        late_ref[LATE_HALF:, :] = other_ref[...]

        def late(index):
            return late_ref[index * D : (index + 1) * D, :].astype(F32)

        low1 = low_half(1)
        gain_a = late_ref[8 * D : 8 * D + 16, :].astype(F32)
        gain_m = flip(late_ref[8 * D + 16 : 8 * D + 32, :].astype(F32))
        for r in range(4):
            flat[r : r + 1, :] = gain_a[r : r + 1]
        flat[4:5, :] = jnp.where(low1, gain_a[4:5], gain_m[0:1])
        for r in range(4):
            flat[5 + r : 6 + r, :] = jnp.where(low1, gain_m[r : r + 1], gain_m[r + 1 : r + 2])
        put_wide(flat, tmp, [late(t) for t in range(Q_TILES)], D, 9)
        pairs = D // 2
        for t in range(3):
            tmp[pl.ds(t * D, D), :] = late(Q_TILES + t)
        even = [tmp[pl.ds(i * D, pairs, stride=2), :] for i in range(3)]
        odd = [tmp[pl.ds(i * D + 1, pairs, stride=2), :] for i in range(3)]
        low = low_half(pairs)
        turned = [flip(odd[0]), flip(odd[1]), flip(even[1]), flip(even[2])]
        rows = (
            (2601, even[0]),
            (2602, jnp.where(low, even[1], turned[0])),
            (2603, jnp.where(low, turned[0], turned[1])),
            (3465, jnp.where(low, turned[2], turned[3])),
            (3466, jnp.where(low, turned[3], odd[1])),
            (3467, odd[2]),
        )
        for row, value in rows:
            flat[pl.ds(row, pairs, stride=3), :] = value

        def gradient(c, start, count):
            return flat[pl.ds(pl.multiple_of(c * CHUNK + start, 8), count), :]

        drain = chunks.run(lambda c: None, gradient)
        start = LATE_CHUNKS * CHUNK
        extra.finish(flat[start : start + 304, :], rule)
        drain()
        extra.drain()


def vmem():
    return pl.BlockSpec(memory_space=pltpu.VMEM)


def smem():
    return pl.BlockSpec(memory_space=pltpu.SMEM)


def hbm():
    return pl.BlockSpec(memory_space=pl.ANY)


def call(kernel, outs, in_specs, out_specs, scratch, flops, name, limit, aliases=None):
    n_bytes = sum(math.prod(shape) * jnp.dtype(kind).itemsize for shape, kind in outs)
    return pl.pallas_call(
        kernel,
        out_shape=[jax.ShapeDtypeStruct(shape, kind) for shape, kind in outs],
        in_specs=in_specs,
        out_specs=out_specs,
        scratch_shapes=scratch,
        input_output_aliases=aliases or {},
        compiler_params=pltpu.CompilerParams(vmem_limit_bytes=limit * MIB),
        cost_estimate=pl.CostEstimate(
            flops=int(flops), bytes_accessed=int(2 * n_bytes), transcendentals=0
        ),
        name=name,
    )


def rope_tables(seq_len):
    lane = jnp.arange(LANES, dtype=jnp.int32)
    which = (lane % (HD // 2)).astype(F32)
    frequency = jnp.exp(which * (-2.0 * math.log(10000.0) / HD))
    angles = jnp.arange(seq_len, dtype=F32)[:, None] * frequency[None, :]
    sign = jnp.where(lane % HD < HD // 2, -1.0, 1.0)
    return jnp.cos(angles), jnp.sin(angles) * sign[None, :]


def run_prepare(core, own, other):
    outs = [
        ((1, D), F32),
        ((1, D), F32),
        ((D, PAD_D), BF),
        ((D, KV_COLS), BF),
        ((PAD_D, D), BF),
        ((D, FF), BF),
        ((D, FF), BF),
        ((FF, D), BF),
    ]
    scratch = [
        pltpu.VMEM((2, HALF_ROWS, LANES), BF),
        pltpu.VMEM((FLAT_SCRATCH, LANES), F32),
        pltpu.VMEM((Q_TILES * D, LANES), F32),
        pltpu.SemaphoreType.DMA((2,)),
    ]
    return call(
        prepare_weights,
        outs,
        [smem()] + [hbm()] * 2,
        [vmem()] * 8,
        scratch,
        1e10,
        "prepare_weights",
        60,
    )(core, own, other)


def run_attention_forward(x, gain, wq, wkv, wo, cosine, sine):
    seq_len = x.shape[0]
    outs = [
        ((seq_len, D), F32),
        ((seq_len, PAD_D), BF),
        ((Q_TILES, seq_len, LANES), BF),
        ((6, seq_len, LANES), BF),
        ((6, seq_len, LANES), BF),
        ((16, seq_len), F32),
    ]
    return call(
        attention_forward,
        outs,
        [vmem()] * 7,
        [vmem()] * 6,
        [pltpu.VMEM((Q_TILES, BLOCK, LANES), F32)],
        1.5e10,
        "attention_forward",
        60,
    )(x, gain, wq, wkv, wo, cosine, sine)


def run_mlp(core, slot, lengths, assignment, hidden1, cot, mixed, gain, wo, wg, wu, wd):
    seq_len = hidden1.shape[0]
    outs = [
        ((seq_len, D), BF),
        ((seq_len, D), F32),
        ((Q_TILES, seq_len, LANES), BF),
        ((1, D), F32),
        ((EARLY_ROWS, LANES), BF),
        ((EARLY_ROWS, LANES), BF),
    ]
    return call(
        mlp_pass,
        outs,
        [smem()] * 4 + [hbm()] * 3 + [vmem()] + [hbm()] * 4,
        [hbm()] * 3 + [vmem()] + [hbm()] * 2,
        [
            pltpu.VMEM((seq_len, D), F32),
            pltpu.VMEM((seq_len, D), BF),
            pltpu.VMEM((seq_len, PAD_D), BF),
            pltpu.VMEM((PAD_D, D), BF),
            pltpu.VMEM((D, FF), BF),
            pltpu.VMEM((D, FF), BF),
            pltpu.VMEM((FF, D), BF),
            pltpu.VMEM((seq_len, D), BF),
            pltpu.VMEM((seq_len, D), F32),
            pltpu.VMEM((Q_TILES, seq_len, LANES), BF),
            pltpu.VMEM((PAD_D, seq_len), BF),
            pltpu.VMEM((PAD_D, seq_len), BF),
            pltpu.VMEM((seq_len, FF), BF),
            pltpu.VMEM((seq_len, FF), BF),
            pltpu.VMEM((seq_len, FF), BF),
            pltpu.VMEM((seq_len, D), BF),
            pltpu.VMEM((2, EARLY_ROWS, LANES), BF),
            pltpu.SemaphoreType.DMA((7,)),
            pltpu.SemaphoreType.DMA((seq_len // MLP_BLOCK, 3)),
            pltpu.SemaphoreType.DMA((FF_TILES // 2 + 1, 2)),
        ],
        2.5e10,
        "mlp_pass",
        60,
    )(core, slot, lengths, assignment, hidden1, cot, mixed, gain, wo, wg, wu, wd)


def run_backward_groups(first, count, q, dm, k, v, lse):
    seq_len = q.shape[1]
    fixed = pl.BlockSpec((Q_TILES, seq_len, LANES), lambda i: (0, 0, 0))
    sides = pl.BlockSpec((2, seq_len, LANES), lambda i: (first + i, 0, 0))
    single = pl.BlockSpec((1, seq_len, LANES), lambda i: (i, 0, 0))
    outs = [(count, 2, seq_len, LANES), (count, seq_len, LANES), (count, seq_len, LANES)]
    return pl.pallas_call(
        functools.partial(backward_groups, first),
        grid=(count,),
        out_shape=[jax.ShapeDtypeStruct(shape, F32) for shape in outs],
        in_specs=[
            fixed,
            fixed,
            sides,
            sides,
            pl.BlockSpec((16, seq_len), lambda i: (0, 0)),
        ],
        out_specs=[
            pl.BlockSpec((1, 2, seq_len, LANES), lambda i: (i, 0, 0, 0)),
            single,
            single,
        ],
        scratch_shapes=[pltpu.VMEM((2, seq_len, LANES), F32)] * 2,
        compiler_params=pltpu.CompilerParams(vmem_limit_bytes=60 * MIB),
        cost_estimate=pl.CostEstimate(
            flops=int(8e9) * count, bytes_accessed=int(3e6) * count, transcendentals=0
        ),
        name="backward_groups",
    )(q, dm, k, v, lse)


def run_backward_finish(x, gain, dh1, groups, wq, wkv, cosine, sine):
    seq_len = x.shape[0]
    outs = [
        ((seq_len, D), BF),
        ((seq_len, PAD_D), BF),
        ((seq_len, KV_COLS), BF),
        ((seq_len, D), BF),
        ((1, D), F32),
    ]
    return call(
        backward_finish,
        outs,
        [vmem()] * 13,
        [vmem()] * 5,
        [],
        4e9,
        "backward_finish",
        60,
    )(x, gain, dh1, *groups[0], *groups[1], wq, wkv, cosine, sine)


def run_late_weights(core, normed, d_query, d_kv, gga, ggm):
    outs = [((LATE_HALF, LANES), BF), ((LATE_HALF, LANES), BF)]
    return call(
        late_weights,
        outs,
        [smem()] + [vmem()] * 5,
        [hbm()] * 2,
        [pltpu.VMEM((2 * LATE_HALF, LANES), BF), pltpu.SemaphoreType.DMA((2,))],
        4e9,
        "late_weights",
        60,
    )(core, normed, d_query, d_kv, gga, ggm)


def run_sum(bits, kept, got, split, merge=False, n_parts=None):
    joined = n_parts is not None
    n_parts = n_parts or len(kept)
    rows = kept[0].shape[0] // (n_parts if joined else 1)
    kinds = 2 if split else 1
    n_out = 1 if merge else n_parts
    out_rows = rows // kinds * (n_parts if merge else 1)
    results = call(
        functools.partial(
            gather_sum, n_parts=n_parts, rows=rows, split=split, merge=merge, joined=joined
        ),
        [((out_rows, LANES), BF)] * (kinds * n_out),
        [smem()] + [vmem()] * (2 * len(kept)),
        [hbm()] * (kinds * n_out),
        [pltpu.VMEM((n_parts, rows, LANES), BF), pltpu.SemaphoreType.DMA((2 * n_parts,))],
        1e6,
        "gather_sum",
        12,
    )(bits, *kept, *got)
    return list(results[:n_out]), list(results[n_out:])


def run_join(bits, own, got, n_parts):
    merged = len(own) < n_parts
    rows = own[0].shape[0] // (n_parts if merged else 1)
    return call(
        functools.partial(join_halves, n_parts=n_parts, rows=rows, merged=merged),
        [((2 * rows, LANES), BF)] * n_parts,
        [smem()] + [hbm()] * (2 * len(own)),
        [hbm()] * n_parts,
        [pltpu.SemaphoreType.DMA((2 * n_parts,))],
        1e6,
        "join_halves",
        4,
    )(bits, *own, *got)


def chunk_scratch(count):
    return [
        pltpu.VMEM((3 * count * CHUNK * LANES,), F32),
        pltpu.VMEM((4 * count * CHUNK * LANES,), F32),
        pltpu.SemaphoreType.DMA((12, 3)),
        pltpu.SemaphoreType.DMA((12, 4)),
    ]


def extra_scratch(count, n_rows):
    bufs = [pltpu.VMEM((count,), F32)] * 7 + [pltpu.VMEM((n_rows * LANES,), F32)]
    return bufs + [pltpu.SemaphoreType.DMA((7,))]


def run_update_first(scale, rate, core, bits, halves, state):
    scratch = [
        pltpu.VMEM((2 * PART_ROWS, LANES), BF),
        pltpu.VMEM((FLAT_BASE + CHUNK, LANES), F32),
        *chunk_scratch(12),
        pltpu.SemaphoreType.DMA((4,)),
        *extra_scratch(TAIL_ZERO, CHUNK),
    ]
    return call(
        functools.partial(update_first, scale, rate),
        [(state[0].shape, F32)] * 4,
        [smem()] * 2 + [hbm()] * 7,
        [hbm()] * 4,
        scratch,
        1e9,
        "update_first",
        60,
    )(core, bits, *halves, *state)


def run_update_second(scale, rate, core, bits, halves, state, done):
    scratch = [
        pltpu.VMEM((FLAT_BASE + CHUNK + 8, LANES), F32),
        pltpu.VMEM((Q_TILES * D, LANES), F32),
        pltpu.VMEM((2 * REST_SLOT + PART_ROWS, LANES), BF),
        pltpu.VMEM((PART_ROWS, LANES), BF),
        pltpu.VMEM((32, LANES), BF),
        *chunk_scratch(11),
        pltpu.SemaphoreType.DMA((8,)),
        *extra_scratch(TAIL_ONE, CHUNK + 8),
        *extra_scratch(5 * LANES, 8),
    ]
    return call(
        functools.partial(update_second, scale, rate),
        [(state[0].shape, F32)] * 4,
        [smem()] * 2 + [hbm()] * 15,
        [hbm()] * 4,
        scratch,
        1e9,
        "update_second",
        60,
        {13 + i: i for i in range(4)},
    )(core, bits, *halves, *state, *done)


def run_update_late(scale, rate, core, own, other, state, done):
    last_rows = O_ROW - LATE_CHUNKS * CHUNK
    scratch = [
        pltpu.VMEM((4336, LANES), F32),
        pltpu.VMEM((Q_TILES * D, LANES), F32),
        pltpu.VMEM((2 * LATE_HALF, LANES), BF),
        *chunk_scratch(LATE_CHUNKS),
        *extra_scratch(last_rows * LANES, 304),
    ]
    return call(
        functools.partial(update_late, scale, rate),
        [(state[0].shape, F32)] * 4,
        [smem()] + [vmem()] * 2 + [hbm()] * 7,
        [hbm()] * 4,
        scratch,
        1e9,
        "update_late",
        60,
        {6 + i: i for i in range(4)},
    )(core, own, other, *state, *done)


def add_low(a, b):
    return (a.astype(F32) + b.astype(F32)).astype(BF)


def xor_swap(value, bit):
    size = lax.axis_size("dp")
    return lax.ppermute(value, "dp", [(i, i ^ (1 << bit)) for i in range(size)])


def tie(value, *others):
    return lax.optimization_barrier((value, *others))


def my_bits(orders, step):
    index = lax.axis_index("dp")
    return jnp.stack([(index >> order[step]) & 1 for order in orders]).astype(jnp.int32)


def spread(blocks, far):
    size = lax.axis_size("dp")
    near = min(size, 4)
    if far:
        groups = [[g * near + i for g in range(size // near)] for i in range(near)]
    else:
        groups = [[g * near + i for i in range(near)] for g in range(size // near)]
    return lax.all_to_all(
        blocks, "dp", split_axis=0, concat_axis=0, tiled=True, axis_index_groups=groups
    )


def group_size(far):
    size = lax.axis_size("dp")
    return size // min(size, 4) if far else min(size, 4)


def scatter_sum(value):
    count = group_size(False)
    blocks = spread(value.reshape(count, value.shape[0] // count, LANES), False)
    return jnp.sum(blocks.astype(F32), axis=0).astype(BF)


def copies(value, far):
    return spread(jnp.broadcast_to(value[None], (group_size(far), *value.shape)), far)


def bit_orders():
    n_bits = lax.axis_size("dp").bit_length() - 1
    base = list(range(n_bits))
    head = base[:3] if n_bits >= 3 else base
    return [head[r:] + head[:r] + base[len(head) :] for r in range(3)]


def on_device(inputs, cotangent, lengths, assignment, return_order, master, momentum, average):
    nseq_all, block_rows, _ = inputs.shape
    axes = ("dp", "shard")
    seq_len = block_rows * lax.axis_size("dp") * lax.axis_size("shard")
    my_slot = lax.axis_index(axes)
    core = lax.axis_index("shard")
    core_arr = core.astype(jnp.int32).reshape(1)

    seq_ids = jnp.arange(nseq_all, dtype=jnp.int32)
    inverse = jnp.sum(
        jnp.where(return_order[None, :] == seq_ids[:, None], seq_ids[None, :], 0), axis=1
    )

    def pick(array, index):
        return array.at[index].get(mode="promise_in_bounds")

    def exchange(value):
        return lax.all_to_all(value, axes, split_axis=0, concat_axis=0, tiled=True)

    sent_in, master_in = tie(pick(inputs, assignment), master)
    x = exchange(sent_in).reshape(seq_len, D)
    slot_arr = my_slot.astype(jnp.int32).reshape(1)

    own = jnp.pad(master_in.astype(BF), (0, HALF_ROWS * LANES - master.shape[0]))
    own = own.reshape(HALF_ROWS, LANES)
    other = lax.ppermute(own, "shard", [(0, 1), (1, 0)])
    gain_attn, gain_mlp, wq, wkv, wo, wg, wu, wd = run_prepare(core_arr, own, other)

    cosine, sine = rope_tables(seq_len)
    sent_cot, gain_attn, cosine = tie(pick(cotangent, inverse), gain_attn, cosine)
    cot = exchange(sent_cot).reshape(seq_len, D)
    hidden1, mixed, q, k, v, lse = run_attention_forward(x, gain_attn, wq, wkv, wo, cosine, sine)
    result, dh1, dm, ggm, early_keep, early_send = run_mlp(
        core_arr, slot_arr, lengths, assignment, hidden1, cot, mixed, gain_mlp, wo, wg, wu, wd
    )
    back_out = exchange(result.reshape(nseq_all, block_rows, D))

    orders = bit_orders()
    n_bits = len(orders[0])

    def swap_parts(parts, step):
        return [xor_swap(part, order[step]) for part, order in zip(parts, orders)]

    got = lax.ppermute(early_send, "shard", [(0, 1), (1, 0)])
    groups = [run_backward_groups(0, 1, q, dm, k, v, lse)]
    lse, got = tie(lse, got)
    sent, kept = run_sum(my_bits(orders, 0), [early_keep], [got], True, n_parts=3)
    lse, *kept = tie(lse, *kept)
    got = swap_parts(sent, 0)
    groups.append(run_backward_groups(1, KV - 1, q, dm, k, v, lse))
    sent, kept = run_sum(my_bits(orders, 1), kept, got, True)
    dh1, back_out, *kept = tie(dh1, back_out, *kept)
    got = swap_parts(sent, 1)
    d_stream, d_query, d_kv, normed, gga = run_backward_finish(
        x, gain_attn, dh1, groups, wq, wkv, cosine, sine
    )
    last_bit = n_bits - 1
    for step in range(2, n_bits):
        if step > 2:
            got = swap_parts(sent, step - 1)
        sent, kept = run_sum(my_bits(orders, step), kept, got, True, merge=step == last_bit)
        if step == 2:
            gga, *kept = tie(gga, *kept)
            late_keep, late_send = run_late_weights(core_arr, normed, d_query, d_kv, gga, ggm)
            late_send, *kept = tie(late_send, *kept)
        if step == last_bit:
            late_send, sent[0] = tie(late_send, sent[0])
    got = [xor_swap(sent[0], last_bit)]
    late_got = lax.ppermute(late_send, "shard", [(0, 1), (1, 0)])
    early, _ = run_sum(my_bits(orders, last_bit)[:1], kept, got, False)
    late, _ = run_sum(my_bits(orders, 0)[:1], [late_keep], [late_got], False)
    late, block_output, early[0] = tie(late[0], pick(back_out, return_order), early[0])
    late = scatter_sum(late)
    early = run_join(my_bits(orders, last_bit), early, [xor_swap(early[0], last_bit)], 3)
    late, *early = tie(late, *early)
    late = jnp.sum(copies(late, True).astype(F32), axis=0).astype(BF)
    for step in reversed(range(1, last_bit)):
        early = run_join(my_bits(orders, step), early, swap_parts(early, step), 3)
        if step == last_bit - 1:
            late, *early = tie(late, *early)
            late = copies(late, False).reshape(-1, LANES)
    got = swap_parts(early, 0)
    swap_own = lax.ppermute(early[2], "shard", [(0, 1)])
    bits = my_bits(orders, 0)
    scale = 1.0 / nseq_all
    rate = (nseq_all / (0.6 * seq_len)) ** 0.5 / D**0.5
    state = (master, momentum, average)
    d_stream, late, swap_own, *got = tie(d_stream, late, swap_own, *got)
    back_grad = exchange(d_stream.reshape(nseq_all, block_rows, D))
    late_other = lax.ppermute(late, "shard", [(1, 0)])
    swap_got = lax.ppermute(got[2], "shard", [(0, 1)])
    halves = [early[0], got[0], early[1], got[1], early[2], got[2], swap_own, swap_got]
    done = run_update_first(scale, rate, core_arr, bits, halves[:4], state)
    done = run_update_second(scale, rate, core_arr, bits, halves, state, done)
    weight_grad, new_momentum, new_master, new_average = run_update_late(
        scale, rate, core_arr, late, late_other, state, done
    )
    input_grad = pick(back_grad, return_order)
    return (block_output, input_grad, weight_grad, new_momentum, new_master, new_average)


def solution(mesh):
    rows = P(None, ("dp", "shard"), None)
    flat = P("shard")
    return jax.shard_map(
        on_device,
        mesh=mesh,
        in_specs=(rows, rows, P(), P(), P(), flat, flat, flat),
        out_specs=(rows, rows, flat, flat, flat, flat),
        check_vma=False,
    )
```

```python
import functools
import math

import jax
import jax.numpy as jnp
from jax import lax
from jax.experimental import pallas as pl
from jax.experimental.pallas import tpu as pltpu
from jax.sharding import PartitionSpec as P

D = 576
H = 9
KV = 3
HD = 64
FF = 1536
LANES = 128
BLOCK = 256
Q_TILES = 5
PAD_D = Q_TILES * LANES
KV_COLS = 2 * KV * HD
FF_TILES = FF // LANES
DOWN_FIRST = 4
EARLY_TILES = 21
EARLY_ROWS = 12288
EXTRA = EARLY_TILES * D
HALF = 27657 * LANES // 2
PART_ROWS = EARLY_ROWS // 3
SWAP_START = EXTRA - DOWN_FIRST * D - 2 * PART_ROWS
SWAP_TAIL = EXTRA + 16 - 2 * PART_ROWS
REST_FIRST = 2 * PART_ROWS - FF_TILES * D
REST_SLOT = REST_FIRST + 16
REST = REST_SLOT + 16
LATE_HALF = 2432
FLAT_SCRATCH = 13848
O_ROW = 4329
GATE_ROW = 6921
MLP_COLS = 256
WIDEN = 512
MLP_UNROLL = 6
MLP_BLOCK = 256
CHUNK = 576
STEP = 288
LATE_CHUNKS = 7

EPSILON = 1e-05
MOMENTUM_DECAY = 0.55
AVERAGE_DECAY = 0.45
MASKED = -1000000000.0

BF = jnp.bfloat16
F32 = jnp.float32
MIB = 1024 * 1024


def nn(a, b):
    return jnp.dot(a, b, preferred_element_type=F32)


def nt(a, b):
    return lax.dot_general(a, b, (((1,), (1,)), ((), ())), preferred_element_type=F32)


def tn(a, b):
    return lax.dot_general(a, b, (((0,), (0,)), ((), ())), preferred_element_type=F32)


def tile(value, index):
    return value[:, index * LANES : (index + 1) * LANES]


def low_half(rows):
    return lax.broadcasted_iota(jnp.int32, (rows, LANES), 1) < HD


def swap_halves(value):
    lane = lax.broadcasted_iota(jnp.int32, value.shape, 1)
    return jnp.where(lane % HD < HD // 2, pltpu.roll(value, 96, 1), pltpu.roll(value, 32, 1))


def flip(value):
    return pltpu.roll(value, HD, 1)


def rms(value):
    return lax.rsqrt(jnp.mean(value * value, axis=-1, keepdims=True) + EPSILON)


def attention_forward(
    x_ref, ga_ref, wq_ref, wkv_ref, wo_ref, cos_ref, sin_ref,
    h1_ref, mixed_ref, q_ref, k_ref, v_ref, lse_ref, o_acc,
):
    seq_len = x_ref.shape[0]
    low = low_half(BLOCK)

    def project(b, carry):
        rows = pl.ds(pl.multiple_of(b * BLOCK, BLOCK), BLOCK)
        stream = x_ref[rows, :].astype(F32)
        normed = (stream * rms(stream) * ga_ref[...]).astype(BF)
        cosine = cos_ref[rows, :]
        sine = sin_ref[rows, :]

        def rope(value):
            return value * cosine + swap_halves(value) * sine

        queries = nn(normed, wq_ref[...])
        for j in range(Q_TILES):
            q_ref[j, rows, :] = (rope(tile(queries, j)) * HD ** (-0.5)).astype(BF)
        keys_values = nn(normed, wkv_ref[...])
        first = rope(tile(keys_values, 0))
        second = tile(keys_values, 1)
        third = tile(keys_values, 2)
        mid = rope(second)

        def put(ref, index, value):
            ref[index, rows, :] = value.astype(BF)

        put(k_ref, 0, jnp.where(low, first, 0.0))
        put(k_ref, 1, jnp.where(low, 0.0, flip(first)))
        put(k_ref, 2, jnp.where(low, flip(first), 0.0))
        put(k_ref, 3, jnp.where(low, 0.0, first))
        put(k_ref, 4, jnp.where(low, mid, 0.0))
        put(k_ref, 5, jnp.where(low, 0.0, flip(mid)))
        put(v_ref, 0, jnp.where(low, flip(second), 0.0))
        put(v_ref, 1, jnp.where(low, 0.0, second))
        put(v_ref, 2, jnp.where(low, third, 0.0))
        put(v_ref, 3, jnp.where(low, 0.0, flip(third)))
        put(v_ref, 4, jnp.where(low, flip(third), 0.0))
        put(v_ref, 5, jnp.where(low, 0.0, third))
        return carry

    lax.fori_loop(0, seq_len // BLOCK, project, 0)
    lane = lax.broadcasted_iota(jnp.int32, (BLOCK, LANES), 1)
    keep = lax.broadcasted_iota(jnp.int32, (BLOCK, BLOCK), 1) <= lax.broadcasted_iota(
        jnp.int32, (BLOCK, BLOCK), 0
    )
    for b in range(seq_len // BLOCK):
        rows = slice(b * BLOCK, (b + 1) * BLOCK)
        n_keys = (b + 1) * BLOCK
        o_acc[...] = jnp.zeros_like(o_acc)

        def group(g, lse, rows=rows, n_keys=n_keys):
            for u in range(3):
                head = 3 * g + u
                j = head // 2
                side = 2 * g + head % 2
                scores = nt(q_ref[j, rows, :], k_ref[side, 0:n_keys, :])
                diag = jnp.where(keep, scores[:, n_keys - BLOCK :], MASKED)
                if n_keys > BLOCK:
                    scores = jnp.concatenate([scores[:, : n_keys - BLOCK], diag], axis=1)
                else:
                    scores = diag
                row_max = jnp.max(scores, axis=-1, keepdims=True)
                exponent = jnp.exp(scores - row_max)
                total = jnp.sum(exponent, axis=-1, keepdims=True)
                prob = (exponent * (1.0 / total)).astype(BF)
                o_acc[j] += nn(prob, v_ref[side, 0:n_keys, :])
                lse = jnp.where(lane == head, row_max + jnp.log(total), lse)
            return lse

        lse = lax.fori_loop(0, KV, group, jnp.zeros((BLOCK, LANES), F32))
        lse_ref[:, rows] = lse.T[:16]
        mixed = jnp.concatenate([o_acc[j].astype(BF) for j in range(Q_TILES)], axis=1)
        mixed_ref[rows, :] = mixed
        h1_ref[rows, :] = x_ref[rows, :].astype(F32) + nn(mixed, wo_ref[...])


def prepare_weights(
    core_ref, own_ref, other_ref,
    ga_ref, gm_ref, wq_ref, wkv_ref, wo_ref, wg_ref, wu_ref, wd_ref,
    first, second, flat, tmp, rest, sem,
):
    core = core_ref[0]
    for which, pair in enumerate(((first, second), (second, first))):

        @pl.when(core == which)
        def _(pair=pair):
            copies = [
                pltpu.make_async_copy(ref, target, sem.at[i])
                for i, (ref, target) in enumerate(zip((own_ref, other_ref), pair))
            ]
            for copy in copies:
                copy.start()
            for copy in copies:
                copy.wait()

    def widen(ref):
        def body(i, carry):
            start = pl.multiple_of(i * WIDEN, WIDEN)
            span = pl.ds(pl.multiple_of(i * WIDEN * LANES, WIDEN * LANES), WIDEN * LANES)
            flat[pl.ds(start, WIDEN), :] = ref[span].reshape(WIDEN, LANES)
            return carry

        whole = HALF // (WIDEN * LANES)
        lax.fori_loop(0, whole, body, 0)
        left = HALF - whole * WIDEN * LANES
        rest[pl.ds(0, left)] = ref[pl.ds(whole * WIDEN * LANES, left)]
        flat[whole * WIDEN : whole * WIDEN + 8, :] = rest[...].reshape(8, LANES)

    def low_precision(value):
        return value.astype(BF).astype(F32)

    def interleave(even, odd, pairs, out_ref, first_row, pad):
        low = low_half(2 * pairs)
        for t in range(Q_TILES):
            tmp[pl.ds(t * D, pairs, stride=2), :] = even[t]
            tmp[pl.ds(t * D + 1, pairs, stride=2), :] = odd[t]
        rows = pl.ds(first_row, 2 * pairs)
        for t in range(Q_TILES):
            value = tmp[t * D : t * D + 2 * pairs, :]
            if t < 4:
                out_ref[rows, t * LANES : (t + 1) * LANES] = value.astype(BF)
            elif pad:
                out_ref[rows, t * LANES :] = jnp.where(low, value, 0.0).astype(BF)
            else:
                out_ref[rows, t * LANES :] = value[:, :HD].astype(BF)

    def wide(row, out_ref, pad):
        pairs = D // 2
        low = low_half(pairs)
        cols = [flat[pl.ds(row + c, pairs, stride=9), :] for c in range(9)]
        turned = [flip(cols[c]) for c in range(4, 9)]
        odd = [jnp.where(low, turned[t], turned[t + 1]) for t in range(4)] + [turned[4]]
        interleave(cols[:5], odd, pairs, out_ref, 0, pad)

    widen(first)
    low1 = low_half(1)
    turned = [flip(flat[4 + r : 5 + r, :]) for r in range(5)]
    for r in range(4):
        ga_ref[:, r * LANES : (r + 1) * LANES] = low_precision(flat[r : r + 1, :])
        gm_ref[:, r * LANES : (r + 1) * LANES] = low_precision(
            jnp.where(low1, turned[r], turned[r + 1])
        )
    ga_ref[:, 4 * LANES :] = low_precision(flat[4:5, :HD])
    gm_ref[:, 4 * LANES :] = low_precision(turned[4][:, :HD])
    wide(9, wq_ref, True)
    wide(O_ROW, wo_ref, False)
    wo_ref[D:, :] = jnp.zeros((PAD_D - D, D), BF)
    pairs = D // 2
    low = low_half(pairs)
    narrow = []
    for row in (2601, 3465):
        cols = [flat[pl.ds(row + c, pairs, stride=3), :] for c in range(3)]
        turned = [flip(cols[1]), flip(cols[2])]
        even = cols[:2]
        odd = [jnp.where(low, turned[0], turned[1]), turned[1]]
        for t in range(2):
            tmp[pl.ds(t * D, pairs, stride=2), :] = even[t]
            tmp[pl.ds(t * D + 1, pairs, stride=2), :] = odd[t]
        narrow.append((tmp[0:D, :], tmp[D : 2 * D, :]))
    (k0, k1), (v0, v1) = narrow
    low = low_half(D)
    v0 = flip(v0)
    v1 = flip(v1)
    wkv_ref[:, 0:LANES] = k0.astype(BF)
    wkv_ref[:, LANES : 2 * LANES] = jnp.where(low, k1, v0).astype(BF)
    wkv_ref[:, 2 * LANES :] = jnp.where(low, v0, v1).astype(BF)
    head = second[pl.ds(0, 1024)].reshape(8, LANES)
    turned = flip(head)
    for r in range(5):
        row = GATE_ROW + FF_TILES * (D - 1) + 7 + r
        before = flat[row : row + 1, :] if r == 0 else turned[r - 1 : r]
        flat[row : row + 1, :] = jnp.where(low1, before, turned[r : r + 1])
    for t in range(FF_TILES):
        wg_ref[:, t * LANES : (t + 1) * LANES] = flat[
            pl.ds(GATE_ROW + t, D, stride=FF_TILES), :
        ].astype(BF)
    widen(second)
    here = flip(flat[pl.ds(4, D, stride=FF_TILES), :])
    for t in range(FF_TILES):
        after = flip(flat[pl.ds(5 + t, D, stride=FF_TILES), :])
        wu_ref[:, t * LANES : (t + 1) * LANES] = jnp.where(low, here, after).astype(BF)
        here = after

    def down(i, carry):
        n_pairs = 96
        low = low_half(n_pairs)
        start = 6916 + 9 * n_pairs * i
        cols = [flat[pl.ds(start + c, n_pairs, stride=9), :] for c in range(10)]
        turned = [flip(cols[c]) for c in range(6)]
        even = [jnp.where(low, turned[c], turned[c + 1]) for c in range(5)]
        interleave(even, cols[5:], n_pairs, wd_ref, pl.multiple_of(2 * n_pairs * i, 16), False)
        return carry

    lax.fori_loop(0, FF // 192, down, 0)


def transposed(value):
    rows = value.shape[0]
    pieces = [tile(value, t) for t in range(4)]
    pieces.append(
        jnp.concatenate([value[:, 4 * LANES :], jnp.zeros((rows, LANES - HD), F32)], axis=1)
    )
    return jnp.concatenate([piece.T for piece in pieces], axis=0)


def mlp_pass(
    core_ref, slot_ref, lengths_ref, assignment_ref,
    h1_hbm, cot_hbm, mixed_hbm, gm_ref, wo_hbm, wg_hbm, wu_hbm, wd_hbm,
    out_hbm, dh1_hbm, dm_hbm, ggm_ref, keep_ref, send_ref,
    h1_ref, cot_ref, mixed_ref, wo_ref, wg_ref, wu_ref, wd_ref, out_ref, dh1_ref, dm_ref,
    nmt_s, backt_s, inner_s, dg_s, du_s, da_s, grads, in_sem, out_sem, sem,
):
    seq_len = h1_ref.shape[0]
    core = core_ref[0]
    live_len = lengths_ref[assignment_ref[slot_ref[0]]]
    n_cols = FF // MLP_COLS
    loads = [
        pltpu.make_async_copy(source, target, in_sem.at[i])
        for i, (source, target) in enumerate(
            (
                (h1_hbm, h1_ref),
                (cot_hbm, cot_ref),
                (wg_hbm, wg_ref),
                (wu_hbm, wu_ref),
                (wd_hbm, wd_ref),
                (wo_hbm, wo_ref),
                (mixed_hbm, mixed_ref),
            )
        )
    ]
    for copy in loads:
        copy.start()
    for copy in loads[:6]:
        copy.wait()

    def results(b):
        rows = pl.ds(pl.multiple_of(b * MLP_BLOCK, MLP_BLOCK), MLP_BLOCK)
        pairs = [(out_ref.at[rows], out_hbm.at[rows]), (dh1_ref.at[rows], dh1_hbm.at[rows])]
        pairs.append((dm_ref.at[:, rows], dm_hbm.at[:, rows]))
        return [
            pltpu.make_async_copy(source, target, out_sem.at[b, i])
            for i, (source, target) in enumerate(pairs)
        ]

    def block(b, ggm):
        start = pl.multiple_of(b * MLP_BLOCK, MLP_BLOCK)
        rows = pl.ds(start, MLP_BLOCK)
        hidden1 = h1_ref[rows, :]
        r2 = rms(hidden1)
        gain = gm_ref[...]
        normed2_wide = hidden1 * r2 * gain
        normed2 = normed2_wide.astype(BF)
        nmt_s[:, rows] = transposed(normed2_wide).astype(BF)
        live = (
            start + lax.broadcasted_iota(jnp.int32, (MLP_BLOCK, 1), 0) < live_len
        ).astype(F32)

        back = cot_ref[rows, :].astype(F32) * live
        back_low = back.astype(BF)
        backt_s[:, rows] = transposed(back).astype(BF)
        def columns(c):
            cols = pl.ds(pl.multiple_of(c * MLP_COLS, MLP_COLS), MLP_COLS)
            gate = nn(normed2, wg_ref[:, cols])
            up = nn(normed2, wu_ref[:, cols])
            d_inner = nt(back_low, wd_ref[cols, :])
            sig = jax.nn.sigmoid(gate)
            silu = gate * sig
            inner_s[rows, cols] = (silu * up).astype(BF)
            dg_s[rows, cols] = (d_inner * up * sig * (1.0 + gate * (1.0 - sig))).astype(BF)
            du_s[rows, cols] = (d_inner * silu).astype(BF)

        def some_columns(i, carry):
            for c in range(MLP_UNROLL):
                columns(MLP_UNROLL * i + c)
            return carry

        lax.fori_loop(0, n_cols // MLP_UNROLL, some_columns, 0)
        out_ref[rows, :] = ((hidden1 + nn(inner_s[rows, :], wd_ref[...])) * live).astype(BF)
        d_normed2 = nt(dg_s[rows, :], wg_ref[...]) + nt(du_s[rows, :], wu_ref[...])
        scaled = d_normed2 * gain
        d_hidden1 = (
            back
            + r2 * scaled
            - hidden1 * (r2 * r2 * r2) * jnp.mean(scaled * hidden1, axis=-1, keepdims=True)
        )
        dh1_ref[rows, :] = d_hidden1
        d_attn = d_hidden1.astype(BF)
        da_s[rows, :] = d_attn

        d_mixed = nt(d_attn, wo_ref[...]).astype(BF)
        for j in range(Q_TILES):
            dm_ref[j, rows, :] = tile(d_mixed, j)
        for copy in results(b):
            copy.start()
        return ggm + jnp.sum(d_normed2 * hidden1 * r2, axis=0, keepdims=True)

    ggm_ref[...] = lax.fori_loop(0, seq_len // MLP_BLOCK, block, jnp.zeros((1, D), F32))

    def put(half, index, value):
        grads[half, pl.ds(pl.multiple_of(index * D, D), D), :] = value

    def leave(c):
        rows = pl.ds(pl.multiple_of(2 * c * D, D), 2 * D)
        return [
            pltpu.make_async_copy(grads.at[1 - core, rows], send_ref.at[rows], sem.at[c, 0]),
            pltpu.make_async_copy(grads.at[core, rows], keep_ref.at[rows], sem.at[c, 1]),
        ]

    def weights(c, carry):
        cols = pl.ds(pl.multiple_of(c * 2 * LANES, 2 * LANES), 2 * LANES)
        grad_gate = nn(nmt_s[:D, :], dg_s[:, cols]).astype(BF)
        grad_up = nn(nmt_s[:D, :], du_s[:, cols]).astype(BF)
        for t in range(2):
            put(0, 2 * c + t, tile(grad_gate, t))
            put(1, 2 * c + t, tile(grad_up, t))
        for copy in leave(c):
            copy.start()
        grad_down = nn(backt_s[:D, :], inner_s[:, cols]).astype(BF)
        part = jnp.where(c < DOWN_FIRST // 2, 0, 1)
        base = jnp.where(c < DOWN_FIRST // 2, FF_TILES + Q_TILES, FF_TILES - DOWN_FIRST)
        for t in range(2):
            put(part, base + 2 * c + t, tile(grad_down, t))
        return carry

    lax.fori_loop(0, n_cols, weights, 0)
    loads[6].wait()
    grad_o = tn(mixed_ref[...], da_s[...])[:D]
    for t in range(4):
        put(0, FF_TILES + t, tile(grad_o, t).astype(BF))
    put(0, FF_TILES + 4, half_tile(grad_o).astype(BF))
    grads[0, EXTRA:, :] = jnp.zeros((EARLY_ROWS - EXTRA, LANES), BF)
    grads[1, EXTRA - D :, :] = jnp.zeros((EARLY_ROWS - EXTRA + D, LANES), BF)
    row = lax.broadcasted_iota(jnp.int32, (16, LANES), 0)
    rest = jnp.zeros((16, LANES), F32)
    for r in range(5):
        start = (8 + r) * D - 16
        last = grads[0, start : start + 16, :].astype(F32)[15:16]
        rest = jnp.where(row == r, jnp.broadcast_to(last, (16, LANES)), rest)
    grads[0, EXTRA + 16 : EXTRA + 32, :] = rest.astype(BF)
    rows = pl.ds(FF_TILES * D, EARLY_ROWS - FF_TILES * D)
    final = [
        pltpu.make_async_copy(grads.at[1 - core, rows], send_ref.at[rows], sem.at[n_cols, 0]),
        pltpu.make_async_copy(grads.at[core, rows], keep_ref.at[rows], sem.at[n_cols, 1]),
    ]
    for copy in final:
        copy.start()

    def drain(c, carry):
        for copy in leave(c):
            copy.wait()
        return carry

    def drain_results(b, carry):
        for copy in results(b):
            copy.wait()
        return carry

    lax.fori_loop(0, n_cols, drain, 0)
    lax.fori_loop(0, seq_len // MLP_BLOCK, drain_results, 0)
    for copy in final:
        copy.wait()


def half_tile(value):
    rows = value.shape[0]
    return jnp.concatenate([value[:, 4 * LANES : D], jnp.zeros((rows, HD), value.dtype)], axis=1)


def gain_rows(value):
    row = lax.broadcasted_iota(jnp.int32, (16, LANES), 0)
    whole = jnp.zeros((16, LANES), F32)
    for t in range(Q_TILES):
        piece = tile(value, t) if t < 4 else half_tile(value)
        whole = jnp.where(row == t, jnp.broadcast_to(piece, (16, LANES)), whole)
    return whole


def backward_groups(
    first, q_ref, dm_ref, k_ref, v_ref, lse_ref, dq_ref, dk_ref, dv_ref, dk_acc, dv_acc
):
    seq_len = q_ref.shape[1]
    group = first + pl.program_id(0)
    dq_ref[...] = jnp.zeros_like(dq_ref)
    dk_acc[...] = jnp.zeros_like(dk_acc)
    dv_acc[...] = jnp.zeros_like(dv_acc)
    keep = lax.broadcasted_iota(jnp.int32, (BLOCK, BLOCK), 0) <= lax.broadcasted_iota(
        jnp.int32, (BLOCK, BLOCK), 1
    )
    for b in range(seq_len // BLOCK):
        rows = slice(b * BLOCK, (b + 1) * BLOCK)
        n_keys = (b + 1) * BLOCK
        for u in range(3):
            head = 3 * group + u
            j = lax.shift_right_logical(head, 1)
            own = j - lax.shift_right_logical(3 * group, 1)
            side = head - 2 * j
            queries = q_ref[j, rows, :]
            d_mixed = dm_ref[j, rows, :]
            keys = k_ref[side, 0:n_keys, :]
            values = v_ref[side, 0:n_keys, :]
            prob = jnp.exp(nt(keys, queries) - lse_ref[pl.ds(head, 1), rows])
            diag = jnp.where(keep, prob[n_keys - BLOCK :, :], 0.0)
            if n_keys > BLOCK:
                prob = jnp.concatenate([prob[: n_keys - BLOCK, :], diag], axis=0)
            else:
                prob = diag
            d_prob = nt(values, d_mixed)
            delta = jnp.sum(d_prob * prob, axis=0, keepdims=True)
            d_score = (prob * (d_prob - delta)).astype(BF)
            dv_acc[side, 0:n_keys, :] += nn(prob.astype(BF), d_mixed)
            dk_acc[side, 0:n_keys, :] += nn(d_score, queries)
            dq_ref[0, own, rows, :] += tn(d_score, keys)
    dk_ref[0] = dk_acc[0] + flip(dk_acc[1])
    dv_ref[0] = dv_acc[0] + flip(dv_acc[1])


def backward_finish(
    x_ref, ga_ref, dh1_ref, dqa_ref, dka_ref, dva_ref, dqb_ref, dkb_ref, dvb_ref,
    wq_ref, wkv_ref, cos_ref, sin_ref,
    dx_ref, dq_s, dkv_s, nm_s, gga_ref,
):
    seq_len = x_ref.shape[0]
    low = low_half(BLOCK)

    def block(b, gga):
        rows = pl.ds(pl.multiple_of(b * BLOCK, BLOCK), BLOCK)
        cosine = cos_ref[rows, :]
        sine = sin_ref[rows, :]

        def unrope(value):
            return value * cosine - swap_halves(value) * sine

        d_rot = [
            dqa_ref[0, 0, rows, :],
            dqa_ref[0, 1, rows, :] + dqb_ref[0, 0, rows, :],
            dqb_ref[0, 1, rows, :],
            dqb_ref[1, 0, rows, :],
            dqb_ref[1, 1, rows, :],
        ]
        for j in range(Q_TILES):
            d_query = unrope(d_rot[j]) * HD ** (-0.5)
            dq_s[rows, j * LANES : (j + 1) * LANES] = d_query.astype(BF)
        dk = [dka_ref[0, rows, :], dkb_ref[0, rows, :], dkb_ref[1, rows, :]]
        dv = [dva_ref[0, rows, :], dvb_ref[0, rows, :], dvb_ref[1, rows, :]]
        first = unrope(jnp.where(low, dk[0], flip(dk[1])))
        second = jnp.where(low, unrope(dk[2]), flip(dv[0]))
        third = jnp.where(low, dv[1], flip(dv[2]))
        dkv_s[rows, 0:LANES] = first.astype(BF)
        dkv_s[rows, LANES : 2 * LANES] = second.astype(BF)
        dkv_s[rows, 2 * LANES :] = third.astype(BF)
        d_normed = nt(dq_s[rows, :], wq_ref[...]) + nt(dkv_s[rows, :], wkv_ref[...])
        stream = x_ref[rows, :].astype(F32)
        r1 = rms(stream)
        gain = ga_ref[...]
        nm_s[rows, :] = (stream * r1 * gain).astype(BF)
        scaled = d_normed * gain
        dx_ref[rows, :] = (
            dh1_ref[rows, :]
            + r1 * scaled
            - stream * (r1 * r1 * r1) * jnp.mean(scaled * stream, axis=-1, keepdims=True)
        ).astype(BF)
        return gga + jnp.sum(d_normed * stream * r1, axis=0, keepdims=True)

    gga_ref[...] = lax.fori_loop(0, seq_len // BLOCK, block, jnp.zeros((1, D), F32))


def late_weights(
    core_ref, nm_s, dq_s, dkv_s, gga_ref, ggm_ref, keep_ref, send_ref, late, sem
):
    grad_q = tn(nm_s[...], dq_s[...]).astype(BF)
    grad_kv = tn(nm_s[...], dkv_s[...]).astype(BF)
    for t in range(Q_TILES):
        late[t * D : (t + 1) * D, :] = tile(grad_q, t)
    for t in range(3):
        late[(Q_TILES + t) * D : (Q_TILES + t + 1) * D, :] = tile(grad_kv, t)
    late[8 * D :, :] = jnp.zeros((2 * LATE_HALF - 8 * D, LANES), BF)
    late[8 * D : 8 * D + 16, :] = gain_rows(gga_ref[...]).astype(BF)
    late[8 * D + 16 : 8 * D + 32, :] = gain_rows(ggm_ref[...]).astype(BF)
    copies = []
    for i, (which, ref) in enumerate(((1 - core_ref[0], send_ref), (core_ref[0], keep_ref))):
        rows = pl.ds(pl.multiple_of(which * LATE_HALF, 8), LATE_HALF)
        copies.append(pltpu.make_async_copy(late.at[rows], ref, sem.at[i]))
    for copy in copies:
        copy.start()
    for copy in copies:
        copy.wait()


def gather_sum(bits_ref, *refs, n_parts, rows, split, merge, joined):
    n_in = 1 if joined else n_parts
    kept, got = refs[:n_in], refs[n_in : 2 * n_in]
    kinds = 2 if split else 1
    n_out = kinds * (1 if merge else n_parts)
    outs = refs[2 * n_in : 2 * n_in + n_out]
    scratch, sem = refs[2 * n_in + n_out :]
    size = rows // kinds
    copies = []
    for p in range(n_parts):
        if joined:
            part = slice(p * rows, (p + 1) * rows)
            total = kept[0][part, :].astype(F32) + got[0][part, :].astype(F32)
        else:
            total = kept[p][...].astype(F32) + got[p][...].astype(F32)
        scratch[p] = total.astype(BF)
        for i in range(kinds):
            if merge:
                target = outs[i].at[pl.ds(p * size, size)]
            else:
                target = outs[p + i * n_parts]
            start = (bits_ref[p] if i else 1 - bits_ref[p]) * size if split else 0
            source = scratch.at[p, pl.ds(pl.multiple_of(start, 8), size)]
            copies.append(pltpu.make_async_copy(source, target, sem.at[2 * p + i]))
            copies[-1].start()
    for copy in copies:
        copy.wait()


def join_halves(bits_ref, *refs, n_parts, rows, merged):
    n_in = 1 if merged else n_parts
    own, got, outs = refs[:n_in], refs[n_in : 2 * n_in], refs[2 * n_in : 2 * n_in + n_parts]
    sem = refs[2 * n_in + n_parts]
    copies = []
    for p in range(n_parts):
        for i, (group, which) in enumerate(((own, bits_ref[p]), (got, 1 - bits_ref[p]))):
            source = group[0].at[pl.ds(p * rows, rows)] if merged else group[p]
            span = pl.ds(pl.multiple_of(which * rows, 8), rows)
            copies.append(pltpu.make_async_copy(source, outs[p].at[span], sem.at[2 * p + i]))
            copies[-1].start()
    for copy in copies:
        copy.wait()


def put_wide(flat, tmp, values, rows, row):
    pairs = rows // 2
    for index, value in enumerate(values):
        tmp[pl.ds(index * D, rows), :] = value
    even = [tmp[pl.ds(i * D, pairs, stride=2), :] for i in range(Q_TILES)]
    odd = [flip(tmp[pl.ds(i * D + 1, pairs, stride=2), :]) for i in range(Q_TILES)]
    low = low_half(pairs)
    for c in range(4):
        flat[pl.ds(row + c, pairs, stride=9), :] = even[c]
    flat[pl.ds(row + 4, pairs, stride=9), :] = jnp.where(low, even[4], odd[0])
    for c in range(4):
        flat[pl.ds(row + 5 + c, pairs, stride=9), :] = jnp.where(low, odd[c], odd[c + 1])


def update_rule(scale, rate, grad, master, momentum, average):
    weight_grad = grad * scale
    new_momentum = MOMENTUM_DECAY * momentum + weight_grad
    new_master = master - rate * (weight_grad + MOMENTUM_DECAY * new_momentum)
    new_average = AVERAGE_DECAY * average + (1.0 - AVERAGE_DECAY) * new_master
    return weight_grad, new_momentum, new_master, new_average


class Chunks:
    def __init__(self, rows, base, count, rule, refs):
        self.rows, self.base, self.count, self.rule = rows, base, count, rule
        self.ins, self.outs, self.in_buf, self.out_buf, self.in_sem, self.out_sem = refs
        self.size = rows * LANES

    def span(self, c):
        return pl.ds(pl.multiple_of((self.base + c * self.rows) * LANES, LANES), self.size)

    def place(self, index, start=0, length=None):
        start = pl.multiple_of(index * self.size + start, 8 * LANES)
        return pl.ds(start, self.size if length is None else length)

    def fetch(self, c):
        return [
            pltpu.make_async_copy(
                self.ins[i].at[self.span(c)],
                self.in_buf.at[self.place(c * 3 + i)],
                self.in_sem.at[c, i],
            )
            for i in range(3)
        ]

    def flush(self, c):
        return [
            pltpu.make_async_copy(
                self.out_buf.at[self.place(c * 4 + i)],
                self.outs[i].at[self.span(c)],
                self.out_sem.at[c, i],
            )
            for i in range(4)
        ]

    def start(self):
        def body(c, carry):
            for copy in self.fetch(c):
                copy.start()
            return carry

        lax.fori_loop(0, self.count, body, 0)

    def run(self, stage, gradient):
        sub = STEP * LANES

        def body(c, carry):
            stage(c)
            for copy in self.fetch(c):
                copy.wait()

            def step(s, inner):
                grad = gradient(c, s * STEP, STEP).reshape(sub)
                values = self.rule(
                    grad, *[self.in_buf[self.place(c * 3 + i, s * sub, sub)] for i in range(3)]
                )
                for i in range(4):
                    self.out_buf[self.place(c * 4 + i, s * sub, sub)] = values[i]
                return inner

            lax.fori_loop(0, self.rows // STEP, step, 0)
            for copy in self.flush(c):
                copy.start()
            return carry

        def drain(c, carry):
            for copy in self.flush(c):
                copy.wait()
            return carry

        lax.fori_loop(0, self.count, body, 0)
        return lambda: lax.fori_loop(0, self.count, drain, 0)


class Extra:
    def __init__(self, start, ins, outs, rest):
        self.bufs, self.sem = rest[:8], rest[8]
        count = self.bufs[0].shape[0]
        span = pl.ds(start, count)
        self.count = count
        self.loads = [
            pltpu.make_async_copy(ins[i].at[span], self.bufs[i], self.sem.at[i]) for i in range(3)
        ]
        self.stores = [
            pltpu.make_async_copy(self.bufs[3 + i], outs[i].at[span], self.sem.at[3 + i])
            for i in range(4)
        ]

    def start(self):
        for copy in self.loads:
            copy.start()

    def finish(self, grad, rule):
        for copy in self.loads:
            copy.wait()
        self.bufs[7][...] = grad.reshape(grad.shape[0] * LANES)
        values = rule(self.bufs[7][pl.ds(0, self.count)], *[self.bufs[i][...] for i in range(3)])
        for i in range(4):
            self.bufs[3 + i][...] = values[i]
            self.stores[i].start()

    def drain(self):
        for copy in self.stores:
            copy.wait()


def shifted(flat, row, count):
    here = flip(flat[pl.ds(row - 1, count), :])
    after = flip(flat[pl.ds(row, count), :])
    return jnp.where(low_half(count), here, after)


def load_parts(pieces, sem):
    copies = [
        pltpu.make_async_copy(source, target, sem.at[i]) for i, (source, target) in enumerate(pieces)
    ]
    for copy in copies:
        copy.start()
    return copies


FLAT_BASE = 8
TAIL_ZERO = HALF - (GATE_ROW + 11 * CHUNK) * LANES
TAIL_ONE = HALF - (6916 + 11 * CHUNK) * LANES


def update_first(scale, rate, core_ref, bits_ref, *rest):
    halves, ins, outs = rest[:4], rest[4:7], rest[7:11]
    early_ref, flat, in_buf, out_buf, in_sem, out_sem, part_sem = rest[11:18]
    refs = (ins, outs, in_buf, out_buf, in_sem, out_sem)
    core = core_ref[0]
    rule = functools.partial(update_rule, scale, rate)
    half = PART_ROWS // 2
    pieces = []
    for p in range(2):
        for i, which in enumerate((bits_ref[p], 1 - bits_ref[p])):
            span = pl.ds(pl.multiple_of(p * PART_ROWS + which * half, 8), half)
            pieces.append((halves[2 * p + i], early_ref.at[span]))
    copies = load_parts(pieces, part_sem)
    extra = Extra((GATE_ROW + 11 * CHUNK) * LANES, ins, outs, rest[18:])
    base = jnp.where(core == 0, GATE_ROW, 4)
    chunks = Chunks(CHUNK, base, 11 + core, rule, refs)
    chunks.start()

    @pl.when(core == 0)
    def _():
        extra.start()

    for copy in copies:
        copy.wait()
    flat[0:FLAT_BASE, :] = jnp.zeros((FLAT_BASE, LANES), F32)

    def stage(c):
        for t in range(FF_TILES):
            rows = pl.ds(pl.multiple_of(t * D + c * 48, 16), 48)
            flat[pl.ds(FLAT_BASE + t, 48, stride=FF_TILES), :] = early_ref[rows, :].astype(F32)

    def gradient(c, start, count):
        row = pl.multiple_of(FLAT_BASE + start, 8)
        return jnp.where(core == 0, flat[pl.ds(row, count), :], shifted(flat, row, count))

    def stage_next(c):
        flat[FLAT_BASE - 1 : FLAT_BASE, :] = flat[FLAT_BASE + CHUNK - 1 : FLAT_BASE + CHUNK, :]
        stage(c)

    drain = chunks.run(stage_next, gradient)

    @pl.when(core == 0)
    def _():
        stage(11)
        extra.finish(flat[FLAT_BASE : FLAT_BASE + CHUNK, :], rule)

    drain()

    @pl.when(core == 0)
    def _():
        extra.drain()


def update_second(scale, rate, core_ref, bits_ref, *rest):
    halves, ins, outs = rest[:8], rest[8:11], rest[15:19]
    flat, tmp, part_ref, swap_ref, first_ref, in_buf, out_buf, in_sem, out_sem, part_sem = rest[19:29]
    refs = (ins, outs, in_buf, out_buf, in_sem, out_sem)
    tail = Extra((6916 + 11 * CHUNK) * LANES, ins, outs, rest[29:38])
    head = Extra(0, ins, outs, rest[38:])
    rule = functools.partial(update_rule, scale, rate)
    half = PART_ROWS // 2
    pieces = []
    for i in range(2):
        which = [1 - bits_ref[p] if i else bits_ref[p] for p in range(3)]

        def rows(start, p, size, which=which):
            return pl.ds(pl.multiple_of(start + which[p] * size, 16), size)

        source = halves[2 + i].at[pl.ds(half - REST_SLOT, REST_SLOT)]
        pieces.append((source, part_ref.at[rows(0, 1, REST_SLOT)]))
        pieces.append((halves[4 + i], part_ref.at[rows(2 * REST_SLOT, 2, half)]))
        pieces.append((halves[6 + i], swap_ref.at[rows(0, 2, half)]))
        pieces.append((halves[i].at[pl.ds(0, 16)], first_ref.at[rows(0, 0, 16)]))
    parts = load_parts(pieces, part_sem)

    @pl.when(core_ref[0] == 0)
    def _():
        def stage(c):
            values = []
            for t in range(Q_TILES):
                rows = pl.ds(pl.multiple_of(REST + t * D + c * 64, 16), 64)
                values.append(part_ref[rows, :].astype(F32))
            put_wide(flat, tmp, values, 64, FLAT_BASE)

        def gradient(c, start, count):
            return flat[pl.ds(pl.multiple_of(FLAT_BASE + start, 8), count), :]

        chunks = Chunks(CHUNK // 2, O_ROW, 9, rule, refs)
        chunks.start()
        for copy in parts:
            copy.wait()
        chunks.run(stage, gradient)()

    @pl.when(core_ref[0] == 1)
    def _():
        head.start()
        chunks = Chunks(CHUNK, 6916, 11, rule, refs)
        chunks.start()
        tail.start()
        for copy in parts:
            copy.wait()
        flat[0:FLAT_BASE, :] = jnp.zeros((FLAT_BASE, LANES), F32)
        flat[FLAT_BASE : FLAT_BASE + 8, :] = swap_ref[SWAP_TAIL : SWAP_TAIL + 16, :].astype(F32)[0:8]
        flat[FLAT_BASE + 5 : FLAT_BASE + 6, :] = first_ref[0:16, :].astype(F32)[0:1]
        head.finish(shifted(flat, FLAT_BASE + 1, 8), rule)
        row = FLAT_BASE + CHUNK - 1
        flat[row : row + 1, :] = part_ref[REST - 16 : REST, :].astype(F32)[15:16]

        def stage(c):
            flat[FLAT_BASE - 1 : FLAT_BASE, :] = flat[FLAT_BASE + CHUNK - 1 : FLAT_BASE + CHUNK, :]
            inside = c < DOWN_FIRST
            here = pl.ds(pl.multiple_of(SWAP_START + jnp.where(inside, c, 0) * D, 16), D)
            there = pl.ds(pl.multiple_of(REST + jnp.where(inside, 0, c - DOWN_FIRST) * D, 16), D)
            whole = jnp.where(inside, swap_ref[here, :].astype(F32), part_ref[there, :].astype(F32))
            pieces = [whole[i * LANES : (i + 1) * LANES].T for i in range(4)]
            half = jnp.concatenate([whole[4 * LANES :], jnp.zeros((LANES - HD, LANES), F32)], axis=0)
            put_wide(flat, tmp, pieces + [half.T], LANES, FLAT_BASE)

        def gradient(c, start, count):
            return shifted(flat, FLAT_BASE + start, count)

        drain = chunks.run(stage, gradient)
        stage(11)
        flat[FLAT_BASE + CHUNK :, :] = jnp.zeros((8, LANES), F32)
        tail.finish(shifted(flat, FLAT_BASE, CHUNK + 8), rule)
        head.drain()
        drain()
        tail.drain()


def update_late(scale, rate, core_ref, own_ref, other_ref, *rest):
    ins, outs = rest[:3], rest[7:11]
    flat, tmp, late_ref, in_buf, out_buf, in_sem, out_sem, part_sem = rest[11:19]
    refs = (ins, outs, in_buf, out_buf, in_sem, out_sem)
    extra = Extra(LATE_CHUNKS * CHUNK * LANES, ins, outs, rest[19:])
    rule = functools.partial(update_rule, scale, rate)

    @pl.when(core_ref[0] == 0)
    def _():
        chunks = Chunks(CHUNK, 0, LATE_CHUNKS, rule, refs)
        chunks.start()
        extra.start()
        pieces = [
            (own_ref, late_ref.at[pl.ds(0, LATE_HALF)]),
            (other_ref, late_ref.at[pl.ds(LATE_HALF, LATE_HALF)]),
        ]
        for copy in load_parts(pieces, part_sem):
            copy.wait()

        def late(index):
            return late_ref[index * D : (index + 1) * D, :].astype(F32)

        low1 = low_half(1)
        gain_a = late_ref[8 * D : 8 * D + 16, :].astype(F32)
        gain_m = flip(late_ref[8 * D + 16 : 8 * D + 32, :].astype(F32))
        for r in range(4):
            flat[r : r + 1, :] = gain_a[r : r + 1]
        flat[4:5, :] = jnp.where(low1, gain_a[4:5], gain_m[0:1])
        for r in range(4):
            flat[5 + r : 6 + r, :] = jnp.where(low1, gain_m[r : r + 1], gain_m[r + 1 : r + 2])
        put_wide(flat, tmp, [late(t) for t in range(Q_TILES)], D, 9)
        pairs = D // 2
        for t in range(3):
            tmp[pl.ds(t * D, D), :] = late(Q_TILES + t)
        even = [tmp[pl.ds(i * D, pairs, stride=2), :] for i in range(3)]
        odd = [tmp[pl.ds(i * D + 1, pairs, stride=2), :] for i in range(3)]
        low = low_half(pairs)
        turned = [flip(odd[0]), flip(odd[1]), flip(even[1]), flip(even[2])]
        rows = (
            (2601, even[0]),
            (2602, jnp.where(low, even[1], turned[0])),
            (2603, jnp.where(low, turned[0], turned[1])),
            (3465, jnp.where(low, turned[2], turned[3])),
            (3466, jnp.where(low, turned[3], odd[1])),
            (3467, odd[2]),
        )
        for row, value in rows:
            flat[pl.ds(row, pairs, stride=3), :] = value

        def gradient(c, start, count):
            return flat[pl.ds(pl.multiple_of(c * CHUNK + start, 8), count), :]

        drain = chunks.run(lambda c: None, gradient)
        start = LATE_CHUNKS * CHUNK
        extra.finish(flat[start : start + 304, :], rule)
        drain()
        extra.drain()


def vmem():
    return pl.BlockSpec(memory_space=pltpu.VMEM)


def smem():
    return pl.BlockSpec(memory_space=pltpu.SMEM)


def hbm():
    return pl.BlockSpec(memory_space=pl.ANY)


def call(kernel, outs, in_specs, out_specs, scratch, flops, name, limit, aliases=None):
    n_bytes = sum(math.prod(shape) * jnp.dtype(kind).itemsize for shape, kind in outs)
    return pl.pallas_call(
        kernel,
        out_shape=[jax.ShapeDtypeStruct(shape, kind) for shape, kind in outs],
        in_specs=in_specs,
        out_specs=out_specs,
        scratch_shapes=scratch,
        input_output_aliases=aliases or {},
        compiler_params=pltpu.CompilerParams(vmem_limit_bytes=limit * MIB),
        cost_estimate=pl.CostEstimate(
            flops=int(flops), bytes_accessed=int(2 * n_bytes), transcendentals=0
        ),
        name=name,
    )


def rope_tables(seq_len):
    lane = jnp.arange(LANES, dtype=jnp.int32)
    which = (lane % (HD // 2)).astype(F32)
    frequency = jnp.exp(which * (-2.0 * math.log(10000.0) / HD))
    angles = jnp.arange(seq_len, dtype=F32)[:, None] * frequency[None, :]
    sign = jnp.where(lane % HD < HD // 2, -1.0, 1.0)
    return jnp.cos(angles), jnp.sin(angles) * sign[None, :]


def run_prepare(core, own, other):
    outs = [
        ((1, D), F32),
        ((1, D), F32),
        ((D, PAD_D), BF),
        ((D, KV_COLS), BF),
        ((PAD_D, D), BF),
        ((D, FF), BF),
        ((D, FF), BF),
        ((FF, D), BF),
    ]
    scratch = [
        pltpu.VMEM((HALF,), F32),
        pltpu.VMEM((HALF,), F32),
        pltpu.VMEM((FLAT_SCRATCH, LANES), F32),
        pltpu.VMEM((Q_TILES * D, LANES), F32),
        pltpu.VMEM((8 * LANES,), F32),
        pltpu.SemaphoreType.DMA((2,)),
    ]
    return call(
        prepare_weights,
        outs,
        [smem()] + [hbm()] * 2,
        [vmem()] * 8,
        scratch,
        1e10,
        "prepare_weights",
        56,
    )(core, own, other)


def run_attention_forward(x, gain, wq, wkv, wo, cosine, sine):
    seq_len = x.shape[0]
    outs = [
        ((seq_len, D), F32),
        ((seq_len, PAD_D), BF),
        ((Q_TILES, seq_len, LANES), BF),
        ((6, seq_len, LANES), BF),
        ((6, seq_len, LANES), BF),
        ((16, seq_len), F32),
    ]
    return call(
        attention_forward,
        outs,
        [vmem()] * 7,
        [vmem()] * 6,
        [pltpu.VMEM((Q_TILES, BLOCK, LANES), F32)],
        1.5e10,
        "attention_forward",
        56,
    )(x, gain, wq, wkv, wo, cosine, sine)


def run_mlp(core, slot, lengths, assignment, hidden1, cot, mixed, gain, wo, wg, wu, wd):
    seq_len = hidden1.shape[0]
    outs = [
        ((seq_len, D), BF),
        ((seq_len, D), F32),
        ((Q_TILES, seq_len, LANES), BF),
        ((1, D), F32),
        ((EARLY_ROWS, LANES), BF),
        ((EARLY_ROWS, LANES), BF),
    ]
    return call(
        mlp_pass,
        outs,
        [smem()] * 4 + [hbm()] * 3 + [vmem()] + [hbm()] * 4,
        [hbm()] * 3 + [vmem()] + [hbm()] * 2,
        [
            pltpu.VMEM((seq_len, D), F32),
            pltpu.VMEM((seq_len, D), BF),
            pltpu.VMEM((seq_len, PAD_D), BF),
            pltpu.VMEM((PAD_D, D), BF),
            pltpu.VMEM((D, FF), BF),
            pltpu.VMEM((D, FF), BF),
            pltpu.VMEM((FF, D), BF),
            pltpu.VMEM((seq_len, D), BF),
            pltpu.VMEM((seq_len, D), F32),
            pltpu.VMEM((Q_TILES, seq_len, LANES), BF),
            pltpu.VMEM((PAD_D, seq_len), BF),
            pltpu.VMEM((PAD_D, seq_len), BF),
            pltpu.VMEM((seq_len, FF), BF),
            pltpu.VMEM((seq_len, FF), BF),
            pltpu.VMEM((seq_len, FF), BF),
            pltpu.VMEM((seq_len, D), BF),
            pltpu.VMEM((2, EARLY_ROWS, LANES), BF),
            pltpu.SemaphoreType.DMA((7,)),
            pltpu.SemaphoreType.DMA((seq_len // MLP_BLOCK, 3)),
            pltpu.SemaphoreType.DMA((FF_TILES // 2 + 1, 2)),
        ],
        2.5e10,
        "mlp_pass",
        56,
    )(core, slot, lengths, assignment, hidden1, cot, mixed, gain, wo, wg, wu, wd)


def run_backward_groups(first, count, q, dm, k, v, lse):
    seq_len = q.shape[1]
    fixed = pl.BlockSpec((Q_TILES, seq_len, LANES), lambda i: (0, 0, 0))
    sides = pl.BlockSpec((2, seq_len, LANES), lambda i: (first + i, 0, 0))
    single = pl.BlockSpec((1, seq_len, LANES), lambda i: (i, 0, 0))
    outs = [(count, 2, seq_len, LANES), (count, seq_len, LANES), (count, seq_len, LANES)]
    return pl.pallas_call(
        functools.partial(backward_groups, first),
        grid=(count,),
        out_shape=[jax.ShapeDtypeStruct(shape, F32) for shape in outs],
        in_specs=[
            fixed,
            fixed,
            sides,
            sides,
            pl.BlockSpec((16, seq_len), lambda i: (0, 0)),
        ],
        out_specs=[
            pl.BlockSpec((1, 2, seq_len, LANES), lambda i: (i, 0, 0, 0)),
            single,
            single,
        ],
        scratch_shapes=[pltpu.VMEM((2, seq_len, LANES), F32)] * 2,
        compiler_params=pltpu.CompilerParams(vmem_limit_bytes=56 * MIB),
        cost_estimate=pl.CostEstimate(
            flops=int(8e9) * count, bytes_accessed=int(3e6) * count, transcendentals=0
        ),
        name="backward_groups",
    )(q, dm, k, v, lse)


def run_backward_finish(x, gain, dh1, groups, wq, wkv, cosine, sine):
    seq_len = x.shape[0]
    outs = [
        ((seq_len, D), BF),
        ((seq_len, PAD_D), BF),
        ((seq_len, KV_COLS), BF),
        ((seq_len, D), BF),
        ((1, D), F32),
    ]
    return call(
        backward_finish,
        outs,
        [vmem()] * 13,
        [vmem()] * 5,
        [],
        4e9,
        "backward_finish",
        56,
    )(x, gain, dh1, *groups[0], *groups[1], wq, wkv, cosine, sine)


def run_late_weights(core, normed, d_query, d_kv, gga, ggm):
    outs = [((LATE_HALF, LANES), BF), ((LATE_HALF, LANES), BF)]
    return call(
        late_weights,
        outs,
        [smem()] + [vmem()] * 5,
        [hbm()] * 2,
        [pltpu.VMEM((2 * LATE_HALF, LANES), BF), pltpu.SemaphoreType.DMA((2,))],
        4e9,
        "late_weights",
        56,
    )(core, normed, d_query, d_kv, gga, ggm)


def run_sum(bits, kept, got, split, merge=False, n_parts=None):
    joined = n_parts is not None
    n_parts = n_parts or len(kept)
    rows = kept[0].shape[0] // (n_parts if joined else 1)
    kinds = 2 if split else 1
    n_out = 1 if merge else n_parts
    out_rows = rows // kinds * (n_parts if merge else 1)
    results = call(
        functools.partial(
            gather_sum, n_parts=n_parts, rows=rows, split=split, merge=merge, joined=joined
        ),
        [((out_rows, LANES), BF)] * (kinds * n_out),
        [smem()] + [vmem()] * (2 * len(kept)),
        [hbm()] * (kinds * n_out),
        [pltpu.VMEM((n_parts, rows, LANES), BF), pltpu.SemaphoreType.DMA((2 * n_parts,))],
        1e6,
        "gather_sum",
        12,
    )(bits, *kept, *got)
    return list(results[:n_out]), list(results[n_out:])


def run_join(bits, own, got, n_parts):
    merged = len(own) < n_parts
    rows = own[0].shape[0] // (n_parts if merged else 1)
    return call(
        functools.partial(join_halves, n_parts=n_parts, rows=rows, merged=merged),
        [((2 * rows, LANES), BF)] * n_parts,
        [smem()] + [hbm()] * (2 * len(own)),
        [hbm()] * n_parts,
        [pltpu.SemaphoreType.DMA((2 * n_parts,))],
        1e6,
        "join_halves",
        4,
    )(bits, *own, *got)


def chunk_scratch(count):
    return [
        pltpu.VMEM((3 * count * CHUNK * LANES,), F32),
        pltpu.VMEM((4 * count * CHUNK * LANES,), F32),
        pltpu.SemaphoreType.DMA((12, 3)),
        pltpu.SemaphoreType.DMA((12, 4)),
    ]


def extra_scratch(count, n_rows):
    bufs = [pltpu.VMEM((count,), F32)] * 7 + [pltpu.VMEM((n_rows * LANES,), F32)]
    return bufs + [pltpu.SemaphoreType.DMA((7,))]


def run_update_first(scale, rate, core, bits, halves, state):
    scratch = [
        pltpu.VMEM((2 * PART_ROWS, LANES), BF),
        pltpu.VMEM((FLAT_BASE + CHUNK, LANES), F32),
        *chunk_scratch(12),
        pltpu.SemaphoreType.DMA((4,)),
        *extra_scratch(TAIL_ZERO, CHUNK),
    ]
    return call(
        functools.partial(update_first, scale, rate),
        [(state[0].shape, F32)] * 4,
        [smem()] * 2 + [hbm()] * 7,
        [hbm()] * 4,
        scratch,
        1e9,
        "update_first",
        56,
    )(core, bits, *halves, *state)


def run_update_second(scale, rate, core, bits, halves, state, done):
    scratch = [
        pltpu.VMEM((FLAT_BASE + CHUNK + 8, LANES), F32),
        pltpu.VMEM((Q_TILES * D, LANES), F32),
        pltpu.VMEM((2 * REST_SLOT + PART_ROWS, LANES), BF),
        pltpu.VMEM((PART_ROWS, LANES), BF),
        pltpu.VMEM((32, LANES), BF),
        *chunk_scratch(11),
        pltpu.SemaphoreType.DMA((8,)),
        *extra_scratch(TAIL_ONE, CHUNK + 8),
        *extra_scratch(5 * LANES, 8),
    ]
    return call(
        functools.partial(update_second, scale, rate),
        [(state[0].shape, F32)] * 4,
        [smem()] * 2 + [hbm()] * 15,
        [hbm()] * 4,
        scratch,
        1e9,
        "update_second",
        56,
        {13 + i: i for i in range(4)},
    )(core, bits, *halves, *state, *done)


def run_update_late(scale, rate, core, own, other, state, done):
    last_rows = O_ROW - LATE_CHUNKS * CHUNK
    scratch = [
        pltpu.VMEM((4336, LANES), F32),
        pltpu.VMEM((Q_TILES * D, LANES), F32),
        pltpu.VMEM((2 * LATE_HALF, LANES), BF),
        *chunk_scratch(LATE_CHUNKS),
        pltpu.SemaphoreType.DMA((2,)),
        *extra_scratch(last_rows * LANES, 304),
    ]
    return call(
        functools.partial(update_late, scale, rate),
        [(state[0].shape, F32)] * 4,
        [smem()] + [hbm()] * 9,
        [hbm()] * 4,
        scratch,
        1e9,
        "update_late",
        56,
        {6 + i: i for i in range(4)},
    )(core, own, other, *state, *done)


def add_low(a, b):
    return (a.astype(F32) + b.astype(F32)).astype(BF)


def xor_swap(value, bit):
    size = lax.axis_size("dp")
    return lax.ppermute(value, "dp", [(i, i ^ (1 << bit)) for i in range(size)])


def tie(value, *others):
    return lax.optimization_barrier((value, *others))


def my_bits(orders, step):
    index = lax.axis_index("dp")
    return jnp.stack([(index >> order[step]) & 1 for order in orders]).astype(jnp.int32)


def near_size():
    return min(lax.axis_size("dp"), 4)


def spread(blocks):
    size, near = lax.axis_size("dp"), near_size()
    groups = [[g * near + i for i in range(near)] for g in range(size // near)]
    return lax.all_to_all(
        blocks, "dp", split_axis=0, concat_axis=0, tiled=True, axis_index_groups=groups
    )


def scatter_sum(value):
    count = near_size()
    blocks = spread(value.reshape(count, value.shape[0] // count, LANES))
    return jnp.sum(blocks.astype(F32), axis=0).astype(BF)


def bit_orders():
    n_bits = lax.axis_size("dp").bit_length() - 1
    base = list(range(n_bits))
    head = base[:3] if n_bits >= 3 else base
    return [head[r:] + head[:r] + base[len(head) :] for r in range(3)]


def on_device(inputs, cotangent, lengths, assignment, return_order, master, momentum, average):
    nseq_all, block_rows, _ = inputs.shape
    axes = ("dp", "shard")
    seq_len = block_rows * lax.axis_size("dp") * lax.axis_size("shard")
    my_slot = lax.axis_index(axes)
    core = lax.axis_index("shard")
    core_arr = core.astype(jnp.int32).reshape(1)

    seq_ids = jnp.arange(nseq_all, dtype=jnp.int32)
    inverse = jnp.sum(
        jnp.where(return_order[None, :] == seq_ids[:, None], seq_ids[None, :], 0), axis=1
    )

    def pick(array, index):
        return array.at[index].get(mode="promise_in_bounds")

    def exchange(value):
        return lax.all_to_all(value, axes, split_axis=0, concat_axis=0, tiled=True)

    x = exchange(pick(inputs, assignment)).reshape(seq_len, D)
    slot_arr = my_slot.astype(jnp.int32).reshape(1)

    other = lax.ppermute(master, "shard", [(0, 1), (1, 0)])
    gain_attn, gain_mlp, wq, wkv, wo, wg, wu, wd = run_prepare(core_arr, master, other)

    cosine, sine = rope_tables(seq_len)
    sent_cot, gain_attn, cosine = tie(pick(cotangent, inverse), gain_attn, cosine)
    cot = exchange(sent_cot).reshape(seq_len, D)
    hidden1, mixed, q, k, v, lse = run_attention_forward(x, gain_attn, wq, wkv, wo, cosine, sine)
    result, dh1, dm, ggm, early_keep, early_send = run_mlp(
        core_arr, slot_arr, lengths, assignment, hidden1, cot, mixed, gain_mlp, wo, wg, wu, wd
    )
    back_out = exchange(result.reshape(nseq_all, block_rows, D))

    orders = bit_orders()
    n_bits = len(orders[0])

    def swap_parts(parts, step):
        return [xor_swap(part, order[step]) for part, order in zip(parts, orders)]

    got = lax.ppermute(early_send, "shard", [(0, 1), (1, 0)])
    groups = [run_backward_groups(0, 1, q, dm, k, v, lse)]
    lse, got = tie(lse, got)
    sent, kept = run_sum(my_bits(orders, 0), [early_keep], [got], True, n_parts=3)
    lse, *kept = tie(lse, *kept)
    got = swap_parts(sent, 0)
    groups.append(run_backward_groups(1, KV - 1, q, dm, k, v, lse))
    sent, kept = run_sum(my_bits(orders, 1), kept, got, True)
    dh1, back_out, *kept = tie(dh1, back_out, *kept)
    got = swap_parts(sent, 1)
    d_stream, d_query, d_kv, normed, gga = run_backward_finish(
        x, gain_attn, dh1, groups, wq, wkv, cosine, sine
    )
    last_bit = n_bits - 1
    for step in range(2, n_bits):
        if step > 2:
            got = swap_parts(sent, step - 1)
        sent, kept = run_sum(my_bits(orders, step), kept, got, True, merge=step == last_bit)
        if step == 2:
            gga, *kept = tie(gga, *kept)
            late_keep, late_send = run_late_weights(core_arr, normed, d_query, d_kv, gga, ggm)
            late_send, *kept = tie(late_send, *kept)
        if step == last_bit:
            late_send, sent[0] = tie(late_send, sent[0])
    got = [xor_swap(sent[0], last_bit)]
    late_got = lax.ppermute(late_send, "shard", [(0, 1), (1, 0)])
    late, _ = run_sum(my_bits(orders, 0)[:1], [late_keep], [late_got], False)
    late, block_output, *got = tie(scatter_sum(late[0]), pick(back_out, return_order), *got)
    early, _ = run_sum(my_bits(orders, last_bit)[:1], kept, got, False)
    far_bits = list(range(near_size().bit_length() - 1, n_bits))

    def add_far(late, early):
        late, *early = tie(late, *early)
        return add_low(late, xor_swap(late, far_bits.pop(0))), early

    got = xor_swap(early[0], last_bit)
    late = add_low(late, xor_swap(late, far_bits.pop(0)))
    late, got = tie(late, got)
    early = run_join(my_bits(orders, last_bit), early, [got], 3)
    whole = None
    for step in reversed(range(1, last_bit)):
        if far_bits:
            late, early = add_far(late, early)
        elif whole is None:
            late, *early = tie(late, *early)
            whole = spread(jnp.broadcast_to(late[None], (near_size(), *late.shape)))
        got = swap_parts(early, step)
        late, *got = tie(late, *got)
        early = run_join(my_bits(orders, step), early, got, 3)
    while far_bits:
        late, early = add_far(late, early)
    if whole is None:
        whole = spread(jnp.broadcast_to(late[None], (near_size(), *late.shape)))
    late = whole.reshape(-1, LANES)
    got = swap_parts(early, 0)
    swap_own = lax.ppermute(early[2], "shard", [(0, 1)])
    bits = my_bits(orders, 0)
    scale = 1.0 / nseq_all
    rate = (nseq_all / (0.6 * seq_len)) ** 0.5 / D**0.5
    state = (master, momentum, average)
    d_stream, late, swap_own, *got = tie(d_stream, late, swap_own, *got)
    back_grad = exchange(d_stream.reshape(nseq_all, block_rows, D))
    late_other = lax.ppermute(late, "shard", [(1, 0)])
    swap_got = lax.ppermute(got[2], "shard", [(0, 1)])
    halves = [early[0], got[0], early[1], got[1], early[2], got[2], swap_own, swap_got]
    done = run_update_first(scale, rate, core_arr, bits, halves[:4], state)
    done = run_update_second(scale, rate, core_arr, bits, halves, state, done)
    weight_grad, new_momentum, new_master, new_average = run_update_late(
        scale, rate, core_arr, late, late_other, state, done
    )
    input_grad = pick(back_grad, return_order)
    return (block_output, input_grad, weight_grad, new_momentum, new_master, new_average)


def solution(mesh):
    rows = P(None, ("dp", "shard"), None)
    flat = P("shard")
    return jax.shard_map(
        on_device,
        mesh=mesh,
        in_specs=(rows, rows, P(), P(), P(), flat, flat, flat),
        out_specs=(rows, rows, flat, flat, flat, flat),
        check_vma=False,
    )
```

```python
import functools
import math

import jax
import jax.numpy as jnp
from jax import lax
from jax.experimental import pallas as pl
from jax.experimental.pallas import tpu as pltpu
from jax.sharding import PartitionSpec as P

D = 576
H = 9
KV = 3
HD = 64
FF = 1536
LANES = 128
BLOCK = 256
Q_TILES = 5
PAD_D = Q_TILES * LANES
KV_COLS = 2 * KV * HD
FF_TILES = FF // LANES
DOWN_FIRST = 4
EARLY_TILES = 21
EARLY_ROWS = 12288
EXTRA = EARLY_TILES * D
HALF = 27657 * LANES // 2
PART_ROWS = EARLY_ROWS // 3
SWAP_START = EXTRA - DOWN_FIRST * D - 2 * PART_ROWS
SWAP_TAIL = EXTRA + 16 - 2 * PART_ROWS
REST_FIRST = 2 * PART_ROWS - FF_TILES * D
REST_SLOT = REST_FIRST + 16
REST = REST_SLOT + 16
LATE_HALF = 2432
FLAT_SCRATCH = 13848
O_ROW = 4329
GATE_ROW = 6921
MLP_COLS = 256
WIDEN = 512
MLP_UNROLL = 6
MLP_BLOCK = 256
CHUNK = 576
STEP = 288
LATE_CHUNKS = 7

EPSILON = 1e-05
MOMENTUM_DECAY = 0.55
AVERAGE_DECAY = 0.45
MASKED = -1000000000.0

BF = jnp.bfloat16
F32 = jnp.float32
MIB = 1024 * 1024


def nn(a, b):
    return jnp.dot(a, b, preferred_element_type=F32)


def nt(a, b):
    return lax.dot_general(a, b, (((1,), (1,)), ((), ())), preferred_element_type=F32)


def tn(a, b):
    return lax.dot_general(a, b, (((0,), (0,)), ((), ())), preferred_element_type=F32)


def tile(value, index):
    return value[:, index * LANES : (index + 1) * LANES]


def low_half(rows):
    return lax.broadcasted_iota(jnp.int32, (rows, LANES), 1) < HD


def swap_halves(value):
    lane = lax.broadcasted_iota(jnp.int32, value.shape, 1)
    return jnp.where(lane % HD < HD // 2, pltpu.roll(value, 96, 1), pltpu.roll(value, 32, 1))


def flip(value):
    return pltpu.roll(value, HD, 1)


def rms(value):
    return lax.rsqrt(jnp.mean(value * value, axis=-1, keepdims=True) + EPSILON)


def attention_forward(
    x_ref, ga_ref, wq_ref, wkv_ref, wo_hbm, cos_ref, sin_ref,
    h1_hbm, mixed_hbm, q_hbm, k_hbm, v_hbm, lse_ref,
    h1_ref, mixed_ref, q_ref, k_ref, v_ref, wo_ref, o_acc, sem, block_sem,
):
    seq_len = x_ref.shape[0]
    low = low_half(BLOCK)

    def project(b, carry):
        rows = pl.ds(pl.multiple_of(b * BLOCK, BLOCK), BLOCK)
        stream = x_ref[rows, :].astype(F32)
        normed = (stream * rms(stream) * ga_ref[...]).astype(BF)
        cosine = cos_ref[rows, :]
        sine = sin_ref[rows, :]

        def rope(value):
            return value * cosine + swap_halves(value) * sine

        queries = nn(normed, wq_ref[...])
        for j in range(Q_TILES):
            q_ref[j, rows, :] = (rope(tile(queries, j)) * HD ** (-0.5)).astype(BF)
        keys_values = nn(normed, wkv_ref[...])
        first = rope(tile(keys_values, 0))
        second = tile(keys_values, 1)
        third = tile(keys_values, 2)
        mid = rope(second)

        def put(ref, index, value):
            ref[index, rows, :] = value.astype(BF)

        put(k_ref, 0, jnp.where(low, first, 0.0))
        put(k_ref, 1, jnp.where(low, 0.0, flip(first)))
        put(k_ref, 2, jnp.where(low, flip(first), 0.0))
        put(k_ref, 3, jnp.where(low, 0.0, first))
        put(k_ref, 4, jnp.where(low, mid, 0.0))
        put(k_ref, 5, jnp.where(low, 0.0, flip(mid)))
        put(v_ref, 0, jnp.where(low, flip(second), 0.0))
        put(v_ref, 1, jnp.where(low, 0.0, second))
        put(v_ref, 2, jnp.where(low, third, 0.0))
        put(v_ref, 3, jnp.where(low, 0.0, flip(third)))
        put(v_ref, 4, jnp.where(low, flip(third), 0.0))
        put(v_ref, 5, jnp.where(low, 0.0, third))
        return carry

    load = pltpu.make_async_copy(wo_hbm, wo_ref, sem.at[3])
    load.start()
    lax.fori_loop(0, seq_len // BLOCK, project, 0)
    stores = [
        pltpu.make_async_copy(source, target, sem.at[i])
        for i, (source, target) in enumerate(((q_ref, q_hbm), (k_ref, k_hbm), (v_ref, v_hbm)))
    ]
    for copy in stores:
        copy.start()
    lane = lax.broadcasted_iota(jnp.int32, (BLOCK, LANES), 1)
    keep = lax.broadcasted_iota(jnp.int32, (BLOCK, BLOCK), 1) <= lax.broadcasted_iota(
        jnp.int32, (BLOCK, BLOCK), 0
    )
    for b in range(seq_len // BLOCK):
        rows = slice(b * BLOCK, (b + 1) * BLOCK)
        n_keys = (b + 1) * BLOCK
        o_acc[...] = jnp.zeros_like(o_acc)

        def group(g, lse, rows=rows, n_keys=n_keys):
            for u in range(3):
                head = 3 * g + u
                j = head // 2
                side = 2 * g + head % 2
                scores = nt(q_ref[j, rows, :], k_ref[side, 0:n_keys, :])
                diag = jnp.where(keep, scores[:, n_keys - BLOCK :], MASKED)
                if n_keys > BLOCK:
                    scores = jnp.concatenate([scores[:, : n_keys - BLOCK], diag], axis=1)
                else:
                    scores = diag
                row_max = jnp.max(scores, axis=-1, keepdims=True)
                exponent = jnp.exp(scores - row_max)
                total = jnp.sum(exponent, axis=-1, keepdims=True)
                mixed = nn(exponent.astype(BF), v_ref[side, 0:n_keys, :])
                o_acc[j] += mixed * (1.0 / total)
                lse = jnp.where(lane == head, row_max + jnp.log(total), lse)
            return lse

        lse = lax.fori_loop(0, KV, group, jnp.zeros((BLOCK, LANES), F32))
        lse_ref[:, rows] = lse.T[:16]
        mixed = jnp.concatenate([o_acc[j].astype(BF) for j in range(Q_TILES)], axis=1)
        mixed_ref[rows, :] = mixed
        if b == 0:
            load.wait()
        h1_ref[rows, :] = x_ref[rows, :].astype(F32) + nn(mixed, wo_ref[...])
        for i, (source, target) in enumerate(((mixed_ref, mixed_hbm), (h1_ref, h1_hbm))):
            stores.append(
                pltpu.make_async_copy(source.at[rows], target.at[rows], block_sem.at[b, i])
            )
            stores[-1].start()
    for copy in stores:
        copy.wait()


def prepare_weights(
    core_ref, own_ref, other_ref,
    ga_ref, gm_ref, wq_ref, wkv_ref, wo_ref, wg_ref, wu_ref, wd_ref,
    first, second, flat, tmp, rest, sem,
):
    core = core_ref[0]
    for which, pair in enumerate(((first, second), (second, first))):

        @pl.when(core == which)
        def _(pair=pair):
            copies = [
                pltpu.make_async_copy(ref, target, sem.at[i])
                for i, (ref, target) in enumerate(zip((own_ref, other_ref), pair))
            ]
            for copy in copies:
                copy.start()
            for copy in copies:
                copy.wait()

    def widen(ref):
        def body(i, carry):
            start = pl.multiple_of(i * WIDEN, WIDEN)
            span = pl.ds(pl.multiple_of(i * WIDEN * LANES, WIDEN * LANES), WIDEN * LANES)
            flat[pl.ds(start, WIDEN), :] = ref[span].reshape(WIDEN, LANES)
            return carry

        whole = HALF // (WIDEN * LANES)
        lax.fori_loop(0, whole, body, 0)
        left = HALF - whole * WIDEN * LANES
        rest[pl.ds(0, left)] = ref[pl.ds(whole * WIDEN * LANES, left)]
        flat[whole * WIDEN : whole * WIDEN + 8, :] = rest[...].reshape(8, LANES)

    def low_precision(value):
        return value.astype(BF).astype(F32)

    def interleave(even, odd, pairs, out_ref, first_row, pad):
        low = low_half(2 * pairs)
        for t in range(Q_TILES):
            tmp[pl.ds(t * D, pairs, stride=2), :] = even[t]
            tmp[pl.ds(t * D + 1, pairs, stride=2), :] = odd[t]
        rows = pl.ds(first_row, 2 * pairs)
        for t in range(Q_TILES):
            value = tmp[t * D : t * D + 2 * pairs, :]
            if t < 4:
                out_ref[rows, t * LANES : (t + 1) * LANES] = value.astype(BF)
            elif pad:
                out_ref[rows, t * LANES :] = jnp.where(low, value, 0.0).astype(BF)
            else:
                out_ref[rows, t * LANES :] = value[:, :HD].astype(BF)

    def wide(row, out_ref, pad):
        pairs = D // 2
        low = low_half(pairs)
        cols = [flat[pl.ds(row + c, pairs, stride=9), :] for c in range(9)]
        turned = [flip(cols[c]) for c in range(4, 9)]
        odd = [jnp.where(low, turned[t], turned[t + 1]) for t in range(4)] + [turned[4]]
        interleave(cols[:5], odd, pairs, out_ref, 0, pad)

    widen(first)
    low1 = low_half(1)
    turned = [flip(flat[4 + r : 5 + r, :]) for r in range(5)]
    for r in range(4):
        ga_ref[:, r * LANES : (r + 1) * LANES] = low_precision(flat[r : r + 1, :])
        gm_ref[:, r * LANES : (r + 1) * LANES] = low_precision(
            jnp.where(low1, turned[r], turned[r + 1])
        )
    ga_ref[:, 4 * LANES :] = low_precision(flat[4:5, :HD])
    gm_ref[:, 4 * LANES :] = low_precision(turned[4][:, :HD])
    wide(9, wq_ref, True)
    wide(O_ROW, wo_ref, False)
    wo_ref[D:, :] = jnp.zeros((PAD_D - D, D), BF)
    pairs = D // 2
    low = low_half(pairs)
    narrow = []
    for row in (2601, 3465):
        cols = [flat[pl.ds(row + c, pairs, stride=3), :] for c in range(3)]
        turned = [flip(cols[1]), flip(cols[2])]
        even = cols[:2]
        odd = [jnp.where(low, turned[0], turned[1]), turned[1]]
        for t in range(2):
            tmp[pl.ds(t * D, pairs, stride=2), :] = even[t]
            tmp[pl.ds(t * D + 1, pairs, stride=2), :] = odd[t]
        narrow.append((tmp[0:D, :], tmp[D : 2 * D, :]))
    (k0, k1), (v0, v1) = narrow
    low = low_half(D)
    v0 = flip(v0)
    v1 = flip(v1)
    wkv_ref[:, 0:LANES] = k0.astype(BF)
    wkv_ref[:, LANES : 2 * LANES] = jnp.where(low, k1, v0).astype(BF)
    wkv_ref[:, 2 * LANES :] = jnp.where(low, v0, v1).astype(BF)
    head = second[pl.ds(0, 1024)].reshape(8, LANES)
    turned = flip(head)
    for r in range(5):
        row = GATE_ROW + FF_TILES * (D - 1) + 7 + r
        before = flat[row : row + 1, :] if r == 0 else turned[r - 1 : r]
        flat[row : row + 1, :] = jnp.where(low1, before, turned[r : r + 1])
    for t in range(FF_TILES):
        wg_ref[:, t * LANES : (t + 1) * LANES] = flat[
            pl.ds(GATE_ROW + t, D, stride=FF_TILES), :
        ].astype(BF)
    widen(second)
    here = flip(flat[pl.ds(4, D, stride=FF_TILES), :])
    for t in range(FF_TILES):
        after = flip(flat[pl.ds(5 + t, D, stride=FF_TILES), :])
        wu_ref[:, t * LANES : (t + 1) * LANES] = jnp.where(low, here, after).astype(BF)
        here = after

    def down(i, carry):
        n_pairs = 96
        low = low_half(n_pairs)
        start = 6916 + 9 * n_pairs * i
        cols = [flat[pl.ds(start + c, n_pairs, stride=9), :] for c in range(10)]
        turned = [flip(cols[c]) for c in range(6)]
        even = [jnp.where(low, turned[c], turned[c + 1]) for c in range(5)]
        interleave(even, cols[5:], n_pairs, wd_ref, pl.multiple_of(2 * n_pairs * i, 16), False)
        return carry

    lax.fori_loop(0, FF // 192, down, 0)


def transposed(value):
    rows = value.shape[0]
    pieces = [tile(value, t) for t in range(4)]
    pieces.append(
        jnp.concatenate([value[:, 4 * LANES :], jnp.zeros((rows, LANES - HD), F32)], axis=1)
    )
    return jnp.concatenate([piece.T for piece in pieces], axis=0)


def mlp_pass(
    core_ref, slot_ref, lengths_ref, assignment_ref, return_ref,
    h1_hbm, cot_hbm, mixed_hbm, gm_ref, wo_hbm, wg_hbm, wu_hbm, wd_hbm,
    out_hbm, dh1_hbm, dm_hbm, ggm_ref, keep_ref, send_ref,
    h1_ref, cot_ref, mixed_ref, wo_ref, wg_ref, wu_ref, wd_ref, out_ref, dh1_ref, dm_ref,
    nmt_s, backt_s, inner_s, dg_s, du_s, da_s, grads, in_sem, out_sem, sem,
):
    seq_len = h1_ref.shape[0]
    core = core_ref[0]
    live_len = lengths_ref[assignment_ref[return_ref[slot_ref[0]]]]
    n_cols = FF // MLP_COLS
    loads = [
        pltpu.make_async_copy(source, target, in_sem.at[i])
        for i, (source, target) in enumerate(
            (
                (h1_hbm, h1_ref),
                (cot_hbm, cot_ref),
                (wg_hbm, wg_ref),
                (wu_hbm, wu_ref),
                (wd_hbm, wd_ref),
                (wo_hbm, wo_ref),
                (mixed_hbm, mixed_ref),
            )
        )
    ]
    for copy in loads:
        copy.start()
    for copy in loads[:6]:
        copy.wait()

    def results(b):
        rows = pl.ds(pl.multiple_of(b * MLP_BLOCK, MLP_BLOCK), MLP_BLOCK)
        pairs = [(out_ref.at[rows], out_hbm.at[rows]), (dh1_ref.at[rows], dh1_hbm.at[rows])]
        pairs.append((dm_ref.at[:, rows], dm_hbm.at[:, rows]))
        return [
            pltpu.make_async_copy(source, target, out_sem.at[b, i])
            for i, (source, target) in enumerate(pairs)
        ]

    def block(b, ggm):
        start = pl.multiple_of(b * MLP_BLOCK, MLP_BLOCK)
        rows = pl.ds(start, MLP_BLOCK)
        hidden1 = h1_ref[rows, :]
        r2 = rms(hidden1)
        gain = gm_ref[...]
        normed2_wide = hidden1 * r2 * gain
        normed2 = normed2_wide.astype(BF)
        nmt_s[:, rows] = transposed(normed2_wide).astype(BF)
        live = (
            start + lax.broadcasted_iota(jnp.int32, (MLP_BLOCK, 1), 0) < live_len
        ).astype(F32)

        back = cot_ref[rows, :].astype(F32) * live
        back_low = back.astype(BF)
        backt_s[:, rows] = transposed(back).astype(BF)
        def columns(c):
            cols = pl.ds(pl.multiple_of(c * MLP_COLS, MLP_COLS), MLP_COLS)
            gate = nn(normed2, wg_ref[:, cols])
            up = nn(normed2, wu_ref[:, cols])
            d_inner = nt(back_low, wd_ref[cols, :])
            sig = jax.nn.sigmoid(gate)
            silu = gate * sig
            inner_s[rows, cols] = (silu * up).astype(BF)
            dg_s[rows, cols] = (d_inner * up * sig * (1.0 + gate * (1.0 - sig))).astype(BF)
            du_s[rows, cols] = (d_inner * silu).astype(BF)

        def some_columns(i, carry):
            for c in range(MLP_UNROLL):
                columns(MLP_UNROLL * i + c)
            return carry

        lax.fori_loop(0, n_cols // MLP_UNROLL, some_columns, 0)
        out_ref[rows, :] = ((hidden1 + nn(inner_s[rows, :], wd_ref[...])) * live).astype(BF)
        d_normed2 = nt(dg_s[rows, :], wg_ref[...]) + nt(du_s[rows, :], wu_ref[...])
        scaled = d_normed2 * gain
        d_hidden1 = (
            back
            + r2 * scaled
            - hidden1 * (r2 * r2 * r2) * jnp.mean(scaled * hidden1, axis=-1, keepdims=True)
        )
        dh1_ref[rows, :] = d_hidden1
        d_attn = d_hidden1.astype(BF)
        da_s[rows, :] = d_attn

        d_mixed = nt(d_attn, wo_ref[...]).astype(BF)
        for j in range(Q_TILES):
            dm_ref[j, rows, :] = tile(d_mixed, j)
        for copy in results(b):
            copy.start()
        return ggm + jnp.sum(d_normed2 * hidden1 * r2, axis=0, keepdims=True)

    ggm_ref[...] = lax.fori_loop(0, seq_len // MLP_BLOCK, block, jnp.zeros((1, D), F32))

    def put(half, index, value):
        grads[half, pl.ds(pl.multiple_of(index * D, D), D), :] = value

    def leave(c):
        rows = pl.ds(pl.multiple_of(2 * c * D, D), 2 * D)
        return [
            pltpu.make_async_copy(grads.at[1 - core, rows], send_ref.at[rows], sem.at[c, 0]),
            pltpu.make_async_copy(grads.at[core, rows], keep_ref.at[rows], sem.at[c, 1]),
        ]

    def weights(c, carry):
        cols = pl.ds(pl.multiple_of(c * 2 * LANES, 2 * LANES), 2 * LANES)
        grad_gate = nn(nmt_s[:D, :], dg_s[:, cols]).astype(BF)
        grad_up = nn(nmt_s[:D, :], du_s[:, cols]).astype(BF)
        for t in range(2):
            put(0, 2 * c + t, tile(grad_gate, t))
            put(1, 2 * c + t, tile(grad_up, t))
        for copy in leave(c):
            copy.start()
        grad_down = nn(backt_s[:D, :], inner_s[:, cols]).astype(BF)
        part = jnp.where(c < DOWN_FIRST // 2, 0, 1)
        base = jnp.where(c < DOWN_FIRST // 2, FF_TILES + Q_TILES, FF_TILES - DOWN_FIRST)
        for t in range(2):
            put(part, base + 2 * c + t, tile(grad_down, t))
        return carry

    lax.fori_loop(0, n_cols, weights, 0)
    loads[6].wait()
    grad_o = tn(mixed_ref[...], da_s[...])[:D]
    for t in range(4):
        put(0, FF_TILES + t, tile(grad_o, t).astype(BF))
    put(0, FF_TILES + 4, half_tile(grad_o).astype(BF))
    grads[0, EXTRA:, :] = jnp.zeros((EARLY_ROWS - EXTRA, LANES), BF)
    grads[1, EXTRA - D :, :] = jnp.zeros((EARLY_ROWS - EXTRA + D, LANES), BF)
    row = lax.broadcasted_iota(jnp.int32, (16, LANES), 0)
    rest = jnp.zeros((16, LANES), F32)
    for r in range(5):
        start = (8 + r) * D - 16
        last = grads[0, start : start + 16, :].astype(F32)[15:16]
        rest = jnp.where(row == r, jnp.broadcast_to(last, (16, LANES)), rest)
    grads[0, EXTRA + 16 : EXTRA + 32, :] = rest.astype(BF)
    rows = pl.ds(FF_TILES * D, EARLY_ROWS - FF_TILES * D)
    final = [
        pltpu.make_async_copy(grads.at[1 - core, rows], send_ref.at[rows], sem.at[n_cols, 0]),
        pltpu.make_async_copy(grads.at[core, rows], keep_ref.at[rows], sem.at[n_cols, 1]),
    ]
    for copy in final:
        copy.start()

    def drain(c, carry):
        for copy in leave(c):
            copy.wait()
        return carry

    def drain_results(b, carry):
        for copy in results(b):
            copy.wait()
        return carry

    lax.fori_loop(0, n_cols, drain, 0)
    lax.fori_loop(0, seq_len // MLP_BLOCK, drain_results, 0)
    for copy in final:
        copy.wait()


def half_tile(value):
    rows = value.shape[0]
    return jnp.concatenate([value[:, 4 * LANES : D], jnp.zeros((rows, HD), value.dtype)], axis=1)


def gain_rows(value):
    row = lax.broadcasted_iota(jnp.int32, (16, LANES), 0)
    whole = jnp.zeros((16, LANES), F32)
    for t in range(Q_TILES):
        piece = tile(value, t) if t < 4 else half_tile(value)
        whole = jnp.where(row == t, jnp.broadcast_to(piece, (16, LANES)), whole)
    return whole


def backward_groups(
    first, q_ref, dm_ref, k_ref, v_ref, lse_ref, dq_ref, dk_ref, dv_ref, dk_acc, dv_acc
):
    seq_len = q_ref.shape[1]
    group = first + pl.program_id(0)
    dq_ref[...] = jnp.zeros_like(dq_ref)
    dk_acc[...] = jnp.zeros_like(dk_acc)
    dv_acc[...] = jnp.zeros_like(dv_acc)
    keep = lax.broadcasted_iota(jnp.int32, (BLOCK, BLOCK), 0) <= lax.broadcasted_iota(
        jnp.int32, (BLOCK, BLOCK), 1
    )
    for b in range(seq_len // BLOCK):
        rows = slice(b * BLOCK, (b + 1) * BLOCK)
        n_keys = (b + 1) * BLOCK
        for u in range(3):
            head = 3 * group + u
            j = lax.shift_right_logical(head, 1)
            own = j - lax.shift_right_logical(3 * group, 1)
            side = head - 2 * j
            queries = q_ref[j, rows, :]
            d_mixed = dm_ref[j, rows, :]
            keys = k_ref[side, 0:n_keys, :]
            values = v_ref[side, 0:n_keys, :]
            prob = jnp.exp(nt(keys, queries) - lse_ref[pl.ds(head, 1), rows])
            diag = jnp.where(keep, prob[n_keys - BLOCK :, :], 0.0)
            if n_keys > BLOCK:
                prob = jnp.concatenate([prob[: n_keys - BLOCK, :], diag], axis=0)
            else:
                prob = diag
            d_prob = nt(values, d_mixed)
            delta = jnp.sum(d_prob * prob, axis=0, keepdims=True)
            d_score = (prob * (d_prob - delta)).astype(BF)
            dv_acc[side, 0:n_keys, :] += nn(prob.astype(BF), d_mixed)
            dk_acc[side, 0:n_keys, :] += nn(d_score, queries)
            dq_ref[0, own, rows, :] += tn(d_score, keys)
    dk_ref[0] = dk_acc[0] + flip(dk_acc[1])
    dv_ref[0] = dv_acc[0] + flip(dv_acc[1])


def backward_finish(
    x_ref, ga_ref, dh1_ref, dqa_ref, dka_ref, dva_ref, dqb_ref, dkb_ref, dvb_ref,
    wq_ref, wkv_ref, cos_ref, sin_ref,
    dx_ref, dq_s, dkv_s, nm_s, gga_ref,
):
    seq_len = x_ref.shape[0]
    low = low_half(BLOCK)

    def block(b, gga):
        rows = pl.ds(pl.multiple_of(b * BLOCK, BLOCK), BLOCK)
        cosine = cos_ref[rows, :]
        sine = sin_ref[rows, :]

        def unrope(value):
            return value * cosine - swap_halves(value) * sine

        d_rot = [
            dqa_ref[0, 0, rows, :],
            dqa_ref[0, 1, rows, :] + dqb_ref[0, 0, rows, :],
            dqb_ref[0, 1, rows, :],
            dqb_ref[1, 0, rows, :],
            dqb_ref[1, 1, rows, :],
        ]
        for j in range(Q_TILES):
            d_query = unrope(d_rot[j]) * HD ** (-0.5)
            dq_s[rows, j * LANES : (j + 1) * LANES] = d_query.astype(BF)
        dk = [dka_ref[0, rows, :], dkb_ref[0, rows, :], dkb_ref[1, rows, :]]
        dv = [dva_ref[0, rows, :], dvb_ref[0, rows, :], dvb_ref[1, rows, :]]
        first = unrope(jnp.where(low, dk[0], flip(dk[1])))
        second = jnp.where(low, unrope(dk[2]), flip(dv[0]))
        third = jnp.where(low, dv[1], flip(dv[2]))
        dkv_s[rows, 0:LANES] = first.astype(BF)
        dkv_s[rows, LANES : 2 * LANES] = second.astype(BF)
        dkv_s[rows, 2 * LANES :] = third.astype(BF)
        d_normed = nt(dq_s[rows, :], wq_ref[...]) + nt(dkv_s[rows, :], wkv_ref[...])
        stream = x_ref[rows, :].astype(F32)
        r1 = rms(stream)
        gain = ga_ref[...]
        nm_s[rows, :] = (stream * r1 * gain).astype(BF)
        scaled = d_normed * gain
        dx_ref[rows, :] = (
            dh1_ref[rows, :]
            + r1 * scaled
            - stream * (r1 * r1 * r1) * jnp.mean(scaled * stream, axis=-1, keepdims=True)
        ).astype(BF)
        return gga + jnp.sum(d_normed * stream * r1, axis=0, keepdims=True)

    gga_ref[...] = lax.fori_loop(0, seq_len // BLOCK, block, jnp.zeros((1, D), F32))


def late_weights(
    core_ref, nm_s, dq_s, dkv_s, gga_ref, ggm_ref, keep_ref, send_ref, late, sem
):
    grad_q = tn(nm_s[...], dq_s[...]).astype(BF)
    grad_kv = tn(nm_s[...], dkv_s[...]).astype(BF)
    for t in range(Q_TILES):
        late[t * D : (t + 1) * D, :] = tile(grad_q, t)
    for t in range(3):
        late[(Q_TILES + t) * D : (Q_TILES + t + 1) * D, :] = tile(grad_kv, t)
    late[8 * D :, :] = jnp.zeros((2 * LATE_HALF - 8 * D, LANES), BF)
    late[8 * D : 8 * D + 16, :] = gain_rows(gga_ref[...]).astype(BF)
    late[8 * D + 16 : 8 * D + 32, :] = gain_rows(ggm_ref[...]).astype(BF)
    copies = []
    for i, (which, ref) in enumerate(((1 - core_ref[0], send_ref), (core_ref[0], keep_ref))):
        rows = pl.ds(pl.multiple_of(which * LATE_HALF, 8), LATE_HALF)
        copies.append(pltpu.make_async_copy(late.at[rows], ref, sem.at[i]))
    for copy in copies:
        copy.start()
    for copy in copies:
        copy.wait()


def gather_sum(bits_ref, *refs, n_parts, rows, split, merge, joined):
    n_in = 1 if joined else n_parts
    kept, got = refs[:n_in], refs[n_in : 2 * n_in]
    kinds = 2 if split else 1
    n_out = kinds * (1 if merge else n_parts)
    outs = refs[2 * n_in : 2 * n_in + n_out]
    scratch, sem = refs[2 * n_in + n_out :]
    size = rows // kinds
    copies = []
    for p in range(n_parts):
        if joined:
            part = slice(p * rows, (p + 1) * rows)
            total = kept[0][part, :].astype(F32) + got[0][part, :].astype(F32)
        else:
            total = kept[p][...].astype(F32) + got[p][...].astype(F32)
        scratch[p] = total.astype(BF)
        for i in range(kinds):
            if merge:
                target = outs[i].at[pl.ds(p * size, size)]
            else:
                target = outs[p + i * n_parts]
            start = (bits_ref[p] if i else 1 - bits_ref[p]) * size if split else 0
            source = scratch.at[p, pl.ds(pl.multiple_of(start, 8), size)]
            copies.append(pltpu.make_async_copy(source, target, sem.at[2 * p + i]))
            copies[-1].start()
    for copy in copies:
        copy.wait()


def join_halves(bits_ref, *refs, n_parts, rows, merged):
    n_in = 1 if merged else n_parts
    own, got, outs = refs[:n_in], refs[n_in : 2 * n_in], refs[2 * n_in : 2 * n_in + n_parts]
    sem = refs[2 * n_in + n_parts]
    copies = []
    for p in range(n_parts):
        for i, (group, which) in enumerate(((own, bits_ref[p]), (got, 1 - bits_ref[p]))):
            source = group[0].at[pl.ds(p * rows, rows)] if merged else group[p]
            span = pl.ds(pl.multiple_of(which * rows, 8), rows)
            copies.append(pltpu.make_async_copy(source, outs[p].at[span], sem.at[2 * p + i]))
            copies[-1].start()
    for copy in copies:
        copy.wait()


def put_wide(flat, tmp, values, rows, row):
    pairs = rows // 2
    for index, value in enumerate(values):
        tmp[pl.ds(index * D, rows), :] = value
    even = [tmp[pl.ds(i * D, pairs, stride=2), :] for i in range(Q_TILES)]
    odd = [flip(tmp[pl.ds(i * D + 1, pairs, stride=2), :]) for i in range(Q_TILES)]
    low = low_half(pairs)
    for c in range(4):
        flat[pl.ds(row + c, pairs, stride=9), :] = even[c]
    flat[pl.ds(row + 4, pairs, stride=9), :] = jnp.where(low, even[4], odd[0])
    for c in range(4):
        flat[pl.ds(row + 5 + c, pairs, stride=9), :] = jnp.where(low, odd[c], odd[c + 1])


def copy_array(source_ref, target_ref, sem):
    copy = pltpu.make_async_copy(source_ref, target_ref, sem)
    copy.start()
    copy.wait()


def update_rule(scale, rate, grad, master, momentum, average):
    weight_grad = grad * scale
    new_momentum = MOMENTUM_DECAY * momentum + weight_grad
    new_master = master - rate * (weight_grad + MOMENTUM_DECAY * new_momentum)
    new_average = AVERAGE_DECAY * average + (1.0 - AVERAGE_DECAY) * new_master
    return weight_grad, new_momentum, new_master, new_average


class Chunks:
    def __init__(self, rows, base, count, rule, refs):
        self.rows, self.base, self.count, self.rule = rows, base, count, rule
        self.ins, self.outs, self.in_buf, self.out_buf, self.in_sem, self.out_sem = refs
        self.size = rows * LANES

    def span(self, c):
        return pl.ds(pl.multiple_of((self.base + c * self.rows) * LANES, LANES), self.size)

    def place(self, index, start=0, length=None):
        start = pl.multiple_of(index * self.size + start, 8 * LANES)
        return pl.ds(start, self.size if length is None else length)

    def fetch(self, c):
        return [
            pltpu.make_async_copy(
                self.ins[i].at[self.span(c)],
                self.in_buf.at[self.place(c * 3 + i)],
                self.in_sem.at[c, i],
            )
            for i in range(3)
        ]

    def flush(self, c):
        return [
            pltpu.make_async_copy(
                self.out_buf.at[self.place(c * 4 + i)],
                self.outs[i].at[self.span(c)],
                self.out_sem.at[c, i],
            )
            for i in range(4)
        ]

    def start(self):
        def body(c, carry):
            for copy in self.fetch(c):
                copy.start()
            return carry

        lax.fori_loop(0, self.count, body, 0)

    def run(self, stage, gradient):
        sub = STEP * LANES

        def body(c, carry):
            stage(c)
            for copy in self.fetch(c):
                copy.wait()

            def step(s, inner):
                grad = gradient(c, s * STEP, STEP).reshape(sub)
                values = self.rule(
                    grad, *[self.in_buf[self.place(c * 3 + i, s * sub, sub)] for i in range(3)]
                )
                for i in range(4):
                    self.out_buf[self.place(c * 4 + i, s * sub, sub)] = values[i]
                return inner

            lax.fori_loop(0, self.rows // STEP, step, 0)
            for copy in self.flush(c):
                copy.start()
            return carry

        def drain(c, carry):
            for copy in self.flush(c):
                copy.wait()
            return carry

        lax.fori_loop(0, self.count, body, 0)
        return lambda: lax.fori_loop(0, self.count, drain, 0)


class Extra:
    def __init__(self, start, ins, outs, rest):
        self.bufs, self.sem = rest[:8], rest[8]
        count = self.bufs[0].shape[0]
        span = pl.ds(start, count)
        self.count = count
        self.loads = [
            pltpu.make_async_copy(ins[i].at[span], self.bufs[i], self.sem.at[i]) for i in range(3)
        ]
        self.stores = [
            pltpu.make_async_copy(self.bufs[3 + i], outs[i].at[span], self.sem.at[3 + i])
            for i in range(4)
        ]

    def start(self):
        for copy in self.loads:
            copy.start()

    def finish(self, grad, rule):
        for copy in self.loads:
            copy.wait()
        self.bufs[7][...] = grad.reshape(grad.shape[0] * LANES)
        values = rule(self.bufs[7][pl.ds(0, self.count)], *[self.bufs[i][...] for i in range(3)])
        for i in range(4):
            self.bufs[3 + i][...] = values[i]
            self.stores[i].start()

    def drain(self):
        for copy in self.stores:
            copy.wait()


def shifted(flat, row, count):
    here = flip(flat[pl.ds(row - 1, count), :])
    after = flip(flat[pl.ds(row, count), :])
    return jnp.where(low_half(count), here, after)


def load_parts(pieces, sem):
    copies = [
        pltpu.make_async_copy(source, target, sem.at[i]) for i, (source, target) in enumerate(pieces)
    ]
    for copy in copies:
        copy.start()
    return copies


FLAT_BASE = 8
TAIL_ZERO = HALF - (GATE_ROW + 11 * CHUNK) * LANES
TAIL_ONE = HALF - (6916 + 11 * CHUNK) * LANES


def update_first(scale, rate, core_ref, bits_ref, *rest):
    halves, ins, outs = rest[:4], rest[4:7], rest[7:11]
    early_ref, flat, in_buf, out_buf, in_sem, out_sem, part_sem = rest[11:18]
    refs = (ins, outs, in_buf, out_buf, in_sem, out_sem)
    core = core_ref[0]
    rule = functools.partial(update_rule, scale, rate)
    half = PART_ROWS // 2
    pieces = []
    for p in range(2):
        for i, which in enumerate((bits_ref[p], 1 - bits_ref[p])):
            span = pl.ds(pl.multiple_of(p * PART_ROWS + which * half, 8), half)
            pieces.append((halves[2 * p + i], early_ref.at[span]))
    copies = load_parts(pieces, part_sem)
    extra = Extra((GATE_ROW + 11 * CHUNK) * LANES, ins, outs, rest[18:])
    base = jnp.where(core == 0, GATE_ROW, 4)
    chunks = Chunks(CHUNK, base, 11 + core, rule, refs)
    chunks.start()

    @pl.when(core == 0)
    def _():
        extra.start()

    for copy in copies:
        copy.wait()
    flat[0:FLAT_BASE, :] = jnp.zeros((FLAT_BASE, LANES), F32)

    def stage(c):
        for t in range(FF_TILES):
            rows = pl.ds(pl.multiple_of(t * D + c * 48, 16), 48)
            flat[pl.ds(FLAT_BASE + t, 48, stride=FF_TILES), :] = early_ref[rows, :].astype(F32)

    def gradient(c, start, count):
        row = pl.multiple_of(FLAT_BASE + start, 8)
        return jnp.where(core == 0, flat[pl.ds(row, count), :], shifted(flat, row, count))

    def stage_next(c):
        flat[FLAT_BASE - 1 : FLAT_BASE, :] = flat[FLAT_BASE + CHUNK - 1 : FLAT_BASE + CHUNK, :]
        stage(c)

    drain = chunks.run(stage_next, gradient)

    @pl.when(core == 0)
    def _():
        stage(11)
        extra.finish(flat[FLAT_BASE : FLAT_BASE + CHUNK, :], rule)

    drain()

    @pl.when(core == 0)
    def _():
        extra.drain()


def lay_out_late(flat, tmp, late_ref):
    def late(index):
        return late_ref[index * D : (index + 1) * D, :].astype(F32)

    low1 = low_half(1)
    gain_a = late_ref[8 * D : 8 * D + 16, :].astype(F32)
    gain_m = flip(late_ref[8 * D + 16 : 8 * D + 32, :].astype(F32))
    for r in range(4):
        flat[r : r + 1, :] = gain_a[r : r + 1]
    flat[4:5, :] = jnp.where(low1, gain_a[4:5], gain_m[0:1])
    for r in range(4):
        flat[5 + r : 6 + r, :] = jnp.where(low1, gain_m[r : r + 1], gain_m[r + 1 : r + 2])
    put_wide(flat, tmp, [late(t) for t in range(Q_TILES)], D, 9)
    pairs = D // 2
    for t in range(3):
        tmp[pl.ds(t * D, D), :] = late(Q_TILES + t)
    even = [tmp[pl.ds(i * D, pairs, stride=2), :] for i in range(3)]
    odd = [tmp[pl.ds(i * D + 1, pairs, stride=2), :] for i in range(3)]
    low = low_half(pairs)
    turned = [flip(odd[0]), flip(odd[1]), flip(even[1]), flip(even[2])]
    rows = (
        (2601, even[0]),
        (2602, jnp.where(low, even[1], turned[0])),
        (2603, jnp.where(low, turned[0], turned[1])),
        (3465, jnp.where(low, turned[2], turned[3])),
        (3466, jnp.where(low, turned[3], odd[1])),
        (3467, odd[2]),
    )
    for row, value in rows:
        flat[pl.ds(row, pairs, stride=3), :] = value


def update_second(scale, rate, core_ref, bits_ref, *rest):
    halves, late_halves, ins, outs = rest[:8], rest[8:10], rest[10:13], rest[17:21]
    flat, tmp, part_ref, swap_ref, first_ref, in_buf, out_buf, in_sem, out_sem, part_sem = rest[21:31]
    refs = (ins, outs, in_buf, out_buf, in_sem, out_sem)
    tail = Extra((6916 + 11 * CHUNK) * LANES, ins, outs, rest[31:40])
    head = Extra(0, ins, outs, rest[40:49])
    late_flat, late_ref, late_in, late_out, late_in_sem, late_out_sem, late_sem = rest[49:56]
    late_last = Extra(LATE_CHUNKS * CHUNK * LANES, ins, outs, rest[56:])
    rule = functools.partial(update_rule, scale, rate)
    half = PART_ROWS // 2
    pieces = []
    for i in range(2):
        which = [1 - bits_ref[p] if i else bits_ref[p] for p in range(3)]

        def rows(start, p, size, which=which):
            return pl.ds(pl.multiple_of(start + which[p] * size, 16), size)

        source = halves[2 + i].at[pl.ds(half - REST_SLOT, REST_SLOT)]
        pieces.append((source, part_ref.at[rows(0, 1, REST_SLOT)]))
        pieces.append((halves[4 + i], part_ref.at[rows(2 * REST_SLOT, 2, half)]))
        pieces.append((halves[6 + i], swap_ref.at[rows(0, 2, half)]))
        pieces.append((halves[i].at[pl.ds(0, 16)], first_ref.at[rows(0, 0, 16)]))
    parts = load_parts(pieces, part_sem)

    @pl.when(core_ref[0] == 0)
    def _():
        def stage(c):
            values = []
            for t in range(Q_TILES):
                rows = pl.ds(pl.multiple_of(REST + t * D + c * 64, 16), 64)
                values.append(part_ref[rows, :].astype(F32))
            put_wide(flat, tmp, values, 64, FLAT_BASE)

        def gradient(c, start, count):
            return flat[pl.ds(pl.multiple_of(FLAT_BASE + start, 8), count), :]

        chunks = Chunks(CHUNK // 2, O_ROW, 9, rule, refs)
        late_refs = (ins, outs, late_in, late_out, late_in_sem, late_out_sem)
        late_chunks = Chunks(CHUNK, 0, LATE_CHUNKS, rule, late_refs)
        pieces = [
            (ref, late_ref.at[pl.ds(i * LATE_HALF, LATE_HALF)]) for i, ref in enumerate(late_halves)
        ]
        chunks.start()
        late_parts = load_parts(pieces, late_sem)
        late_chunks.start()
        late_last.start()
        for copy in parts:
            copy.wait()
        drain = chunks.run(stage, gradient)
        for copy in late_parts:
            copy.wait()
        lay_out_late(late_flat, tmp, late_ref)

        def late_gradient(c, start, count):
            return late_flat[pl.ds(pl.multiple_of(c * CHUNK + start, 8), count), :]

        late_drain = late_chunks.run(lambda c: None, late_gradient)
        start = LATE_CHUNKS * CHUNK
        late_last.finish(late_flat[start : start + 304, :], rule)
        drain()
        late_drain()
        late_last.drain()

    @pl.when(core_ref[0] == 1)
    def _():
        head.start()
        chunks = Chunks(CHUNK, 6916, 11, rule, refs)
        chunks.start()
        tail.start()
        for copy in parts:
            copy.wait()
        flat[0:FLAT_BASE, :] = jnp.zeros((FLAT_BASE, LANES), F32)
        flat[FLAT_BASE : FLAT_BASE + 8, :] = swap_ref[SWAP_TAIL : SWAP_TAIL + 16, :].astype(F32)[0:8]
        flat[FLAT_BASE + 5 : FLAT_BASE + 6, :] = first_ref[0:16, :].astype(F32)[0:1]
        head.finish(shifted(flat, FLAT_BASE + 1, 8), rule)
        row = FLAT_BASE + CHUNK - 1
        flat[row : row + 1, :] = part_ref[REST - 16 : REST, :].astype(F32)[15:16]

        def stage(c):
            flat[FLAT_BASE - 1 : FLAT_BASE, :] = flat[FLAT_BASE + CHUNK - 1 : FLAT_BASE + CHUNK, :]
            inside = c < DOWN_FIRST
            here = pl.ds(pl.multiple_of(SWAP_START + jnp.where(inside, c, 0) * D, 16), D)
            there = pl.ds(pl.multiple_of(REST + jnp.where(inside, 0, c - DOWN_FIRST) * D, 16), D)
            whole = jnp.where(inside, swap_ref[here, :].astype(F32), part_ref[there, :].astype(F32))
            pieces = [whole[i * LANES : (i + 1) * LANES].T for i in range(4)]
            half = jnp.concatenate([whole[4 * LANES :], jnp.zeros((LANES - HD, LANES), F32)], axis=0)
            put_wide(flat, tmp, pieces + [half.T], LANES, FLAT_BASE)

        def gradient(c, start, count):
            return shifted(flat, FLAT_BASE + start, count)

        drain = chunks.run(stage, gradient)
        stage(11)
        flat[FLAT_BASE + CHUNK :, :] = jnp.zeros((8, LANES), F32)
        tail.finish(shifted(flat, FLAT_BASE, CHUNK + 8), rule)
        head.drain()
        drain()
        tail.drain()


def vmem():
    return pl.BlockSpec(memory_space=pltpu.VMEM)


def smem():
    return pl.BlockSpec(memory_space=pltpu.SMEM)


def hbm():
    return pl.BlockSpec(memory_space=pl.ANY)


def call(kernel, outs, in_specs, out_specs, scratch, flops, name, limit, aliases=None):
    n_bytes = sum(math.prod(shape) * jnp.dtype(kind).itemsize for shape, kind in outs)
    return pl.pallas_call(
        kernel,
        out_shape=[jax.ShapeDtypeStruct(shape, kind) for shape, kind in outs],
        in_specs=in_specs,
        out_specs=out_specs,
        scratch_shapes=scratch,
        input_output_aliases=aliases or {},
        compiler_params=pltpu.CompilerParams(vmem_limit_bytes=limit * MIB),
        cost_estimate=pl.CostEstimate(
            flops=int(flops), bytes_accessed=int(2 * n_bytes), transcendentals=0
        ),
        name=name,
    )


def rope_tables(seq_len):
    lane = jnp.arange(LANES, dtype=jnp.int32)
    which = (lane % (HD // 2)).astype(F32)
    frequency = jnp.exp(which * (-2.0 * math.log(10000.0) / HD))
    angles = jnp.arange(seq_len, dtype=F32)[:, None] * frequency[None, :]
    sign = jnp.where(lane % HD < HD // 2, -1.0, 1.0)
    return jnp.cos(angles), jnp.sin(angles) * sign[None, :]


def run_prepare(core, own, other):
    outs = [
        ((1, D), F32),
        ((1, D), F32),
        ((D, PAD_D), BF),
        ((D, KV_COLS), BF),
        ((PAD_D, D), BF),
        ((D, FF), BF),
        ((D, FF), BF),
        ((FF, D), BF),
    ]
    scratch = [
        pltpu.VMEM((HALF,), F32),
        pltpu.VMEM((HALF,), F32),
        pltpu.VMEM((FLAT_SCRATCH, LANES), F32),
        pltpu.VMEM((Q_TILES * D, LANES), F32),
        pltpu.VMEM((8 * LANES,), F32),
        pltpu.SemaphoreType.DMA((2,)),
    ]
    return call(
        prepare_weights,
        outs,
        [smem()] + [hbm()] * 2,
        [vmem()] * 8,
        scratch,
        1e10,
        "prepare_weights",
        56,
    )(core, own, other)


def run_attention_forward(x, gain, wq, wkv, wo, cosine, sine):
    seq_len = x.shape[0]
    outs = [
        ((seq_len, D), F32),
        ((seq_len, PAD_D), BF),
        ((Q_TILES, seq_len, LANES), BF),
        ((6, seq_len, LANES), BF),
        ((6, seq_len, LANES), BF),
        ((16, seq_len), F32),
    ]
    return call(
        attention_forward,
        outs,
        [vmem()] * 4 + [hbm()] + [vmem()] * 2,
        [hbm()] * 5 + [vmem()],
        [pltpu.VMEM(shape, kind) for shape, kind in outs[:5]]
        + [
            pltpu.VMEM((PAD_D, D), BF),
            pltpu.VMEM((Q_TILES, BLOCK, LANES), F32),
            pltpu.SemaphoreType.DMA((4,)),
            pltpu.SemaphoreType.DMA((seq_len // BLOCK, 2)),
        ],
        1.5e10,
        "attention_forward",
        56,
    )(x, gain, wq, wkv, wo, cosine, sine)


def run_mlp(core, slot, lengths, assignment, return_order, hidden1, cot, mixed, gain, wo, wg, wu, wd):
    seq_len = hidden1.shape[0]
    outs = [
        ((seq_len, D), BF),
        ((seq_len, D), F32),
        ((Q_TILES, seq_len, LANES), BF),
        ((1, D), F32),
        ((EARLY_ROWS, LANES), BF),
        ((EARLY_ROWS, LANES), BF),
    ]
    return call(
        mlp_pass,
        outs,
        [smem()] * 5 + [hbm()] * 3 + [vmem()] + [hbm()] * 4,
        [hbm()] * 3 + [vmem()] + [hbm()] * 2,
        [
            pltpu.VMEM((seq_len, D), F32),
            pltpu.VMEM((seq_len, D), BF),
            pltpu.VMEM((seq_len, PAD_D), BF),
            pltpu.VMEM((PAD_D, D), BF),
            pltpu.VMEM((D, FF), BF),
            pltpu.VMEM((D, FF), BF),
            pltpu.VMEM((FF, D), BF),
            pltpu.VMEM((seq_len, D), BF),
            pltpu.VMEM((seq_len, D), F32),
            pltpu.VMEM((Q_TILES, seq_len, LANES), BF),
            pltpu.VMEM((PAD_D, seq_len), BF),
            pltpu.VMEM((PAD_D, seq_len), BF),
            pltpu.VMEM((seq_len, FF), BF),
            pltpu.VMEM((seq_len, FF), BF),
            pltpu.VMEM((seq_len, FF), BF),
            pltpu.VMEM((seq_len, D), BF),
            pltpu.VMEM((2, EARLY_ROWS, LANES), BF),
            pltpu.SemaphoreType.DMA((7,)),
            pltpu.SemaphoreType.DMA((seq_len // MLP_BLOCK, 3)),
            pltpu.SemaphoreType.DMA((FF_TILES // 2 + 1, 2)),
        ],
        2.5e10,
        "mlp_pass",
        56,
    )(core, slot, lengths, assignment, return_order, hidden1, cot, mixed, gain, wo, wg, wu, wd)


def run_backward_groups(first, count, q, dm, k, v, lse):
    seq_len = q.shape[1]
    fixed = pl.BlockSpec((Q_TILES, seq_len, LANES), lambda i: (0, 0, 0))
    sides = pl.BlockSpec((2, seq_len, LANES), lambda i: (first + i, 0, 0))
    single = pl.BlockSpec((1, seq_len, LANES), lambda i: (i, 0, 0))
    outs = [(count, 2, seq_len, LANES), (count, seq_len, LANES), (count, seq_len, LANES)]
    return pl.pallas_call(
        functools.partial(backward_groups, first),
        grid=(count,),
        out_shape=[jax.ShapeDtypeStruct(shape, F32) for shape in outs],
        in_specs=[
            fixed,
            fixed,
            sides,
            sides,
            pl.BlockSpec((16, seq_len), lambda i: (0, 0)),
        ],
        out_specs=[
            pl.BlockSpec((1, 2, seq_len, LANES), lambda i: (i, 0, 0, 0)),
            single,
            single,
        ],
        scratch_shapes=[pltpu.VMEM((2, seq_len, LANES), F32)] * 2,
        compiler_params=pltpu.CompilerParams(vmem_limit_bytes=56 * MIB),
        cost_estimate=pl.CostEstimate(
            flops=int(8e9) * count, bytes_accessed=int(3e6) * count, transcendentals=0
        ),
        name="backward_groups",
    )(q, dm, k, v, lse)


def run_backward_finish(x, gain, dh1, groups, wq, wkv, cosine, sine):
    seq_len = x.shape[0]
    outs = [
        ((seq_len, D), BF),
        ((seq_len, PAD_D), BF),
        ((seq_len, KV_COLS), BF),
        ((seq_len, D), BF),
        ((1, D), F32),
    ]
    return call(
        backward_finish,
        outs,
        [vmem()] * 13,
        [vmem()] * 5,
        [],
        4e9,
        "backward_finish",
        56,
    )(x, gain, dh1, *groups[0], *groups[1], wq, wkv, cosine, sine)


def run_late_weights(core, normed, d_query, d_kv, gga, ggm):
    outs = [((LATE_HALF, LANES), BF), ((LATE_HALF, LANES), BF)]
    return call(
        late_weights,
        outs,
        [smem()] + [vmem()] * 5,
        [hbm()] * 2,
        [pltpu.VMEM((2 * LATE_HALF, LANES), BF), pltpu.SemaphoreType.DMA((2,))],
        4e9,
        "late_weights",
        56,
    )(core, normed, d_query, d_kv, gga, ggm)


def run_sum(bits, kept, got, split, merge=False, n_parts=None):
    joined = n_parts is not None
    n_parts = n_parts or len(kept)
    rows = kept[0].shape[0] // (n_parts if joined else 1)
    kinds = 2 if split else 1
    n_out = 1 if merge else n_parts
    out_rows = rows // kinds * (n_parts if merge else 1)
    results = call(
        functools.partial(
            gather_sum, n_parts=n_parts, rows=rows, split=split, merge=merge, joined=joined
        ),
        [((out_rows, LANES), BF)] * (kinds * n_out),
        [smem()] + [vmem()] * (2 * len(kept)),
        [hbm()] * (kinds * n_out),
        [pltpu.VMEM((n_parts, rows, LANES), BF), pltpu.SemaphoreType.DMA((2 * n_parts,))],
        1e6,
        "gather_sum",
        12,
    )(bits, *kept, *got)
    return list(results[:n_out]), list(results[n_out:])


def run_join(bits, own, got, n_parts):
    merged = len(own) < n_parts
    rows = own[0].shape[0] // (n_parts if merged else 1)
    return call(
        functools.partial(join_halves, n_parts=n_parts, rows=rows, merged=merged),
        [((2 * rows, LANES), BF)] * n_parts,
        [smem()] + [hbm()] * (2 * len(own)),
        [hbm()] * n_parts,
        [pltpu.SemaphoreType.DMA((2 * n_parts,))],
        1e6,
        "join_halves",
        4,
    )(bits, *own, *got)


def run_copy(value):
    outs = [(value.shape, value.dtype)]
    scratch = [pltpu.SemaphoreType.DMA]
    return call(copy_array, outs, [hbm()], [hbm()], scratch, 1e6, "copy_array", 4)(value)[0]


def chunk_scratch(count):
    return [
        pltpu.VMEM((3 * count * CHUNK * LANES,), F32),
        pltpu.VMEM((4 * count * CHUNK * LANES,), F32),
        pltpu.SemaphoreType.DMA((12, 3)),
        pltpu.SemaphoreType.DMA((12, 4)),
    ]


def extra_scratch(count, n_rows):
    bufs = [pltpu.VMEM((count,), F32)] * 7 + [pltpu.VMEM((n_rows * LANES,), F32)]
    return bufs + [pltpu.SemaphoreType.DMA((7,))]


def run_update_first(scale, rate, core, bits, halves, state):
    scratch = [
        pltpu.VMEM((2 * PART_ROWS, LANES), BF),
        pltpu.VMEM((FLAT_BASE + CHUNK, LANES), F32),
        *chunk_scratch(12),
        pltpu.SemaphoreType.DMA((4,)),
        *extra_scratch(TAIL_ZERO, CHUNK),
    ]
    return call(
        functools.partial(update_first, scale, rate),
        [(state[0].shape, F32)] * 4,
        [smem()] * 2 + [hbm()] * 7,
        [hbm()] * 4,
        scratch,
        1e9,
        "update_first",
        56,
    )(core, bits, *halves, *state)


def run_update_second(scale, rate, core, bits, halves, late_halves, state, done):
    scratch = [
        pltpu.VMEM((FLAT_BASE + CHUNK + 8, LANES), F32),
        pltpu.VMEM((Q_TILES * D, LANES), F32),
        pltpu.VMEM((2 * REST_SLOT + PART_ROWS, LANES), BF),
        pltpu.VMEM((PART_ROWS, LANES), BF),
        pltpu.VMEM((32, LANES), BF),
        *chunk_scratch(11),
        pltpu.SemaphoreType.DMA((8,)),
        *extra_scratch(TAIL_ONE, CHUNK + 8),
        *extra_scratch(5 * LANES, 8),
        pltpu.VMEM((4336, LANES), F32),
        pltpu.VMEM((2 * LATE_HALF, LANES), BF),
        *chunk_scratch(LATE_CHUNKS),
        pltpu.SemaphoreType.DMA((2,)),
        *extra_scratch((O_ROW - LATE_CHUNKS * CHUNK) * LANES, 304),
    ]
    return call(
        functools.partial(update_second, scale, rate),
        [(state[0].shape, F32)] * 4,
        [smem()] * 2 + [hbm()] * 17,
        [hbm()] * 4,
        scratch,
        1e9,
        "update_second",
        56,
        {15 + i: i for i in range(4)},
    )(core, bits, *halves, *late_halves, *state, *done)


def add_low(a, b):
    return (a.astype(F32) + b.astype(F32)).astype(BF)


def xor_swap(value, bit):
    size = lax.axis_size("dp")
    return lax.ppermute(value, "dp", [(i, i ^ (1 << bit)) for i in range(size)])


def tie(value, *others):
    return lax.optimization_barrier((value, *others))


def my_bits(orders, step):
    index = lax.axis_index("dp")
    return jnp.stack([(index >> order[step]) & 1 for order in orders]).astype(jnp.int32)


def near_size():
    return min(lax.axis_size("dp"), 4)


def spread(blocks):
    size, near = lax.axis_size("dp"), near_size()
    groups = [[g * near + i for i in range(near)] for g in range(size // near)]
    return lax.all_to_all(
        blocks, "dp", split_axis=0, concat_axis=0, tiled=True, axis_index_groups=groups
    )


def scatter_sum(value):
    count = near_size()
    blocks = spread(value.reshape(count, value.shape[0] // count, LANES))
    return jnp.sum(blocks.astype(F32), axis=0).astype(BF)


def bit_orders():
    n_bits = lax.axis_size("dp").bit_length() - 1
    base = list(range(n_bits))
    head = base[:3] if n_bits >= 3 else base
    return [head[r:] + head[:r] + base[len(head) :] for r in range(3)]


def on_device(inputs, cotangent, lengths, assignment, return_order, master, momentum, average):
    nseq_all, block_rows, _ = inputs.shape
    axes = ("dp", "shard")
    seq_len = block_rows * lax.axis_size("dp") * lax.axis_size("shard")
    my_slot = lax.axis_index(axes)
    core = lax.axis_index("shard")
    core_arr = core.astype(jnp.int32).reshape(1)

    seq_ids = jnp.arange(nseq_all, dtype=jnp.int32)
    sequence = jnp.sum(
        jnp.where(return_order[:, None] == seq_ids[None, :], assignment[None, :], 0), axis=1
    )

    def pick(array, index):
        return array.at[index].get(mode="promise_in_bounds")

    def exchange(value):
        return lax.all_to_all(value, axes, split_axis=0, concat_axis=0, tiled=True)

    x = exchange(pick(inputs, sequence)).reshape(seq_len, D)
    slot_arr = my_slot.astype(jnp.int32).reshape(1)

    other = lax.ppermute(master, "shard", [(0, 1), (1, 0)])
    gain_attn, gain_mlp, wq, wkv, wo, wg, wu, wd = run_prepare(core_arr, master, other)

    cosine, sine = rope_tables(seq_len)
    sent_cot, gain_attn, cosine = tie(cotangent, gain_attn, cosine)
    cot = exchange(sent_cot).reshape(seq_len, D)
    hidden1, mixed, q, k, v, lse = run_attention_forward(x, gain_attn, wq, wkv, wo, cosine, sine)
    result, dh1, dm, ggm, early_keep, early_send = run_mlp(
        core_arr, slot_arr, lengths, assignment, return_order, hidden1, cot, mixed, gain_mlp, wo, wg, wu, wd
    )
    back_out = exchange(result.reshape(nseq_all, block_rows, D))

    orders = bit_orders()
    n_bits = len(orders[0])

    def swap_parts(parts, step):
        return [xor_swap(part, order[step]) for part, order in zip(parts, orders)]

    got = lax.ppermute(early_send, "shard", [(0, 1), (1, 0)])
    groups = [run_backward_groups(0, 1, q, dm, k, v, lse)]
    lse, got = tie(lse, got)
    sent, kept = run_sum(my_bits(orders, 0), [early_keep], [got], True, n_parts=3)
    lse, *kept = tie(lse, *kept)
    got = swap_parts(sent, 0)
    groups.append(run_backward_groups(1, KV - 1, q, dm, k, v, lse))
    sent, kept = run_sum(my_bits(orders, 1), kept, got, True)
    dh1, back_out, *kept = tie(dh1, back_out, *kept)
    got = swap_parts(sent, 1)
    d_stream, d_query, d_kv, normed, gga = run_backward_finish(
        x, gain_attn, dh1, groups, wq, wkv, cosine, sine
    )
    last_bit = n_bits - 1
    for step in range(2, n_bits):
        if step > 2:
            got = swap_parts(sent, step - 1)
        sent, kept = run_sum(my_bits(orders, step), kept, got, True, merge=step == last_bit)
        if step == 2:
            gga, *kept = tie(gga, *kept)
            late_keep, late_send = run_late_weights(core_arr, normed, d_query, d_kv, gga, ggm)
            late_send, *kept = tie(late_send, *kept)
        if step == last_bit:
            late_send, sent[0] = tie(late_send, sent[0])
    got = [xor_swap(sent[0], last_bit)]
    late_got = lax.ppermute(late_send, "shard", [(0, 1), (1, 0)])
    late, _ = run_sum(my_bits(orders, 0)[:1], [late_keep], [late_got], False)
    late, block_output, *got = tie(late[0], run_copy(back_out), *got)
    early, _ = run_sum(my_bits(orders, last_bit)[:1], kept, got, False)
    late = scatter_sum(late)
    got = xor_swap(early[0], last_bit)
    late, got = tie(late, got)
    early = run_join(my_bits(orders, last_bit), early, [got], 3)
    far_bits = list(range(near_size().bit_length() - 1, n_bits))

    def add_far(late, early):
        late, *early = tie(late, *early)
        return add_low(late, xor_swap(late, far_bits.pop(0))), early

    for step in reversed(range(1, last_bit)):
        if far_bits:
            late, early = add_far(late, early)
        got = swap_parts(early, step)
        late, *got = tie(late, *got)
        early = run_join(my_bits(orders, step), early, got, 3)
    while far_bits:
        late, early = add_far(late, early)
    late, *early = tie(late, *early)
    late = spread(jnp.broadcast_to(late[None], (near_size(), *late.shape))).reshape(-1, LANES)
    got = swap_parts(early, 0)
    swap_own = lax.ppermute(early[2], "shard", [(0, 1)])
    bits = my_bits(orders, 0)
    scale = 1.0 / nseq_all
    rate = (nseq_all / (0.6 * seq_len)) ** 0.5 / D**0.5
    state = (master, momentum, average)
    d_stream, late, swap_own, *got = tie(d_stream, late, swap_own, *got)
    back_grad = exchange(d_stream.reshape(nseq_all, block_rows, D))
    late_other = lax.ppermute(late, "shard", [(1, 0)])
    swap_got = lax.ppermute(got[2], "shard", [(0, 1)])
    halves = [early[0], got[0], early[1], got[1], early[2], got[2], swap_own, swap_got]
    done = run_update_first(scale, rate, core_arr, bits, halves[:4], state)
    weight_grad, new_momentum, new_master, new_average = run_update_second(
        scale, rate, core_arr, bits, halves, (late, late_other), state, done
    )
    return (block_output, back_grad, weight_grad, new_momentum, new_master, new_average)


def solution(mesh):
    rows = P(None, ("dp", "shard"), None)
    flat = P("shard")
    return jax.shard_map(
        on_device,
        mesh=mesh,
        in_specs=(rows, rows, P(), P(), P(), flat, flat, flat),
        out_specs=(rows, rows, flat, flat, flat, flat),
        check_vma=False,
    )
```

```python
import functools
import math

import jax
import jax.numpy as jnp
from jax import lax
from jax.experimental import pallas as pl
from jax.experimental.pallas import tpu as pltpu
from jax.sharding import PartitionSpec as P

D = 576
H = 9
KV = 3
HD = 64
FF = 1536
LANES = 128
BLOCK = 256
Q_TILES = 5
PAD_D = Q_TILES * LANES
KV_COLS = 2 * KV * HD
FF_TILES = FF // LANES
DOWN_FIRST = 4
EARLY_TILES = 21
EARLY_ROWS = 12288
EXTRA = EARLY_TILES * D
HALF = 27657 * LANES // 2
PART_ROWS = EARLY_ROWS // 3
SWAP_START = EXTRA - DOWN_FIRST * D - 2 * PART_ROWS
SWAP_TAIL = EXTRA + 16 - 2 * PART_ROWS
REST_FIRST = 2 * PART_ROWS - FF_TILES * D
REST_SLOT = REST_FIRST + 16
REST = REST_SLOT + 16
LATE_HALF = 2432
FLAT_SCRATCH = 13848
O_ROW = 4329
GATE_ROW = 6921
MLP_COLS = 256
WIDEN = 512
MLP_UNROLL = 6
MLP_BLOCK = 256
CHUNK = 576
STEP = 288
LATE_CHUNKS = 7

EPSILON = 1e-05
MOMENTUM_DECAY = 0.55
AVERAGE_DECAY = 0.45
MASKED = -1000000000.0

BF = jnp.bfloat16
F32 = jnp.float32
MIB = 1024 * 1024


def nn(a, b):
    return jnp.dot(a, b, preferred_element_type=F32)


def nt(a, b):
    return lax.dot_general(a, b, (((1,), (1,)), ((), ())), preferred_element_type=F32)


def tn(a, b):
    return lax.dot_general(a, b, (((0,), (0,)), ((), ())), preferred_element_type=F32)


def tile(value, index):
    return value[:, index * LANES : (index + 1) * LANES]


def low_half(rows):
    return lax.broadcasted_iota(jnp.int32, (rows, LANES), 1) < HD


def swap_halves(value):
    lane = lax.broadcasted_iota(jnp.int32, value.shape, 1)
    return jnp.where(lane % HD < HD // 2, pltpu.roll(value, 96, 1), pltpu.roll(value, 32, 1))


def flip(value):
    return pltpu.roll(value, HD, 1)


def rms(value):
    return lax.rsqrt(jnp.mean(value * value, axis=-1, keepdims=True) + EPSILON)


def attention_forward(
    x_ref, ga_ref, wq_ref, wkv_ref, wo_hbm, cos_ref, sin_ref,
    h1_hbm, mixed_hbm, q_hbm, k_hbm, v_hbm, lse_ref,
    h1_ref, mixed_ref, q_ref, k_ref, v_ref, wo_ref, o_acc, sem, block_sem,
):
    seq_len = x_ref.shape[0]
    low = low_half(BLOCK)

    def project(b, carry):
        rows = pl.ds(pl.multiple_of(b * BLOCK, BLOCK), BLOCK)
        stream = x_ref[rows, :].astype(F32)
        normed = (stream * rms(stream) * ga_ref[...]).astype(BF)
        cosine = cos_ref[rows, :]
        sine = sin_ref[rows, :]

        def rope(value):
            return value * cosine + swap_halves(value) * sine

        queries = nn(normed, wq_ref[...])
        for j in range(Q_TILES):
            q_ref[j, rows, :] = (rope(tile(queries, j)) * HD ** (-0.5)).astype(BF)
        keys_values = nn(normed, wkv_ref[...])
        first = rope(tile(keys_values, 0))
        second = tile(keys_values, 1)
        third = tile(keys_values, 2)
        mid = rope(second)

        def put(ref, index, value):
            ref[index, rows, :] = value.astype(BF)

        put(k_ref, 0, jnp.where(low, first, 0.0))
        put(k_ref, 1, jnp.where(low, 0.0, flip(first)))
        put(k_ref, 2, jnp.where(low, flip(first), 0.0))
        put(k_ref, 3, jnp.where(low, 0.0, first))
        put(k_ref, 4, jnp.where(low, mid, 0.0))
        put(k_ref, 5, jnp.where(low, 0.0, flip(mid)))
        put(v_ref, 0, jnp.where(low, flip(second), 0.0))
        put(v_ref, 1, jnp.where(low, 0.0, second))
        put(v_ref, 2, jnp.where(low, third, 0.0))
        put(v_ref, 3, jnp.where(low, 0.0, flip(third)))
        put(v_ref, 4, jnp.where(low, flip(third), 0.0))
        put(v_ref, 5, jnp.where(low, 0.0, third))
        return carry

    load = pltpu.make_async_copy(wo_hbm, wo_ref, sem.at[3])
    load.start()
    lax.fori_loop(0, seq_len // BLOCK, project, 0)
    stores = [
        pltpu.make_async_copy(source, target, sem.at[i])
        for i, (source, target) in enumerate(((q_ref, q_hbm), (k_ref, k_hbm), (v_ref, v_hbm)))
    ]
    for copy in stores:
        copy.start()
    lane = lax.broadcasted_iota(jnp.int32, (BLOCK, LANES), 1)
    keep = lax.broadcasted_iota(jnp.int32, (BLOCK, BLOCK), 1) <= lax.broadcasted_iota(
        jnp.int32, (BLOCK, BLOCK), 0
    )
    for b in range(seq_len // BLOCK):
        rows = slice(b * BLOCK, (b + 1) * BLOCK)
        n_keys = (b + 1) * BLOCK
        o_acc[...] = jnp.zeros_like(o_acc)

        def group(g, lse, rows=rows, n_keys=n_keys):
            for u in range(3):
                head = 3 * g + u
                j = head // 2
                side = 2 * g + head % 2
                scores = nt(q_ref[j, rows, :], k_ref[side, 0:n_keys, :])
                diag = jnp.where(keep, scores[:, n_keys - BLOCK :], MASKED)
                if n_keys > BLOCK:
                    scores = jnp.concatenate([scores[:, : n_keys - BLOCK], diag], axis=1)
                else:
                    scores = diag
                row_max = jnp.max(scores, axis=-1, keepdims=True)
                exponent = jnp.exp(scores - row_max)
                total = jnp.sum(exponent, axis=-1, keepdims=True)
                mixed = nn(exponent.astype(BF), v_ref[side, 0:n_keys, :])
                o_acc[j] += mixed * (1.0 / total)
                lse = jnp.where(lane == head, row_max + jnp.log(total), lse)
            return lse

        lse = lax.fori_loop(0, KV, group, jnp.zeros((BLOCK, LANES), F32))
        lse_ref[:, rows] = lse.T[:16]
        mixed = jnp.concatenate([o_acc[j].astype(BF) for j in range(Q_TILES)], axis=1)
        mixed_ref[rows, :] = mixed
        if b == 0:
            load.wait()
        h1_ref[rows, :] = x_ref[rows, :].astype(F32) + nn(mixed, wo_ref[...])
        for i, (source, target) in enumerate(((mixed_ref, mixed_hbm), (h1_ref, h1_hbm))):
            stores.append(
                pltpu.make_async_copy(source.at[rows], target.at[rows], block_sem.at[b, i])
            )
            stores[-1].start()
    for copy in stores:
        copy.wait()


def prepare_weights(
    core_ref, own_ref, other_ref,
    ga_ref, gm_ref, wq_ref, wkv_ref, wo_ref, wg_ref, wu_ref, wd_ref,
    first, second, flat, tmp, rest, sem,
):
    core = core_ref[0]
    for which, pair in enumerate(((first, second), (second, first))):

        @pl.when(core == which)
        def _(pair=pair):
            copies = [
                pltpu.make_async_copy(ref, target, sem.at[i])
                for i, (ref, target) in enumerate(zip((own_ref, other_ref), pair))
            ]
            for copy in copies:
                copy.start()
            for copy in copies:
                copy.wait()

    def widen(ref):
        def body(i, carry):
            start = pl.multiple_of(i * WIDEN, WIDEN)
            span = pl.ds(pl.multiple_of(i * WIDEN * LANES, WIDEN * LANES), WIDEN * LANES)
            flat[pl.ds(start, WIDEN), :] = ref[span].reshape(WIDEN, LANES)
            return carry

        whole = HALF // (WIDEN * LANES)
        lax.fori_loop(0, whole, body, 0)
        left = HALF - whole * WIDEN * LANES
        rest[pl.ds(0, left)] = ref[pl.ds(whole * WIDEN * LANES, left)]
        flat[whole * WIDEN : whole * WIDEN + 8, :] = rest[...].reshape(8, LANES)

    def low_precision(value):
        return value.astype(BF).astype(F32)

    def interleave(even, odd, pairs, out_ref, first_row, pad):
        low = low_half(2 * pairs)
        for t in range(Q_TILES):
            tmp[pl.ds(t * D, pairs, stride=2), :] = even[t]
            tmp[pl.ds(t * D + 1, pairs, stride=2), :] = odd[t]
        rows = pl.ds(first_row, 2 * pairs)
        for t in range(Q_TILES):
            value = tmp[t * D : t * D + 2 * pairs, :]
            if t < 4:
                out_ref[rows, t * LANES : (t + 1) * LANES] = value.astype(BF)
            elif pad:
                out_ref[rows, t * LANES :] = jnp.where(low, value, 0.0).astype(BF)
            else:
                out_ref[rows, t * LANES :] = value[:, :HD].astype(BF)

    def wide(row, out_ref, pad):
        pairs = D // 2
        low = low_half(pairs)
        cols = [flat[pl.ds(row + c, pairs, stride=9), :] for c in range(9)]
        turned = [flip(cols[c]) for c in range(4, 9)]
        odd = [jnp.where(low, turned[t], turned[t + 1]) for t in range(4)] + [turned[4]]
        interleave(cols[:5], odd, pairs, out_ref, 0, pad)

    widen(first)
    low1 = low_half(1)
    turned = [flip(flat[4 + r : 5 + r, :]) for r in range(5)]
    for r in range(4):
        ga_ref[:, r * LANES : (r + 1) * LANES] = low_precision(flat[r : r + 1, :])
        gm_ref[:, r * LANES : (r + 1) * LANES] = low_precision(
            jnp.where(low1, turned[r], turned[r + 1])
        )
    ga_ref[:, 4 * LANES :] = low_precision(flat[4:5, :HD])
    gm_ref[:, 4 * LANES :] = low_precision(turned[4][:, :HD])
    wide(9, wq_ref, True)
    wide(O_ROW, wo_ref, False)
    wo_ref[D:, :] = jnp.zeros((PAD_D - D, D), BF)
    pairs = D // 2
    low = low_half(pairs)
    narrow = []
    for row in (2601, 3465):
        cols = [flat[pl.ds(row + c, pairs, stride=3), :] for c in range(3)]
        turned = [flip(cols[1]), flip(cols[2])]
        even = cols[:2]
        odd = [jnp.where(low, turned[0], turned[1]), turned[1]]
        for t in range(2):
            tmp[pl.ds(t * D, pairs, stride=2), :] = even[t]
            tmp[pl.ds(t * D + 1, pairs, stride=2), :] = odd[t]
        narrow.append((tmp[0:D, :], tmp[D : 2 * D, :]))
    (k0, k1), (v0, v1) = narrow
    low = low_half(D)
    v0 = flip(v0)
    v1 = flip(v1)
    wkv_ref[:, 0:LANES] = k0.astype(BF)
    wkv_ref[:, LANES : 2 * LANES] = jnp.where(low, k1, v0).astype(BF)
    wkv_ref[:, 2 * LANES :] = jnp.where(low, v0, v1).astype(BF)
    head = second[pl.ds(0, 1024)].reshape(8, LANES)
    turned = flip(head)
    for r in range(5):
        row = GATE_ROW + FF_TILES * (D - 1) + 7 + r
        before = flat[row : row + 1, :] if r == 0 else turned[r - 1 : r]
        flat[row : row + 1, :] = jnp.where(low1, before, turned[r : r + 1])
    for t in range(FF_TILES):
        wg_ref[:, t * LANES : (t + 1) * LANES] = flat[
            pl.ds(GATE_ROW + t, D, stride=FF_TILES), :
        ].astype(BF)
    widen(second)
    here = flip(flat[pl.ds(4, D, stride=FF_TILES), :])
    for t in range(FF_TILES):
        after = flip(flat[pl.ds(5 + t, D, stride=FF_TILES), :])
        wu_ref[:, t * LANES : (t + 1) * LANES] = jnp.where(low, here, after).astype(BF)
        here = after

    def down(i, carry):
        n_pairs = 96
        low = low_half(n_pairs)
        start = 6916 + 9 * n_pairs * i
        cols = [flat[pl.ds(start + c, n_pairs, stride=9), :] for c in range(10)]
        turned = [flip(cols[c]) for c in range(6)]
        even = [jnp.where(low, turned[c], turned[c + 1]) for c in range(5)]
        interleave(even, cols[5:], n_pairs, wd_ref, pl.multiple_of(2 * n_pairs * i, 16), False)
        return carry

    lax.fori_loop(0, FF // 192, down, 0)


def transposed(value):
    rows = value.shape[0]
    pieces = [tile(value, t) for t in range(4)]
    pieces.append(
        jnp.concatenate([value[:, 4 * LANES :], jnp.zeros((rows, LANES - HD), F32)], axis=1)
    )
    return jnp.concatenate([piece.T for piece in pieces], axis=0)


def mlp_pass(
    core_ref, slot_ref, lengths_ref, assignment_ref, return_ref,
    h1_hbm, cot_hbm, mixed_hbm, gm_ref, wo_hbm, wg_hbm, wu_hbm, wd_hbm,
    out_hbm, dh1_hbm, dm_hbm, ggm_ref, keep_ref, send_ref,
    h1_ref, cot_ref, mixed_ref, wo_ref, wg_ref, wu_ref, wd_ref, out_ref, dh1_ref, dm_ref,
    nmt_s, backt_s, inner_s, dg_s, du_s, da_s, grads, in_sem, out_sem, sem,
):
    seq_len = h1_ref.shape[0]
    core = core_ref[0]
    live_len = lengths_ref[assignment_ref[return_ref[slot_ref[0]]]]
    n_cols = FF // MLP_COLS
    loads = [
        pltpu.make_async_copy(source, target, in_sem.at[i])
        for i, (source, target) in enumerate(
            (
                (h1_hbm, h1_ref),
                (cot_hbm, cot_ref),
                (wg_hbm, wg_ref),
                (wu_hbm, wu_ref),
                (wd_hbm, wd_ref),
                (wo_hbm, wo_ref),
                (mixed_hbm, mixed_ref),
            )
        )
    ]
    for copy in loads:
        copy.start()
    for copy in loads[:6]:
        copy.wait()

    def results(b):
        rows = pl.ds(pl.multiple_of(b * MLP_BLOCK, MLP_BLOCK), MLP_BLOCK)
        pairs = [(out_ref.at[rows], out_hbm.at[rows]), (dh1_ref.at[rows], dh1_hbm.at[rows])]
        pairs.append((dm_ref.at[:, rows], dm_hbm.at[:, rows]))
        return [
            pltpu.make_async_copy(source, target, out_sem.at[b, i])
            for i, (source, target) in enumerate(pairs)
        ]

    def block(b, ggm):
        start = pl.multiple_of(b * MLP_BLOCK, MLP_BLOCK)
        rows = pl.ds(start, MLP_BLOCK)
        hidden1 = h1_ref[rows, :]
        r2 = rms(hidden1)
        gain = gm_ref[...]
        normed2_wide = hidden1 * r2 * gain
        normed2 = normed2_wide.astype(BF)
        nmt_s[:, rows] = transposed(normed2_wide).astype(BF)
        live = (
            start + lax.broadcasted_iota(jnp.int32, (MLP_BLOCK, 1), 0) < live_len
        ).astype(F32)

        back = cot_ref[rows, :].astype(F32) * live
        back_low = back.astype(BF)
        backt_s[:, rows] = transposed(back).astype(BF)
        def columns(c):
            cols = pl.ds(pl.multiple_of(c * MLP_COLS, MLP_COLS), MLP_COLS)
            gate = nn(normed2, wg_ref[:, cols])
            up = nn(normed2, wu_ref[:, cols])
            d_inner = nt(back_low, wd_ref[cols, :])
            sig = jax.nn.sigmoid(gate)
            silu = gate * sig
            inner_s[rows, cols] = (silu * up).astype(BF)
            dg_s[rows, cols] = (d_inner * up * sig * (1.0 + gate * (1.0 - sig))).astype(BF)
            du_s[rows, cols] = (d_inner * silu).astype(BF)

        def some_columns(i, carry):
            for c in range(MLP_UNROLL):
                columns(MLP_UNROLL * i + c)
            return carry

        lax.fori_loop(0, n_cols // MLP_UNROLL, some_columns, 0)
        out_ref[rows, :] = ((hidden1 + nn(inner_s[rows, :], wd_ref[...])) * live).astype(BF)
        d_normed2 = nt(dg_s[rows, :], wg_ref[...]) + nt(du_s[rows, :], wu_ref[...])
        scaled = d_normed2 * gain
        d_hidden1 = (
            back
            + r2 * scaled
            - hidden1 * (r2 * r2 * r2) * jnp.mean(scaled * hidden1, axis=-1, keepdims=True)
        )
        dh1_ref[rows, :] = d_hidden1
        d_attn = d_hidden1.astype(BF)
        da_s[rows, :] = d_attn

        d_mixed = nt(d_attn, wo_ref[...]).astype(BF)
        for j in range(Q_TILES):
            dm_ref[j, rows, :] = tile(d_mixed, j)
        for copy in results(b):
            copy.start()
        return ggm + jnp.sum(d_normed2 * hidden1 * r2, axis=0, keepdims=True)

    ggm_ref[...] = lax.fori_loop(0, seq_len // MLP_BLOCK, block, jnp.zeros((1, D), F32))

    def put(half, index, value):
        grads[half, pl.ds(pl.multiple_of(index * D, D), D), :] = value

    def leave(c):
        rows = pl.ds(pl.multiple_of(2 * c * D, D), 2 * D)
        return [
            pltpu.make_async_copy(grads.at[1 - core, rows], send_ref.at[rows], sem.at[c, 0]),
            pltpu.make_async_copy(grads.at[core, rows], keep_ref.at[rows], sem.at[c, 1]),
        ]

    def weights(c, carry):
        cols = pl.ds(pl.multiple_of(c * 2 * LANES, 2 * LANES), 2 * LANES)
        grad_gate = nn(nmt_s[:D, :], dg_s[:, cols]).astype(BF)
        grad_up = nn(nmt_s[:D, :], du_s[:, cols]).astype(BF)
        for t in range(2):
            put(0, 2 * c + t, tile(grad_gate, t))
            put(1, 2 * c + t, tile(grad_up, t))
        for copy in leave(c):
            copy.start()
        grad_down = nn(backt_s[:D, :], inner_s[:, cols]).astype(BF)
        part = jnp.where(c < DOWN_FIRST // 2, 0, 1)
        base = jnp.where(c < DOWN_FIRST // 2, FF_TILES + Q_TILES, FF_TILES - DOWN_FIRST)
        for t in range(2):
            put(part, base + 2 * c + t, tile(grad_down, t))
        return carry

    lax.fori_loop(0, n_cols, weights, 0)
    loads[6].wait()
    grad_o = tn(mixed_ref[...], da_s[...])[:D]
    for t in range(4):
        put(0, FF_TILES + t, tile(grad_o, t).astype(BF))
    put(0, FF_TILES + 4, half_tile(grad_o).astype(BF))
    grads[0, EXTRA:, :] = jnp.zeros((EARLY_ROWS - EXTRA, LANES), BF)
    grads[1, EXTRA - D :, :] = jnp.zeros((EARLY_ROWS - EXTRA + D, LANES), BF)
    row = lax.broadcasted_iota(jnp.int32, (16, LANES), 0)
    rest = jnp.zeros((16, LANES), F32)
    for r in range(5):
        start = (8 + r) * D - 16
        last = grads[0, start : start + 16, :].astype(F32)[15:16]
        rest = jnp.where(row == r, jnp.broadcast_to(last, (16, LANES)), rest)
    grads[0, EXTRA + 16 : EXTRA + 32, :] = rest.astype(BF)
    rows = pl.ds(FF_TILES * D, EARLY_ROWS - FF_TILES * D)
    final = [
        pltpu.make_async_copy(grads.at[1 - core, rows], send_ref.at[rows], sem.at[n_cols, 0]),
        pltpu.make_async_copy(grads.at[core, rows], keep_ref.at[rows], sem.at[n_cols, 1]),
    ]
    for copy in final:
        copy.start()

    def drain(c, carry):
        for copy in leave(c):
            copy.wait()
        return carry

    def drain_results(b, carry):
        for copy in results(b):
            copy.wait()
        return carry

    lax.fori_loop(0, n_cols, drain, 0)
    lax.fori_loop(0, seq_len // MLP_BLOCK, drain_results, 0)
    for copy in final:
        copy.wait()


def half_tile(value):
    rows = value.shape[0]
    return jnp.concatenate([value[:, 4 * LANES : D], jnp.zeros((rows, HD), value.dtype)], axis=1)


def gain_rows(value):
    row = lax.broadcasted_iota(jnp.int32, (16, LANES), 0)
    whole = jnp.zeros((16, LANES), F32)
    for t in range(Q_TILES):
        piece = tile(value, t) if t < 4 else half_tile(value)
        whole = jnp.where(row == t, jnp.broadcast_to(piece, (16, LANES)), whole)
    return whole


def backward_groups(
    first, q_ref, dm_ref, k_ref, v_ref, lse_ref, dq_ref, dk_ref, dv_ref, dk_acc, dv_acc
):
    seq_len = q_ref.shape[1]
    group = first + pl.program_id(0)
    dq_ref[...] = jnp.zeros_like(dq_ref)
    dk_acc[...] = jnp.zeros_like(dk_acc)
    dv_acc[...] = jnp.zeros_like(dv_acc)
    keep = lax.broadcasted_iota(jnp.int32, (BLOCK, BLOCK), 0) <= lax.broadcasted_iota(
        jnp.int32, (BLOCK, BLOCK), 1
    )
    for b in range(seq_len // BLOCK):
        rows = slice(b * BLOCK, (b + 1) * BLOCK)
        n_keys = (b + 1) * BLOCK
        for u in range(3):
            head = 3 * group + u
            j = lax.shift_right_logical(head, 1)
            own = j - lax.shift_right_logical(3 * group, 1)
            side = head - 2 * j
            queries = q_ref[j, rows, :]
            d_mixed = dm_ref[j, rows, :]
            keys = k_ref[side, 0:n_keys, :]
            values = v_ref[side, 0:n_keys, :]
            prob = jnp.exp(nt(keys, queries) - lse_ref[pl.ds(head, 1), rows])
            diag = jnp.where(keep, prob[n_keys - BLOCK :, :], 0.0)
            if n_keys > BLOCK:
                prob = jnp.concatenate([prob[: n_keys - BLOCK, :], diag], axis=0)
            else:
                prob = diag
            d_prob = nt(values, d_mixed)
            delta = jnp.sum(d_prob * prob, axis=0, keepdims=True)
            d_score = (prob * (d_prob - delta)).astype(BF)
            dv_acc[side, 0:n_keys, :] += nn(prob.astype(BF), d_mixed)
            dk_acc[side, 0:n_keys, :] += nn(d_score, queries)
            dq_ref[0, own, rows, :] += tn(d_score, keys)
    dk_ref[0] = dk_acc[0] + flip(dk_acc[1])
    dv_ref[0] = dv_acc[0] + flip(dv_acc[1])


def backward_finish(
    x_ref, ga_ref, dh1_ref, dqa_ref, dka_ref, dva_ref, dqb_ref, dkb_ref, dvb_ref,
    wq_ref, wkv_ref, cos_ref, sin_ref,
    dx_ref, dq_s, dkv_s, nm_s, gga_ref,
):
    seq_len = x_ref.shape[0]
    low = low_half(BLOCK)

    def block(b, gga):
        rows = pl.ds(pl.multiple_of(b * BLOCK, BLOCK), BLOCK)
        cosine = cos_ref[rows, :]
        sine = sin_ref[rows, :]

        def unrope(value):
            return value * cosine - swap_halves(value) * sine

        d_rot = [
            dqa_ref[0, 0, rows, :],
            dqa_ref[0, 1, rows, :] + dqb_ref[0, 0, rows, :],
            dqb_ref[0, 1, rows, :],
            dqb_ref[1, 0, rows, :],
            dqb_ref[1, 1, rows, :],
        ]
        for j in range(Q_TILES):
            d_query = unrope(d_rot[j]) * HD ** (-0.5)
            dq_s[rows, j * LANES : (j + 1) * LANES] = d_query.astype(BF)
        dk = [dka_ref[0, rows, :], dkb_ref[0, rows, :], dkb_ref[1, rows, :]]
        dv = [dva_ref[0, rows, :], dvb_ref[0, rows, :], dvb_ref[1, rows, :]]
        first = unrope(jnp.where(low, dk[0], flip(dk[1])))
        second = jnp.where(low, unrope(dk[2]), flip(dv[0]))
        third = jnp.where(low, dv[1], flip(dv[2]))
        dkv_s[rows, 0:LANES] = first.astype(BF)
        dkv_s[rows, LANES : 2 * LANES] = second.astype(BF)
        dkv_s[rows, 2 * LANES :] = third.astype(BF)
        d_normed = nt(dq_s[rows, :], wq_ref[...]) + nt(dkv_s[rows, :], wkv_ref[...])
        stream = x_ref[rows, :].astype(F32)
        r1 = rms(stream)
        gain = ga_ref[...]
        nm_s[rows, :] = (stream * r1 * gain).astype(BF)
        scaled = d_normed * gain
        dx_ref[rows, :] = (
            dh1_ref[rows, :]
            + r1 * scaled
            - stream * (r1 * r1 * r1) * jnp.mean(scaled * stream, axis=-1, keepdims=True)
        ).astype(BF)
        return gga + jnp.sum(d_normed * stream * r1, axis=0, keepdims=True)

    gga_ref[...] = lax.fori_loop(0, seq_len // BLOCK, block, jnp.zeros((1, D), F32))


def late_weights(
    core_ref, nm_s, dq_s, dkv_s, gga_ref, ggm_ref, keep_ref, send_ref, late, sem
):
    grad_q = tn(nm_s[...], dq_s[...]).astype(BF)
    grad_kv = tn(nm_s[...], dkv_s[...]).astype(BF)
    for t in range(Q_TILES):
        late[t * D : (t + 1) * D, :] = tile(grad_q, t)
    for t in range(3):
        late[(Q_TILES + t) * D : (Q_TILES + t + 1) * D, :] = tile(grad_kv, t)
    late[8 * D :, :] = jnp.zeros((2 * LATE_HALF - 8 * D, LANES), BF)
    late[8 * D : 8 * D + 16, :] = gain_rows(gga_ref[...]).astype(BF)
    late[8 * D + 16 : 8 * D + 32, :] = gain_rows(ggm_ref[...]).astype(BF)
    copies = []
    for i, (which, ref) in enumerate(((1 - core_ref[0], send_ref), (core_ref[0], keep_ref))):
        rows = pl.ds(pl.multiple_of(which * LATE_HALF, 8), LATE_HALF)
        copies.append(pltpu.make_async_copy(late.at[rows], ref, sem.at[i]))
    for copy in copies:
        copy.start()
    for copy in copies:
        copy.wait()


def gather_sum(bits_ref, *refs, n_parts, rows, split, merge, joined):
    n_in = 1 if joined else n_parts
    kept, got = refs[:n_in], refs[n_in : 2 * n_in]
    kinds = 2 if split else 1
    n_out = kinds * (1 if merge else n_parts)
    outs = refs[2 * n_in : 2 * n_in + n_out]
    scratch, sem = refs[2 * n_in + n_out :]
    size = rows // kinds
    copies = []
    for p in range(n_parts):
        if joined:
            part = slice(p * rows, (p + 1) * rows)
            total = kept[0][part, :].astype(F32) + got[0][part, :].astype(F32)
        else:
            total = kept[p][...].astype(F32) + got[p][...].astype(F32)
        scratch[p] = total.astype(BF)
        for i in range(kinds):
            if merge:
                target = outs[i].at[pl.ds(p * size, size)]
            else:
                target = outs[p + i * n_parts]
            start = (bits_ref[p] if i else 1 - bits_ref[p]) * size if split else 0
            source = scratch.at[p, pl.ds(pl.multiple_of(start, 8), size)]
            copies.append(pltpu.make_async_copy(source, target, sem.at[2 * p + i]))
            copies[-1].start()
    for copy in copies:
        copy.wait()


def join_halves(bits_ref, *refs, n_parts, rows, merged):
    n_in = 1 if merged else n_parts
    own, got, outs = refs[:n_in], refs[n_in : 2 * n_in], refs[2 * n_in : 2 * n_in + n_parts]
    sem = refs[2 * n_in + n_parts]
    copies = []
    for p in range(n_parts):
        for i, (group, which) in enumerate(((own, bits_ref[p]), (got, 1 - bits_ref[p]))):
            source = group[0].at[pl.ds(p * rows, rows)] if merged else group[p]
            span = pl.ds(pl.multiple_of(which * rows, 8), rows)
            copies.append(pltpu.make_async_copy(source, outs[p].at[span], sem.at[2 * p + i]))
            copies[-1].start()
    for copy in copies:
        copy.wait()


def put_wide(flat, tmp, values, rows, row):
    pairs = rows // 2
    for index, value in enumerate(values):
        tmp[pl.ds(index * D, rows), :] = value
    even = [tmp[pl.ds(i * D, pairs, stride=2), :] for i in range(Q_TILES)]
    odd = [flip(tmp[pl.ds(i * D + 1, pairs, stride=2), :]) for i in range(Q_TILES)]
    low = low_half(pairs)
    for c in range(4):
        flat[pl.ds(row + c, pairs, stride=9), :] = even[c]
    flat[pl.ds(row + 4, pairs, stride=9), :] = jnp.where(low, even[4], odd[0])
    for c in range(4):
        flat[pl.ds(row + 5 + c, pairs, stride=9), :] = jnp.where(low, odd[c], odd[c + 1])


def copy_array(source_ref, target_ref, sem):
    copy = pltpu.make_async_copy(source_ref, target_ref, sem)
    copy.start()
    copy.wait()


def update_rule(scale, rate, grad, master, momentum, average):
    weight_grad = grad * scale
    new_momentum = MOMENTUM_DECAY * momentum + weight_grad
    new_master = master - rate * (weight_grad + MOMENTUM_DECAY * new_momentum)
    new_average = AVERAGE_DECAY * average + (1.0 - AVERAGE_DECAY) * new_master
    return weight_grad, new_momentum, new_master, new_average


class Chunks:
    def __init__(self, rows, base, count, rule, refs):
        self.rows, self.base, self.count, self.rule = rows, base, count, rule
        self.ins, self.outs, self.in_buf, self.out_buf, self.in_sem, self.out_sem = refs
        self.size = rows * LANES

    def span(self, c):
        return pl.ds(pl.multiple_of((self.base + c * self.rows) * LANES, LANES), self.size)

    def place(self, index, start=0, length=None):
        start = pl.multiple_of(index * self.size + start, 8 * LANES)
        return pl.ds(start, self.size if length is None else length)

    def fetch(self, c):
        return [
            pltpu.make_async_copy(
                self.ins[i].at[self.span(c)],
                self.in_buf.at[self.place(c * 3 + i)],
                self.in_sem.at[c, i],
            )
            for i in range(3)
        ]

    def flush(self, c):
        return [
            pltpu.make_async_copy(
                self.out_buf.at[self.place(c * 4 + i)],
                self.outs[i].at[self.span(c)],
                self.out_sem.at[c, i],
            )
            for i in range(4)
        ]

    def start(self):
        def body(c, carry):
            for copy in self.fetch(c):
                copy.start()
            return carry

        lax.fori_loop(0, self.count, body, 0)

    def run(self, stage, gradient):
        sub = STEP * LANES

        def body(c, carry):
            stage(c)
            for copy in self.fetch(c):
                copy.wait()

            def step(s, inner):
                grad = gradient(c, s * STEP, STEP).reshape(sub)
                values = self.rule(
                    grad, *[self.in_buf[self.place(c * 3 + i, s * sub, sub)] for i in range(3)]
                )
                for i in range(4):
                    self.out_buf[self.place(c * 4 + i, s * sub, sub)] = values[i]
                return inner

            lax.fori_loop(0, self.rows // STEP, step, 0)
            for copy in self.flush(c):
                copy.start()
            return carry

        def drain(c, carry):
            for copy in self.flush(c):
                copy.wait()
            return carry

        lax.fori_loop(0, self.count, body, 0)
        return lambda: lax.fori_loop(0, self.count, drain, 0)


class Extra:
    def __init__(self, start, ins, outs, rest):
        self.bufs, self.sem = rest[:8], rest[8]
        count = self.bufs[0].shape[0]
        span = pl.ds(start, count)
        self.count = count
        self.loads = [
            pltpu.make_async_copy(ins[i].at[span], self.bufs[i], self.sem.at[i]) for i in range(3)
        ]
        self.stores = [
            pltpu.make_async_copy(self.bufs[3 + i], outs[i].at[span], self.sem.at[3 + i])
            for i in range(4)
        ]

    def start(self):
        for copy in self.loads:
            copy.start()

    def finish(self, grad, rule):
        for copy in self.loads:
            copy.wait()
        self.bufs[7][...] = grad.reshape(grad.shape[0] * LANES)
        values = rule(self.bufs[7][pl.ds(0, self.count)], *[self.bufs[i][...] for i in range(3)])
        for i in range(4):
            self.bufs[3 + i][...] = values[i]
            self.stores[i].start()

    def drain(self):
        for copy in self.stores:
            copy.wait()


def shifted(flat, row, count):
    here = flip(flat[pl.ds(row - 1, count), :])
    after = flip(flat[pl.ds(row, count), :])
    return jnp.where(low_half(count), here, after)


def load_parts(pieces, sem):
    copies = [
        pltpu.make_async_copy(source, target, sem.at[i]) for i, (source, target) in enumerate(pieces)
    ]
    for copy in copies:
        copy.start()
    return copies


FLAT_BASE = 8
TAIL_ZERO = HALF - (GATE_ROW + 11 * CHUNK) * LANES
TAIL_ONE = HALF - (6916 + 11 * CHUNK) * LANES


def update_first(scale, rate, core_ref, bits_ref, *rest):
    halves, ins, outs = rest[:4], rest[4:7], rest[7:11]
    early_ref, flat, in_buf, out_buf, in_sem, out_sem, part_sem = rest[11:18]
    refs = (ins, outs, in_buf, out_buf, in_sem, out_sem)
    core = core_ref[0]
    rule = functools.partial(update_rule, scale, rate)
    half = PART_ROWS // 2
    pieces = []
    for p in range(2):
        for i, which in enumerate((bits_ref[p], 1 - bits_ref[p])):
            span = pl.ds(pl.multiple_of(p * PART_ROWS + which * half, 8), half)
            pieces.append((halves[2 * p + i], early_ref.at[span]))
    copies = load_parts(pieces, part_sem)
    extra = Extra((GATE_ROW + 11 * CHUNK) * LANES, ins, outs, rest[18:])
    base = jnp.where(core == 0, GATE_ROW, 4)
    chunks = Chunks(CHUNK, base, 11 + core, rule, refs)
    chunks.start()

    @pl.when(core == 0)
    def _():
        extra.start()

    for copy in copies:
        copy.wait()
    flat[0:FLAT_BASE, :] = jnp.zeros((FLAT_BASE, LANES), F32)

    def stage(c):
        for t in range(FF_TILES):
            rows = pl.ds(pl.multiple_of(t * D + c * 48, 16), 48)
            flat[pl.ds(FLAT_BASE + t, 48, stride=FF_TILES), :] = early_ref[rows, :].astype(F32)

    def gradient(c, start, count):
        row = pl.multiple_of(FLAT_BASE + start, 8)
        return jnp.where(core == 0, flat[pl.ds(row, count), :], shifted(flat, row, count))

    def stage_next(c):
        flat[FLAT_BASE - 1 : FLAT_BASE, :] = flat[FLAT_BASE + CHUNK - 1 : FLAT_BASE + CHUNK, :]
        stage(c)

    drain = chunks.run(stage_next, gradient)

    @pl.when(core == 0)
    def _():
        stage(11)
        extra.finish(flat[FLAT_BASE : FLAT_BASE + CHUNK, :], rule)

    drain()

    @pl.when(core == 0)
    def _():
        extra.drain()


def lay_out_late(flat, tmp, late_ref):
    def late(index):
        return late_ref[index * D : (index + 1) * D, :].astype(F32)

    low1 = low_half(1)
    gain_a = late_ref[8 * D : 8 * D + 16, :].astype(F32)
    gain_m = flip(late_ref[8 * D + 16 : 8 * D + 32, :].astype(F32))
    for r in range(4):
        flat[r : r + 1, :] = gain_a[r : r + 1]
    flat[4:5, :] = jnp.where(low1, gain_a[4:5], gain_m[0:1])
    for r in range(4):
        flat[5 + r : 6 + r, :] = jnp.where(low1, gain_m[r : r + 1], gain_m[r + 1 : r + 2])
    put_wide(flat, tmp, [late(t) for t in range(Q_TILES)], D, 9)
    pairs = D // 2
    for t in range(3):
        tmp[pl.ds(t * D, D), :] = late(Q_TILES + t)
    even = [tmp[pl.ds(i * D, pairs, stride=2), :] for i in range(3)]
    odd = [tmp[pl.ds(i * D + 1, pairs, stride=2), :] for i in range(3)]
    low = low_half(pairs)
    turned = [flip(odd[0]), flip(odd[1]), flip(even[1]), flip(even[2])]
    rows = (
        (2601, even[0]),
        (2602, jnp.where(low, even[1], turned[0])),
        (2603, jnp.where(low, turned[0], turned[1])),
        (3465, jnp.where(low, turned[2], turned[3])),
        (3466, jnp.where(low, turned[3], odd[1])),
        (3467, odd[2]),
    )
    for row, value in rows:
        flat[pl.ds(row, pairs, stride=3), :] = value


def update_second(scale, rate, core_ref, bits_ref, *rest):
    halves, late_halves, ins, outs = rest[:8], rest[8:10], rest[10:13], rest[17:21]
    flat, tmp, part_ref, swap_ref, first_ref, in_buf, out_buf, in_sem, out_sem, part_sem = rest[21:31]
    refs = (ins, outs, in_buf, out_buf, in_sem, out_sem)
    tail = Extra((6916 + 11 * CHUNK) * LANES, ins, outs, rest[31:40])
    head = Extra(0, ins, outs, rest[40:49])
    late_flat, late_ref, late_in, late_out, late_in_sem, late_out_sem, late_sem = rest[49:56]
    late_last = Extra(LATE_CHUNKS * CHUNK * LANES, ins, outs, rest[56:])
    rule = functools.partial(update_rule, scale, rate)
    half = PART_ROWS // 2
    pieces = []
    for i in range(2):
        which = [1 - bits_ref[p] if i else bits_ref[p] for p in range(3)]

        def rows(start, p, size, which=which):
            return pl.ds(pl.multiple_of(start + which[p] * size, 16), size)

        source = halves[2 + i].at[pl.ds(half - REST_SLOT, REST_SLOT)]
        pieces.append((source, part_ref.at[rows(0, 1, REST_SLOT)]))
        pieces.append((halves[4 + i], part_ref.at[rows(2 * REST_SLOT, 2, half)]))
        pieces.append((halves[6 + i], swap_ref.at[rows(0, 2, half)]))
        pieces.append((halves[i].at[pl.ds(0, 16)], first_ref.at[rows(0, 0, 16)]))
    parts = load_parts(pieces, part_sem)

    @pl.when(core_ref[0] == 0)
    def _():
        def stage(c):
            values = []
            for t in range(Q_TILES):
                rows = pl.ds(pl.multiple_of(REST + t * D + c * 64, 16), 64)
                values.append(part_ref[rows, :].astype(F32))
            put_wide(flat, tmp, values, 64, FLAT_BASE)

        def gradient(c, start, count):
            return flat[pl.ds(pl.multiple_of(FLAT_BASE + start, 8), count), :]

        chunks = Chunks(CHUNK // 2, O_ROW, 9, rule, refs)
        late_refs = (ins, outs, late_in, late_out, late_in_sem, late_out_sem)
        late_chunks = Chunks(CHUNK, 0, LATE_CHUNKS, rule, late_refs)
        pieces = [
            (ref, late_ref.at[pl.ds(i * LATE_HALF, LATE_HALF)]) for i, ref in enumerate(late_halves)
        ]
        chunks.start()
        late_parts = load_parts(pieces, late_sem)
        late_chunks.start()
        late_last.start()
        for copy in parts:
            copy.wait()
        drain = chunks.run(stage, gradient)
        for copy in late_parts:
            copy.wait()
        lay_out_late(late_flat, tmp, late_ref)

        def late_gradient(c, start, count):
            return late_flat[pl.ds(pl.multiple_of(c * CHUNK + start, 8), count), :]

        late_drain = late_chunks.run(lambda c: None, late_gradient)
        start = LATE_CHUNKS * CHUNK
        late_last.finish(late_flat[start : start + 304, :], rule)
        drain()
        late_drain()
        late_last.drain()

    @pl.when(core_ref[0] == 1)
    def _():
        head.start()
        chunks = Chunks(CHUNK, 6916, 11, rule, refs)
        chunks.start()
        tail.start()
        for copy in parts:
            copy.wait()
        flat[0:FLAT_BASE, :] = jnp.zeros((FLAT_BASE, LANES), F32)
        flat[FLAT_BASE : FLAT_BASE + 8, :] = swap_ref[SWAP_TAIL : SWAP_TAIL + 16, :].astype(F32)[0:8]
        flat[FLAT_BASE + 5 : FLAT_BASE + 6, :] = first_ref[0:16, :].astype(F32)[0:1]
        head.finish(shifted(flat, FLAT_BASE + 1, 8), rule)
        row = FLAT_BASE + CHUNK - 1
        flat[row : row + 1, :] = part_ref[REST - 16 : REST, :].astype(F32)[15:16]

        def stage(c):
            flat[FLAT_BASE - 1 : FLAT_BASE, :] = flat[FLAT_BASE + CHUNK - 1 : FLAT_BASE + CHUNK, :]
            inside = c < DOWN_FIRST
            here = pl.ds(pl.multiple_of(SWAP_START + jnp.where(inside, c, 0) * D, 16), D)
            there = pl.ds(pl.multiple_of(REST + jnp.where(inside, 0, c - DOWN_FIRST) * D, 16), D)
            whole = jnp.where(inside, swap_ref[here, :].astype(F32), part_ref[there, :].astype(F32))
            pieces = [whole[i * LANES : (i + 1) * LANES].T for i in range(4)]
            half = jnp.concatenate([whole[4 * LANES :], jnp.zeros((LANES - HD, LANES), F32)], axis=0)
            put_wide(flat, tmp, pieces + [half.T], LANES, FLAT_BASE)

        def gradient(c, start, count):
            return shifted(flat, FLAT_BASE + start, count)

        drain = chunks.run(stage, gradient)
        stage(11)
        flat[FLAT_BASE + CHUNK :, :] = jnp.zeros((8, LANES), F32)
        tail.finish(shifted(flat, FLAT_BASE, CHUNK + 8), rule)
        head.drain()
        drain()
        tail.drain()


def vmem():
    return pl.BlockSpec(memory_space=pltpu.VMEM)


def smem():
    return pl.BlockSpec(memory_space=pltpu.SMEM)


def hbm():
    return pl.BlockSpec(memory_space=pl.ANY)


def call(kernel, outs, in_specs, out_specs, scratch, flops, name, limit, aliases=None):
    n_bytes = sum(math.prod(shape) * jnp.dtype(kind).itemsize for shape, kind in outs)
    return pl.pallas_call(
        kernel,
        out_shape=[jax.ShapeDtypeStruct(shape, kind) for shape, kind in outs],
        in_specs=in_specs,
        out_specs=out_specs,
        scratch_shapes=scratch,
        input_output_aliases=aliases or {},
        compiler_params=pltpu.CompilerParams(vmem_limit_bytes=limit * MIB),
        cost_estimate=pl.CostEstimate(
            flops=int(flops), bytes_accessed=int(2 * n_bytes), transcendentals=0
        ),
        name=name,
    )


def rope_tables(seq_len):
    lane = jnp.arange(LANES, dtype=jnp.int32)
    which = (lane % (HD // 2)).astype(F32)
    frequency = jnp.exp(which * (-2.0 * math.log(10000.0) / HD))
    angles = jnp.arange(seq_len, dtype=F32)[:, None] * frequency[None, :]
    sign = jnp.where(lane % HD < HD // 2, -1.0, 1.0)
    return jnp.cos(angles), jnp.sin(angles) * sign[None, :]


def run_prepare(core, own, other):
    outs = [
        ((1, D), F32),
        ((1, D), F32),
        ((D, PAD_D), BF),
        ((D, KV_COLS), BF),
        ((PAD_D, D), BF),
        ((D, FF), BF),
        ((D, FF), BF),
        ((FF, D), BF),
    ]
    scratch = [
        pltpu.VMEM((HALF,), F32),
        pltpu.VMEM((HALF,), F32),
        pltpu.VMEM((FLAT_SCRATCH, LANES), F32),
        pltpu.VMEM((Q_TILES * D + 8, LANES), F32),
        pltpu.VMEM((8 * LANES,), F32),
        pltpu.SemaphoreType.DMA((2,)),
    ]
    return call(
        prepare_weights,
        outs,
        [smem()] + [hbm()] * 2,
        [vmem()] * 8,
        scratch,
        1e10,
        "prepare_weights",
        56,
    )(core, own, other)


def run_attention_forward(x, gain, wq, wkv, wo, cosine, sine):
    seq_len = x.shape[0]
    outs = [
        ((seq_len, D), F32),
        ((seq_len, PAD_D), BF),
        ((Q_TILES, seq_len, LANES), BF),
        ((6, seq_len, LANES), BF),
        ((6, seq_len, LANES), BF),
        ((16, seq_len), F32),
    ]
    return call(
        attention_forward,
        outs,
        [vmem()] * 4 + [hbm()] + [vmem()] * 2,
        [hbm()] * 5 + [vmem()],
        [pltpu.VMEM(shape, kind) for shape, kind in outs[:5]]
        + [
            pltpu.VMEM((PAD_D, D), BF),
            pltpu.VMEM((Q_TILES, BLOCK, LANES), F32),
            pltpu.SemaphoreType.DMA((4,)),
            pltpu.SemaphoreType.DMA((seq_len // BLOCK, 2)),
        ],
        1.5e10,
        "attention_forward",
        56,
    )(x, gain, wq, wkv, wo, cosine, sine)


def run_mlp(core, slot, lengths, assignment, return_order, hidden1, cot, mixed, gain, wo, wg, wu, wd):
    seq_len = hidden1.shape[0]
    outs = [
        ((seq_len, D), BF),
        ((seq_len, D), F32),
        ((Q_TILES, seq_len, LANES), BF),
        ((1, D), F32),
        ((EARLY_ROWS, LANES), BF),
        ((EARLY_ROWS, LANES), BF),
    ]
    return call(
        mlp_pass,
        outs,
        [smem()] * 5 + [hbm()] * 3 + [vmem()] + [hbm()] * 4,
        [hbm()] * 3 + [vmem()] + [hbm()] * 2,
        [
            pltpu.VMEM((seq_len, D), F32),
            pltpu.VMEM((seq_len, D), BF),
            pltpu.VMEM((seq_len, PAD_D), BF),
            pltpu.VMEM((PAD_D, D), BF),
            pltpu.VMEM((D, FF), BF),
            pltpu.VMEM((D, FF), BF),
            pltpu.VMEM((FF, D), BF),
            pltpu.VMEM((seq_len, D), BF),
            pltpu.VMEM((seq_len, D), F32),
            pltpu.VMEM((Q_TILES, seq_len, LANES), BF),
            pltpu.VMEM((PAD_D, seq_len), BF),
            pltpu.VMEM((PAD_D, seq_len), BF),
            pltpu.VMEM((seq_len, FF), BF),
            pltpu.VMEM((seq_len, FF), BF),
            pltpu.VMEM((seq_len, FF), BF),
            pltpu.VMEM((seq_len, D), BF),
            pltpu.VMEM((2, EARLY_ROWS, LANES), BF),
            pltpu.SemaphoreType.DMA((7,)),
            pltpu.SemaphoreType.DMA((seq_len // MLP_BLOCK, 3)),
            pltpu.SemaphoreType.DMA((FF_TILES // 2 + 1, 2)),
        ],
        2.5e10,
        "mlp_pass",
        56,
    )(core, slot, lengths, assignment, return_order, hidden1, cot, mixed, gain, wo, wg, wu, wd)


def run_backward_groups(first, count, q, dm, k, v, lse):
    seq_len = q.shape[1]
    fixed = pl.BlockSpec((Q_TILES, seq_len, LANES), lambda i: (0, 0, 0))
    sides = pl.BlockSpec((2, seq_len, LANES), lambda i: (first + i, 0, 0))
    single = pl.BlockSpec((1, seq_len, LANES), lambda i: (i, 0, 0))
    outs = [(count, 2, seq_len, LANES), (count, seq_len, LANES), (count, seq_len, LANES)]
    return pl.pallas_call(
        functools.partial(backward_groups, first),
        grid=(count,),
        out_shape=[jax.ShapeDtypeStruct(shape, F32) for shape in outs],
        in_specs=[
            fixed,
            fixed,
            sides,
            sides,
            pl.BlockSpec((16, seq_len), lambda i: (0, 0)),
        ],
        out_specs=[
            pl.BlockSpec((1, 2, seq_len, LANES), lambda i: (i, 0, 0, 0)),
            single,
            single,
        ],
        scratch_shapes=[pltpu.VMEM((2, seq_len, LANES), F32)] * 2,
        compiler_params=pltpu.CompilerParams(vmem_limit_bytes=56 * MIB),
        cost_estimate=pl.CostEstimate(
            flops=int(8e9) * count, bytes_accessed=int(3e6) * count, transcendentals=0
        ),
        name="backward_groups",
    )(q, dm, k, v, lse)


def run_backward_finish(x, gain, dh1, groups, wq, wkv, cosine, sine):
    seq_len = x.shape[0]
    outs = [
        ((seq_len, D), BF),
        ((seq_len, PAD_D), BF),
        ((seq_len, KV_COLS), BF),
        ((seq_len, D), BF),
        ((1, D), F32),
    ]
    return call(
        backward_finish,
        outs,
        [vmem()] * 13,
        [vmem()] * 5,
        [],
        4e9,
        "backward_finish",
        56,
    )(x, gain, dh1, *groups[0], *groups[1], wq, wkv, cosine, sine)


def run_late_weights(core, normed, d_query, d_kv, gga, ggm):
    outs = [((LATE_HALF, LANES), BF), ((LATE_HALF, LANES), BF)]
    return call(
        late_weights,
        outs,
        [smem()] + [vmem()] * 5,
        [hbm()] * 2,
        [pltpu.VMEM((2 * LATE_HALF, LANES), BF), pltpu.SemaphoreType.DMA((2,))],
        4e9,
        "late_weights",
        56,
    )(core, normed, d_query, d_kv, gga, ggm)


def run_sum(bits, kept, got, split, merge=False, n_parts=None):
    joined = n_parts is not None
    n_parts = n_parts or len(kept)
    rows = kept[0].shape[0] // (n_parts if joined else 1)
    kinds = 2 if split else 1
    n_out = 1 if merge else n_parts
    out_rows = rows // kinds * (n_parts if merge else 1)
    results = call(
        functools.partial(
            gather_sum, n_parts=n_parts, rows=rows, split=split, merge=merge, joined=joined
        ),
        [((out_rows, LANES), BF)] * (kinds * n_out),
        [smem()] + [vmem()] * (2 * len(kept)),
        [hbm()] * (kinds * n_out),
        [pltpu.VMEM((n_parts, rows, LANES), BF), pltpu.SemaphoreType.DMA((2 * n_parts,))],
        1e6,
        "gather_sum",
        12,
    )(bits, *kept, *got)
    return list(results[:n_out]), list(results[n_out:])


def run_join(bits, own, got, n_parts):
    merged = len(own) < n_parts
    rows = own[0].shape[0] // (n_parts if merged else 1)
    return call(
        functools.partial(join_halves, n_parts=n_parts, rows=rows, merged=merged),
        [((2 * rows, LANES), BF)] * n_parts,
        [smem()] + [hbm()] * (2 * len(own)),
        [hbm()] * n_parts,
        [pltpu.SemaphoreType.DMA((2 * n_parts,))],
        1e6,
        "join_halves",
        4,
    )(bits, *own, *got)


def run_copy(value):
    outs = [(value.shape, value.dtype)]
    scratch = [pltpu.SemaphoreType.DMA]
    return call(copy_array, outs, [hbm()], [hbm()], scratch, 1e6, "copy_array", 4)(value)[0]


def chunk_scratch(count):
    return [
        pltpu.VMEM((3 * count * CHUNK * LANES,), F32),
        pltpu.VMEM((4 * count * CHUNK * LANES,), F32),
        pltpu.SemaphoreType.DMA((12, 3)),
        pltpu.SemaphoreType.DMA((12, 4)),
    ]


def extra_scratch(count, n_rows):
    bufs = [pltpu.VMEM((count,), F32)] * 7 + [pltpu.VMEM((n_rows * LANES,), F32)]
    return bufs + [pltpu.SemaphoreType.DMA((7,))]


def run_update_first(scale, rate, core, bits, halves, state):
    scratch = [
        pltpu.VMEM((2 * PART_ROWS, LANES), BF),
        pltpu.VMEM((FLAT_BASE + CHUNK + 16, LANES), F32),
        *chunk_scratch(12),
        pltpu.SemaphoreType.DMA((4,)),
        *extra_scratch(TAIL_ZERO, CHUNK),
    ]
    return call(
        functools.partial(update_first, scale, rate),
        [(state[0].shape, F32)] * 4,
        [smem()] * 2 + [hbm()] * 7,
        [hbm()] * 4,
        scratch,
        1e9,
        "update_first",
        56,
    )(core, bits, *halves, *state)


def run_update_second(scale, rate, core, bits, halves, late_halves, state, done):
    scratch = [
        pltpu.VMEM((FLAT_BASE + CHUNK + 8, LANES), F32),
        pltpu.VMEM((Q_TILES * D + 8, LANES), F32),
        pltpu.VMEM((2 * REST_SLOT + PART_ROWS, LANES), BF),
        pltpu.VMEM((PART_ROWS, LANES), BF),
        pltpu.VMEM((32, LANES), BF),
        *chunk_scratch(11),
        pltpu.SemaphoreType.DMA((8,)),
        *extra_scratch(TAIL_ONE, CHUNK + 8),
        *extra_scratch(5 * LANES, 8),
        pltpu.VMEM((4336, LANES), F32),
        pltpu.VMEM((2 * LATE_HALF, LANES), BF),
        *chunk_scratch(LATE_CHUNKS),
        pltpu.SemaphoreType.DMA((2,)),
        *extra_scratch((O_ROW - LATE_CHUNKS * CHUNK) * LANES, 304),
    ]
    return call(
        functools.partial(update_second, scale, rate),
        [(state[0].shape, F32)] * 4,
        [smem()] * 2 + [hbm()] * 17,
        [hbm()] * 4,
        scratch,
        1e9,
        "update_second",
        56,
        {15 + i: i for i in range(4)},
    )(core, bits, *halves, *late_halves, *state, *done)


def add_low(a, b):
    return (a.astype(F32) + b.astype(F32)).astype(BF)


def xor_swap(value, bit):
    size = lax.axis_size("dp")
    return lax.ppermute(value, "dp", [(i, i ^ (1 << bit)) for i in range(size)])


def tie(value, *others):
    return lax.optimization_barrier((value, *others))


def my_bits(orders, step):
    index = lax.axis_index("dp")
    return jnp.stack([(index >> order[step]) & 1 for order in orders]).astype(jnp.int32)


def near_size():
    return min(lax.axis_size("dp"), 4)


def spread(blocks):
    size, near = lax.axis_size("dp"), near_size()
    groups = [[g * near + i for i in range(near)] for g in range(size // near)]
    return lax.all_to_all(
        blocks, "dp", split_axis=0, concat_axis=0, tiled=True, axis_index_groups=groups
    )


def scatter_sum(value):
    count = near_size()
    blocks = spread(value.reshape(count, value.shape[0] // count, LANES))
    return jnp.sum(blocks.astype(F32), axis=0).astype(BF)


def bit_orders():
    n_bits = lax.axis_size("dp").bit_length() - 1
    base = list(range(n_bits))
    head = base[:3] if n_bits >= 3 else base
    return [head[r:] + head[:r] + base[len(head) :] for r in range(3)]


def on_device(inputs, cotangent, lengths, assignment, return_order, master, momentum, average):
    nseq_all, block_rows, _ = inputs.shape
    axes = ("dp", "shard")
    seq_len = block_rows * lax.axis_size("dp") * lax.axis_size("shard")
    my_slot = lax.axis_index(axes)
    core = lax.axis_index("shard")
    core_arr = core.astype(jnp.int32).reshape(1)

    seq_ids = jnp.arange(nseq_all, dtype=jnp.int32)
    sequence = jnp.sum(
        jnp.where(return_order[:, None] == seq_ids[None, :], assignment[None, :], 0), axis=1
    )

    def pick(array, index):
        return array.at[index].get(mode="promise_in_bounds")

    def exchange(value):
        return lax.all_to_all(value, axes, split_axis=0, concat_axis=0, tiled=True)

    x = exchange(pick(inputs, sequence)).reshape(seq_len, D)
    slot_arr = my_slot.astype(jnp.int32).reshape(1)

    other = lax.ppermute(master, "shard", [(0, 1), (1, 0)])
    gain_attn, gain_mlp, wq, wkv, wo, wg, wu, wd = run_prepare(core_arr, master, other)

    cosine, sine = rope_tables(seq_len)
    sent_cot, gain_attn, cosine = tie(cotangent, gain_attn, cosine)
    cot = exchange(sent_cot).reshape(seq_len, D)
    hidden1, mixed, q, k, v, lse = run_attention_forward(x, gain_attn, wq, wkv, wo, cosine, sine)
    result, dh1, dm, ggm, early_keep, early_send = run_mlp(
        core_arr, slot_arr, lengths, assignment, return_order, hidden1, cot, mixed, gain_mlp, wo, wg, wu, wd
    )
    back_out = exchange(result.reshape(nseq_all, block_rows, D))

    orders = bit_orders()
    n_bits = len(orders[0])

    def swap_parts(parts, step):
        return [xor_swap(part, order[step]) for part, order in zip(parts, orders)]

    got = lax.ppermute(early_send, "shard", [(0, 1), (1, 0)])
    groups = [run_backward_groups(0, 1, q, dm, k, v, lse)]
    lse, got = tie(lse, got)
    sent, kept = run_sum(my_bits(orders, 0), [early_keep], [got], True, n_parts=3)
    lse, *kept = tie(lse, *kept)
    got = swap_parts(sent, 0)
    groups.append(run_backward_groups(1, KV - 1, q, dm, k, v, lse))
    sent, kept = run_sum(my_bits(orders, 1), kept, got, True)
    dh1, back_out, *kept = tie(dh1, back_out, *kept)
    got = swap_parts(sent, 1)
    d_stream, d_query, d_kv, normed, gga = run_backward_finish(
        x, gain_attn, dh1, groups, wq, wkv, cosine, sine
    )
    last_bit = n_bits - 1
    for step in range(2, n_bits):
        if step > 2:
            got = swap_parts(sent, step - 1)
        sent, kept = run_sum(my_bits(orders, step), kept, got, True, merge=step == last_bit)
        if step == 2:
            gga, *kept = tie(gga, *kept)
            late_keep, late_send = run_late_weights(core_arr, normed, d_query, d_kv, gga, ggm)
            late_send, *kept = tie(late_send, *kept)
        if step == last_bit:
            late_send, sent[0] = tie(late_send, sent[0])
    got = [xor_swap(sent[0], last_bit)]
    late_got = lax.ppermute(late_send, "shard", [(0, 1), (1, 0)])
    late, _ = run_sum(my_bits(orders, 0)[:1], [late_keep], [late_got], False)
    late, block_output, *got = tie(late[0], run_copy(back_out), *got)
    early, _ = run_sum(my_bits(orders, last_bit)[:1], kept, got, False)
    late = scatter_sum(late)
    got = xor_swap(early[0], last_bit)
    late, got = tie(late, got)
    early = run_join(my_bits(orders, last_bit), early, [got], 3)
    far_bits = list(range(near_size().bit_length() - 1, n_bits))

    def add_far(late, early):
        late, *early = tie(late, *early)
        return add_low(late, xor_swap(late, far_bits.pop(0))), early

    for step in reversed(range(1, last_bit)):
        if far_bits:
            late, early = add_far(late, early)
        got = swap_parts(early, step)
        late, *got = tie(late, *got)
        early = run_join(my_bits(orders, step), early, got, 3)
    while far_bits:
        late, early = add_far(late, early)
    late, *early = tie(late, *early)
    late = spread(jnp.broadcast_to(late[None], (near_size(), *late.shape))).reshape(-1, LANES)
    got = swap_parts(early, 0)
    swap_own = lax.ppermute(early[2], "shard", [(0, 1)])
    bits = my_bits(orders, 0)
    scale = 1.0 / nseq_all
    rate = (nseq_all / (0.6 * seq_len)) ** 0.5 / D**0.5
    state = (master, momentum, average)
    d_stream, late, swap_own, *got = tie(d_stream, late, swap_own, *got)
    back_grad = exchange(d_stream.reshape(nseq_all, block_rows, D))
    late_other = lax.ppermute(late, "shard", [(1, 0)])
    swap_got = lax.ppermute(got[2], "shard", [(0, 1)])
    halves = [early[0], got[0], early[1], got[1], early[2], got[2], swap_own, swap_got]
    done = run_update_first(scale, rate, core_arr, bits, halves[:4], state)
    weight_grad, new_momentum, new_master, new_average = run_update_second(
        scale, rate, core_arr, bits, halves, (late, late_other), state, done
    )
    return (block_output, back_grad, weight_grad, new_momentum, new_master, new_average)


def solution(mesh):
    rows = P(None, ("dp", "shard"), None)
    flat = P("shard")
    return jax.shard_map(
        on_device,
        mesh=mesh,
        in_specs=(rows, rows, P(), P(), P(), flat, flat, flat),
        out_specs=(rows, rows, flat, flat, flat, flat),
        check_vma=False,
    )
```

```python
import functools
import math

import jax
import jax.numpy as jnp
from jax import lax
from jax.experimental import pallas as pl
from jax.experimental.pallas import tpu as pltpu
from jax.sharding import PartitionSpec as P

D = 576
H = 9
KV = 3
HD = 64
FF = 1536
LANES = 128
BLOCK = 256
Q_TILES = 5
PAD_D = Q_TILES * LANES
KV_COLS = 2 * KV * HD
FF_TILES = FF // LANES
DOWN_FIRST = 4
EARLY_TILES = 21
EARLY_ROWS = 12288
EXTRA = EARLY_TILES * D
HALF = 27657 * LANES // 2
PART_ROWS = EARLY_ROWS // 3
SWAP_START = EXTRA - DOWN_FIRST * D - 2 * PART_ROWS
SWAP_TAIL = EXTRA + 16 - 2 * PART_ROWS
REST_FIRST = 2 * PART_ROWS - FF_TILES * D
REST_SLOT = REST_FIRST + 16
REST = REST_SLOT + 16
LATE_HALF = 2432
FLAT_SCRATCH = 13848
O_ROW = 4329
GATE_ROW = 6921
MLP_COLS = 256
WIDEN = 512
MLP_UNROLL = 6
MLP_BLOCK = 256
CHUNK = 576
STEP = 288
LATE_CHUNKS = 7

EPSILON = 1e-05
MOMENTUM_DECAY = 0.55
AVERAGE_DECAY = 0.45
MASKED = -1000000000.0

BF = jnp.bfloat16
F32 = jnp.float32
MIB = 1024 * 1024


def nn(a, b):
    return jnp.dot(a, b, preferred_element_type=F32)


def nt(a, b):
    return lax.dot_general(a, b, (((1,), (1,)), ((), ())), preferred_element_type=F32)


def tn(a, b):
    return lax.dot_general(a, b, (((0,), (0,)), ((), ())), preferred_element_type=F32)


def tile(value, index):
    return value[:, index * LANES : (index + 1) * LANES]


def low_half(rows):
    return lax.broadcasted_iota(jnp.int32, (rows, LANES), 1) < HD


def swap_halves(value):
    lane = lax.broadcasted_iota(jnp.int32, value.shape, 1)
    return jnp.where(lane % HD < HD // 2, pltpu.roll(value, 96, 1), pltpu.roll(value, 32, 1))


def flip(value):
    return pltpu.roll(value, HD, 1)


def rms(value):
    return lax.rsqrt(jnp.mean(value * value, axis=-1, keepdims=True) + EPSILON)


def attention_forward(
    x_ref, ga_ref, wq_ref, wkv_ref, wo_hbm, cos_ref, sin_ref,
    h1_hbm, mixed_hbm, q_hbm, k_hbm, v_hbm, lse_ref,
    h1_ref, mixed_ref, q_ref, k_ref, v_ref, wo_ref, o_acc, sem, block_sem,
):
    seq_len = x_ref.shape[0]
    low = low_half(BLOCK)

    def project(b, carry):
        rows = pl.ds(pl.multiple_of(b * BLOCK, BLOCK), BLOCK)
        stream = x_ref[rows, :].astype(F32)
        normed = (stream * rms(stream) * ga_ref[...]).astype(BF)
        cosine = cos_ref[rows, :]
        sine = sin_ref[rows, :]

        def rope(value):
            return value * cosine + swap_halves(value) * sine

        queries = nn(normed, wq_ref[...])
        for j in range(Q_TILES):
            q_ref[j, rows, :] = (rope(tile(queries, j)) * HD ** (-0.5)).astype(BF)
        keys_values = nn(normed, wkv_ref[...])
        first = rope(tile(keys_values, 0))
        second = tile(keys_values, 1)
        third = tile(keys_values, 2)
        mid = rope(second)

        def put(ref, index, value):
            ref[index, rows, :] = value.astype(BF)

        put(k_ref, 0, jnp.where(low, first, 0.0))
        put(k_ref, 1, jnp.where(low, 0.0, flip(first)))
        put(k_ref, 2, jnp.where(low, flip(first), 0.0))
        put(k_ref, 3, jnp.where(low, 0.0, first))
        put(k_ref, 4, jnp.where(low, mid, 0.0))
        put(k_ref, 5, jnp.where(low, 0.0, flip(mid)))
        put(v_ref, 0, jnp.where(low, flip(second), 0.0))
        put(v_ref, 1, jnp.where(low, 0.0, second))
        put(v_ref, 2, jnp.where(low, third, 0.0))
        put(v_ref, 3, jnp.where(low, 0.0, flip(third)))
        put(v_ref, 4, jnp.where(low, flip(third), 0.0))
        put(v_ref, 5, jnp.where(low, 0.0, third))
        return carry

    load = pltpu.make_async_copy(wo_hbm, wo_ref, sem.at[3])
    load.start()
    lax.fori_loop(0, seq_len // BLOCK, project, 0)
    stores = [
        pltpu.make_async_copy(source, target, sem.at[i])
        for i, (source, target) in enumerate(((q_ref, q_hbm), (k_ref, k_hbm), (v_ref, v_hbm)))
    ]
    for copy in stores:
        copy.start()
    lane = lax.broadcasted_iota(jnp.int32, (BLOCK, LANES), 1)
    keep = lax.broadcasted_iota(jnp.int32, (BLOCK, BLOCK), 1) <= lax.broadcasted_iota(
        jnp.int32, (BLOCK, BLOCK), 0
    )
    for b in range(seq_len // BLOCK):
        rows = slice(b * BLOCK, (b + 1) * BLOCK)
        n_keys = (b + 1) * BLOCK
        o_acc[...] = jnp.zeros_like(o_acc)

        def group(g, lse, rows=rows, n_keys=n_keys):
            for u in range(3):
                head = 3 * g + u
                j = head // 2
                side = 2 * g + head % 2
                scores = nt(q_ref[j, rows, :], k_ref[side, 0:n_keys, :])
                diag = jnp.where(keep, scores[:, n_keys - BLOCK :], MASKED)
                if n_keys > BLOCK:
                    scores = jnp.concatenate([scores[:, : n_keys - BLOCK], diag], axis=1)
                else:
                    scores = diag
                row_max = jnp.max(scores, axis=-1, keepdims=True)
                exponent = jnp.exp(scores - row_max)
                total = jnp.sum(exponent, axis=-1, keepdims=True)
                mixed = nn(exponent.astype(BF), v_ref[side, 0:n_keys, :])
                o_acc[j] += mixed * (1.0 / total)
                lse = jnp.where(lane == head, row_max + jnp.log(total), lse)
            return lse

        lse = lax.fori_loop(0, KV, group, jnp.zeros((BLOCK, LANES), F32))
        lse_ref[:, rows] = lse.T[:16]
        mixed = jnp.concatenate([o_acc[j].astype(BF) for j in range(Q_TILES)], axis=1)
        mixed_ref[rows, :] = mixed
        if b == 0:
            load.wait()
        h1_ref[rows, :] = x_ref[rows, :].astype(F32) + nn(mixed, wo_ref[...])
        for i, (source, target) in enumerate(((mixed_ref, mixed_hbm), (h1_ref, h1_hbm))):
            stores.append(
                pltpu.make_async_copy(source.at[rows], target.at[rows], block_sem.at[b, i])
            )
            stores[-1].start()
    for copy in stores:
        copy.wait()


def prepare_weights(
    core_ref, own_ref, other_ref,
    ga_ref, gm_ref, wq_ref, wkv_ref, wo_ref, wg_ref, wu_ref, wd_ref,
    first, second, flat, tmp, rest, sem,
):
    core = core_ref[0]
    for which, pair in enumerate(((first, second), (second, first))):

        @pl.when(core == which)
        def _(pair=pair):
            copies = [
                pltpu.make_async_copy(ref, target, sem.at[i])
                for i, (ref, target) in enumerate(zip((own_ref, other_ref), pair))
            ]
            for copy in copies:
                copy.start()
            for copy in copies:
                copy.wait()

    def widen(ref):
        def body(i, carry):
            start = pl.multiple_of(i * WIDEN, WIDEN)
            span = pl.ds(pl.multiple_of(i * WIDEN * LANES, WIDEN * LANES), WIDEN * LANES)
            flat[pl.ds(start, WIDEN), :] = ref[span].reshape(WIDEN, LANES)
            return carry

        whole = HALF // (WIDEN * LANES)
        lax.fori_loop(0, whole, body, 0)
        left = HALF - whole * WIDEN * LANES
        rest[pl.ds(0, left)] = ref[pl.ds(whole * WIDEN * LANES, left)]
        flat[whole * WIDEN : whole * WIDEN + 8, :] = rest[...].reshape(8, LANES)

    def low_precision(value):
        return value.astype(BF).astype(F32)

    def interleave(even, odd, pairs, out_ref, first_row, pad):
        low = low_half(2 * pairs)
        for t in range(Q_TILES):
            tmp[pl.ds(t * D, pairs, stride=2), :] = even[t]
            tmp[pl.ds(t * D + 1, pairs, stride=2), :] = odd[t]
        rows = pl.ds(first_row, 2 * pairs)
        for t in range(Q_TILES):
            value = tmp[t * D : t * D + 2 * pairs, :]
            if t < 4:
                out_ref[rows, t * LANES : (t + 1) * LANES] = value.astype(BF)
            elif pad:
                out_ref[rows, t * LANES :] = jnp.where(low, value, 0.0).astype(BF)
            else:
                out_ref[rows, t * LANES :] = value[:, :HD].astype(BF)

    def wide(row, out_ref, pad):
        pairs = D // 2
        low = low_half(pairs)
        cols = [flat[pl.ds(row + c, pairs, stride=9), :] for c in range(9)]
        turned = [flip(cols[c]) for c in range(4, 9)]
        odd = [jnp.where(low, turned[t], turned[t + 1]) for t in range(4)] + [turned[4]]
        interleave(cols[:5], odd, pairs, out_ref, 0, pad)

    widen(first)
    low1 = low_half(1)
    turned = [flip(flat[4 + r : 5 + r, :]) for r in range(5)]
    for r in range(4):
        ga_ref[:, r * LANES : (r + 1) * LANES] = low_precision(flat[r : r + 1, :])
        gm_ref[:, r * LANES : (r + 1) * LANES] = low_precision(
            jnp.where(low1, turned[r], turned[r + 1])
        )
    ga_ref[:, 4 * LANES :] = low_precision(flat[4:5, :HD])
    gm_ref[:, 4 * LANES :] = low_precision(turned[4][:, :HD])
    wide(9, wq_ref, True)
    wide(O_ROW, wo_ref, False)
    wo_ref[D:, :] = jnp.zeros((PAD_D - D, D), BF)
    pairs = D // 2
    low = low_half(pairs)
    narrow = []
    for row in (2601, 3465):
        cols = [flat[pl.ds(row + c, pairs, stride=3), :] for c in range(3)]
        turned = [flip(cols[1]), flip(cols[2])]
        even = cols[:2]
        odd = [jnp.where(low, turned[0], turned[1]), turned[1]]
        for t in range(2):
            tmp[pl.ds(t * D, pairs, stride=2), :] = even[t]
            tmp[pl.ds(t * D + 1, pairs, stride=2), :] = odd[t]
        narrow.append((tmp[0:D, :], tmp[D : 2 * D, :]))
    (k0, k1), (v0, v1) = narrow
    low = low_half(D)
    v0 = flip(v0)
    v1 = flip(v1)
    wkv_ref[:, 0:LANES] = k0.astype(BF)
    wkv_ref[:, LANES : 2 * LANES] = jnp.where(low, k1, v0).astype(BF)
    wkv_ref[:, 2 * LANES :] = jnp.where(low, v0, v1).astype(BF)
    head = second[pl.ds(0, 1024)].reshape(8, LANES)
    turned = flip(head)
    for r in range(5):
        row = GATE_ROW + FF_TILES * (D - 1) + 7 + r
        before = flat[row : row + 1, :] if r == 0 else turned[r - 1 : r]
        flat[row : row + 1, :] = jnp.where(low1, before, turned[r : r + 1])
    for t in range(FF_TILES):
        wg_ref[:, t * LANES : (t + 1) * LANES] = flat[
            pl.ds(GATE_ROW + t, D, stride=FF_TILES), :
        ].astype(BF)
    widen(second)
    here = flip(flat[pl.ds(4, D, stride=FF_TILES), :])
    for t in range(FF_TILES):
        after = flip(flat[pl.ds(5 + t, D, stride=FF_TILES), :])
        wu_ref[:, t * LANES : (t + 1) * LANES] = jnp.where(low, here, after).astype(BF)
        here = after

    def down(i, carry):
        n_pairs = 96
        low = low_half(n_pairs)
        start = 6916 + 9 * n_pairs * i
        cols = [flat[pl.ds(start + c, n_pairs, stride=9), :] for c in range(10)]
        turned = [flip(cols[c]) for c in range(6)]
        even = [jnp.where(low, turned[c], turned[c + 1]) for c in range(5)]
        interleave(even, cols[5:], n_pairs, wd_ref, pl.multiple_of(2 * n_pairs * i, 16), False)
        return carry

    lax.fori_loop(0, FF // 192, down, 0)


def transposed(value):
    rows = value.shape[0]
    pieces = [tile(value, t) for t in range(4)]
    pieces.append(
        jnp.concatenate([value[:, 4 * LANES :], jnp.zeros((rows, LANES - HD), F32)], axis=1)
    )
    return jnp.concatenate([piece.T for piece in pieces], axis=0)


def mlp_pass(
    core_ref, slot_ref, lengths_ref, assignment_ref, return_ref,
    h1_hbm, cot_hbm, mixed_hbm, gm_ref, wo_hbm, wg_hbm, wu_hbm, wd_hbm,
    out_hbm, dh1_hbm, dm_hbm, ggm_ref, keep_ref, send_ref,
    h1_ref, cot_ref, mixed_ref, wo_ref, wg_ref, wu_ref, wd_ref, out_ref, dh1_ref, dm_ref,
    nmt_s, backt_s, inner_s, dg_s, du_s, da_s, grads, in_sem, out_sem, sem,
):
    seq_len = h1_ref.shape[0]
    core = core_ref[0]
    live_len = lengths_ref[assignment_ref[return_ref[slot_ref[0]]]]
    n_cols = FF // MLP_COLS
    loads = [
        pltpu.make_async_copy(source, target, in_sem.at[i])
        for i, (source, target) in enumerate(
            (
                (h1_hbm, h1_ref),
                (cot_hbm, cot_ref),
                (wg_hbm, wg_ref),
                (wu_hbm, wu_ref),
                (wd_hbm, wd_ref),
                (wo_hbm, wo_ref),
                (mixed_hbm, mixed_ref),
            )
        )
    ]
    for copy in loads:
        copy.start()
    for copy in loads[:6]:
        copy.wait()

    def results(b):
        rows = pl.ds(pl.multiple_of(b * MLP_BLOCK, MLP_BLOCK), MLP_BLOCK)
        pairs = [(out_ref.at[rows], out_hbm.at[rows]), (dh1_ref.at[rows], dh1_hbm.at[rows])]
        pairs.append((dm_ref.at[:, rows], dm_hbm.at[:, rows]))
        return [
            pltpu.make_async_copy(source, target, out_sem.at[b, i])
            for i, (source, target) in enumerate(pairs)
        ]

    def block(b, ggm):
        start = pl.multiple_of(b * MLP_BLOCK, MLP_BLOCK)
        rows = pl.ds(start, MLP_BLOCK)
        hidden1 = h1_ref[rows, :]
        r2 = rms(hidden1)
        gain = gm_ref[...]
        normed2_wide = hidden1 * r2 * gain
        normed2 = normed2_wide.astype(BF)
        nmt_s[:, rows] = transposed(normed2_wide).astype(BF)
        live = (
            start + lax.broadcasted_iota(jnp.int32, (MLP_BLOCK, 1), 0) < live_len
        ).astype(F32)

        back = cot_ref[rows, :].astype(F32) * live
        back_low = back.astype(BF)
        backt_s[:, rows] = transposed(back).astype(BF)
        def columns(c):
            cols = pl.ds(pl.multiple_of(c * MLP_COLS, MLP_COLS), MLP_COLS)
            gate = nn(normed2, wg_ref[:, cols])
            up = nn(normed2, wu_ref[:, cols])
            d_inner = nt(back_low, wd_ref[cols, :])
            sig = jax.nn.sigmoid(gate)
            silu = gate * sig
            inner_s[rows, cols] = (silu * up).astype(BF)
            dg_s[rows, cols] = (d_inner * up * sig * (1.0 + gate * (1.0 - sig))).astype(BF)
            du_s[rows, cols] = (d_inner * silu).astype(BF)

        def some_columns(i, carry):
            for c in range(MLP_UNROLL):
                columns(MLP_UNROLL * i + c)
            return carry

        lax.fori_loop(0, n_cols // MLP_UNROLL, some_columns, 0)
        out_ref[rows, :] = ((hidden1 + nn(inner_s[rows, :], wd_ref[...])) * live).astype(BF)
        d_normed2 = nt(dg_s[rows, :], wg_ref[...]) + nt(du_s[rows, :], wu_ref[...])
        scaled = d_normed2 * gain
        d_hidden1 = (
            back
            + r2 * scaled
            - hidden1 * (r2 * r2 * r2) * jnp.mean(scaled * hidden1, axis=-1, keepdims=True)
        )
        dh1_ref[rows, :] = d_hidden1
        d_attn = d_hidden1.astype(BF)
        da_s[rows, :] = d_attn

        d_mixed = nt(d_attn, wo_ref[...]).astype(BF)
        for j in range(Q_TILES):
            dm_ref[j, rows, :] = tile(d_mixed, j)
        for copy in results(b):
            copy.start()
        return ggm + jnp.sum(d_normed2 * hidden1 * r2, axis=0, keepdims=True)

    ggm_ref[...] = lax.fori_loop(0, seq_len // MLP_BLOCK, block, jnp.zeros((1, D), F32))

    def put(half, index, value):
        grads[half, pl.ds(pl.multiple_of(index * D, D), D), :] = value

    def leave(c):
        rows = pl.ds(pl.multiple_of(2 * c * D, D), 2 * D)
        return [
            pltpu.make_async_copy(grads.at[1 - core, rows], send_ref.at[rows], sem.at[c, 0]),
            pltpu.make_async_copy(grads.at[core, rows], keep_ref.at[rows], sem.at[c, 1]),
        ]

    def weights(c, carry):
        cols = pl.ds(pl.multiple_of(c * 2 * LANES, 2 * LANES), 2 * LANES)
        grad_gate = nn(nmt_s[:D, :], dg_s[:, cols]).astype(BF)
        grad_up = nn(nmt_s[:D, :], du_s[:, cols]).astype(BF)
        for t in range(2):
            put(0, 2 * c + t, tile(grad_gate, t))
            put(1, 2 * c + t, tile(grad_up, t))
        for copy in leave(c):
            copy.start()
        grad_down = nn(backt_s[:D, :], inner_s[:, cols]).astype(BF)
        part = jnp.where(c < DOWN_FIRST // 2, 0, 1)
        base = jnp.where(c < DOWN_FIRST // 2, FF_TILES + Q_TILES, FF_TILES - DOWN_FIRST)
        for t in range(2):
            put(part, base + 2 * c + t, tile(grad_down, t))
        return carry

    lax.fori_loop(0, n_cols, weights, 0)
    loads[6].wait()
    grad_o = tn(mixed_ref[...], da_s[...])[:D]
    for t in range(4):
        put(0, FF_TILES + t, tile(grad_o, t).astype(BF))
    put(0, FF_TILES + 4, half_tile(grad_o).astype(BF))
    grads[0, EXTRA:, :] = jnp.zeros((EARLY_ROWS - EXTRA, LANES), BF)
    grads[1, EXTRA - D :, :] = jnp.zeros((EARLY_ROWS - EXTRA + D, LANES), BF)
    row = lax.broadcasted_iota(jnp.int32, (16, LANES), 0)
    rest = jnp.zeros((16, LANES), F32)
    for r in range(5):
        start = (8 + r) * D - 16
        last = grads[0, start : start + 16, :].astype(F32)[15:16]
        rest = jnp.where(row == r, jnp.broadcast_to(last, (16, LANES)), rest)
    grads[0, EXTRA + 16 : EXTRA + 32, :] = rest.astype(BF)
    rows = pl.ds(FF_TILES * D, EARLY_ROWS - FF_TILES * D)
    final = [
        pltpu.make_async_copy(grads.at[1 - core, rows], send_ref.at[rows], sem.at[n_cols, 0]),
        pltpu.make_async_copy(grads.at[core, rows], keep_ref.at[rows], sem.at[n_cols, 1]),
    ]
    for copy in final:
        copy.start()

    def drain(c, carry):
        for copy in leave(c):
            copy.wait()
        return carry

    def drain_results(b, carry):
        for copy in results(b):
            copy.wait()
        return carry

    lax.fori_loop(0, n_cols, drain, 0)
    lax.fori_loop(0, seq_len // MLP_BLOCK, drain_results, 0)
    for copy in final:
        copy.wait()


def half_tile(value):
    rows = value.shape[0]
    return jnp.concatenate([value[:, 4 * LANES : D], jnp.zeros((rows, HD), value.dtype)], axis=1)


def gain_rows(value):
    row = lax.broadcasted_iota(jnp.int32, (16, LANES), 0)
    whole = jnp.zeros((16, LANES), F32)
    for t in range(Q_TILES):
        piece = tile(value, t) if t < 4 else half_tile(value)
        whole = jnp.where(row == t, jnp.broadcast_to(piece, (16, LANES)), whole)
    return whole


def backward_groups(
    first, q_ref, dm_ref, k_ref, v_ref, lse_ref, dq_ref, dk_ref, dv_ref, dk_acc, dv_acc
):
    seq_len = q_ref.shape[1]
    group = first + pl.program_id(0)
    dq_ref[...] = jnp.zeros_like(dq_ref)
    dk_acc[...] = jnp.zeros_like(dk_acc)
    dv_acc[...] = jnp.zeros_like(dv_acc)
    keep = lax.broadcasted_iota(jnp.int32, (BLOCK, BLOCK), 0) <= lax.broadcasted_iota(
        jnp.int32, (BLOCK, BLOCK), 1
    )
    for b in range(seq_len // BLOCK):
        rows = slice(b * BLOCK, (b + 1) * BLOCK)
        n_keys = (b + 1) * BLOCK
        for u in range(3):
            head = 3 * group + u
            j = lax.shift_right_logical(head, 1)
            own = j - lax.shift_right_logical(3 * group, 1)
            side = head - 2 * j
            queries = q_ref[j, rows, :]
            d_mixed = dm_ref[j, rows, :]
            keys = k_ref[side, 0:n_keys, :]
            values = v_ref[side, 0:n_keys, :]
            prob = jnp.exp(nt(keys, queries) - lse_ref[pl.ds(head, 1), rows])
            diag = jnp.where(keep, prob[n_keys - BLOCK :, :], 0.0)
            if n_keys > BLOCK:
                prob = jnp.concatenate([prob[: n_keys - BLOCK, :], diag], axis=0)
            else:
                prob = diag
            d_prob = nt(values, d_mixed)
            delta = jnp.sum(d_prob * prob, axis=0, keepdims=True)
            d_score = (prob * (d_prob - delta)).astype(BF)
            dv_acc[side, 0:n_keys, :] += nn(prob.astype(BF), d_mixed)
            dk_acc[side, 0:n_keys, :] += nn(d_score, queries)
            dq_ref[0, own, rows, :] += tn(d_score, keys)
    dk_ref[0] = dk_acc[0] + flip(dk_acc[1])
    dv_ref[0] = dv_acc[0] + flip(dv_acc[1])


def backward_finish(
    x_hbm, ga_ref, dh1_hbm, dqa_hbm, dka_hbm, dva_hbm, dqb_hbm, dkb_hbm, dvb_hbm,
    wq_ref, wkv_ref, cos_hbm, sin_hbm,
    dx_hbm, dq_hbm, dkv_hbm, nm_hbm, gga_ref,
    x_ref, dh1_ref, cos_ref, sin_ref, dqa_ref, dka_ref, dva_ref, dqb_ref, dkb_ref, dvb_ref,
    dx_ref, dq_s, dkv_s, nm_s, in_sem, out_sem,
):
    seq_len = x_ref.shape[0]
    low = low_half(BLOCK)

    def rows_of(ref, b):
        rows = pl.ds(pl.multiple_of(b * BLOCK, BLOCK), BLOCK)
        return ref.at[(slice(None),) * (len(ref.shape) - 2) + (rows,)]

    def moves(pairs, b, sem):
        return [
            pltpu.make_async_copy(rows_of(source, b), rows_of(target, b), sem.at[b, i])
            for i, (source, target) in enumerate(pairs)
        ]

    inward = (
        (x_hbm, x_ref), (dh1_hbm, dh1_ref), (cos_hbm, cos_ref), (sin_hbm, sin_ref),
        (dqa_hbm, dqa_ref), (dka_hbm, dka_ref), (dva_hbm, dva_ref),
        (dqb_hbm, dqb_ref), (dkb_hbm, dkb_ref), (dvb_hbm, dvb_ref),
    )
    outward = ((dx_ref, dx_hbm), (dq_s, dq_hbm), (dkv_s, dkv_hbm), (nm_s, nm_hbm))
    n_blocks = seq_len // BLOCK
    for b in range(n_blocks):
        for copy in moves(inward, b, in_sem):
            copy.start()

    def block(b, gga):
        for copy in moves(inward, b, in_sem):
            copy.wait()
        rows = pl.ds(pl.multiple_of(b * BLOCK, BLOCK), BLOCK)
        cosine = cos_ref[rows, :]
        sine = sin_ref[rows, :]

        def unrope(value):
            return value * cosine - swap_halves(value) * sine

        d_rot = [
            dqa_ref[0, 0, rows, :],
            dqa_ref[0, 1, rows, :] + dqb_ref[0, 0, rows, :],
            dqb_ref[0, 1, rows, :],
            dqb_ref[1, 0, rows, :],
            dqb_ref[1, 1, rows, :],
        ]
        for j in range(Q_TILES):
            d_query = unrope(d_rot[j]) * HD ** (-0.5)
            dq_s[rows, j * LANES : (j + 1) * LANES] = d_query.astype(BF)
        dk = [dka_ref[0, rows, :], dkb_ref[0, rows, :], dkb_ref[1, rows, :]]
        dv = [dva_ref[0, rows, :], dvb_ref[0, rows, :], dvb_ref[1, rows, :]]
        first = unrope(jnp.where(low, dk[0], flip(dk[1])))
        second = jnp.where(low, unrope(dk[2]), flip(dv[0]))
        third = jnp.where(low, dv[1], flip(dv[2]))
        dkv_s[rows, 0:LANES] = first.astype(BF)
        dkv_s[rows, LANES : 2 * LANES] = second.astype(BF)
        dkv_s[rows, 2 * LANES :] = third.astype(BF)
        d_normed = nt(dq_s[rows, :], wq_ref[...]) + nt(dkv_s[rows, :], wkv_ref[...])
        stream = x_ref[rows, :].astype(F32)
        r1 = rms(stream)
        gain = ga_ref[...]
        nm_s[rows, :] = (stream * r1 * gain).astype(BF)
        scaled = d_normed * gain
        dx_ref[rows, :] = (
            dh1_ref[rows, :]
            + r1 * scaled
            - stream * (r1 * r1 * r1) * jnp.mean(scaled * stream, axis=-1, keepdims=True)
        ).astype(BF)
        for copy in moves(outward, b, out_sem):
            copy.start()
        return gga + jnp.sum(d_normed * stream * r1, axis=0, keepdims=True)

    gga_ref[...] = lax.fori_loop(0, seq_len // BLOCK, block, jnp.zeros((1, D), F32))
    for b in range(n_blocks):
        for copy in moves(outward, b, out_sem):
            copy.wait()


def late_weights(
    core_ref, nm_s, dq_s, dkv_s, gga_ref, ggm_ref, keep_ref, send_ref, late, sem
):
    grad_q = tn(nm_s[...], dq_s[...]).astype(BF)
    grad_kv = tn(nm_s[...], dkv_s[...]).astype(BF)
    for t in range(Q_TILES):
        late[t * D : (t + 1) * D, :] = tile(grad_q, t)
    for t in range(3):
        late[(Q_TILES + t) * D : (Q_TILES + t + 1) * D, :] = tile(grad_kv, t)
    late[8 * D :, :] = jnp.zeros((2 * LATE_HALF - 8 * D, LANES), BF)
    late[8 * D : 8 * D + 16, :] = gain_rows(gga_ref[...]).astype(BF)
    late[8 * D + 16 : 8 * D + 32, :] = gain_rows(ggm_ref[...]).astype(BF)
    copies = []
    for i, (which, ref) in enumerate(((1 - core_ref[0], send_ref), (core_ref[0], keep_ref))):
        rows = pl.ds(pl.multiple_of(which * LATE_HALF, 8), LATE_HALF)
        copies.append(pltpu.make_async_copy(late.at[rows], ref, sem.at[i]))
    for copy in copies:
        copy.start()
    for copy in copies:
        copy.wait()


def gather_sum(bits_ref, *refs, n_parts, rows, split, merge, joined):
    n_in = 1 if joined else n_parts
    kept, got = refs[:n_in], refs[n_in : 2 * n_in]
    kinds = 2 if split else 1
    n_out = kinds * (1 if merge else n_parts)
    outs = refs[2 * n_in : 2 * n_in + n_out]
    scratch, sem = refs[2 * n_in + n_out :]
    size = rows // kinds
    copies = []
    for p in range(n_parts):
        if joined:
            part = slice(p * rows, (p + 1) * rows)
            total = kept[0][part, :].astype(F32) + got[0][part, :].astype(F32)
        else:
            total = kept[p][...].astype(F32) + got[p][...].astype(F32)
        scratch[p] = total.astype(BF)
        for i in range(kinds):
            if merge:
                target = outs[i].at[pl.ds(p * size, size)]
            else:
                target = outs[p + i * n_parts]
            start = (bits_ref[p] if i else 1 - bits_ref[p]) * size if split else 0
            source = scratch.at[p, pl.ds(pl.multiple_of(start, 8), size)]
            copies.append(pltpu.make_async_copy(source, target, sem.at[2 * p + i]))
            copies[-1].start()
    for copy in copies:
        copy.wait()


def join_halves(bits_ref, *refs, n_parts, rows, merged):
    n_in = 1 if merged else n_parts
    own, got, outs = refs[:n_in], refs[n_in : 2 * n_in], refs[2 * n_in : 2 * n_in + n_parts]
    sem = refs[2 * n_in + n_parts]
    copies = []
    for p in range(n_parts):
        for i, (group, which) in enumerate(((own, bits_ref[p]), (got, 1 - bits_ref[p]))):
            source = group[0].at[pl.ds(p * rows, rows)] if merged else group[p]
            span = pl.ds(pl.multiple_of(which * rows, 8), rows)
            copies.append(pltpu.make_async_copy(source, outs[p].at[span], sem.at[2 * p + i]))
            copies[-1].start()
    for copy in copies:
        copy.wait()


def put_wide(flat, tmp, values, rows, row):
    pairs = rows // 2
    for index, value in enumerate(values):
        tmp[pl.ds(index * D, rows), :] = value
    even = [tmp[pl.ds(i * D, pairs, stride=2), :] for i in range(Q_TILES)]
    odd = [flip(tmp[pl.ds(i * D + 1, pairs, stride=2), :]) for i in range(Q_TILES)]
    low = low_half(pairs)
    for c in range(4):
        flat[pl.ds(row + c, pairs, stride=9), :] = even[c]
    flat[pl.ds(row + 4, pairs, stride=9), :] = jnp.where(low, even[4], odd[0])
    for c in range(4):
        flat[pl.ds(row + 5 + c, pairs, stride=9), :] = jnp.where(low, odd[c], odd[c + 1])


def copy_array(source_ref, target_ref, sem):
    copy = pltpu.make_async_copy(source_ref, target_ref, sem)
    copy.start()
    copy.wait()


def update_rule(scale, rate, grad, master, momentum, average):
    weight_grad = grad * scale
    new_momentum = MOMENTUM_DECAY * momentum + weight_grad
    new_master = master - rate * (weight_grad + MOMENTUM_DECAY * new_momentum)
    new_average = AVERAGE_DECAY * average + (1.0 - AVERAGE_DECAY) * new_master
    return weight_grad, new_momentum, new_master, new_average


class Chunks:
    def __init__(self, rows, base, count, rule, refs):
        self.rows, self.base, self.count, self.rule = rows, base, count, rule
        self.ins, self.outs, self.in_buf, self.out_buf, self.in_sem, self.out_sem = refs
        self.size = rows * LANES

    def span(self, c):
        return pl.ds(pl.multiple_of((self.base + c * self.rows) * LANES, LANES), self.size)

    def place(self, index, start=0, length=None):
        start = pl.multiple_of(index * self.size + start, 8 * LANES)
        return pl.ds(start, self.size if length is None else length)

    def fetch(self, c):
        return [
            pltpu.make_async_copy(
                self.ins[i].at[self.span(c)],
                self.in_buf.at[self.place(c * 3 + i)],
                self.in_sem.at[c, i],
            )
            for i in range(3)
        ]

    def flush(self, c):
        return [
            pltpu.make_async_copy(
                self.out_buf.at[self.place(c * 4 + i)],
                self.outs[i].at[self.span(c)],
                self.out_sem.at[c, i],
            )
            for i in range(4)
        ]

    def start(self):
        def body(c, carry):
            for copy in self.fetch(c):
                copy.start()
            return carry

        lax.fori_loop(0, self.count, body, 0)

    def run(self, stage, gradient):
        sub = STEP * LANES

        def body(c, carry):
            stage(c)
            for copy in self.fetch(c):
                copy.wait()

            def step(s, inner):
                grad = gradient(c, s * STEP, STEP).reshape(sub)
                values = self.rule(
                    grad, *[self.in_buf[self.place(c * 3 + i, s * sub, sub)] for i in range(3)]
                )
                for i in range(4):
                    self.out_buf[self.place(c * 4 + i, s * sub, sub)] = values[i]
                return inner

            lax.fori_loop(0, self.rows // STEP, step, 0)
            for copy in self.flush(c):
                copy.start()
            return carry

        def drain(c, carry):
            for copy in self.flush(c):
                copy.wait()
            return carry

        lax.fori_loop(0, self.count, body, 0)
        return lambda: lax.fori_loop(0, self.count, drain, 0)


class Extra:
    def __init__(self, start, ins, outs, rest):
        self.bufs, self.sem = rest[:8], rest[8]
        count = self.bufs[0].shape[0]
        span = pl.ds(start, count)
        self.count = count
        self.loads = [
            pltpu.make_async_copy(ins[i].at[span], self.bufs[i], self.sem.at[i]) for i in range(3)
        ]
        self.stores = [
            pltpu.make_async_copy(self.bufs[3 + i], outs[i].at[span], self.sem.at[3 + i])
            for i in range(4)
        ]

    def start(self):
        for copy in self.loads:
            copy.start()

    def finish(self, grad, rule):
        for copy in self.loads:
            copy.wait()
        self.bufs[7][...] = grad.reshape(grad.shape[0] * LANES)
        values = rule(self.bufs[7][pl.ds(0, self.count)], *[self.bufs[i][...] for i in range(3)])
        for i in range(4):
            self.bufs[3 + i][...] = values[i]
            self.stores[i].start()

    def drain(self):
        for copy in self.stores:
            copy.wait()


def shifted(flat, row, count):
    here = flip(flat[pl.ds(row - 1, count), :])
    after = flip(flat[pl.ds(row, count), :])
    return jnp.where(low_half(count), here, after)


def load_parts(pieces, sem):
    copies = [
        pltpu.make_async_copy(source, target, sem.at[i]) for i, (source, target) in enumerate(pieces)
    ]
    for copy in copies:
        copy.start()
    return copies


FLAT_BASE = 8
TAIL_ZERO = HALF - (GATE_ROW + 11 * CHUNK) * LANES
TAIL_ONE = HALF - (6916 + 11 * CHUNK) * LANES


def update_first(scale, rate, core_ref, bits_ref, *rest):
    halves, ins, outs = rest[:4], rest[4:7], rest[7:11]
    early_ref, flat, in_buf, out_buf, in_sem, out_sem, part_sem = rest[11:18]
    refs = (ins, outs, in_buf, out_buf, in_sem, out_sem)
    core = core_ref[0]
    rule = functools.partial(update_rule, scale, rate)
    half = PART_ROWS // 2
    pieces = []
    for p in range(2):
        for i, which in enumerate((bits_ref[p], 1 - bits_ref[p])):
            span = pl.ds(pl.multiple_of(p * PART_ROWS + which * half, 8), half)
            pieces.append((halves[2 * p + i], early_ref.at[span]))
    copies = load_parts(pieces, part_sem)
    extra = Extra((GATE_ROW + 11 * CHUNK) * LANES, ins, outs, rest[18:])
    base = jnp.where(core == 0, GATE_ROW, 4)
    chunks = Chunks(CHUNK, base, 11 + core, rule, refs)
    chunks.start()

    @pl.when(core == 0)
    def _():
        extra.start()

    for copy in copies:
        copy.wait()
    flat[0:FLAT_BASE, :] = jnp.zeros((FLAT_BASE, LANES), F32)

    def stage(c):
        for t in range(FF_TILES):
            rows = pl.ds(pl.multiple_of(t * D + c * 48, 16), 48)
            flat[pl.ds(FLAT_BASE + t, 48, stride=FF_TILES), :] = early_ref[rows, :].astype(F32)

    def gradient(c, start, count):
        row = pl.multiple_of(FLAT_BASE + start, 8)
        return jnp.where(core == 0, flat[pl.ds(row, count), :], shifted(flat, row, count))

    def stage_next(c):
        flat[FLAT_BASE - 1 : FLAT_BASE, :] = flat[FLAT_BASE + CHUNK - 1 : FLAT_BASE + CHUNK, :]
        stage(c)

    drain = chunks.run(stage_next, gradient)

    @pl.when(core == 0)
    def _():
        stage(11)
        extra.finish(flat[FLAT_BASE : FLAT_BASE + CHUNK, :], rule)

    drain()

    @pl.when(core == 0)
    def _():
        extra.drain()


def lay_out_late(flat, tmp, late_ref):
    def late(index):
        return late_ref[index * D : (index + 1) * D, :].astype(F32)

    low1 = low_half(1)
    gain_a = late_ref[8 * D : 8 * D + 16, :].astype(F32)
    gain_m = flip(late_ref[8 * D + 16 : 8 * D + 32, :].astype(F32))
    for r in range(4):
        flat[r : r + 1, :] = gain_a[r : r + 1]
    flat[4:5, :] = jnp.where(low1, gain_a[4:5], gain_m[0:1])
    for r in range(4):
        flat[5 + r : 6 + r, :] = jnp.where(low1, gain_m[r : r + 1], gain_m[r + 1 : r + 2])
    put_wide(flat, tmp, [late(t) for t in range(Q_TILES)], D, 9)
    pairs = D // 2
    for t in range(3):
        tmp[pl.ds(t * D, D), :] = late(Q_TILES + t)
    even = [tmp[pl.ds(i * D, pairs, stride=2), :] for i in range(3)]
    odd = [tmp[pl.ds(i * D + 1, pairs, stride=2), :] for i in range(3)]
    low = low_half(pairs)
    turned = [flip(odd[0]), flip(odd[1]), flip(even[1]), flip(even[2])]
    rows = (
        (2601, even[0]),
        (2602, jnp.where(low, even[1], turned[0])),
        (2603, jnp.where(low, turned[0], turned[1])),
        (3465, jnp.where(low, turned[2], turned[3])),
        (3466, jnp.where(low, turned[3], odd[1])),
        (3467, odd[2]),
    )
    for row, value in rows:
        flat[pl.ds(row, pairs, stride=3), :] = value


def update_second(scale, rate, core_ref, bits_ref, *rest):
    halves, late_halves, ins, outs = rest[:8], rest[8:10], rest[10:13], rest[17:21]
    flat, tmp, part_ref, swap_ref, first_ref, in_buf, out_buf, in_sem, out_sem, part_sem = rest[21:31]
    refs = (ins, outs, in_buf, out_buf, in_sem, out_sem)
    tail = Extra((6916 + 11 * CHUNK) * LANES, ins, outs, rest[31:40])
    head = Extra(0, ins, outs, rest[40:49])
    late_flat, late_ref, late_in, late_out, late_in_sem, late_out_sem, late_sem = rest[49:56]
    late_last = Extra(LATE_CHUNKS * CHUNK * LANES, ins, outs, rest[56:])
    rule = functools.partial(update_rule, scale, rate)
    half = PART_ROWS // 2
    pieces = []
    for i in range(2):
        which = [1 - bits_ref[p] if i else bits_ref[p] for p in range(3)]

        def rows(start, p, size, which=which):
            return pl.ds(pl.multiple_of(start + which[p] * size, 16), size)

        source = halves[2 + i].at[pl.ds(half - REST_SLOT, REST_SLOT)]
        pieces.append((source, part_ref.at[rows(0, 1, REST_SLOT)]))
        pieces.append((halves[4 + i], part_ref.at[rows(2 * REST_SLOT, 2, half)]))
        pieces.append((halves[6 + i], swap_ref.at[rows(0, 2, half)]))
        pieces.append((halves[i].at[pl.ds(0, 16)], first_ref.at[rows(0, 0, 16)]))
    parts = load_parts(pieces, part_sem)

    @pl.when(core_ref[0] == 0)
    def _():
        def stage(c):
            values = []
            for t in range(Q_TILES):
                rows = pl.ds(pl.multiple_of(REST + t * D + c * 64, 16), 64)
                values.append(part_ref[rows, :].astype(F32))
            put_wide(flat, tmp, values, 64, FLAT_BASE)

        def gradient(c, start, count):
            return flat[pl.ds(pl.multiple_of(FLAT_BASE + start, 8), count), :]

        chunks = Chunks(CHUNK // 2, O_ROW, 9, rule, refs)
        late_refs = (ins, outs, late_in, late_out, late_in_sem, late_out_sem)
        late_chunks = Chunks(CHUNK, 0, LATE_CHUNKS, rule, late_refs)
        pieces = [
            (ref, late_ref.at[pl.ds(i * LATE_HALF, LATE_HALF)]) for i, ref in enumerate(late_halves)
        ]
        chunks.start()
        late_parts = load_parts(pieces, late_sem)
        late_chunks.start()
        late_last.start()
        for copy in parts:
            copy.wait()
        drain = chunks.run(stage, gradient)
        for copy in late_parts:
            copy.wait()
        lay_out_late(late_flat, tmp, late_ref)

        def late_gradient(c, start, count):
            return late_flat[pl.ds(pl.multiple_of(c * CHUNK + start, 8), count), :]

        late_drain = late_chunks.run(lambda c: None, late_gradient)
        start = LATE_CHUNKS * CHUNK
        late_last.finish(late_flat[start : start + 304, :], rule)
        drain()
        late_drain()
        late_last.drain()

    @pl.when(core_ref[0] == 1)
    def _():
        head.start()
        chunks = Chunks(CHUNK, 6916, 11, rule, refs)
        chunks.start()
        tail.start()
        for copy in parts:
            copy.wait()
        flat[0:FLAT_BASE, :] = jnp.zeros((FLAT_BASE, LANES), F32)
        flat[FLAT_BASE : FLAT_BASE + 8, :] = swap_ref[SWAP_TAIL : SWAP_TAIL + 16, :].astype(F32)[0:8]
        flat[FLAT_BASE + 5 : FLAT_BASE + 6, :] = first_ref[0:16, :].astype(F32)[0:1]
        head.finish(shifted(flat, FLAT_BASE + 1, 8), rule)
        row = FLAT_BASE + CHUNK - 1
        flat[row : row + 1, :] = part_ref[REST - 16 : REST, :].astype(F32)[15:16]

        def stage(c):
            flat[FLAT_BASE - 1 : FLAT_BASE, :] = flat[FLAT_BASE + CHUNK - 1 : FLAT_BASE + CHUNK, :]
            inside = c < DOWN_FIRST
            here = pl.ds(pl.multiple_of(SWAP_START + jnp.where(inside, c, 0) * D, 16), D)
            there = pl.ds(pl.multiple_of(REST + jnp.where(inside, 0, c - DOWN_FIRST) * D, 16), D)
            whole = jnp.where(inside, swap_ref[here, :].astype(F32), part_ref[there, :].astype(F32))
            pieces = [whole[i * LANES : (i + 1) * LANES].T for i in range(4)]
            half = jnp.concatenate([whole[4 * LANES :], jnp.zeros((LANES - HD, LANES), F32)], axis=0)
            put_wide(flat, tmp, pieces + [half.T], LANES, FLAT_BASE)

        def gradient(c, start, count):
            return shifted(flat, FLAT_BASE + start, count)

        drain = chunks.run(stage, gradient)
        stage(11)
        flat[FLAT_BASE + CHUNK :, :] = jnp.zeros((8, LANES), F32)
        tail.finish(shifted(flat, FLAT_BASE, CHUNK + 8), rule)
        head.drain()
        drain()
        tail.drain()


def vmem():
    return pl.BlockSpec(memory_space=pltpu.VMEM)


def smem():
    return pl.BlockSpec(memory_space=pltpu.SMEM)


def hbm():
    return pl.BlockSpec(memory_space=pl.ANY)


def call(kernel, outs, in_specs, out_specs, scratch, flops, name, limit, aliases=None):
    n_bytes = sum(math.prod(shape) * jnp.dtype(kind).itemsize for shape, kind in outs)
    return pl.pallas_call(
        kernel,
        out_shape=[jax.ShapeDtypeStruct(shape, kind) for shape, kind in outs],
        in_specs=in_specs,
        out_specs=out_specs,
        scratch_shapes=scratch,
        input_output_aliases=aliases or {},
        compiler_params=pltpu.CompilerParams(vmem_limit_bytes=limit * MIB),
        cost_estimate=pl.CostEstimate(
            flops=int(flops), bytes_accessed=int(2 * n_bytes), transcendentals=0
        ),
        name=name,
    )


def rope_tables(seq_len):
    lane = jnp.arange(LANES, dtype=jnp.int32)
    which = (lane % (HD // 2)).astype(F32)
    frequency = jnp.exp(which * (-2.0 * math.log(10000.0) / HD))
    angles = jnp.arange(seq_len, dtype=F32)[:, None] * frequency[None, :]
    sign = jnp.where(lane % HD < HD // 2, -1.0, 1.0)
    return jnp.cos(angles), jnp.sin(angles) * sign[None, :]


def run_prepare(core, own, other):
    outs = [
        ((1, D), F32),
        ((1, D), F32),
        ((D, PAD_D), BF),
        ((D, KV_COLS), BF),
        ((PAD_D, D), BF),
        ((D, FF), BF),
        ((D, FF), BF),
        ((FF, D), BF),
    ]
    scratch = [
        pltpu.VMEM((HALF,), F32),
        pltpu.VMEM((HALF,), F32),
        pltpu.VMEM((FLAT_SCRATCH, LANES), F32),
        pltpu.VMEM((Q_TILES * D + 8, LANES), F32),
        pltpu.VMEM((8 * LANES,), F32),
        pltpu.SemaphoreType.DMA((2,)),
    ]
    return call(
        prepare_weights,
        outs,
        [smem()] + [hbm()] * 2,
        [vmem()] * 8,
        scratch,
        1e10,
        "prepare_weights",
        56,
    )(core, own, other)


def run_attention_forward(x, gain, wq, wkv, wo, cosine, sine):
    seq_len = x.shape[0]
    outs = [
        ((seq_len, D), F32),
        ((seq_len, PAD_D), BF),
        ((Q_TILES, seq_len, LANES), BF),
        ((6, seq_len, LANES), BF),
        ((6, seq_len, LANES), BF),
        ((16, seq_len), F32),
    ]
    return call(
        attention_forward,
        outs,
        [vmem()] * 4 + [hbm()] + [vmem()] * 2,
        [hbm()] * 5 + [vmem()],
        [pltpu.VMEM(shape, kind) for shape, kind in outs[:5]]
        + [
            pltpu.VMEM((PAD_D, D), BF),
            pltpu.VMEM((Q_TILES, BLOCK, LANES), F32),
            pltpu.SemaphoreType.DMA((4,)),
            pltpu.SemaphoreType.DMA((seq_len // BLOCK, 2)),
        ],
        1.5e10,
        "attention_forward",
        56,
    )(x, gain, wq, wkv, wo, cosine, sine)


def run_mlp(core, slot, lengths, assignment, return_order, hidden1, cot, mixed, gain, wo, wg, wu, wd):
    seq_len = hidden1.shape[0]
    outs = [
        ((seq_len, D), BF),
        ((seq_len, D), F32),
        ((Q_TILES, seq_len, LANES), BF),
        ((1, D), F32),
        ((EARLY_ROWS, LANES), BF),
        ((EARLY_ROWS, LANES), BF),
    ]
    return call(
        mlp_pass,
        outs,
        [smem()] * 5 + [hbm()] * 3 + [vmem()] + [hbm()] * 4,
        [hbm()] * 3 + [vmem()] + [hbm()] * 2,
        [
            pltpu.VMEM((seq_len, D), F32),
            pltpu.VMEM((seq_len, D), BF),
            pltpu.VMEM((seq_len, PAD_D), BF),
            pltpu.VMEM((PAD_D, D), BF),
            pltpu.VMEM((D, FF), BF),
            pltpu.VMEM((D, FF), BF),
            pltpu.VMEM((FF, D), BF),
            pltpu.VMEM((seq_len, D), BF),
            pltpu.VMEM((seq_len, D), F32),
            pltpu.VMEM((Q_TILES, seq_len, LANES), BF),
            pltpu.VMEM((PAD_D, seq_len), BF),
            pltpu.VMEM((PAD_D, seq_len), BF),
            pltpu.VMEM((seq_len, FF), BF),
            pltpu.VMEM((seq_len, FF), BF),
            pltpu.VMEM((seq_len, FF), BF),
            pltpu.VMEM((seq_len, D), BF),
            pltpu.VMEM((2, EARLY_ROWS, LANES), BF),
            pltpu.SemaphoreType.DMA((7,)),
            pltpu.SemaphoreType.DMA((seq_len // MLP_BLOCK, 3)),
            pltpu.SemaphoreType.DMA((FF_TILES // 2 + 1, 2)),
        ],
        2.5e10,
        "mlp_pass",
        56,
    )(core, slot, lengths, assignment, return_order, hidden1, cot, mixed, gain, wo, wg, wu, wd)


def run_backward_groups(first, count, q, dm, k, v, lse):
    seq_len = q.shape[1]
    fixed = pl.BlockSpec((Q_TILES, seq_len, LANES), lambda i: (0, 0, 0))
    sides = pl.BlockSpec((2, seq_len, LANES), lambda i: (first + i, 0, 0))
    single = pl.BlockSpec((1, seq_len, LANES), lambda i: (i, 0, 0))
    outs = [(count, 2, seq_len, LANES), (count, seq_len, LANES), (count, seq_len, LANES)]
    return pl.pallas_call(
        functools.partial(backward_groups, first),
        grid=(count,),
        out_shape=[jax.ShapeDtypeStruct(shape, F32) for shape in outs],
        in_specs=[
            fixed,
            fixed,
            sides,
            sides,
            pl.BlockSpec((16, seq_len), lambda i: (0, 0)),
        ],
        out_specs=[
            pl.BlockSpec((1, 2, seq_len, LANES), lambda i: (i, 0, 0, 0)),
            single,
            single,
        ],
        scratch_shapes=[pltpu.VMEM((2, seq_len, LANES), F32)] * 2,
        compiler_params=pltpu.CompilerParams(vmem_limit_bytes=56 * MIB),
        cost_estimate=pl.CostEstimate(
            flops=int(8e9) * count, bytes_accessed=int(3e6) * count, transcendentals=0
        ),
        name="backward_groups",
    )(q, dm, k, v, lse)


def run_backward_finish(x, gain, dh1, groups, wq, wkv, cosine, sine):
    seq_len = x.shape[0]
    outs = [
        ((seq_len, D), BF),
        ((seq_len, PAD_D), BF),
        ((seq_len, KV_COLS), BF),
        ((seq_len, D), BF),
        ((1, D), F32),
    ]
    return call(
        backward_finish,
        outs,
        [hbm(), vmem()] + [hbm()] * 7 + [vmem()] * 2 + [hbm()] * 2,
        [hbm()] * 4 + [vmem()],
        [
            pltpu.VMEM(value.shape, value.dtype)
            for value in (x, dh1, cosine, sine, *groups[0], *groups[1])
        ]
        + [pltpu.VMEM(shape, kind) for shape, kind in outs[:4]]
        + [
            pltpu.SemaphoreType.DMA((seq_len // BLOCK, 10)),
            pltpu.SemaphoreType.DMA((seq_len // BLOCK, 4)),
        ],
        4e9,
        "backward_finish",
        56,
    )(x, gain, dh1, *groups[0], *groups[1], wq, wkv, cosine, sine)


def run_late_weights(core, normed, d_query, d_kv, gga, ggm):
    outs = [((LATE_HALF, LANES), BF), ((LATE_HALF, LANES), BF)]
    return call(
        late_weights,
        outs,
        [smem()] + [vmem()] * 5,
        [hbm()] * 2,
        [pltpu.VMEM((2 * LATE_HALF, LANES), BF), pltpu.SemaphoreType.DMA((2,))],
        4e9,
        "late_weights",
        56,
    )(core, normed, d_query, d_kv, gga, ggm)


def run_sum(bits, kept, got, split, merge=False, n_parts=None):
    joined = n_parts is not None
    n_parts = n_parts or len(kept)
    rows = kept[0].shape[0] // (n_parts if joined else 1)
    kinds = 2 if split else 1
    n_out = 1 if merge else n_parts
    out_rows = rows // kinds * (n_parts if merge else 1)
    results = call(
        functools.partial(
            gather_sum, n_parts=n_parts, rows=rows, split=split, merge=merge, joined=joined
        ),
        [((out_rows, LANES), BF)] * (kinds * n_out),
        [smem()] + [vmem()] * (2 * len(kept)),
        [hbm()] * (kinds * n_out),
        [pltpu.VMEM((n_parts, rows, LANES), BF), pltpu.SemaphoreType.DMA((2 * n_parts,))],
        1e6,
        "gather_sum",
        12,
    )(bits, *kept, *got)
    return list(results[:n_out]), list(results[n_out:])


def run_join(bits, own, got, n_parts):
    merged = len(own) < n_parts
    rows = own[0].shape[0] // (n_parts if merged else 1)
    return call(
        functools.partial(join_halves, n_parts=n_parts, rows=rows, merged=merged),
        [((2 * rows, LANES), BF)] * n_parts,
        [smem()] + [hbm()] * (2 * len(own)),
        [hbm()] * n_parts,
        [pltpu.SemaphoreType.DMA((2 * n_parts,))],
        1e6,
        "join_halves",
        4,
    )(bits, *own, *got)


def run_copy(value):
    outs = [(value.shape, value.dtype)]
    scratch = [pltpu.SemaphoreType.DMA]
    return call(copy_array, outs, [hbm()], [hbm()], scratch, 1e6, "copy_array", 4)(value)[0]


def chunk_scratch(count):
    return [
        pltpu.VMEM((3 * count * CHUNK * LANES,), F32),
        pltpu.VMEM((4 * count * CHUNK * LANES,), F32),
        pltpu.SemaphoreType.DMA((12, 3)),
        pltpu.SemaphoreType.DMA((12, 4)),
    ]


def extra_scratch(count, n_rows):
    bufs = [pltpu.VMEM((count,), F32)] * 7 + [pltpu.VMEM((n_rows * LANES,), F32)]
    return bufs + [pltpu.SemaphoreType.DMA((7,))]


def run_update_first(scale, rate, core, bits, halves, state):
    scratch = [
        pltpu.VMEM((2 * PART_ROWS, LANES), BF),
        pltpu.VMEM((FLAT_BASE + CHUNK + 16, LANES), F32),
        *chunk_scratch(12),
        pltpu.SemaphoreType.DMA((4,)),
        *extra_scratch(TAIL_ZERO, CHUNK),
    ]
    return call(
        functools.partial(update_first, scale, rate),
        [(state[0].shape, F32)] * 4,
        [smem()] * 2 + [hbm()] * 7,
        [hbm()] * 4,
        scratch,
        1e9,
        "update_first",
        56,
    )(core, bits, *halves, *state)


def run_update_second(scale, rate, core, bits, halves, late_halves, state, done):
    scratch = [
        pltpu.VMEM((FLAT_BASE + CHUNK + 8, LANES), F32),
        pltpu.VMEM((Q_TILES * D + 8, LANES), F32),
        pltpu.VMEM((2 * REST_SLOT + PART_ROWS, LANES), BF),
        pltpu.VMEM((PART_ROWS, LANES), BF),
        pltpu.VMEM((32, LANES), BF),
        *chunk_scratch(11),
        pltpu.SemaphoreType.DMA((8,)),
        *extra_scratch(TAIL_ONE, CHUNK + 8),
        *extra_scratch(5 * LANES, 8),
        pltpu.VMEM((4336, LANES), F32),
        pltpu.VMEM((2 * LATE_HALF, LANES), BF),
        *chunk_scratch(LATE_CHUNKS),
        pltpu.SemaphoreType.DMA((2,)),
        *extra_scratch((O_ROW - LATE_CHUNKS * CHUNK) * LANES, 304),
    ]
    return call(
        functools.partial(update_second, scale, rate),
        [(state[0].shape, F32)] * 4,
        [smem()] * 2 + [hbm()] * 17,
        [hbm()] * 4,
        scratch,
        1e9,
        "update_second",
        56,
        {15 + i: i for i in range(4)},
    )(core, bits, *halves, *late_halves, *state, *done)


def add_low(a, b):
    return (a.astype(F32) + b.astype(F32)).astype(BF)


def xor_swap(value, bit):
    size = lax.axis_size("dp")
    return lax.ppermute(value, "dp", [(i, i ^ (1 << bit)) for i in range(size)])


def tie(value, *others):
    return lax.optimization_barrier((value, *others))


def my_bits(orders, step):
    index = lax.axis_index("dp")
    return jnp.stack([(index >> order[step]) & 1 for order in orders]).astype(jnp.int32)


def near_size():
    return min(lax.axis_size("dp"), 4)


def spread(blocks):
    size, near = lax.axis_size("dp"), near_size()
    groups = [[g * near + i for i in range(near)] for g in range(size // near)]
    return lax.all_to_all(
        blocks, "dp", split_axis=0, concat_axis=0, tiled=True, axis_index_groups=groups
    )


def scatter_sum(value):
    count = near_size()
    blocks = spread(value.reshape(count, value.shape[0] // count, LANES))
    return jnp.sum(blocks.astype(F32), axis=0).astype(BF)


def bit_orders():
    n_bits = lax.axis_size("dp").bit_length() - 1
    base = list(range(n_bits))
    head = base[:3] if n_bits >= 3 else base
    return [head[r:] + head[:r] + base[len(head) :] for r in range(3)]


def on_device(inputs, cotangent, lengths, assignment, return_order, master, momentum, average):
    nseq_all, block_rows, _ = inputs.shape
    axes = ("dp", "shard")
    seq_len = block_rows * lax.axis_size("dp") * lax.axis_size("shard")
    my_slot = lax.axis_index(axes)
    core = lax.axis_index("shard")
    core_arr = core.astype(jnp.int32).reshape(1)

    seq_ids = jnp.arange(nseq_all, dtype=jnp.int32)
    sequence = jnp.sum(
        jnp.where(return_order[:, None] == seq_ids[None, :], assignment[None, :], 0), axis=1
    )

    def pick(array, index):
        return array.at[index].get(mode="promise_in_bounds")

    def exchange(value):
        return lax.all_to_all(value, axes, split_axis=0, concat_axis=0, tiled=True)

    x = exchange(pick(inputs, sequence)).reshape(seq_len, D)
    slot_arr = my_slot.astype(jnp.int32).reshape(1)

    other = lax.ppermute(master, "shard", [(0, 1), (1, 0)])
    gain_attn, gain_mlp, wq, wkv, wo, wg, wu, wd = run_prepare(core_arr, master, other)

    cosine, sine = rope_tables(seq_len)
    sent_cot, gain_attn, cosine = tie(cotangent, gain_attn, cosine)
    cot = exchange(sent_cot).reshape(seq_len, D)
    hidden1, mixed, q, k, v, lse = run_attention_forward(x, gain_attn, wq, wkv, wo, cosine, sine)
    result, dh1, dm, ggm, early_keep, early_send = run_mlp(
        core_arr, slot_arr, lengths, assignment, return_order, hidden1, cot, mixed, gain_mlp, wo, wg, wu, wd
    )
    back_out = exchange(result.reshape(nseq_all, block_rows, D))

    orders = bit_orders()
    n_bits = len(orders[0])

    def swap_parts(parts, step):
        return [xor_swap(part, order[step]) for part, order in zip(parts, orders)]

    got = lax.ppermute(early_send, "shard", [(0, 1), (1, 0)])
    groups = [run_backward_groups(0, 1, q, dm, k, v, lse)]
    lse, got = tie(lse, got)
    sent, kept = run_sum(my_bits(orders, 0), [early_keep], [got], True, n_parts=3)
    lse, *kept = tie(lse, *kept)
    got = swap_parts(sent, 0)
    groups.append(run_backward_groups(1, KV - 1, q, dm, k, v, lse))
    sent, kept = run_sum(my_bits(orders, 1), kept, got, True)
    dh1, back_out, *kept = tie(dh1, back_out, *kept)
    got = swap_parts(sent, 1)
    d_stream, d_query, d_kv, normed, gga = run_backward_finish(
        x, gain_attn, dh1, groups, wq, wkv, cosine, sine
    )
    last_bit = n_bits - 1
    for step in range(2, n_bits):
        if step > 2:
            got = swap_parts(sent, step - 1)
        sent, kept = run_sum(my_bits(orders, step), kept, got, True, merge=step == last_bit)
        if step == 2:
            gga, *kept = tie(gga, *kept)
            late_keep, late_send = run_late_weights(core_arr, normed, d_query, d_kv, gga, ggm)
            late_send, *kept = tie(late_send, *kept)
        if step == last_bit:
            late_send, sent[0] = tie(late_send, sent[0])
    got = [xor_swap(sent[0], last_bit)]
    late_got = lax.ppermute(late_send, "shard", [(0, 1), (1, 0)])
    late, _ = run_sum(my_bits(orders, 0)[:1], [late_keep], [late_got], False)
    late, block_output, *got = tie(late[0], run_copy(back_out), *got)
    early, _ = run_sum(my_bits(orders, last_bit)[:1], kept, got, False)
    late = scatter_sum(late)
    got = xor_swap(early[0], last_bit)
    late, got = tie(late, got)
    early = run_join(my_bits(orders, last_bit), early, [got], 3)
    far_bits = list(range(near_size().bit_length() - 1, n_bits))

    def add_far(late, early):
        late, *early = tie(late, *early)
        return add_low(late, xor_swap(late, far_bits.pop(0))), early

    for step in reversed(range(1, last_bit)):
        if far_bits:
            late, early = add_far(late, early)
        got = swap_parts(early, step)
        late, *got = tie(late, *got)
        early = run_join(my_bits(orders, step), early, got, 3)
    while far_bits:
        late, early = add_far(late, early)
    late, *early = tie(late, *early)
    late = spread(jnp.broadcast_to(late[None], (near_size(), *late.shape))).reshape(-1, LANES)
    got = swap_parts(early, 0)
    swap_own = lax.ppermute(early[2], "shard", [(0, 1)])
    bits = my_bits(orders, 0)
    scale = 1.0 / nseq_all
    rate = (nseq_all / (0.6 * seq_len)) ** 0.5 / D**0.5
    state = (master, momentum, average)
    d_stream, late, swap_own, *got = tie(d_stream, late, swap_own, *got)
    back_grad = exchange(d_stream.reshape(nseq_all, block_rows, D))
    late_other = lax.ppermute(late, "shard", [(1, 0)])
    swap_got = lax.ppermute(got[2], "shard", [(0, 1)])
    halves = [early[0], got[0], early[1], got[1], early[2], got[2], swap_own, swap_got]
    done = run_update_first(scale, rate, core_arr, bits, halves[:4], state)
    weight_grad, new_momentum, new_master, new_average = run_update_second(
        scale, rate, core_arr, bits, halves, (late, late_other), state, done
    )
    return (block_output, back_grad, weight_grad, new_momentum, new_master, new_average)


def solution(mesh):
    rows = P(None, ("dp", "shard"), None)
    flat = P("shard")
    return jax.shard_map(
        on_device,
        mesh=mesh,
        in_specs=(rows, rows, P(), P(), P(), flat, flat, flat),
        out_specs=(rows, rows, flat, flat, flat, flat),
        check_vma=False,
    )
```

```python
import functools
import math

import jax
import jax.numpy as jnp
from jax import lax
from jax.experimental import pallas as pl
from jax.experimental.pallas import tpu as pltpu
from jax.sharding import PartitionSpec as P

D = 576
H = 9
KV = 3
HD = 64
FF = 1536
LANES = 128
BLOCK = 256
Q_TILES = 5
PAD_D = Q_TILES * LANES
KV_COLS = 2 * KV * HD
FF_TILES = FF // LANES
DOWN_FIRST = 4
EARLY_TILES = 21
EARLY_ROWS = 12288
EXTRA = EARLY_TILES * D
HALF = 27657 * LANES // 2
PART_ROWS = EARLY_ROWS // 3
SWAP_START = EXTRA - DOWN_FIRST * D - 2 * PART_ROWS
SWAP_TAIL = EXTRA + 16 - 2 * PART_ROWS
REST_FIRST = 2 * PART_ROWS - FF_TILES * D
REST_SLOT = REST_FIRST + 16
REST = REST_SLOT + 16
LATE_HALF = 2432
FLAT_SCRATCH = 13848
O_ROW = 4329
GATE_ROW = 6921
MLP_COLS = 256
WIDEN = 512
MLP_UNROLL = 6
MLP_BLOCK = 256
CHUNK = 576
STEP = 288
LATE_CHUNKS = 7

EPSILON = 1e-05
MOMENTUM_DECAY = 0.55
AVERAGE_DECAY = 0.45
MASKED = -1000000000.0

BF = jnp.bfloat16
F32 = jnp.float32
MIB = 1024 * 1024


def nn(a, b):
    return jnp.dot(a, b, preferred_element_type=F32)


def nt(a, b):
    return lax.dot_general(a, b, (((1,), (1,)), ((), ())), preferred_element_type=F32)


def tn(a, b):
    return lax.dot_general(a, b, (((0,), (0,)), ((), ())), preferred_element_type=F32)


def tile(value, index):
    return value[:, index * LANES : (index + 1) * LANES]


def low_half(rows):
    return lax.broadcasted_iota(jnp.int32, (rows, LANES), 1) < HD


def swap_halves(value):
    lane = lax.broadcasted_iota(jnp.int32, value.shape, 1)
    return jnp.where(lane % HD < HD // 2, pltpu.roll(value, 96, 1), pltpu.roll(value, 32, 1))


def flip(value):
    return pltpu.roll(value, HD, 1)


def rms(value):
    return lax.rsqrt(jnp.mean(value * value, axis=-1, keepdims=True) + EPSILON)


def attention_forward(
    x_ref, ga_ref, wq_ref, wkv_ref, wo_hbm, cos_ref, sin_ref,
    h1_hbm, mixed_hbm, q_hbm, k_hbm, v_hbm, lse_ref,
    h1_ref, mixed_ref, q_ref, k_ref, v_ref, wo_ref, o_acc, sem, block_sem,
):
    seq_len = x_ref.shape[0]
    low = low_half(BLOCK)

    def project(b, carry):
        rows = pl.ds(pl.multiple_of(b * BLOCK, BLOCK), BLOCK)
        stream = x_ref[rows, :].astype(F32)
        normed = (stream * rms(stream) * ga_ref[...]).astype(BF)
        cosine = cos_ref[rows, :]
        sine = sin_ref[rows, :]

        def rope(value):
            return value * cosine + swap_halves(value) * sine

        queries = nn(normed, wq_ref[...])
        for j in range(Q_TILES):
            q_ref[j, rows, :] = (rope(tile(queries, j)) * HD ** (-0.5)).astype(BF)
        keys_values = nn(normed, wkv_ref[...])
        first = rope(tile(keys_values, 0))
        second = tile(keys_values, 1)
        third = tile(keys_values, 2)
        mid = rope(second)

        def put(ref, index, value):
            ref[index, rows, :] = value.astype(BF)

        put(k_ref, 0, jnp.where(low, first, 0.0))
        put(k_ref, 1, jnp.where(low, 0.0, flip(first)))
        put(k_ref, 2, jnp.where(low, flip(first), 0.0))
        put(k_ref, 3, jnp.where(low, 0.0, first))
        put(k_ref, 4, jnp.where(low, mid, 0.0))
        put(k_ref, 5, jnp.where(low, 0.0, flip(mid)))
        put(v_ref, 0, jnp.where(low, flip(second), 0.0))
        put(v_ref, 1, jnp.where(low, 0.0, second))
        put(v_ref, 2, jnp.where(low, third, 0.0))
        put(v_ref, 3, jnp.where(low, 0.0, flip(third)))
        put(v_ref, 4, jnp.where(low, flip(third), 0.0))
        put(v_ref, 5, jnp.where(low, 0.0, third))
        return carry

    load = pltpu.make_async_copy(wo_hbm, wo_ref, sem.at[3])
    load.start()
    lax.fori_loop(0, seq_len // BLOCK, project, 0)
    stores = [
        pltpu.make_async_copy(source, target, sem.at[i])
        for i, (source, target) in enumerate(((q_ref, q_hbm), (k_ref, k_hbm), (v_ref, v_hbm)))
    ]
    for copy in stores:
        copy.start()
    lane = lax.broadcasted_iota(jnp.int32, (BLOCK, LANES), 1)
    keep = lax.broadcasted_iota(jnp.int32, (BLOCK, BLOCK), 1) <= lax.broadcasted_iota(
        jnp.int32, (BLOCK, BLOCK), 0
    )
    for b in range(seq_len // BLOCK):
        rows = slice(b * BLOCK, (b + 1) * BLOCK)
        n_keys = (b + 1) * BLOCK
        o_acc[...] = jnp.zeros_like(o_acc)

        def group(g, lse, rows=rows, n_keys=n_keys):
            for u in range(3):
                head = 3 * g + u
                j = head // 2
                side = 2 * g + head % 2
                scores = nt(q_ref[j, rows, :], k_ref[side, 0:n_keys, :])
                diag = jnp.where(keep, scores[:, n_keys - BLOCK :], MASKED)
                if n_keys > BLOCK:
                    scores = jnp.concatenate([scores[:, : n_keys - BLOCK], diag], axis=1)
                else:
                    scores = diag
                row_max = jnp.max(scores, axis=-1, keepdims=True)
                exponent = jnp.exp(scores - row_max)
                total = jnp.sum(exponent, axis=-1, keepdims=True)
                mixed = nn(exponent.astype(BF), v_ref[side, 0:n_keys, :])
                o_acc[j] += mixed * (1.0 / total)
                lse = jnp.where(lane == head, row_max + jnp.log(total), lse)
            return lse

        lse = lax.fori_loop(0, KV, group, jnp.zeros((BLOCK, LANES), F32))
        lse_ref[:, rows] = lse.T[:16]
        mixed = jnp.concatenate([o_acc[j].astype(BF) for j in range(Q_TILES)], axis=1)
        mixed_ref[rows, :] = mixed
        if b == 0:
            load.wait()
        h1_ref[rows, :] = x_ref[rows, :].astype(F32) + nn(mixed, wo_ref[...])
        for i, (source, target) in enumerate(((mixed_ref, mixed_hbm), (h1_ref, h1_hbm))):
            stores.append(
                pltpu.make_async_copy(source.at[rows], target.at[rows], block_sem.at[b, i])
            )
            stores[-1].start()
    for copy in stores:
        copy.wait()


def prepare_weights(
    core_ref, own_ref, other_ref,
    ga_ref, gm_ref, wq_ref, wkv_ref, wo_ref, wg_ref, wu_ref, wd_ref,
    first, second, flat, tmp, rest, sem,
):
    core = core_ref[0]
    for which, pair in enumerate(((first, second), (second, first))):

        @pl.when(core == which)
        def _(pair=pair):
            copies = [
                pltpu.make_async_copy(ref, target, sem.at[i])
                for i, (ref, target) in enumerate(zip((own_ref, other_ref), pair))
            ]
            for copy in copies:
                copy.start()
            for copy in copies:
                copy.wait()

    def widen(ref):
        def body(i, carry):
            start = pl.multiple_of(i * WIDEN, WIDEN)
            span = pl.ds(pl.multiple_of(i * WIDEN * LANES, WIDEN * LANES), WIDEN * LANES)
            flat[pl.ds(start, WIDEN), :] = ref[span].reshape(WIDEN, LANES)
            return carry

        whole = HALF // (WIDEN * LANES)
        lax.fori_loop(0, whole, body, 0)
        left = HALF - whole * WIDEN * LANES
        rest[pl.ds(0, left)] = ref[pl.ds(whole * WIDEN * LANES, left)]
        flat[whole * WIDEN : whole * WIDEN + 8, :] = rest[...].reshape(8, LANES)

    def low_precision(value):
        return value.astype(BF).astype(F32)

    def interleave(even, odd, pairs, out_ref, first_row, pad):
        low = low_half(2 * pairs)
        for t in range(Q_TILES):
            tmp[pl.ds(t * D, pairs, stride=2), :] = even[t]
            tmp[pl.ds(t * D + 1, pairs, stride=2), :] = odd[t]
        rows = pl.ds(first_row, 2 * pairs)
        for t in range(Q_TILES):
            value = tmp[t * D : t * D + 2 * pairs, :]
            if t < 4:
                out_ref[rows, t * LANES : (t + 1) * LANES] = value.astype(BF)
            elif pad:
                out_ref[rows, t * LANES :] = jnp.where(low, value, 0.0).astype(BF)
            else:
                out_ref[rows, t * LANES :] = value[:, :HD].astype(BF)

    def wide(row, out_ref, pad):
        pairs = D // 2
        low = low_half(pairs)
        cols = [flat[pl.ds(row + c, pairs, stride=9), :] for c in range(9)]
        turned = [flip(cols[c]) for c in range(4, 9)]
        odd = [jnp.where(low, turned[t], turned[t + 1]) for t in range(4)] + [turned[4]]
        interleave(cols[:5], odd, pairs, out_ref, 0, pad)

    widen(first)
    low1 = low_half(1)
    turned = [flip(flat[4 + r : 5 + r, :]) for r in range(5)]
    for r in range(4):
        ga_ref[:, r * LANES : (r + 1) * LANES] = low_precision(flat[r : r + 1, :])
        gm_ref[:, r * LANES : (r + 1) * LANES] = low_precision(
            jnp.where(low1, turned[r], turned[r + 1])
        )
    ga_ref[:, 4 * LANES :] = low_precision(flat[4:5, :HD])
    gm_ref[:, 4 * LANES :] = low_precision(turned[4][:, :HD])
    wide(9, wq_ref, True)
    wide(O_ROW, wo_ref, False)
    wo_ref[D:, :] = jnp.zeros((PAD_D - D, D), BF)
    pairs = D // 2
    low = low_half(pairs)
    narrow = []
    for row in (2601, 3465):
        cols = [flat[pl.ds(row + c, pairs, stride=3), :] for c in range(3)]
        turned = [flip(cols[1]), flip(cols[2])]
        even = cols[:2]
        odd = [jnp.where(low, turned[0], turned[1]), turned[1]]
        for t in range(2):
            tmp[pl.ds(t * D, pairs, stride=2), :] = even[t]
            tmp[pl.ds(t * D + 1, pairs, stride=2), :] = odd[t]
        narrow.append((tmp[0:D, :], tmp[D : 2 * D, :]))
    (k0, k1), (v0, v1) = narrow
    low = low_half(D)
    v0 = flip(v0)
    v1 = flip(v1)
    wkv_ref[:, 0:LANES] = k0.astype(BF)
    wkv_ref[:, LANES : 2 * LANES] = jnp.where(low, k1, v0).astype(BF)
    wkv_ref[:, 2 * LANES :] = jnp.where(low, v0, v1).astype(BF)
    head = second[pl.ds(0, 1024)].reshape(8, LANES)
    turned = flip(head)
    for r in range(5):
        row = GATE_ROW + FF_TILES * (D - 1) + 7 + r
        before = flat[row : row + 1, :] if r == 0 else turned[r - 1 : r]
        flat[row : row + 1, :] = jnp.where(low1, before, turned[r : r + 1])
    for t in range(FF_TILES):
        wg_ref[:, t * LANES : (t + 1) * LANES] = flat[
            pl.ds(GATE_ROW + t, D, stride=FF_TILES), :
        ].astype(BF)
    widen(second)
    here = flip(flat[pl.ds(4, D, stride=FF_TILES), :])
    for t in range(FF_TILES):
        after = flip(flat[pl.ds(5 + t, D, stride=FF_TILES), :])
        wu_ref[:, t * LANES : (t + 1) * LANES] = jnp.where(low, here, after).astype(BF)
        here = after

    def down(i, carry):
        n_pairs = 96
        low = low_half(n_pairs)
        start = 6916 + 9 * n_pairs * i
        cols = [flat[pl.ds(start + c, n_pairs, stride=9), :] for c in range(10)]
        turned = [flip(cols[c]) for c in range(6)]
        even = [jnp.where(low, turned[c], turned[c + 1]) for c in range(5)]
        interleave(even, cols[5:], n_pairs, wd_ref, pl.multiple_of(2 * n_pairs * i, 16), False)
        return carry

    lax.fori_loop(0, FF // 192, down, 0)


def transposed(value):
    rows = value.shape[0]
    pieces = [tile(value, t) for t in range(4)]
    pieces.append(
        jnp.concatenate([value[:, 4 * LANES :], jnp.zeros((rows, LANES - HD), F32)], axis=1)
    )
    return jnp.concatenate([piece.T for piece in pieces], axis=0)


def mlp_pass(
    core_ref, slot_ref, lengths_ref, assignment_ref, return_ref,
    h1_hbm, cot_hbm, mixed_hbm, gm_ref, wo_hbm, wg_hbm, wu_hbm, wd_hbm,
    out_hbm, dh1_hbm, dm_hbm, ggm_ref, keep_ref, send_ref,
    h1_ref, cot_ref, mixed_ref, wo_ref, wg_ref, wu_ref, wd_ref, out_ref, dh1_ref, dm_ref,
    nmt_s, backt_s, inner_s, dg_s, du_s, da_s, grads, in_sem, out_sem, sem,
):
    seq_len = h1_ref.shape[0]
    core = core_ref[0]
    live_len = lengths_ref[assignment_ref[return_ref[slot_ref[0]]]]
    n_cols = FF // MLP_COLS
    loads = [
        pltpu.make_async_copy(source, target, in_sem.at[i])
        for i, (source, target) in enumerate(
            (
                (h1_hbm, h1_ref),
                (cot_hbm, cot_ref),
                (wg_hbm, wg_ref),
                (wu_hbm, wu_ref),
                (wd_hbm, wd_ref),
                (wo_hbm, wo_ref),
                (mixed_hbm, mixed_ref),
            )
        )
    ]
    for copy in loads:
        copy.start()
    for copy in loads[:6]:
        copy.wait()

    def results(b):
        rows = pl.ds(pl.multiple_of(b * MLP_BLOCK, MLP_BLOCK), MLP_BLOCK)
        pairs = [(out_ref.at[rows], out_hbm.at[rows]), (dh1_ref.at[rows], dh1_hbm.at[rows])]
        pairs.append((dm_ref.at[:, rows], dm_hbm.at[:, rows]))
        return [
            pltpu.make_async_copy(source, target, out_sem.at[b, i])
            for i, (source, target) in enumerate(pairs)
        ]

    def block(b, ggm):
        start = pl.multiple_of(b * MLP_BLOCK, MLP_BLOCK)
        rows = pl.ds(start, MLP_BLOCK)
        hidden1 = h1_ref[rows, :]
        r2 = rms(hidden1)
        gain = gm_ref[...]
        normed2_wide = hidden1 * r2 * gain
        normed2 = normed2_wide.astype(BF)
        nmt_s[:, rows] = transposed(normed2_wide).astype(BF)
        live = (
            start + lax.broadcasted_iota(jnp.int32, (MLP_BLOCK, 1), 0) < live_len
        ).astype(F32)

        back = cot_ref[rows, :].astype(F32) * live
        back_low = back.astype(BF)
        backt_s[:, rows] = transposed(back).astype(BF)
        def columns(c):
            cols = pl.ds(pl.multiple_of(c * MLP_COLS, MLP_COLS), MLP_COLS)
            gate = nn(normed2, wg_ref[:, cols])
            up = nn(normed2, wu_ref[:, cols])
            d_inner = nt(back_low, wd_ref[cols, :])
            sig = jax.nn.sigmoid(gate)
            silu = gate * sig
            inner_s[rows, cols] = (silu * up).astype(BF)
            dg_s[rows, cols] = (d_inner * up * sig * (1.0 + gate * (1.0 - sig))).astype(BF)
            du_s[rows, cols] = (d_inner * silu).astype(BF)

        def some_columns(i, carry):
            for c in range(MLP_UNROLL):
                columns(MLP_UNROLL * i + c)
            return carry

        lax.fori_loop(0, n_cols // MLP_UNROLL, some_columns, 0)
        out_ref[rows, :] = ((hidden1 + nn(inner_s[rows, :], wd_ref[...])) * live).astype(BF)
        d_normed2 = nt(dg_s[rows, :], wg_ref[...]) + nt(du_s[rows, :], wu_ref[...])
        scaled = d_normed2 * gain
        d_hidden1 = (
            back
            + r2 * scaled
            - hidden1 * (r2 * r2 * r2) * jnp.mean(scaled * hidden1, axis=-1, keepdims=True)
        )
        dh1_ref[rows, :] = d_hidden1
        d_attn = d_hidden1.astype(BF)
        da_s[rows, :] = d_attn

        d_mixed = nt(d_attn, wo_ref[...]).astype(BF)
        for j in range(Q_TILES):
            dm_ref[j, rows, :] = tile(d_mixed, j)
        for copy in results(b):
            copy.start()
        return ggm + jnp.sum(d_normed2 * hidden1 * r2, axis=0, keepdims=True)

    ggm_ref[...] = lax.fori_loop(0, seq_len // MLP_BLOCK, block, jnp.zeros((1, D), F32))

    def put(half, index, value):
        grads[half, pl.ds(pl.multiple_of(index * D, D), D), :] = value

    def leave(c):
        rows = pl.ds(pl.multiple_of(2 * c * D, D), 2 * D)
        return [
            pltpu.make_async_copy(grads.at[1 - core, rows], send_ref.at[rows], sem.at[c, 0]),
            pltpu.make_async_copy(grads.at[core, rows], keep_ref.at[rows], sem.at[c, 1]),
        ]

    def weights(c, carry):
        cols = pl.ds(pl.multiple_of(c * 2 * LANES, 2 * LANES), 2 * LANES)
        grad_gate = nn(nmt_s[:D, :], dg_s[:, cols]).astype(BF)
        grad_up = nn(nmt_s[:D, :], du_s[:, cols]).astype(BF)
        for t in range(2):
            put(0, 2 * c + t, tile(grad_gate, t))
            put(1, 2 * c + t, tile(grad_up, t))
        for copy in leave(c):
            copy.start()
        grad_down = nn(backt_s[:D, :], inner_s[:, cols]).astype(BF)
        part = jnp.where(c < DOWN_FIRST // 2, 0, 1)
        base = jnp.where(c < DOWN_FIRST // 2, FF_TILES + Q_TILES, FF_TILES - DOWN_FIRST)
        for t in range(2):
            put(part, base + 2 * c + t, tile(grad_down, t))
        return carry

    lax.fori_loop(0, n_cols, weights, 0)
    loads[6].wait()
    grad_o = tn(mixed_ref[...], da_s[...])[:D]
    for t in range(4):
        put(0, FF_TILES + t, tile(grad_o, t).astype(BF))
    put(0, FF_TILES + 4, half_tile(grad_o).astype(BF))
    grads[0, EXTRA:, :] = jnp.zeros((EARLY_ROWS - EXTRA, LANES), BF)
    grads[1, EXTRA - D :, :] = jnp.zeros((EARLY_ROWS - EXTRA + D, LANES), BF)
    row = lax.broadcasted_iota(jnp.int32, (16, LANES), 0)
    rest = jnp.zeros((16, LANES), F32)
    for r in range(5):
        start = (8 + r) * D - 16
        last = grads[0, start : start + 16, :].astype(F32)[15:16]
        rest = jnp.where(row == r, jnp.broadcast_to(last, (16, LANES)), rest)
    grads[0, EXTRA + 16 : EXTRA + 32, :] = rest.astype(BF)
    rows = pl.ds(FF_TILES * D, EARLY_ROWS - FF_TILES * D)
    final = [
        pltpu.make_async_copy(grads.at[1 - core, rows], send_ref.at[rows], sem.at[n_cols, 0]),
        pltpu.make_async_copy(grads.at[core, rows], keep_ref.at[rows], sem.at[n_cols, 1]),
    ]
    for copy in final:
        copy.start()

    def drain(c, carry):
        for copy in leave(c):
            copy.wait()
        return carry

    def drain_results(b, carry):
        for copy in results(b):
            copy.wait()
        return carry

    lax.fori_loop(0, n_cols, drain, 0)
    lax.fori_loop(0, seq_len // MLP_BLOCK, drain_results, 0)
    for copy in final:
        copy.wait()


def half_tile(value):
    rows = value.shape[0]
    return jnp.concatenate([value[:, 4 * LANES : D], jnp.zeros((rows, HD), value.dtype)], axis=1)


def gain_rows(value):
    row = lax.broadcasted_iota(jnp.int32, (16, LANES), 0)
    whole = jnp.zeros((16, LANES), F32)
    for t in range(Q_TILES):
        piece = tile(value, t) if t < 4 else half_tile(value)
        whole = jnp.where(row == t, jnp.broadcast_to(piece, (16, LANES)), whole)
    return whole


def backward_groups(
    first, q_ref, dm_ref, k_ref, v_ref, lse_ref, dq_ref, dk_ref, dv_ref, dk_acc, dv_acc
):
    seq_len = q_ref.shape[1]
    group = first + pl.program_id(0)
    dq_ref[...] = jnp.zeros_like(dq_ref)
    dk_acc[...] = jnp.zeros_like(dk_acc)
    dv_acc[...] = jnp.zeros_like(dv_acc)
    keep = lax.broadcasted_iota(jnp.int32, (BLOCK, BLOCK), 0) <= lax.broadcasted_iota(
        jnp.int32, (BLOCK, BLOCK), 1
    )
    for b in range(seq_len // BLOCK):
        rows = slice(b * BLOCK, (b + 1) * BLOCK)
        n_keys = (b + 1) * BLOCK
        for u in range(3):
            head = 3 * group + u
            j = lax.shift_right_logical(head, 1)
            own = j - lax.shift_right_logical(3 * group, 1)
            side = head - 2 * j
            queries = q_ref[j, rows, :]
            d_mixed = dm_ref[j, rows, :]
            keys = k_ref[side, 0:n_keys, :]
            values = v_ref[side, 0:n_keys, :]
            prob = jnp.exp(nt(keys, queries) - lse_ref[pl.ds(head, 1), rows])
            diag = jnp.where(keep, prob[n_keys - BLOCK :, :], 0.0)
            if n_keys > BLOCK:
                prob = jnp.concatenate([prob[: n_keys - BLOCK, :], diag], axis=0)
            else:
                prob = diag
            d_prob = nt(values, d_mixed)
            delta = jnp.sum(d_prob * prob, axis=0, keepdims=True)
            d_score = (prob * (d_prob - delta)).astype(BF)
            dv_acc[side, 0:n_keys, :] += nn(prob.astype(BF), d_mixed)
            dk_acc[side, 0:n_keys, :] += nn(d_score, queries)
            dq_ref[0, own, rows, :] += tn(d_score, keys)
    dk_ref[0] = dk_acc[0] + flip(dk_acc[1])
    dv_ref[0] = dv_acc[0] + flip(dv_acc[1])


def backward_finish(
    x_hbm, ga_ref, dh1_hbm, dqa_hbm, dka_hbm, dva_hbm, dqb_hbm, dkb_hbm, dvb_hbm,
    wq_ref, wkv_ref, cos_hbm, sin_hbm,
    dx_hbm, dq_hbm, dkv_hbm, nm_hbm, gga_ref,
    x_ref, dh1_ref, cos_ref, sin_ref, dqa_ref, dka_ref, dva_ref, dqb_ref, dkb_ref, dvb_ref,
    dx_ref, dq_s, dkv_s, nm_s, in_sem, out_sem,
):
    seq_len = x_ref.shape[0]
    low = low_half(BLOCK)

    def rows_of(ref, b):
        rows = pl.ds(pl.multiple_of(b * BLOCK, BLOCK), BLOCK)
        return ref.at[(slice(None),) * (len(ref.shape) - 2) + (rows,)]

    def moves(pairs, b, sem):
        return [
            pltpu.make_async_copy(rows_of(source, b), rows_of(target, b), sem.at[b, i])
            for i, (source, target) in enumerate(pairs)
        ]

    inward = (
        (x_hbm, x_ref), (dh1_hbm, dh1_ref), (cos_hbm, cos_ref), (sin_hbm, sin_ref),
        (dqa_hbm, dqa_ref), (dka_hbm, dka_ref), (dva_hbm, dva_ref),
        (dqb_hbm, dqb_ref), (dkb_hbm, dkb_ref), (dvb_hbm, dvb_ref),
    )
    outward = ((dx_ref, dx_hbm), (dq_s, dq_hbm), (dkv_s, dkv_hbm), (nm_s, nm_hbm))
    n_blocks = seq_len // BLOCK
    for b in range(n_blocks):
        for copy in moves(inward, b, in_sem):
            copy.start()

    def block(b, gga):
        for copy in moves(inward, b, in_sem):
            copy.wait()
        rows = pl.ds(pl.multiple_of(b * BLOCK, BLOCK), BLOCK)
        cosine = cos_ref[rows, :]
        sine = sin_ref[rows, :]

        def unrope(value):
            return value * cosine - swap_halves(value) * sine

        d_rot = [
            dqa_ref[0, 0, rows, :],
            dqa_ref[0, 1, rows, :] + dqb_ref[0, 0, rows, :],
            dqb_ref[0, 1, rows, :],
            dqb_ref[1, 0, rows, :],
            dqb_ref[1, 1, rows, :],
        ]
        for j in range(Q_TILES):
            d_query = unrope(d_rot[j]) * HD ** (-0.5)
            dq_s[rows, j * LANES : (j + 1) * LANES] = d_query.astype(BF)
        dk = [dka_ref[0, rows, :], dkb_ref[0, rows, :], dkb_ref[1, rows, :]]
        dv = [dva_ref[0, rows, :], dvb_ref[0, rows, :], dvb_ref[1, rows, :]]
        first = unrope(jnp.where(low, dk[0], flip(dk[1])))
        second = jnp.where(low, unrope(dk[2]), flip(dv[0]))
        third = jnp.where(low, dv[1], flip(dv[2]))
        dkv_s[rows, 0:LANES] = first.astype(BF)
        dkv_s[rows, LANES : 2 * LANES] = second.astype(BF)
        dkv_s[rows, 2 * LANES :] = third.astype(BF)
        d_normed = nt(dq_s[rows, :], wq_ref[...]) + nt(dkv_s[rows, :], wkv_ref[...])
        stream = x_ref[rows, :].astype(F32)
        r1 = rms(stream)
        gain = ga_ref[...]
        nm_s[rows, :] = (stream * r1 * gain).astype(BF)
        scaled = d_normed * gain
        dx_ref[rows, :] = (
            dh1_ref[rows, :]
            + r1 * scaled
            - stream * (r1 * r1 * r1) * jnp.mean(scaled * stream, axis=-1, keepdims=True)
        ).astype(BF)
        for copy in moves(outward, b, out_sem):
            copy.start()
        return gga + jnp.sum(d_normed * stream * r1, axis=0, keepdims=True)

    gga_ref[...] = lax.fori_loop(0, seq_len // BLOCK, block, jnp.zeros((1, D), F32))
    for b in range(n_blocks):
        for copy in moves(outward, b, out_sem):
            copy.wait()


def late_weights(
    core_ref, nm_s, dq_s, dkv_s, gga_ref, ggm_ref, keep_ref, send_ref, late, sem
):
    both = jnp.concatenate([dq_s[...], dkv_s[...]], axis=1)
    grads = tn(nm_s[...], both).astype(BF)
    grad_q = grads[:, :PAD_D]
    grad_kv = grads[:, PAD_D:]
    for t in range(Q_TILES):
        late[t * D : (t + 1) * D, :] = tile(grad_q, t)
    for t in range(3):
        late[(Q_TILES + t) * D : (Q_TILES + t + 1) * D, :] = tile(grad_kv, t)
    late[8 * D :, :] = jnp.zeros((2 * LATE_HALF - 8 * D, LANES), BF)
    late[8 * D : 8 * D + 16, :] = gain_rows(gga_ref[...]).astype(BF)
    late[8 * D + 16 : 8 * D + 32, :] = gain_rows(ggm_ref[...]).astype(BF)
    copies = []
    for i, (which, ref) in enumerate(((1 - core_ref[0], send_ref), (core_ref[0], keep_ref))):
        rows = pl.ds(pl.multiple_of(which * LATE_HALF, 8), LATE_HALF)
        copies.append(pltpu.make_async_copy(late.at[rows], ref, sem.at[i]))
    for copy in copies:
        copy.start()
    for copy in copies:
        copy.wait()


def gather_sum(bits_ref, *refs, n_parts, rows, split, merge, joined):
    n_in = 1 if joined else n_parts
    kept, got = refs[:n_in], refs[n_in : 2 * n_in]
    kinds = 2 if split else 1
    n_out = kinds * (1 if merge else n_parts)
    outs = refs[2 * n_in : 2 * n_in + n_out]
    scratch, sem = refs[2 * n_in + n_out :]
    size = rows // kinds
    copies = []
    for p in range(n_parts):
        if joined:
            part = slice(p * rows, (p + 1) * rows)
            total = kept[0][part, :].astype(F32) + got[0][part, :].astype(F32)
        else:
            total = kept[p][...].astype(F32) + got[p][...].astype(F32)
        scratch[p] = total.astype(BF)
        for i in range(kinds):
            if merge:
                target = outs[i].at[pl.ds(p * size, size)]
            else:
                target = outs[p + i * n_parts]
            start = (bits_ref[p] if i else 1 - bits_ref[p]) * size if split else 0
            source = scratch.at[p, pl.ds(pl.multiple_of(start, 8), size)]
            copies.append(pltpu.make_async_copy(source, target, sem.at[2 * p + i]))
            copies[-1].start()
    for copy in copies:
        copy.wait()


def join_halves(bits_ref, *refs, n_parts, rows, merged):
    n_in = 1 if merged else n_parts
    own, got, outs = refs[:n_in], refs[n_in : 2 * n_in], refs[2 * n_in : 2 * n_in + n_parts]
    sem = refs[2 * n_in + n_parts]
    copies = []
    for p in range(n_parts):
        for i, (group, which) in enumerate(((own, bits_ref[p]), (got, 1 - bits_ref[p]))):
            source = group[0].at[pl.ds(p * rows, rows)] if merged else group[p]
            span = pl.ds(pl.multiple_of(which * rows, 8), rows)
            copies.append(pltpu.make_async_copy(source, outs[p].at[span], sem.at[2 * p + i]))
            copies[-1].start()
    for copy in copies:
        copy.wait()


def put_wide(flat, tmp, values, rows, row):
    pairs = rows // 2
    for index, value in enumerate(values):
        tmp[pl.ds(index * D, rows), :] = value
    even = [tmp[pl.ds(i * D, pairs, stride=2), :] for i in range(Q_TILES)]
    odd = [flip(tmp[pl.ds(i * D + 1, pairs, stride=2), :]) for i in range(Q_TILES)]
    low = low_half(pairs)
    for c in range(4):
        flat[pl.ds(row + c, pairs, stride=9), :] = even[c]
    flat[pl.ds(row + 4, pairs, stride=9), :] = jnp.where(low, even[4], odd[0])
    for c in range(4):
        flat[pl.ds(row + 5 + c, pairs, stride=9), :] = jnp.where(low, odd[c], odd[c + 1])


def copy_array(source_ref, target_ref, sem):
    copy = pltpu.make_async_copy(source_ref, target_ref, sem)
    copy.start()
    copy.wait()


def update_rule(scale, rate, grad, master, momentum, average):
    weight_grad = grad * scale
    new_momentum = MOMENTUM_DECAY * momentum + weight_grad
    new_master = master - rate * (weight_grad + MOMENTUM_DECAY * new_momentum)
    new_average = AVERAGE_DECAY * average + (1.0 - AVERAGE_DECAY) * new_master
    return weight_grad, new_momentum, new_master, new_average


class Chunks:
    def __init__(self, rows, base, count, rule, refs):
        self.rows, self.base, self.count, self.rule = rows, base, count, rule
        self.ins, self.outs, self.in_buf, self.out_buf, self.in_sem, self.out_sem = refs
        self.size = rows * LANES

    def span(self, c):
        return pl.ds(pl.multiple_of((self.base + c * self.rows) * LANES, LANES), self.size)

    def place(self, index, start=0, length=None):
        start = pl.multiple_of(index * self.size + start, 8 * LANES)
        return pl.ds(start, self.size if length is None else length)

    def fetch(self, c):
        return [
            pltpu.make_async_copy(
                self.ins[i].at[self.span(c)],
                self.in_buf.at[self.place(c * 3 + i)],
                self.in_sem.at[c, i],
            )
            for i in range(3)
        ]

    def flush(self, c):
        return [
            pltpu.make_async_copy(
                self.out_buf.at[self.place(c * 4 + i)],
                self.outs[i].at[self.span(c)],
                self.out_sem.at[c, i],
            )
            for i in range(4)
        ]

    def start(self):
        def body(c, carry):
            for copy in self.fetch(c):
                copy.start()
            return carry

        lax.fori_loop(0, self.count, body, 0)

    def run(self, stage, gradient):
        sub = STEP * LANES

        def body(c, carry):
            stage(c)
            for copy in self.fetch(c):
                copy.wait()

            def step(s, inner):
                grad = gradient(c, s * STEP, STEP).reshape(sub)
                values = self.rule(
                    grad, *[self.in_buf[self.place(c * 3 + i, s * sub, sub)] for i in range(3)]
                )
                for i in range(4):
                    self.out_buf[self.place(c * 4 + i, s * sub, sub)] = values[i]
                return inner

            lax.fori_loop(0, self.rows // STEP, step, 0)
            for copy in self.flush(c):
                copy.start()
            return carry

        def drain(c, carry):
            for copy in self.flush(c):
                copy.wait()
            return carry

        lax.fori_loop(0, self.count, body, 0)
        return lambda: lax.fori_loop(0, self.count, drain, 0)


class Extra:
    def __init__(self, start, ins, outs, rest):
        self.bufs, self.sem = rest[:8], rest[8]
        count = self.bufs[0].shape[0]
        span = pl.ds(start, count)
        self.count = count
        self.loads = [
            pltpu.make_async_copy(ins[i].at[span], self.bufs[i], self.sem.at[i]) for i in range(3)
        ]
        self.stores = [
            pltpu.make_async_copy(self.bufs[3 + i], outs[i].at[span], self.sem.at[3 + i])
            for i in range(4)
        ]

    def start(self):
        for copy in self.loads:
            copy.start()

    def finish(self, grad, rule):
        for copy in self.loads:
            copy.wait()
        self.bufs[7][...] = grad.reshape(grad.shape[0] * LANES)
        values = rule(self.bufs[7][pl.ds(0, self.count)], *[self.bufs[i][...] for i in range(3)])
        for i in range(4):
            self.bufs[3 + i][...] = values[i]
            self.stores[i].start()

    def drain(self):
        for copy in self.stores:
            copy.wait()


def shifted(flat, row, count):
    here = flip(flat[pl.ds(row - 1, count), :])
    after = flip(flat[pl.ds(row, count), :])
    return jnp.where(low_half(count), here, after)


def load_parts(pieces, sem):
    copies = [
        pltpu.make_async_copy(source, target, sem.at[i]) for i, (source, target) in enumerate(pieces)
    ]
    for copy in copies:
        copy.start()
    return copies


FLAT_BASE = 8
TAIL_ZERO = HALF - (GATE_ROW + 11 * CHUNK) * LANES
TAIL_ONE = HALF - (6916 + 11 * CHUNK) * LANES


def update_first(scale, rate, core_ref, bits_ref, *rest):
    halves, ins, outs = rest[:4], rest[4:7], rest[7:11]
    early_ref, flat, in_buf, out_buf, in_sem, out_sem, part_sem = rest[11:18]
    refs = (ins, outs, in_buf, out_buf, in_sem, out_sem)
    core = core_ref[0]
    rule = functools.partial(update_rule, scale, rate)
    half = PART_ROWS // 2
    pieces = []
    for p in range(2):
        for i, which in enumerate((bits_ref[p], 1 - bits_ref[p])):
            span = pl.ds(pl.multiple_of(p * PART_ROWS + which * half, 8), half)
            pieces.append((halves[2 * p + i], early_ref.at[span]))
    copies = load_parts(pieces, part_sem)
    extra = Extra((GATE_ROW + 11 * CHUNK) * LANES, ins, outs, rest[18:])
    base = jnp.where(core == 0, GATE_ROW, 4)
    chunks = Chunks(CHUNK, base, 11 + core, rule, refs)
    chunks.start()

    @pl.when(core == 0)
    def _():
        extra.start()

    for copy in copies:
        copy.wait()
    flat[0:FLAT_BASE, :] = jnp.zeros((FLAT_BASE, LANES), F32)

    def stage(c):
        for t in range(FF_TILES):
            rows = pl.ds(pl.multiple_of(t * D + c * 48, 16), 48)
            flat[pl.ds(FLAT_BASE + t, 48, stride=FF_TILES), :] = early_ref[rows, :].astype(F32)

    def gradient(c, start, count):
        row = pl.multiple_of(FLAT_BASE + start, 8)
        return jnp.where(core == 0, flat[pl.ds(row, count), :], shifted(flat, row, count))

    def stage_next(c):
        flat[FLAT_BASE - 1 : FLAT_BASE, :] = flat[FLAT_BASE + CHUNK - 1 : FLAT_BASE + CHUNK, :]
        stage(c)

    drain = chunks.run(stage_next, gradient)

    @pl.when(core == 0)
    def _():
        stage(11)
        extra.finish(flat[FLAT_BASE : FLAT_BASE + CHUNK, :], rule)

    drain()

    @pl.when(core == 0)
    def _():
        extra.drain()


def lay_out_late(flat, tmp, late_ref):
    def late(index):
        return late_ref[index * D : (index + 1) * D, :].astype(F32)

    low1 = low_half(1)
    gain_a = late_ref[8 * D : 8 * D + 16, :].astype(F32)
    gain_m = flip(late_ref[8 * D + 16 : 8 * D + 32, :].astype(F32))
    for r in range(4):
        flat[r : r + 1, :] = gain_a[r : r + 1]
    flat[4:5, :] = jnp.where(low1, gain_a[4:5], gain_m[0:1])
    for r in range(4):
        flat[5 + r : 6 + r, :] = jnp.where(low1, gain_m[r : r + 1], gain_m[r + 1 : r + 2])
    put_wide(flat, tmp, [late(t) for t in range(Q_TILES)], D, 9)
    pairs = D // 2
    for t in range(3):
        tmp[pl.ds(t * D, D), :] = late(Q_TILES + t)
    even = [tmp[pl.ds(i * D, pairs, stride=2), :] for i in range(3)]
    odd = [tmp[pl.ds(i * D + 1, pairs, stride=2), :] for i in range(3)]
    low = low_half(pairs)
    turned = [flip(odd[0]), flip(odd[1]), flip(even[1]), flip(even[2])]
    rows = (
        (2601, even[0]),
        (2602, jnp.where(low, even[1], turned[0])),
        (2603, jnp.where(low, turned[0], turned[1])),
        (3465, jnp.where(low, turned[2], turned[3])),
        (3466, jnp.where(low, turned[3], odd[1])),
        (3467, odd[2]),
    )
    for row, value in rows:
        flat[pl.ds(row, pairs, stride=3), :] = value


def update_second(scale, rate, core_ref, bits_ref, *rest):
    halves, late_halves, ins, outs = rest[:8], rest[8:10], rest[10:13], rest[17:21]
    flat, tmp, part_ref, swap_ref, first_ref, in_buf, out_buf, in_sem, out_sem, part_sem = rest[21:31]
    refs = (ins, outs, in_buf, out_buf, in_sem, out_sem)
    tail = Extra((6916 + 11 * CHUNK) * LANES, ins, outs, rest[31:40])
    head = Extra(0, ins, outs, rest[40:49])
    late_flat, late_ref, late_in, late_out, late_in_sem, late_out_sem, late_sem = rest[49:56]
    late_last = Extra(LATE_CHUNKS * CHUNK * LANES, ins, outs, rest[56:])
    rule = functools.partial(update_rule, scale, rate)
    half = PART_ROWS // 2
    pieces = []
    for i in range(2):
        which = [1 - bits_ref[p] if i else bits_ref[p] for p in range(3)]

        def rows(start, p, size, which=which):
            return pl.ds(pl.multiple_of(start + which[p] * size, 16), size)

        source = halves[2 + i].at[pl.ds(half - REST_SLOT, REST_SLOT)]
        pieces.append((source, part_ref.at[rows(0, 1, REST_SLOT)]))
        pieces.append((halves[4 + i], part_ref.at[rows(2 * REST_SLOT, 2, half)]))
        pieces.append((halves[6 + i], swap_ref.at[rows(0, 2, half)]))
        pieces.append((halves[i].at[pl.ds(0, 16)], first_ref.at[rows(0, 0, 16)]))
    parts = load_parts(pieces, part_sem)

    @pl.when(core_ref[0] == 0)
    def _():
        def stage(c):
            values = []
            for t in range(Q_TILES):
                rows = pl.ds(pl.multiple_of(REST + t * D + c * 64, 16), 64)
                values.append(part_ref[rows, :].astype(F32))
            put_wide(flat, tmp, values, 64, FLAT_BASE)

        def gradient(c, start, count):
            return flat[pl.ds(pl.multiple_of(FLAT_BASE + start, 8), count), :]

        chunks = Chunks(CHUNK // 2, O_ROW, 9, rule, refs)
        late_refs = (ins, outs, late_in, late_out, late_in_sem, late_out_sem)
        late_chunks = Chunks(CHUNK, 0, LATE_CHUNKS, rule, late_refs)
        pieces = [
            (ref, late_ref.at[pl.ds(i * LATE_HALF, LATE_HALF)]) for i, ref in enumerate(late_halves)
        ]
        chunks.start()
        late_parts = load_parts(pieces, late_sem)
        late_chunks.start()
        late_last.start()
        for copy in parts:
            copy.wait()
        drain = chunks.run(stage, gradient)
        for copy in late_parts:
            copy.wait()
        lay_out_late(late_flat, tmp, late_ref)

        def late_gradient(c, start, count):
            return late_flat[pl.ds(pl.multiple_of(c * CHUNK + start, 8), count), :]

        late_drain = late_chunks.run(lambda c: None, late_gradient)
        start = LATE_CHUNKS * CHUNK
        late_last.finish(late_flat[start : start + 304, :], rule)
        drain()
        late_drain()
        late_last.drain()

    @pl.when(core_ref[0] == 1)
    def _():
        head.start()
        chunks = Chunks(CHUNK, 6916, 11, rule, refs)
        chunks.start()
        tail.start()
        for copy in parts:
            copy.wait()
        flat[0:FLAT_BASE, :] = jnp.zeros((FLAT_BASE, LANES), F32)
        flat[FLAT_BASE : FLAT_BASE + 8, :] = swap_ref[SWAP_TAIL : SWAP_TAIL + 16, :].astype(F32)[0:8]
        flat[FLAT_BASE + 5 : FLAT_BASE + 6, :] = first_ref[0:16, :].astype(F32)[0:1]
        head.finish(shifted(flat, FLAT_BASE + 1, 8), rule)
        row = FLAT_BASE + CHUNK - 1
        flat[row : row + 1, :] = part_ref[REST - 16 : REST, :].astype(F32)[15:16]

        def stage(c):
            flat[FLAT_BASE - 1 : FLAT_BASE, :] = flat[FLAT_BASE + CHUNK - 1 : FLAT_BASE + CHUNK, :]
            inside = c < DOWN_FIRST
            here = pl.ds(pl.multiple_of(SWAP_START + jnp.where(inside, c, 0) * D, 16), D)
            there = pl.ds(pl.multiple_of(REST + jnp.where(inside, 0, c - DOWN_FIRST) * D, 16), D)
            whole = jnp.where(inside, swap_ref[here, :].astype(F32), part_ref[there, :].astype(F32))
            pieces = [whole[i * LANES : (i + 1) * LANES].T for i in range(4)]
            half = jnp.concatenate([whole[4 * LANES :], jnp.zeros((LANES - HD, LANES), F32)], axis=0)
            put_wide(flat, tmp, pieces + [half.T], LANES, FLAT_BASE)

        def gradient(c, start, count):
            return shifted(flat, FLAT_BASE + start, count)

        drain = chunks.run(stage, gradient)
        stage(11)
        flat[FLAT_BASE + CHUNK :, :] = jnp.zeros((8, LANES), F32)
        tail.finish(shifted(flat, FLAT_BASE, CHUNK + 8), rule)
        head.drain()
        drain()
        tail.drain()


def vmem():
    return pl.BlockSpec(memory_space=pltpu.VMEM)


def smem():
    return pl.BlockSpec(memory_space=pltpu.SMEM)


def hbm():
    return pl.BlockSpec(memory_space=pl.ANY)


def call(kernel, outs, in_specs, out_specs, scratch, flops, name, limit, aliases=None):
    n_bytes = sum(math.prod(shape) * jnp.dtype(kind).itemsize for shape, kind in outs)
    return pl.pallas_call(
        kernel,
        out_shape=[jax.ShapeDtypeStruct(shape, kind) for shape, kind in outs],
        in_specs=in_specs,
        out_specs=out_specs,
        scratch_shapes=scratch,
        input_output_aliases=aliases or {},
        compiler_params=pltpu.CompilerParams(vmem_limit_bytes=limit * MIB),
        cost_estimate=pl.CostEstimate(
            flops=int(flops), bytes_accessed=int(2 * n_bytes), transcendentals=0
        ),
        name=name,
    )


def rope_tables(seq_len):
    lane = jnp.arange(LANES, dtype=jnp.int32)
    which = (lane % (HD // 2)).astype(F32)
    frequency = jnp.exp(which * (-2.0 * math.log(10000.0) / HD))
    angles = jnp.arange(seq_len, dtype=F32)[:, None] * frequency[None, :]
    sign = jnp.where(lane % HD < HD // 2, -1.0, 1.0)
    return jnp.cos(angles), jnp.sin(angles) * sign[None, :]


def run_prepare(core, own, other):
    outs = [
        ((1, D), F32),
        ((1, D), F32),
        ((D, PAD_D), BF),
        ((D, KV_COLS), BF),
        ((PAD_D, D), BF),
        ((D, FF), BF),
        ((D, FF), BF),
        ((FF, D), BF),
    ]
    scratch = [
        pltpu.VMEM((HALF,), F32),
        pltpu.VMEM((HALF,), F32),
        pltpu.VMEM((FLAT_SCRATCH, LANES), F32),
        pltpu.VMEM((Q_TILES * D + 8, LANES), F32),
        pltpu.VMEM((8 * LANES,), F32),
        pltpu.SemaphoreType.DMA((2,)),
    ]
    return call(
        prepare_weights,
        outs,
        [smem()] + [hbm()] * 2,
        [vmem()] * 8,
        scratch,
        1e10,
        "prepare_weights",
        56,
    )(core, own, other)


def run_attention_forward(x, gain, wq, wkv, wo, cosine, sine):
    seq_len = x.shape[0]
    outs = [
        ((seq_len, D), F32),
        ((seq_len, PAD_D), BF),
        ((Q_TILES, seq_len, LANES), BF),
        ((6, seq_len, LANES), BF),
        ((6, seq_len, LANES), BF),
        ((16, seq_len), F32),
    ]
    return call(
        attention_forward,
        outs,
        [vmem()] * 4 + [hbm()] + [vmem()] * 2,
        [hbm()] * 5 + [vmem()],
        [pltpu.VMEM(shape, kind) for shape, kind in outs[:5]]
        + [
            pltpu.VMEM((PAD_D, D), BF),
            pltpu.VMEM((Q_TILES, BLOCK, LANES), F32),
            pltpu.SemaphoreType.DMA((4,)),
            pltpu.SemaphoreType.DMA((seq_len // BLOCK, 2)),
        ],
        1.5e10,
        "attention_forward",
        56,
    )(x, gain, wq, wkv, wo, cosine, sine)


def run_mlp(core, slot, lengths, assignment, return_order, hidden1, cot, mixed, gain, wo, wg, wu, wd):
    seq_len = hidden1.shape[0]
    outs = [
        ((seq_len, D), BF),
        ((seq_len, D), F32),
        ((Q_TILES, seq_len, LANES), BF),
        ((1, D), F32),
        ((EARLY_ROWS, LANES), BF),
        ((EARLY_ROWS, LANES), BF),
    ]
    return call(
        mlp_pass,
        outs,
        [smem()] * 5 + [hbm()] * 3 + [vmem()] + [hbm()] * 4,
        [hbm()] * 3 + [vmem()] + [hbm()] * 2,
        [
            pltpu.VMEM((seq_len, D), F32),
            pltpu.VMEM((seq_len, D), BF),
            pltpu.VMEM((seq_len, PAD_D), BF),
            pltpu.VMEM((PAD_D, D), BF),
            pltpu.VMEM((D, FF), BF),
            pltpu.VMEM((D, FF), BF),
            pltpu.VMEM((FF, D), BF),
            pltpu.VMEM((seq_len, D), BF),
            pltpu.VMEM((seq_len, D), F32),
            pltpu.VMEM((Q_TILES, seq_len, LANES), BF),
            pltpu.VMEM((PAD_D, seq_len), BF),
            pltpu.VMEM((PAD_D, seq_len), BF),
            pltpu.VMEM((seq_len, FF), BF),
            pltpu.VMEM((seq_len, FF), BF),
            pltpu.VMEM((seq_len, FF), BF),
            pltpu.VMEM((seq_len, D), BF),
            pltpu.VMEM((2, EARLY_ROWS, LANES), BF),
            pltpu.SemaphoreType.DMA((7,)),
            pltpu.SemaphoreType.DMA((seq_len // MLP_BLOCK, 3)),
            pltpu.SemaphoreType.DMA((FF_TILES // 2 + 1, 2)),
        ],
        2.5e10,
        "mlp_pass",
        56,
    )(core, slot, lengths, assignment, return_order, hidden1, cot, mixed, gain, wo, wg, wu, wd)


def run_backward_groups(first, count, q, dm, k, v, lse):
    seq_len = q.shape[1]
    fixed = pl.BlockSpec((Q_TILES, seq_len, LANES), lambda i: (0, 0, 0))
    sides = pl.BlockSpec((2, seq_len, LANES), lambda i: (first + i, 0, 0))
    single = pl.BlockSpec((1, seq_len, LANES), lambda i: (i, 0, 0))
    outs = [(count, 2, seq_len, LANES), (count, seq_len, LANES), (count, seq_len, LANES)]
    return pl.pallas_call(
        functools.partial(backward_groups, first),
        grid=(count,),
        out_shape=[jax.ShapeDtypeStruct(shape, F32) for shape in outs],
        in_specs=[
            fixed,
            fixed,
            sides,
            sides,
            pl.BlockSpec((16, seq_len), lambda i: (0, 0)),
        ],
        out_specs=[
            pl.BlockSpec((1, 2, seq_len, LANES), lambda i: (i, 0, 0, 0)),
            single,
            single,
        ],
        scratch_shapes=[pltpu.VMEM((2, seq_len, LANES), F32)] * 2,
        compiler_params=pltpu.CompilerParams(vmem_limit_bytes=56 * MIB),
        cost_estimate=pl.CostEstimate(
            flops=int(8e9) * count, bytes_accessed=int(3e6) * count, transcendentals=0
        ),
        name="backward_groups",
    )(q, dm, k, v, lse)


def run_backward_finish(x, gain, dh1, groups, wq, wkv, cosine, sine):
    seq_len = x.shape[0]
    outs = [
        ((seq_len, D), BF),
        ((seq_len, PAD_D), BF),
        ((seq_len, KV_COLS), BF),
        ((seq_len, D), BF),
        ((1, D), F32),
    ]
    return call(
        backward_finish,
        outs,
        [hbm(), vmem()] + [hbm()] * 7 + [vmem()] * 2 + [hbm()] * 2,
        [hbm()] * 4 + [vmem()],
        [
            pltpu.VMEM(value.shape, value.dtype)
            for value in (x, dh1, cosine, sine, *groups[0], *groups[1])
        ]
        + [pltpu.VMEM(shape, kind) for shape, kind in outs[:4]]
        + [
            pltpu.SemaphoreType.DMA((seq_len // BLOCK, 10)),
            pltpu.SemaphoreType.DMA((seq_len // BLOCK, 4)),
        ],
        4e9,
        "backward_finish",
        56,
    )(x, gain, dh1, *groups[0], *groups[1], wq, wkv, cosine, sine)


def run_late_weights(core, normed, d_query, d_kv, gga, ggm):
    outs = [((LATE_HALF, LANES), BF), ((LATE_HALF, LANES), BF)]
    return call(
        late_weights,
        outs,
        [smem()] + [vmem()] * 5,
        [hbm()] * 2,
        [pltpu.VMEM((2 * LATE_HALF, LANES), BF), pltpu.SemaphoreType.DMA((2,))],
        4e9,
        "late_weights",
        56,
    )(core, normed, d_query, d_kv, gga, ggm)


def run_sum(bits, kept, got, split, merge=False, n_parts=None):
    joined = n_parts is not None
    n_parts = n_parts or len(kept)
    rows = kept[0].shape[0] // (n_parts if joined else 1)
    kinds = 2 if split else 1
    n_out = 1 if merge else n_parts
    out_rows = rows // kinds * (n_parts if merge else 1)
    results = call(
        functools.partial(
            gather_sum, n_parts=n_parts, rows=rows, split=split, merge=merge, joined=joined
        ),
        [((out_rows, LANES), BF)] * (kinds * n_out),
        [smem()] + [vmem()] * (2 * len(kept)),
        [hbm()] * (kinds * n_out),
        [pltpu.VMEM((n_parts, rows, LANES), BF), pltpu.SemaphoreType.DMA((2 * n_parts,))],
        1e6,
        "gather_sum",
        12,
    )(bits, *kept, *got)
    return list(results[:n_out]), list(results[n_out:])


def run_join(bits, own, got, n_parts):
    merged = len(own) < n_parts
    rows = own[0].shape[0] // (n_parts if merged else 1)
    return call(
        functools.partial(join_halves, n_parts=n_parts, rows=rows, merged=merged),
        [((2 * rows, LANES), BF)] * n_parts,
        [smem()] + [hbm()] * (2 * len(own)),
        [hbm()] * n_parts,
        [pltpu.SemaphoreType.DMA((2 * n_parts,))],
        1e6,
        "join_halves",
        4,
    )(bits, *own, *got)


def run_copy(value):
    outs = [(value.shape, value.dtype)]
    scratch = [pltpu.SemaphoreType.DMA]
    return call(copy_array, outs, [hbm()], [hbm()], scratch, 1e6, "copy_array", 4)(value)[0]


def chunk_scratch(count):
    return [
        pltpu.VMEM((3 * count * CHUNK * LANES,), F32),
        pltpu.VMEM((4 * count * CHUNK * LANES,), F32),
        pltpu.SemaphoreType.DMA((12, 3)),
        pltpu.SemaphoreType.DMA((12, 4)),
    ]


def extra_scratch(count, n_rows):
    bufs = [pltpu.VMEM((count,), F32)] * 7 + [pltpu.VMEM((n_rows * LANES,), F32)]
    return bufs + [pltpu.SemaphoreType.DMA((7,))]


def run_update_first(scale, rate, core, bits, halves, state):
    scratch = [
        pltpu.VMEM((2 * PART_ROWS, LANES), BF),
        pltpu.VMEM((FLAT_BASE + CHUNK + 16, LANES), F32),
        *chunk_scratch(12),
        pltpu.SemaphoreType.DMA((4,)),
        *extra_scratch(TAIL_ZERO, CHUNK),
    ]
    return call(
        functools.partial(update_first, scale, rate),
        [(state[0].shape, F32)] * 4,
        [smem()] * 2 + [hbm()] * 7,
        [hbm()] * 4,
        scratch,
        1e9,
        "update_first",
        56,
    )(core, bits, *halves, *state)


def run_update_second(scale, rate, core, bits, halves, late_halves, state, done):
    scratch = [
        pltpu.VMEM((FLAT_BASE + CHUNK + 8, LANES), F32),
        pltpu.VMEM((Q_TILES * D + 8, LANES), F32),
        pltpu.VMEM((2 * REST_SLOT + PART_ROWS, LANES), BF),
        pltpu.VMEM((PART_ROWS, LANES), BF),
        pltpu.VMEM((32, LANES), BF),
        *chunk_scratch(11),
        pltpu.SemaphoreType.DMA((8,)),
        *extra_scratch(TAIL_ONE, CHUNK + 8),
        *extra_scratch(5 * LANES, 8),
        pltpu.VMEM((4336, LANES), F32),
        pltpu.VMEM((2 * LATE_HALF, LANES), BF),
        *chunk_scratch(LATE_CHUNKS),
        pltpu.SemaphoreType.DMA((2,)),
        *extra_scratch((O_ROW - LATE_CHUNKS * CHUNK) * LANES, 304),
    ]
    return call(
        functools.partial(update_second, scale, rate),
        [(state[0].shape, F32)] * 4,
        [smem()] * 2 + [hbm()] * 17,
        [hbm()] * 4,
        scratch,
        1e9,
        "update_second",
        56,
        {15 + i: i for i in range(4)},
    )(core, bits, *halves, *late_halves, *state, *done)


def add_low(a, b):
    return (a.astype(F32) + b.astype(F32)).astype(BF)


def xor_swap(value, bit):
    size = lax.axis_size("dp")
    return lax.ppermute(value, "dp", [(i, i ^ (1 << bit)) for i in range(size)])


def tie(value, *others):
    return lax.optimization_barrier((value, *others))


def my_bits(orders, step):
    index = lax.axis_index("dp")
    return jnp.stack([(index >> order[step]) & 1 for order in orders]).astype(jnp.int32)


def near_size():
    return min(lax.axis_size("dp"), 4)


def spread(blocks):
    size, near = lax.axis_size("dp"), near_size()
    groups = [[g * near + i for i in range(near)] for g in range(size // near)]
    return lax.all_to_all(
        blocks, "dp", split_axis=0, concat_axis=0, tiled=True, axis_index_groups=groups
    )


def scatter_sum(value):
    count = near_size()
    blocks = spread(value.reshape(count, value.shape[0] // count, LANES))
    return jnp.sum(blocks.astype(F32), axis=0).astype(BF)


def bit_orders():
    n_bits = lax.axis_size("dp").bit_length() - 1
    base = list(range(n_bits))
    head = base[:3] if n_bits >= 3 else base
    return [head[r:] + head[:r] + base[len(head) :] for r in range(3)]


def on_device(inputs, cotangent, lengths, assignment, return_order, master, momentum, average):
    nseq_all, block_rows, _ = inputs.shape
    axes = ("dp", "shard")
    seq_len = block_rows * lax.axis_size("dp") * lax.axis_size("shard")
    my_slot = lax.axis_index(axes)
    core = lax.axis_index("shard")
    core_arr = core.astype(jnp.int32).reshape(1)

    seq_ids = jnp.arange(nseq_all, dtype=jnp.int32)
    sequence = jnp.sum(
        jnp.where(return_order[:, None] == seq_ids[None, :], assignment[None, :], 0), axis=1
    )

    def pick(array, index):
        return array.at[index].get(mode="promise_in_bounds")

    def exchange(value):
        return lax.all_to_all(value, axes, split_axis=0, concat_axis=0, tiled=True)

    x = exchange(pick(inputs, sequence)).reshape(seq_len, D)
    slot_arr = my_slot.astype(jnp.int32).reshape(1)

    other = lax.ppermute(master, "shard", [(0, 1), (1, 0)])
    gain_attn, gain_mlp, wq, wkv, wo, wg, wu, wd = run_prepare(core_arr, master, other)

    cosine, sine = rope_tables(seq_len)
    sent_cot, gain_attn, cosine = tie(cotangent, gain_attn, cosine)
    cot = exchange(sent_cot).reshape(seq_len, D)
    hidden1, mixed, q, k, v, lse = run_attention_forward(x, gain_attn, wq, wkv, wo, cosine, sine)
    result, dh1, dm, ggm, early_keep, early_send = run_mlp(
        core_arr, slot_arr, lengths, assignment, return_order, hidden1, cot, mixed, gain_mlp, wo, wg, wu, wd
    )
    back_out = exchange(result.reshape(nseq_all, block_rows, D))

    orders = bit_orders()
    n_bits = len(orders[0])

    def swap_parts(parts, step):
        return [xor_swap(part, order[step]) for part, order in zip(parts, orders)]

    got = lax.ppermute(early_send, "shard", [(0, 1), (1, 0)])
    groups = [run_backward_groups(0, 1, q, dm, k, v, lse)]
    lse, got = tie(lse, got)
    sent, kept = run_sum(my_bits(orders, 0), [early_keep], [got], True, n_parts=3)
    lse, *kept = tie(lse, *kept)
    got = swap_parts(sent, 0)
    groups.append(run_backward_groups(1, KV - 1, q, dm, k, v, lse))
    sent, kept = run_sum(my_bits(orders, 1), kept, got, True)
    dh1, back_out, *kept = tie(dh1, back_out, *kept)
    got = swap_parts(sent, 1)
    d_stream, d_query, d_kv, normed, gga = run_backward_finish(
        x, gain_attn, dh1, groups, wq, wkv, cosine, sine
    )
    last_bit = n_bits - 1
    for step in range(2, n_bits):
        if step > 2:
            got = swap_parts(sent, step - 1)
        sent, kept = run_sum(my_bits(orders, step), kept, got, True, merge=step == last_bit)
        if step == 2:
            gga, *kept = tie(gga, *kept)
            late_keep, late_send = run_late_weights(core_arr, normed, d_query, d_kv, gga, ggm)
            late_send, *kept = tie(late_send, *kept)
        if step == last_bit:
            late_send, sent[0] = tie(late_send, sent[0])
    got = [xor_swap(sent[0], last_bit)]
    late_got = lax.ppermute(late_send, "shard", [(0, 1), (1, 0)])
    late, _ = run_sum(my_bits(orders, 0)[:1], [late_keep], [late_got], False)
    late, block_output, *got = tie(late[0], run_copy(back_out), *got)
    early, _ = run_sum(my_bits(orders, last_bit)[:1], kept, got, False)
    late = scatter_sum(late)
    got = xor_swap(early[0], last_bit)
    late, got = tie(late, got)
    early = run_join(my_bits(orders, last_bit), early, [got], 3)
    far_bits = list(range(near_size().bit_length() - 1, n_bits))

    def add_far(late, early):
        late, *early = tie(late, *early)
        return add_low(late, xor_swap(late, far_bits.pop(0))), early

    for step in reversed(range(1, last_bit)):
        if far_bits:
            late, early = add_far(late, early)
        got = swap_parts(early, step)
        late, *got = tie(late, *got)
        early = run_join(my_bits(orders, step), early, got, 3)
    while far_bits:
        late, early = add_far(late, early)
    late, *early = tie(late, *early)
    late = spread(jnp.broadcast_to(late[None], (near_size(), *late.shape))).reshape(-1, LANES)
    got = swap_parts(early, 0)
    swap_own = lax.ppermute(early[2], "shard", [(0, 1)])
    bits = my_bits(orders, 0)
    scale = 1.0 / nseq_all
    rate = (nseq_all / (0.6 * seq_len)) ** 0.5 / D**0.5
    state = (master, momentum, average)
    d_stream, late, swap_own, *got = tie(d_stream, late, swap_own, *got)
    back_grad = exchange(d_stream.reshape(nseq_all, block_rows, D))
    late_other = lax.ppermute(late, "shard", [(1, 0)])
    swap_got = lax.ppermute(got[2], "shard", [(0, 1)])
    halves = [early[0], got[0], early[1], got[1], early[2], got[2], swap_own, swap_got]
    done = run_update_first(scale, rate, core_arr, bits, halves[:4], state)
    weight_grad, new_momentum, new_master, new_average = run_update_second(
        scale, rate, core_arr, bits, halves, (late, late_other), state, done
    )
    return (block_output, back_grad, weight_grad, new_momentum, new_master, new_average)


def solution(mesh):
    rows = P(None, ("dp", "shard"), None)
    flat = P("shard")
    return jax.shard_map(
        on_device,
        mesh=mesh,
        in_specs=(rows, rows, P(), P(), P(), flat, flat, flat),
        out_specs=(rows, rows, flat, flat, flat, flat),
        check_vma=False,
    )
```
